32 devices in a mesh: dp: 8 (over z, x), mp: 4 (over y, core).
Axes of the slice: x: 2, y: 2, z: 4, core: 2. Of those that a mesh axis runs over, the one named last changes fastest.
Arguments:
- tokens: bfloat16 [4096, 2048], P('dp'), may hold values from -6 to 6
- cotangent: bfloat16 [4096, 2048], P('dp'), may hold values from -6 to 6
- doc_ids: int32 [4096], P('dp'), may hold values from 0 to 1, as said below
- row_ids: int32 [8], P('dp'), may hold values from 0 to 2, as said below
- offsets: int32 [8], P('dp'), may hold values from 0 to 1536, as said below
- w_query: bfloat16 [2048, 2048], P(None, 'mp'), may hold values from -0.125 to 0.125
- w_key: bfloat16 [2048, 2048], P(None, 'mp'), may hold values from -0.125 to 0.125
- w_value: bfloat16 [2048, 2048], P(None, 'mp'), may hold values from -0.125 to 0.125
- w_output: bfloat16 [2048, 2048], P('mp'), may hold values from -0.125 to 0.125
- w_gate: bfloat16 [2048, 8192], P(None, 'mp'), may hold values from -0.125 to 0.125
- w_up: bfloat16 [2048, 8192], P(None, 'mp'), may hold values from -0.125 to 0.125
- w_down: bfloat16 [8192, 2048], P('mp'), may hold values from -0.0625 to 0.0625
- gain_query: float32 [16, 128], P('mp'), may hold values from 0.1 to 1.9
- gain_key: float32 [16, 128], P('mp'), may hold values from 0.1 to 1.9
- gain_attn: float32 [16, 128], replicated, may hold values from 0.1 to 1.9
- gain_mlp: float32 [16, 128], replicated, may hold values from 0.1 to 1.9
Outputs:
- output: bfloat16 [4096, 2048], P('dp')
- grad_tokens: bfloat16 [4096, 2048], P('dp')
- grad_w_query: float32 [2048, 2048], P('dp', 'mp')
- grad_w_key: float32 [2048, 2048], P('dp', 'mp')
- grad_w_value: float32 [2048, 2048], P('dp', 'mp')
- grad_w_output: float32 [2048, 2048], P('mp', 'dp')
- grad_w_gate: float32 [2048, 8192], P('dp', 'mp')
- grad_w_up: float32 [2048, 8192], P('dp', 'mp')
- grad_w_down: float32 [8192, 2048], P('mp', 'dp')
- grad_gain_query: float32 [16, 128], P('mp', 'dp')
- grad_gain_key: float32 [16, 128], P('mp', 'dp')
- grad_gain_attn: float32 [16, 128], P(None, 'dp')
- grad_gain_mlp: float32 [16, 128], P(None, 'dp')
The draws below stay inside these ranges and needn't reach their ends.
Inputs may be any that keep to these rules, and one draw needn't show every extreme that they name: Index i of dp holds 512 consecutive tokens of row row_ids[i]. Rows 0 and 1 have 1024 tokens, row 2 has 2048, and every block of 512 tokens of every row is held by exactly one index. offsets[i] is the position in its row of the first token of index i; it is a multiple of 512. `doc_ids`: within a row, the document number is 0 at the row's first position and never falls; from one position to the next it rises by 0 or 1. The last position of row 2 has the largest number.
All inputs are finite; a program needn't handle non-finite values.
Results may differ from the reference program's by a relative error of at most 0.025.
Values may be sent and summed in bfloat16 or wider, within the bound.
A program may use at most 192 MiB of HBM per device.

```python
import math
import jax
import jax.numpy as jnp
from jax import lax

D = 2048
HEADS = 16
HD = 128
FF = 8192
TOK_DEV = 512
TOKENS = 4096
ROW_SHORT = 1024
ROW_LONG = 2048
DOC_MEAN = 1536


def span_order(key):
    span_count = TOKENS // TOK_DEV
    return jax.random.permutation(jax.random.fold_in(key, 7), span_count).astype(jnp.int32)


def draw_row_ids(key, part):
    spans = span_order(key)
    quarter = ROW_SHORT // TOK_DEV
    return jnp.where(spans < quarter, 0, jnp.where(spans < 2 * quarter, 1, 2)).astype(jnp.int32)


def draw_offsets(key, part):
    spans = span_order(key)
    quarter = ROW_SHORT // TOK_DEV
    within = jnp.where(spans < quarter, spans, jnp.where(spans < 2 * quarter, spans - quarter, spans - 2 * quarter))
    return (within * TOK_DEV).astype(jnp.int32)


def draw_doc_ids(key, part):
    spans = span_order(key)
    places = jnp.arange(TOKENS, dtype=jnp.int32)
    row_index = jnp.where(places < ROW_SHORT, 0, jnp.where(places < 2 * ROW_SHORT, 1, 2)).astype(jnp.int32)
    row_start = jnp.where(row_index == 0, 0, jnp.where(row_index == 1, ROW_SHORT, 2 * ROW_SHORT)).astype(jnp.int32)
    within = places - row_start
    segment = within // DOC_MEAN
    remain = within % DOC_MEAN
    segment_count = ROW_LONG // DOC_MEAN + 1
    last_remain = (ROW_LONG - 1) % DOC_MEAN
    jitter = jax.random.randint(jax.random.fold_in(key, 11), (3, segment_count), 0, last_remain + 1).astype(jnp.int32)
    jitter = jitter * (jnp.arange(segment_count, dtype=jnp.int32) > 0).astype(jnp.int32)[None, :]
    numbers = segment - (remain < jitter[row_index, segment]).astype(jnp.int32)
    source = (spans[:, None] * TOK_DEV + jnp.arange(TOK_DEV, dtype=jnp.int32)[None, :]).reshape(TOKENS)
    return numbers[source].astype(jnp.int32)


def block_levels(own_key, dims, pieces, smallest, high):
    loudness, own = 1.0, jax.random.fold_in(own_key, 6)
    for position, blocks in pieces:
        draws = jnp.exp(jax.random.uniform(jax.random.fold_in(own, position), (blocks,), jnp.float32, smallest / len(pieces), high / len(pieces)))
        loudness = loudness * jnp.repeat(draws, dims[position] // blocks).reshape([-1 if axis == position else 1 for axis in range(len(dims))])
    return loudness


def gaussian(rng, dims, scale, most, shards=(), kind=jnp.bfloat16):
    values = scale * jax.random.normal(rng, dims, jnp.float32)
    if shards:
        values = values * block_levels(rng, dims, shards, -0.22, 0.18)
    return jnp.clip(values, -most, most).astype(kind)


def setup_inputs(seed: int = 0) -> dict:
    key_list = jax.random.split(jax.random.key(seed), 17)
    tokens = gaussian(key_list[0], (TOKENS, D), 1.0, 6.0, ((0, 8),))
    cotangent = gaussian(key_list[1], (TOKENS, D), 1.0, 6.0, ((0, 8),))
    doc_ids = draw_doc_ids(jax.random.fold_in(key_list[16], 71), 0)
    row_ids = draw_row_ids(jax.random.fold_in(key_list[16], 71), 0)
    offsets = draw_offsets(jax.random.fold_in(key_list[16], 71), 0)
    w_query = gaussian(key_list[5], (D, D), D ** -0.5, 0.125, ((1, 4),))
    w_key = gaussian(key_list[6], (D, D), D ** -0.5, 0.125, ((1, 4),))
    w_value = gaussian(key_list[7], (D, D), D ** -0.5, 0.125, ((1, 4),))
    w_output = gaussian(key_list[8], (D, D), D ** -0.5, 0.125, ((0, 4),))
    w_gate = gaussian(key_list[9], (D, FF), D ** -0.5, 0.125, ((1, 4),))
    w_up = gaussian(key_list[10], (D, FF), D ** -0.5, 0.125, ((1, 4),))
    w_down = gaussian(key_list[11], (FF, D), FF ** -0.5, 0.0625, ((0, 4),))
    gain_query = jnp.clip(1.0 + 0.18 * jax.random.normal(key_list[12], (HEADS, HD), jnp.float32), 0.1, 1.9)
    gain_key = jnp.clip(1.0 + 0.18 * jax.random.normal(key_list[13], (HEADS, HD), jnp.float32), 0.1, 1.9)
    gain_attn = jnp.clip(1.0 + 0.18 * jax.random.normal(key_list[14], (HEADS, HD), jnp.float32), 0.1, 1.9)
    gain_mlp = jnp.clip(1.0 + 0.18 * jax.random.normal(key_list[15], (HEADS, HD), jnp.float32), 0.1, 1.9)
    return dict(tokens=tokens, cotangent=cotangent, doc_ids=doc_ids, row_ids=row_ids, offsets=offsets, w_query=w_query, w_key=w_key, w_value=w_value, w_output=w_output, w_gate=w_gate, w_up=w_up, w_down=w_down, gain_query=gain_query, gain_key=gain_key, gain_attn=gain_attn, gain_mlp=gain_mlp)


epsilon = 1e-06
rope_base = 500000.0
masked_score = -1e+30
highest = lax.Precision.HIGHEST

@jax.custom_vjp
def low(v):
    return lax.optimization_barrier(v.astype(jnp.bfloat16)).astype(jnp.float32)

@jax.custom_vjp
def low_back(v):
    return v

def low_keep(v):
    return (low(v), None)

def low_pass(kept, grad):
    return (grad,)

def back_keep(v):
    return (v, None)

def back_low(kept, grad):
    return (low(grad),)
low.defvjp(low_keep, low_pass)
low_back.defvjp(back_keep, back_low)

def rms_rows(values):
    return values * lax.rsqrt(lax.optimization_barrier(jnp.mean(values * values, axis=-1, keepdims=True)) + epsilon)

def rope_tables(positions, head_width):
    freqs = rope_base ** (-jnp.arange(0, head_width // 2, dtype=jnp.float32) * 2.0 / head_width)
    angles = positions.astype(jnp.float32)[:, None] * freqs[None, :]
    return (jnp.cos(angles)[:, None, :], jnp.sin(angles)[:, None, :])

def rotate(values, cosines, sines):
    half = values.shape[-1] // 2
    first = values[..., :half]
    second = values[..., half:]
    return jnp.concatenate([first * cosines - second * sines, second * cosines + first * sines], axis=-1)

def query_block(queries, keys, values, labels, positions, index, block_rows):
    start = index * block_rows
    block_q = lax.dynamic_slice_in_dim(queries, start, block_rows, 0)
    block_labels = lax.dynamic_slice_in_dim(labels, start, block_rows, 0)
    block_positions = lax.dynamic_slice_in_dim(positions, start, block_rows, 0)
    scores = jnp.einsum('qhd,khd->hqk', block_q, keys, precision=highest) * (1.0 / math.sqrt(HD))
    scores = low_back(scores)
    allowed = (block_labels[:, None] == labels[None, :]) & (block_positions[:, None] >= positions[None, :])
    scores = jnp.where(allowed[None], scores, masked_score)
    probs = jax.nn.softmax(scores, axis=-1)
    return jnp.einsum('hqk,khd->qhd', low(probs), values, precision=highest)

def reference(tokens, cotangent, doc_ids, row_ids, offsets, w_query, w_key, w_value, w_output, w_gate, w_up, w_down, gain_query, gain_key, gain_attn, gain_mlp):
    token_count = tokens.shape[0]
    places = jnp.arange(token_count, dtype=jnp.int32)
    owner = places // TOK_DEV
    positions = (offsets[owner] + places % TOK_DEV).astype(jnp.int32)
    labels = (row_ids[owner] * token_count + doc_ids).astype(jnp.int32)
    cosines, sines = rope_tables(positions, HD)
    block_rows = math.gcd(token_count, 512)
    block_count = token_count // block_rows
    indices = jnp.arange(block_count, dtype=jnp.int32)
    checked_block = jax.checkpoint(query_block, static_argnums=(6,))

    def layer_forward(x_in, wq, wk, wv, wo, wg, wu, wd, gq, gk, ga, gm):
        q_raw = low_back(jnp.dot(x_in, wq, precision=highest))
        k_raw = low_back(jnp.dot(x_in, wk, precision=highest))
        v_all = low(low_back(jnp.dot(x_in, wv, precision=highest)))
        q_n = rms_rows(q_raw) * gq.reshape(-1)
        k_n = rms_rows(k_raw) * gk.reshape(-1)
        queries = low(rotate(q_n.reshape(token_count, HEADS, HD), cosines, sines))
        keys = low(rotate(k_n.reshape(token_count, HEADS, HD), cosines, sines))
        values = v_all.reshape(token_count, HEADS, HD)
        attended = lax.map(lambda index: checked_block(queries, keys, values, labels, positions, index, block_rows), indices)
        attended = low(low_back(attended.reshape(token_count, D)))
        attn = low_back(jnp.dot(attended, wo, precision=highest))
        hidden = x_in + rms_rows(attn) * ga.reshape(-1)
        hidden_low = low(hidden)
        gate = low_back(jnp.dot(hidden_low, wg, precision=highest))
        up_val = low_back(jnp.dot(hidden_low, wu, precision=highest))
        act = low(jax.nn.silu(gate) * up_val)
        mlp = low_back(jnp.dot(act, wd, precision=highest))
        return hidden + rms_rows(mlp) * gm.reshape(-1)
    primals = (tokens.astype(jnp.float32), w_query.astype(jnp.float32), w_key.astype(jnp.float32), w_value.astype(jnp.float32), w_output.astype(jnp.float32), w_gate.astype(jnp.float32), w_up.astype(jnp.float32), w_down.astype(jnp.float32), gain_query.astype(jnp.float32), gain_key.astype(jnp.float32), gain_attn.astype(jnp.float32), gain_mlp.astype(jnp.float32))
    result, pullback = jax.vjp(layer_forward, *primals)
    grads = pullback(cotangent.astype(jnp.float32))
    return (result.astype(jnp.bfloat16), grads[0].astype(jnp.bfloat16), grads[1], grads[2], grads[3], grads[4], grads[5], grads[6], grads[7], grads[8], grads[9], grads[10], grads[11])
```

```python
import functools
import math

import jax
import jax.numpy as jnp
from jax import lax
from jax.experimental import pallas as pl
from jax.experimental.pallas import tpu as pltpu
from jax.sharding import PartitionSpec as P

epsilon = 1e-06
rope_base = 500000.0
masked_score = -1e30


def rope_tables(positions, head_width):
    freqs = rope_base ** (-jnp.arange(0, head_width // 2, dtype=jnp.float32) * 2.0 / head_width)
    angles = positions.astype(jnp.float32)[:, None] * freqs[None, :]
    return (jnp.cos(angles)[:, None, :], jnp.sin(angles)[:, None, :])


def rotate(values, cosines, sines):
    half = values.shape[-1] // 2
    first = values[..., :half]
    second = values[..., half:]
    return jnp.concatenate(
        [first * cosines - second * sines, second * cosines + first * sines], axis=-1
    )


def norm_back(grad_normed, normed, factor):
    return factor * (grad_normed - normed * jnp.mean(grad_normed * normed, axis=-1, keepdims=True))


def on_device_general(
    tokens,
    cotangent,
    doc_ids,
    row_ids,
    offsets,
    w_query,
    w_key,
    w_value,
    w_output,
    w_gate,
    w_up,
    w_down,
    gain_query,
    gain_key,
    gain_attn,
    gain_mlp,
):
    f32 = jnp.float32
    bf16 = jnp.bfloat16
    row_count = tokens.shape[0]
    model_width = tokens.shape[1]
    heads_here = gain_query.shape[0]
    head_width = gain_query.shape[1]
    local_width = heads_here * head_width
    groups = lax.axis_size("dp")
    key_rows = row_count * groups
    block_rows = min(key_rows, row_count * max(1, 512 // row_count))
    block_count = key_rows // block_rows
    score_scale = 1.0 / math.sqrt(head_width)
    positions = offsets[0] + jnp.arange(row_count, dtype=jnp.int32)
    labels = row_ids[0] * key_rows + doc_ids
    cosines, sines = rope_tables(positions, head_width)
    q_raw = jnp.dot(tokens, w_query, preferred_element_type=f32)
    k_raw = jnp.dot(tokens, w_key, preferred_element_type=f32)
    v_raw = jnp.dot(tokens, w_value, preferred_element_type=f32)
    squares = lax.psum(
        jnp.stack([jnp.sum(q_raw * q_raw, axis=1), jnp.sum(k_raw * k_raw, axis=1)]), "mp"
    )
    q_factor = lax.rsqrt(squares[0] / model_width + epsilon)[:, None]
    k_factor = lax.rsqrt(squares[1] / model_width + epsilon)[:, None]
    g_query = gain_query.reshape(local_width)
    g_key = gain_key.reshape(local_width)
    q_normed = q_raw * q_factor
    k_normed = k_raw * k_factor
    queries = rotate(
        (q_normed * g_query).reshape(row_count, heads_here, head_width), cosines, sines
    ).astype(bf16)
    keys_low = rotate(
        (k_normed * g_key).reshape(row_count, heads_here, head_width), cosines, sines
    ).astype(bf16)
    values_low = v_raw.astype(bf16)
    all_keys, all_values, all_labels, all_positions = (
        lax.all_gather(keys_low.reshape(row_count, local_width), "dp", axis=0, tiled=True),
        lax.all_gather(values_low, "dp", axis=0, tiled=True),
        lax.all_gather(labels, "dp", axis=0, tiled=True),
        lax.all_gather(positions, "dp", axis=0, tiled=True),
    )
    key_blocks = all_keys.reshape(block_count, block_rows, heads_here, head_width)
    value_blocks = all_values.reshape(block_count, block_rows, heads_here, head_width)
    label_blocks = all_labels.reshape(block_count, block_rows)
    position_blocks = all_positions.reshape(block_count, block_rows)
    scanned = (key_blocks, value_blocks, label_blocks, position_blocks)
    low_label = jnp.min(labels)
    high_label = jnp.max(labels)

    def scores_of(key_block, label_block, position_block):
        scores = (
            jnp.einsum("qhd,khd->hqk", queries, key_block, preferred_element_type=f32) * score_scale
        )
        allowed = (labels[:, None] == label_block[None, :]) & (
            positions[:, None] >= position_block[None, :]
        )
        return (scores, allowed[None])

    def touches(label_block):
        return (jnp.max(label_block) >= low_label) & (jnp.min(label_block) <= high_label)

    def max_step(carry, blocks_in):
        key_block, value_block, label_block, position_block = blocks_in

        def max_live_block(state):
            running, totals = state
            scores, allowed = scores_of(key_block, label_block, position_block)
            highest = jnp.maximum(
                running, jnp.max(jnp.where(allowed, scores, masked_score), axis=2)
            )
            weights = jnp.where(allowed, jnp.exp(scores - highest[:, :, None]), 0.0)
            return (highest, totals * jnp.exp(running - highest) + jnp.sum(weights, axis=2))

        return (lax.cond(touches(label_block), max_live_block, lambda state: state, carry), None)

    start_state = (
        jnp.full((heads_here, row_count), masked_score, f32),
        jnp.zeros((heads_here, row_count), f32),
    )
    (running_max, running_total), _ = lax.scan(max_step, start_state, scanned)
    log_total = running_max + jnp.log(running_total)

    def value_step(accum, blocks_in):
        key_block, value_block, label_block, position_block = blocks_in

        def value_live_block(current):
            scores, allowed = scores_of(key_block, label_block, position_block)
            probs_low = jnp.where(allowed, jnp.exp(scores - log_total[:, :, None]), 0.0).astype(
                bf16
            )
            return current + jnp.einsum(
                "hqk,khd->qhd", probs_low, value_block, preferred_element_type=f32
            )

        return (
            lax.cond(touches(label_block), value_live_block, lambda current: current, accum),
            None,
        )

    attended, _ = lax.scan(value_step, jnp.zeros((row_count, heads_here, head_width), f32), scanned)
    attended_low = attended.reshape(row_count, local_width).astype(bf16)
    attn_sum = lax.psum(
        jnp.dot(attended_low, w_output, preferred_element_type=f32).astype(jnp.bfloat16), "mp"
    ).astype(jnp.float32)
    attn_factor = lax.rsqrt(jnp.mean(attn_sum * attn_sum, axis=1, keepdims=True) + epsilon)
    attn_normed = attn_sum * attn_factor
    g_attn = gain_attn.reshape(model_width)
    hidden = tokens.astype(f32) + attn_normed * g_attn
    hidden_low = hidden.astype(bf16)
    gate_val = jnp.dot(hidden_low, w_gate, preferred_element_type=f32)
    up_val = jnp.dot(hidden_low, w_up, preferred_element_type=f32)
    sigmoid_gate = jax.nn.sigmoid(gate_val)
    silu_gate = gate_val * sigmoid_gate
    act_low = (silu_gate * up_val).astype(bf16)
    mlp_sum = lax.psum(
        jnp.dot(act_low, w_down, preferred_element_type=f32).astype(jnp.bfloat16), "mp"
    ).astype(jnp.float32)
    mlp_factor = lax.rsqrt(jnp.mean(mlp_sum * mlp_sum, axis=1, keepdims=True) + epsilon)
    mlp_normed = mlp_sum * mlp_factor
    g_mlp = gain_mlp.reshape(model_width)
    output = (hidden + mlp_normed * g_mlp).astype(bf16)
    grad_out = cotangent.astype(f32)
    grad_gain_mlp = jnp.sum(grad_out * mlp_normed, axis=0)
    grad_mlp = norm_back(grad_out * g_mlp, mlp_normed, mlp_factor).astype(bf16)
    grad_w_down = jnp.einsum("tf,td->fd", act_low, grad_mlp, preferred_element_type=f32)
    grad_act = jnp.einsum("td,fd->tf", grad_mlp, w_down, preferred_element_type=f32)
    slope = sigmoid_gate * (1.0 + gate_val * (1.0 - sigmoid_gate))
    grad_gate = (grad_act * up_val * slope).astype(bf16)
    grad_up = (grad_act * silu_gate).astype(bf16)
    branch_grad = jnp.einsum(
        "tf,df->td", grad_gate, w_gate, preferred_element_type=f32
    ) + jnp.einsum("tf,df->td", grad_up, w_up, preferred_element_type=f32)
    grad_hidden = grad_out + lax.psum(branch_grad.astype(jnp.bfloat16), "mp").astype(jnp.float32)
    grad_gain_attn = jnp.sum(grad_hidden * attn_normed, axis=0)
    grad_attn = norm_back(grad_hidden * g_attn, attn_normed, attn_factor).astype(bf16)
    grad_w_output = jnp.einsum("tc,td->cd", attended_low, grad_attn, preferred_element_type=f32)
    grad_attended = (
        jnp.einsum("td,cd->tc", grad_attn, w_output, preferred_element_type=f32)
        .astype(bf16)
        .reshape(row_count, heads_here, head_width)
    )
    delta = jnp.sum(grad_attended.astype(f32) * attended, axis=2).T

    def grad_step(grad_q, blocks_in):
        key_block, value_block, label_block, position_block = blocks_in

        def grad_live_block(current):
            scores, allowed = scores_of(key_block, label_block, position_block)
            probs = jnp.where(allowed, jnp.exp(scores - log_total[:, :, None]), 0.0)
            grad_probs = jnp.einsum(
                "qhd,khd->hqk", grad_attended, value_block, preferred_element_type=f32
            )
            grad_scores = (probs * (grad_probs - delta[:, :, None])).astype(bf16)
            value_term = jnp.einsum(
                "hqk,qhd->khd", probs.astype(bf16), grad_attended, preferred_element_type=f32
            )
            key_term = jnp.einsum("hqk,qhd->khd", grad_scores, queries, preferred_element_type=f32)
            updated = current + jnp.einsum(
                "hqk,khd->qhd", grad_scores, key_block, preferred_element_type=f32
            )
            return (updated, (key_term, value_term))

        def skip_block(current):
            nothing = jnp.zeros((block_rows, heads_here, head_width), f32)
            return (current, (nothing, nothing))

        return lax.cond(touches(label_block), grad_live_block, skip_block, grad_q)

    grad_queries, (key_terms, value_terms) = lax.scan(
        grad_step, jnp.zeros((row_count, heads_here, head_width), f32), scanned
    )
    grad_keys, grad_values = (
        lax.psum_scatter(
            (key_terms.reshape(key_rows, local_width) * score_scale).astype(jnp.bfloat16),
            "dp",
            scatter_dimension=0,
            tiled=True,
        ).astype(jnp.float32),
        lax.psum_scatter(
            value_terms.reshape(key_rows, local_width).astype(jnp.bfloat16),
            "dp",
            scatter_dimension=0,
            tiled=True,
        ).astype(jnp.float32),
    )
    grad_values_low = grad_values.astype(bf16)
    back_q = rotate(grad_queries * score_scale, cosines, -sines).reshape(row_count, local_width)
    back_k = rotate(grad_keys.reshape(row_count, heads_here, head_width), cosines, -sines).reshape(
        row_count, local_width
    )
    grad_gain_query = jnp.sum(back_q * q_normed, axis=0).reshape(heads_here, head_width)
    grad_gain_key = jnp.sum(back_k * k_normed, axis=0).reshape(heads_here, head_width)
    scaled_q = back_q * g_query
    scaled_k = back_k * g_key
    inner = lax.psum(
        jnp.stack([jnp.sum(scaled_q * q_normed, axis=1), jnp.sum(scaled_k * k_normed, axis=1)]),
        "mp",
    )
    grad_q_raw = (q_factor * (scaled_q - q_normed * inner[0][:, None] / model_width)).astype(bf16)
    grad_k_raw = (k_factor * (scaled_k - k_normed * inner[1][:, None] / model_width)).astype(bf16)
    input_term = (
        jnp.einsum("tc,dc->td", grad_q_raw, w_query, preferred_element_type=f32)
        + jnp.einsum("tc,dc->td", grad_k_raw, w_key, preferred_element_type=f32)
        + jnp.einsum("tc,dc->td", grad_values_low, w_value, preferred_element_type=f32)
    )
    grad_tokens = (
        grad_hidden + lax.psum(input_term.astype(jnp.bfloat16), "mp").astype(jnp.float32)
    ).astype(bf16)
    local_w_query = jnp.einsum("td,tc->dc", tokens, grad_q_raw, preferred_element_type=f32)
    local_w_key = jnp.einsum("td,tc->dc", tokens, grad_k_raw, preferred_element_type=f32)
    local_w_value = jnp.einsum("td,tc->dc", tokens, grad_values_low, preferred_element_type=f32)
    local_w_gate = jnp.einsum("td,tf->df", hidden_low, grad_gate, preferred_element_type=f32)
    local_w_up = jnp.einsum("td,tf->df", hidden_low, grad_up, preferred_element_type=f32)
    grad_w_query, grad_w_key, grad_w_value, grad_w_gate, grad_w_up = (
        lax.psum_scatter(
            local_w_query.astype(jnp.bfloat16), "dp", scatter_dimension=0, tiled=True
        ).astype(jnp.float32),
        lax.psum_scatter(
            local_w_key.astype(jnp.bfloat16), "dp", scatter_dimension=0, tiled=True
        ).astype(jnp.float32),
        lax.psum_scatter(
            local_w_value.astype(jnp.bfloat16), "dp", scatter_dimension=0, tiled=True
        ).astype(jnp.float32),
        lax.psum_scatter(
            local_w_gate.astype(jnp.bfloat16), "dp", scatter_dimension=0, tiled=True
        ).astype(jnp.float32),
        lax.psum_scatter(
            local_w_up.astype(jnp.bfloat16), "dp", scatter_dimension=0, tiled=True
        ).astype(jnp.float32),
    )
    summed_out, summed_down, summed_gq, summed_gk, summed_ga, summed_gm = (
        lax.psum_scatter(
            grad_w_output.astype(jnp.bfloat16), "dp", scatter_dimension=1, tiled=True
        ).astype(jnp.float32),
        lax.psum_scatter(
            grad_w_down.astype(jnp.bfloat16), "dp", scatter_dimension=1, tiled=True
        ).astype(jnp.float32),
        lax.psum_scatter(
            grad_gain_query.astype(jnp.bfloat16), "dp", scatter_dimension=1, tiled=True
        ).astype(jnp.float32),
        lax.psum_scatter(
            grad_gain_key.astype(jnp.bfloat16), "dp", scatter_dimension=1, tiled=True
        ).astype(jnp.float32),
        lax.psum_scatter(
            grad_gain_attn.reshape(gain_attn.shape).astype(jnp.bfloat16),
            "dp",
            scatter_dimension=1,
            tiled=True,
        ).astype(jnp.float32),
        lax.psum_scatter(
            grad_gain_mlp.reshape(gain_mlp.shape).astype(jnp.bfloat16),
            "dp",
            scatter_dimension=1,
            tiled=True,
        ).astype(jnp.float32),
    )
    return (
        output,
        grad_tokens,
        grad_w_query,
        grad_w_key,
        grad_w_value,
        summed_out,
        grad_w_gate,
        grad_w_up,
        summed_down,
        summed_gq,
        summed_gk,
        summed_ga,
        summed_gm,
    )


line = 4
pair = 2
low_score = -1e30
start_max = -1e20


def line_shift(value, step):
    moves = [
        (z * pair + x, ((z + step) % line) * pair + x) for z in range(line) for x in range(pair)
    ]
    return lax.ppermute(value, "dp", moves)


def line_send(value, moves):
    return lax.ppermute(
        value, "dp", [(a * pair + x, b * pair + x) for a, b in moves for x in range(pair)]
    )


def x_swap(value):
    return lax.ppermute(value, "dp", [(i, i ^ 1) for i in range(line * pair)])


def core_swap(value):
    return lax.ppermute(value, "mp", [(i, i ^ 1) for i in range(4)])


def y_swap(value):
    return lax.ppermute(value, "mp", [(i, i ^ 2) for i in range(4)])


def token_sum(value):
    half = value.shape[1] // 2
    arrived = core_swap(value)
    value = value + jnp.concatenate([arrived[:, half:], arrived[:, :half]], axis=1)
    return value + y_swap(value)


def reduce_own_rows(partial_low):
    f32 = jnp.float32
    half = partial_low.shape[0] // 2
    arrived = core_swap(partial_low[half:])
    chip_sum = (partial_low[:half].astype(f32) + arrived.astype(f32)).astype(jnp.bfloat16)
    return chip_sum.astype(f32) + y_swap(chip_sum).astype(f32)


def share_rows(own):
    return jnp.concatenate([own, core_swap(own)], axis=0)


def line_scatter(terms, axis, z):
    f32 = jnp.float32
    bf16 = jnp.bfloat16
    width = terms.shape[axis] // line

    def block(index):
        return lax.dynamic_slice_in_dim(terms, index * width, width, axis)

    right, left = None, None
    for step in range(1, line):
        right_term = block(lax.rem(2 * line - step + z, line))
        left_term = block(lax.rem(step + z, line))
        if right is not None:
            right_term = (right_term.astype(f32) + right.astype(f32)).astype(bf16)
            left_term = (left_term.astype(f32) + left.astype(f32)).astype(bf16)
        right = line_send(right_term, [(a, a + 1) for a in range(step)])
        left = line_send(left_term, [(line - 1 - a, line - 2 - a) for a in range(step)])
    return block(z).astype(f32) + right.astype(f32) + left.astype(f32)


def own_columns(value, x):
    width = value.shape[1] // (line * pair)
    return jnp.concatenate(
        [
            lax.dynamic_slice_in_dim(value, (z * pair + x) * width, width, 1)
            for z in range(line)
        ],
        axis=1,
    )


def dot_t(first, second):
    return lax.dot_general(
        first, second, (((0,), (0,)), ((), ())), preferred_element_type=jnp.float32
    )


def dot_nt(first, second):
    return lax.dot_general(
        first, second, (((1,), (1,)), ((), ())), preferred_element_type=jnp.float32
    )


def visible_scores(key, query, key_code, query_code, query_low, factor):
    scores = dot_nt(key, query) * factor
    codes = jnp.concatenate([key_code] * (query.shape[0] // key_code.shape[1]), axis=1)
    return jnp.where((codes <= query_code) & (codes >= query_low), scores, low_score)


def attend_kernel(factor, *refs):
    live, codes, rows = refs[0], refs[1], refs[2]
    query_refs = refs[3:7]
    pair_refs = refs[7:15]
    out_turned, out_log = refs[15], refs[16]
    out_refs = refs[17:21]
    top, total, accum = refs[21:24]
    f32 = jnp.float32
    bf16 = jnp.bfloat16
    for q in range(line):
        top[...] = jnp.full_like(top, start_max)
        total[...] = jnp.zeros_like(total)
        accum[...] = jnp.zeros_like(accum)
        for k in range(2 * line):

            @pl.when(live[q, k] > 0)
            def _(q=q, k=k):
                scores = visible_scores(
                    pair_refs[k][0],
                    query_refs[q][...],
                    codes[k],
                    rows[q : q + 1, :],
                    rows[line + q : line + q + 1, :],
                    factor,
                )
                highest = jnp.maximum(top[...], jnp.max(scores, axis=0, keepdims=True))
                weights = jnp.exp2(scores - highest)
                fade = jnp.exp2(top[...] - highest)
                total[...] = total[...] * fade + jnp.sum(weights, axis=0, keepdims=True)
                accum[...] = accum[...] * fade + dot_t(pair_refs[k][1], weights.astype(bf16))
                top[...] = highest

        turned = accum[...] / total[...]
        out_turned[q] = turned
        out_log[q : q + 1, :] = top[...] + jnp.log2(total[...])
        out_refs[q][...] = turned.T.astype(bf16)


def attend_back_kernel(factor, scale, *refs):
    live, codes, rows = refs[0], refs[1], refs[2]
    query_refs = refs[3:7]
    pair_refs = refs[7:15]
    turned, log_total = refs[15], refs[16]
    grad_refs = refs[17:21]
    out_query = refs[21:25]
    out_pairs = refs[25:33]
    key_sum, value_sum, query_sum = refs[33:36]
    f32 = jnp.float32
    bf16 = jnp.bfloat16
    key_sum[...] = jnp.zeros_like(key_sum)
    value_sum[...] = jnp.zeros_like(value_sum)
    for q in range(line):
        query_sum[...] = jnp.zeros_like(query_sum)
        delta = jnp.sum(
            grad_refs[q][...].astype(f32).T * turned[q], axis=0, keepdims=True
        )
        for k in range(2 * line):

            @pl.when(live[q, k] > 0)
            def _(q=q, k=k, delta=delta):
                query, key, grad = query_refs[q][...], pair_refs[k][0], grad_refs[q][...]
                scores = visible_scores(
                    key,
                    query,
                    codes[k],
                    rows[q : q + 1, :],
                    rows[line + q : line + q + 1, :],
                    factor,
                )
                probs = jnp.exp2(scores - log_total[q : q + 1, :])
                grad_probs = dot_nt(pair_refs[k][1], grad)
                grad_scores = (probs * (grad_probs - delta)).astype(bf16)
                value_sum[k] += jnp.dot(
                    probs.astype(bf16), grad, preferred_element_type=f32
                )
                key_sum[k] += jnp.dot(grad_scores, query, preferred_element_type=f32)
                query_sum[...] += dot_t(key, grad_scores)

        out_query[q][...] = (query_sum[...] * scale).T.astype(bf16)
    for k in range(2 * line):
        out_pairs[k][0] = (key_sum[k] * scale).astype(bf16)
        out_pairs[k][1] = value_sum[k].astype(bf16)


def vmem_specs(count):
    return [pl.BlockSpec(memory_space=pltpu.VMEM)] * count


def attend(live, codes, rows, queries, pairs):
    count, width = queries[0].shape
    factor = math.log2(math.e) / math.sqrt(width)
    f32 = jnp.float32
    return pl.pallas_call(
        functools.partial(attend_kernel, factor),
        out_shape=[
            jax.ShapeDtypeStruct((line, width, count), f32),
            jax.ShapeDtypeStruct((2 * line, count), f32),
        ]
        + [jax.ShapeDtypeStruct((count, width), jnp.bfloat16)] * line,
        in_specs=[pl.BlockSpec(memory_space=pltpu.SMEM)] + vmem_specs(2 + 3 * line),
        out_specs=vmem_specs(2 + line),
        scratch_shapes=[
            pltpu.VMEM((1, count), f32),
            pltpu.VMEM((1, count), f32),
            pltpu.VMEM((width, count), f32),
        ],
        compiler_params=pltpu.CompilerParams(vmem_limit_bytes=40 << 20),
        cost_estimate=pl.CostEstimate(
            flops=10 * 4 * count * count * width,
            bytes_accessed=8 << 20,
            transcendentals=10 * count * count,
        ),
    )(live, codes, rows, *queries, *pairs)


def attend_back(live, codes, rows, queries, pairs, turned, log_total, grads):
    count, width = queries[0].shape
    scale = 1.0 / math.sqrt(width)
    factor = math.log2(math.e) * scale
    f32 = jnp.float32
    return pl.pallas_call(
        functools.partial(attend_back_kernel, factor, scale),
        out_shape=[jax.ShapeDtypeStruct((count, width), jnp.bfloat16)] * line
        + [jax.ShapeDtypeStruct((2, count, width), jnp.bfloat16)] * (2 * line),
        in_specs=[pl.BlockSpec(memory_space=pltpu.SMEM)] + vmem_specs(4 + 4 * line),
        out_specs=vmem_specs(3 * line),
        scratch_shapes=[
            pltpu.VMEM((2 * line, count, width), f32),
            pltpu.VMEM((2 * line, count, width), f32),
            pltpu.VMEM((width, count), f32),
        ],
        compiler_params=pltpu.CompilerParams(vmem_limit_bytes=40 << 20),
        cost_estimate=pl.CostEstimate(
            flops=10 * 10 * count * count * width,
            bytes_accessed=12 << 20,
            transcendentals=10 * count * count,
        ),
    )(live, codes, rows, *queries, *pairs, turned, log_total, *grads)


def on_device_lines(
    tokens,
    cotangent,
    doc_ids,
    row_ids,
    offsets,
    w_query,
    w_key,
    w_value,
    w_output,
    w_gate,
    w_up,
    w_down,
    gain_query,
    gain_key,
    gain_attn,
    gain_mlp,
):
    f32 = jnp.float32
    bf16 = jnp.bfloat16
    row_count, model_width = tokens.shape
    heads_here, head_width = gain_query.shape
    local_width = heads_here * head_width
    half_rows = row_count // 2
    key_rows = row_count * line * pair
    place = lax.axis_index("dp")
    z, x = place // pair, lax.rem(place, pair)
    core = lax.rem(lax.axis_index("mp"), 2)

    def own_rows(value):
        return lax.dynamic_slice_in_dim(value, core * half_rows, half_rows, 0)

    def other_rows(value):
        return lax.dynamic_slice_in_dim(value, (1 - core) * half_rows, half_rows, 0)

    def reorder(value):
        return jnp.concatenate([own_rows(value), other_rows(value)], axis=0)

    def restore(own, other):
        whole = jnp.zeros((row_count,) + own.shape[1:], own.dtype)
        whole = lax.dynamic_update_slice_in_dim(whole, own, core * half_rows, 0)
        return lax.dynamic_update_slice_in_dim(whole, other, (1 - core) * half_rows, 0)

    own_tokens = own_rows(tokens)
    tokens_in = reorder(tokens)
    positions = reorder(offsets[0] + jnp.arange(row_count, dtype=jnp.int32))
    labels = reorder(row_ids[0] * key_rows + doc_ids)

    code = labels * key_rows + positions
    line_codes = [code] + [line_shift(code, d) for d in range(1, line)]
    line_codes = jnp.stack(line_codes)
    all_codes = jnp.concatenate([line_codes, x_swap(line_codes)], axis=0)
    query_low = (line_codes // key_rows) * key_rows
    code_rows = jnp.concatenate([line_codes, query_low], axis=0)
    code_columns = jnp.broadcast_to(all_codes[:, :, None], (2 * line, row_count, 128))
    live = (
        (jnp.min(all_codes, axis=1)[None, :] <= jnp.max(line_codes, axis=1)[:, None])
        & (jnp.max(all_codes, axis=1)[None, :] >= jnp.min(query_low, axis=1)[:, None])
    ).astype(jnp.int32)

    freqs = rope_base ** (-jnp.arange(0, head_width // 2, dtype=f32) * 2.0 / head_width)
    angles = positions.astype(f32)[:, None] * freqs[None, :]
    cosines, sines = jnp.cos(angles), jnp.sin(angles)
    cosines = jnp.concatenate([cosines, cosines], axis=1)
    sines = jnp.concatenate([-sines, sines], axis=1)

    def turn(value, sign_sines):
        swapped = jnp.concatenate(
            [value[:, head_width // 2 :], value[:, : head_width // 2]], axis=1
        )
        return value * cosines + swapped * sign_sines

    other_half_tokens = x_swap(own_columns(own_tokens, 1 - x))
    tokens_half = own_columns(tokens_in, x)
    tokens_half_x = share_rows(other_half_tokens)

    q_raw = jnp.dot(tokens_in, w_query, preferred_element_type=f32)
    k_raw = jnp.dot(tokens_in, w_key, preferred_element_type=f32)
    values_low = jnp.dot(tokens_in, w_value, preferred_element_type=f32).astype(bf16)
    squares = token_sum(
        jnp.stack([jnp.sum(q_raw * q_raw, axis=1), jnp.sum(k_raw * k_raw, axis=1)])
    )
    q_factor = lax.rsqrt(squares[0] / model_width + epsilon)[:, None]
    k_factor = lax.rsqrt(squares[1] / model_width + epsilon)[:, None]
    g_query = gain_query.reshape(1, local_width)
    g_key = gain_key.reshape(1, local_width)
    q_normed = q_raw * q_factor
    k_normed = k_raw * k_factor

    def head_of(value, d):
        return lax.dynamic_slice_in_dim(
            value, lax.rem(z + d, line) * head_width, head_width, 1
        )

    queries, pairs = [], []
    for d in range(line):
        query = turn(head_of(q_normed * g_query, d), sines).astype(bf16)
        key = turn(head_of(k_normed * g_key, d), sines).astype(bf16)
        both = jnp.stack([key, head_of(values_low, d)])
        queries.append(query if d == 0 else line_shift(query, d))
        pairs.append(both if d == 0 else line_shift(both, d))
    pairs = pairs + [x_swap(both) for both in pairs]

    turned, log_total, *attended_out = attend(live, code_columns, code_rows, queries, pairs)

    def gather_heads(pieces):
        home = [pieces[0]] + [line_shift(pieces[d], line - d) for d in range(1, line)]
        twice = jnp.concatenate(home + home, axis=1)
        return lax.dynamic_slice_in_dim(
            twice, lax.rem(line - z, line) * head_width, local_width, 1
        )

    attended_low = gather_heads(attended_out)
    attended_x = x_swap(attended_low)
    attn_sum = reduce_own_rows(
        jnp.dot(attended_low, w_output, preferred_element_type=f32).astype(bf16)
    )
    attn_factor = lax.rsqrt(jnp.mean(attn_sum * attn_sum, axis=1, keepdims=True) + epsilon)
    attn_normed = attn_sum * attn_factor
    g_attn = gain_attn.reshape(1, model_width)
    hidden = own_tokens.astype(f32) + attn_normed * g_attn
    own_hidden_low = hidden.astype(bf16)
    hidden_low = share_rows(own_hidden_low)
    hidden_half = own_columns(hidden_low, x)
    hidden_half_x = share_rows(x_swap(own_columns(own_hidden_low, 1 - x)))

    gate_val = jnp.dot(hidden_low, w_gate, preferred_element_type=f32)
    up_val = jnp.dot(hidden_low, w_up, preferred_element_type=f32)
    sigmoid_gate = jax.nn.sigmoid(gate_val)
    silu_gate = gate_val * sigmoid_gate
    act_low = (silu_gate * up_val).astype(bf16)
    act_x = x_swap(act_low)
    mlp_sum = reduce_own_rows(
        jnp.dot(act_low, w_down, preferred_element_type=f32).astype(bf16)
    )
    mlp_factor = lax.rsqrt(jnp.mean(mlp_sum * mlp_sum, axis=1, keepdims=True) + epsilon)
    mlp_normed = mlp_sum * mlp_factor
    g_mlp = gain_mlp.reshape(1, model_width)
    own_output = (hidden + mlp_normed * g_mlp).astype(bf16)
    output = restore(own_output, core_swap(own_output))

    grad_out = own_rows(cotangent).astype(f32)
    grad_gain_mlp = jnp.sum(grad_out * mlp_normed, axis=0)
    own_grad_mlp = norm_back(grad_out * g_mlp, mlp_normed, mlp_factor).astype(bf16)
    grad_mlp = share_rows(own_grad_mlp)
    grad_mlp_half = own_columns(grad_mlp, x)
    grad_mlp_half_x = share_rows(x_swap(own_columns(own_grad_mlp, 1 - x)))
    grad_act = dot_nt(grad_mlp, w_down)
    slope = sigmoid_gate * (1.0 + gate_val * (1.0 - sigmoid_gate))
    grad_gate = (grad_act * up_val * slope).astype(bf16)
    grad_up = (grad_act * silu_gate).astype(bf16)
    grad_gate_x = x_swap(grad_gate)
    grad_up_x = x_swap(grad_up)
    branch_sum = reduce_own_rows(
        (dot_nt(grad_gate, w_gate) + dot_nt(grad_up, w_up)).astype(bf16)
    )

    terms_down = (dot_t(act_low, grad_mlp_half) + dot_t(act_x, grad_mlp_half_x)).astype(bf16)
    terms_gate = (dot_t(hidden_half, grad_gate) + dot_t(hidden_half_x, grad_gate_x)).astype(bf16)
    terms_up = (dot_t(hidden_half, grad_up) + dot_t(hidden_half_x, grad_up_x)).astype(bf16)
    grad_w_down = line_scatter(terms_down, 1, z)
    grad_w_gate = line_scatter(terms_gate, 0, z)
    grad_w_up = line_scatter(terms_up, 0, z)

    grad_hidden = grad_out + branch_sum
    grad_gain_attn = jnp.sum(grad_hidden * attn_normed, axis=0)
    own_grad_attn = norm_back(grad_hidden * g_attn, attn_normed, attn_factor).astype(bf16)
    grad_attn = share_rows(own_grad_attn)
    grad_attn_half = own_columns(grad_attn, x)
    grad_attn_half_x = share_rows(x_swap(own_columns(own_grad_attn, 1 - x)))
    grad_attended = dot_nt(grad_attn, w_output).astype(bf16)
    grads = [
        head_of(grad_attended, d) if d == 0 else line_shift(head_of(grad_attended, d), d)
        for d in range(line)
    ]
    terms_out = (
        dot_t(attended_low, grad_attn_half) + dot_t(attended_x, grad_attn_half_x)
    ).astype(bf16)
    grad_w_output = line_scatter(terms_out, 1, z)

    back = attend_back(live, code_columns, code_rows, queries, pairs, turned, log_total, grads)
    grad_query_pieces, grad_pairs = back[:line], back[line:]
    grad_queries = gather_heads(grad_query_pieces).astype(f32)
    summed_pairs = [
        (grad_pairs[d].astype(f32) + x_swap(grad_pairs[line + d]).astype(f32)).astype(bf16)
        for d in range(line)
    ]
    home = [summed_pairs[0]] + [line_shift(summed_pairs[d], line - d) for d in range(1, line)]

    def place_heads(index):
        twice = jnp.concatenate([piece[index] for piece in home + home], axis=1)
        return lax.dynamic_slice_in_dim(
            twice, lax.rem(line - z, line) * head_width, local_width, 1
        )

    grad_keys = place_heads(0).astype(f32)
    grad_values_low = place_heads(1)

    def turn_back(value):
        return jnp.concatenate(
            [
                turn(value[:, h * head_width : (h + 1) * head_width], -sines)
                for h in range(heads_here)
            ],
            axis=1,
        )

    back_q = turn_back(grad_queries)
    back_k = turn_back(grad_keys)
    grad_gain_query = jnp.sum(back_q * q_normed, axis=0)
    grad_gain_key = jnp.sum(back_k * k_normed, axis=0)
    scaled_q = back_q * g_query
    scaled_k = back_k * g_key
    inner = token_sum(
        jnp.stack([jnp.sum(scaled_q * q_normed, axis=1), jnp.sum(scaled_k * k_normed, axis=1)])
    )
    grad_q_raw = (q_factor * (scaled_q - q_normed * inner[0][:, None] / model_width)).astype(bf16)
    grad_k_raw = (k_factor * (scaled_k - k_normed * inner[1][:, None] / model_width)).astype(bf16)
    grad_raw = jnp.concatenate([grad_q_raw, grad_k_raw, grad_values_low], axis=1)
    grad_raw_x = x_swap(grad_raw)
    input_sum = reduce_own_rows(
        (
            dot_nt(grad_q_raw, w_query)
            + dot_nt(grad_k_raw, w_key)
            + dot_nt(grad_values_low, w_value)
        ).astype(bf16)
    )
    own_grad_tokens = (grad_hidden + input_sum).astype(bf16)
    grad_tokens = restore(own_grad_tokens, core_swap(own_grad_tokens))
    terms_raw = (dot_t(tokens_half, grad_raw) + dot_t(tokens_half_x, grad_raw_x)).astype(bf16)
    summed_raw = line_scatter(terms_raw, 0, z)

    wide = jnp.concatenate([grad_gain_attn, grad_gain_mlp])
    wide = wide + core_swap(wide)
    gains = jnp.concatenate([wide, grad_gain_query, grad_gain_key])
    gains = gains + x_swap(gains)
    for flip in (1, 2):
        gains = gains + line_send(gains, [(a, a ^ flip) for a in range(line)])
    piece = head_width // (line * pair)

    def gain_piece(start, rows):
        part = gains[start : start + rows * head_width].reshape(rows, head_width)
        return lax.dynamic_slice_in_dim(part, place * piece, piece, 1)

    all_heads = model_width // head_width
    return (
        output,
        grad_tokens,
        summed_raw[:, :local_width],
        summed_raw[:, local_width : 2 * local_width],
        summed_raw[:, 2 * local_width :],
        grad_w_output,
        grad_w_gate,
        grad_w_up,
        grad_w_down,
        gain_piece(2 * model_width, heads_here),
        gain_piece(2 * model_width + local_width, heads_here),
        gain_piece(0, all_heads),
        gain_piece(model_width, all_heads),
    )


def solution(mesh):
    tuned = mesh.shape["dp"] == line * pair and mesh.shape["mp"] == 4
    body = on_device_lines if tuned else on_device_general
    return jax.shard_map(
        body,
        mesh=mesh,
        in_specs=(
            P("dp", None),
            P("dp", None),
            P("dp"),
            P("dp"),
            P("dp"),
            P(None, "mp"),
            P(None, "mp"),
            P(None, "mp"),
            P("mp", None),
            P(None, "mp"),
            P(None, "mp"),
            P("mp", None),
            P("mp", None),
            P("mp", None),
            P(),
            P(),
        ),
        out_specs=(
            P("dp", None),
            P("dp", None),
            P("dp", "mp"),
            P("dp", "mp"),
            P("dp", "mp"),
            P("mp", "dp"),
            P("dp", "mp"),
            P("dp", "mp"),
            P("mp", "dp"),
            P("mp", "dp"),
            P("mp", "dp"),
            P(None, "dp"),
            P(None, "dp"),
        ),
        check_vma=False,
    )
```

```python
import functools
import math

import jax
import jax.numpy as jnp
from jax import lax
from jax.experimental import pallas as pl
from jax.experimental.pallas import tpu as pltpu
from jax.sharding import PartitionSpec as P

epsilon = 1e-06
rope_base = 500000.0
masked_score = -1e30


def rope_tables(positions, head_width):
    freqs = rope_base ** (-jnp.arange(0, head_width // 2, dtype=jnp.float32) * 2.0 / head_width)
    angles = positions.astype(jnp.float32)[:, None] * freqs[None, :]
    return (jnp.cos(angles)[:, None, :], jnp.sin(angles)[:, None, :])


def rotate(values, cosines, sines):
    half = values.shape[-1] // 2
    first = values[..., :half]
    second = values[..., half:]
    return jnp.concatenate(
        [first * cosines - second * sines, second * cosines + first * sines], axis=-1
    )


def norm_back(grad_normed, normed, factor):
    return factor * (grad_normed - normed * jnp.mean(grad_normed * normed, axis=-1, keepdims=True))


def on_device_general(
    tokens,
    cotangent,
    doc_ids,
    row_ids,
    offsets,
    w_query,
    w_key,
    w_value,
    w_output,
    w_gate,
    w_up,
    w_down,
    gain_query,
    gain_key,
    gain_attn,
    gain_mlp,
):
    f32 = jnp.float32
    bf16 = jnp.bfloat16
    row_count = tokens.shape[0]
    model_width = tokens.shape[1]
    heads_here = gain_query.shape[0]
    head_width = gain_query.shape[1]
    local_width = heads_here * head_width
    groups = lax.axis_size("dp")
    key_rows = row_count * groups
    block_rows = min(key_rows, row_count * max(1, 512 // row_count))
    block_count = key_rows // block_rows
    score_scale = 1.0 / math.sqrt(head_width)
    positions = offsets[0] + jnp.arange(row_count, dtype=jnp.int32)
    labels = row_ids[0] * key_rows + doc_ids
    cosines, sines = rope_tables(positions, head_width)
    q_raw = jnp.dot(tokens, w_query, preferred_element_type=f32)
    k_raw = jnp.dot(tokens, w_key, preferred_element_type=f32)
    v_raw = jnp.dot(tokens, w_value, preferred_element_type=f32)
    squares = lax.psum(
        jnp.stack([jnp.sum(q_raw * q_raw, axis=1), jnp.sum(k_raw * k_raw, axis=1)]), "mp"
    )
    q_factor = lax.rsqrt(squares[0] / model_width + epsilon)[:, None]
    k_factor = lax.rsqrt(squares[1] / model_width + epsilon)[:, None]
    g_query = gain_query.reshape(local_width)
    g_key = gain_key.reshape(local_width)
    q_normed = q_raw * q_factor
    k_normed = k_raw * k_factor
    queries = rotate(
        (q_normed * g_query).reshape(row_count, heads_here, head_width), cosines, sines
    ).astype(bf16)
    keys_low = rotate(
        (k_normed * g_key).reshape(row_count, heads_here, head_width), cosines, sines
    ).astype(bf16)
    values_low = v_raw.astype(bf16)
    all_keys, all_values, all_labels, all_positions = (
        lax.all_gather(keys_low.reshape(row_count, local_width), "dp", axis=0, tiled=True),
        lax.all_gather(values_low, "dp", axis=0, tiled=True),
        lax.all_gather(labels, "dp", axis=0, tiled=True),
        lax.all_gather(positions, "dp", axis=0, tiled=True),
    )
    key_blocks = all_keys.reshape(block_count, block_rows, heads_here, head_width)
    value_blocks = all_values.reshape(block_count, block_rows, heads_here, head_width)
    label_blocks = all_labels.reshape(block_count, block_rows)
    position_blocks = all_positions.reshape(block_count, block_rows)
    scanned = (key_blocks, value_blocks, label_blocks, position_blocks)
    low_label = jnp.min(labels)
    high_label = jnp.max(labels)

    def scores_of(key_block, label_block, position_block):
        scores = (
            jnp.einsum("qhd,khd->hqk", queries, key_block, preferred_element_type=f32) * score_scale
        )
        allowed = (labels[:, None] == label_block[None, :]) & (
            positions[:, None] >= position_block[None, :]
        )
        return (scores, allowed[None])

    def touches(label_block):
        return (jnp.max(label_block) >= low_label) & (jnp.min(label_block) <= high_label)

    def max_step(carry, blocks_in):
        key_block, value_block, label_block, position_block = blocks_in

        def max_live_block(state):
            running, totals = state
            scores, allowed = scores_of(key_block, label_block, position_block)
            highest = jnp.maximum(
                running, jnp.max(jnp.where(allowed, scores, masked_score), axis=2)
            )
            weights = jnp.where(allowed, jnp.exp(scores - highest[:, :, None]), 0.0)
            return (highest, totals * jnp.exp(running - highest) + jnp.sum(weights, axis=2))

        return (lax.cond(touches(label_block), max_live_block, lambda state: state, carry), None)

    start_state = (
        jnp.full((heads_here, row_count), masked_score, f32),
        jnp.zeros((heads_here, row_count), f32),
    )
    (running_max, running_total), _ = lax.scan(max_step, start_state, scanned)
    log_total = running_max + jnp.log(running_total)

    def value_step(accum, blocks_in):
        key_block, value_block, label_block, position_block = blocks_in

        def value_live_block(current):
            scores, allowed = scores_of(key_block, label_block, position_block)
            probs_low = jnp.where(allowed, jnp.exp(scores - log_total[:, :, None]), 0.0).astype(
                bf16
            )
            return current + jnp.einsum(
                "hqk,khd->qhd", probs_low, value_block, preferred_element_type=f32
            )

        return (
            lax.cond(touches(label_block), value_live_block, lambda current: current, accum),
            None,
        )

    attended, _ = lax.scan(value_step, jnp.zeros((row_count, heads_here, head_width), f32), scanned)
    attended_low = attended.reshape(row_count, local_width).astype(bf16)
    attn_sum = lax.psum(
        jnp.dot(attended_low, w_output, preferred_element_type=f32).astype(jnp.bfloat16), "mp"
    ).astype(jnp.float32)
    attn_factor = lax.rsqrt(jnp.mean(attn_sum * attn_sum, axis=1, keepdims=True) + epsilon)
    attn_normed = attn_sum * attn_factor
    g_attn = gain_attn.reshape(model_width)
    hidden = tokens.astype(f32) + attn_normed * g_attn
    hidden_low = hidden.astype(bf16)
    gate_val = jnp.dot(hidden_low, w_gate, preferred_element_type=f32)
    up_val = jnp.dot(hidden_low, w_up, preferred_element_type=f32)
    sigmoid_gate = jax.nn.sigmoid(gate_val)
    silu_gate = gate_val * sigmoid_gate
    act_low = (silu_gate * up_val).astype(bf16)
    mlp_sum = lax.psum(
        jnp.dot(act_low, w_down, preferred_element_type=f32).astype(jnp.bfloat16), "mp"
    ).astype(jnp.float32)
    mlp_factor = lax.rsqrt(jnp.mean(mlp_sum * mlp_sum, axis=1, keepdims=True) + epsilon)
    mlp_normed = mlp_sum * mlp_factor
    g_mlp = gain_mlp.reshape(model_width)
    output = (hidden + mlp_normed * g_mlp).astype(bf16)
    grad_out = cotangent.astype(f32)
    grad_gain_mlp = jnp.sum(grad_out * mlp_normed, axis=0)
    grad_mlp = norm_back(grad_out * g_mlp, mlp_normed, mlp_factor).astype(bf16)
    grad_w_down = jnp.einsum("tf,td->fd", act_low, grad_mlp, preferred_element_type=f32)
    grad_act = jnp.einsum("td,fd->tf", grad_mlp, w_down, preferred_element_type=f32)
    slope = sigmoid_gate * (1.0 + gate_val * (1.0 - sigmoid_gate))
    grad_gate = (grad_act * up_val * slope).astype(bf16)
    grad_up = (grad_act * silu_gate).astype(bf16)
    branch_grad = jnp.einsum(
        "tf,df->td", grad_gate, w_gate, preferred_element_type=f32
    ) + jnp.einsum("tf,df->td", grad_up, w_up, preferred_element_type=f32)
    grad_hidden = grad_out + lax.psum(branch_grad.astype(jnp.bfloat16), "mp").astype(jnp.float32)
    grad_gain_attn = jnp.sum(grad_hidden * attn_normed, axis=0)
    grad_attn = norm_back(grad_hidden * g_attn, attn_normed, attn_factor).astype(bf16)
    grad_w_output = jnp.einsum("tc,td->cd", attended_low, grad_attn, preferred_element_type=f32)
    grad_attended = (
        jnp.einsum("td,cd->tc", grad_attn, w_output, preferred_element_type=f32)
        .astype(bf16)
        .reshape(row_count, heads_here, head_width)
    )
    delta = jnp.sum(grad_attended.astype(f32) * attended, axis=2).T

    def grad_step(grad_q, blocks_in):
        key_block, value_block, label_block, position_block = blocks_in

        def grad_live_block(current):
            scores, allowed = scores_of(key_block, label_block, position_block)
            probs = jnp.where(allowed, jnp.exp(scores - log_total[:, :, None]), 0.0)
            grad_probs = jnp.einsum(
                "qhd,khd->hqk", grad_attended, value_block, preferred_element_type=f32
            )
            grad_scores = (probs * (grad_probs - delta[:, :, None])).astype(bf16)
            value_term = jnp.einsum(
                "hqk,qhd->khd", probs.astype(bf16), grad_attended, preferred_element_type=f32
            )
            key_term = jnp.einsum("hqk,qhd->khd", grad_scores, queries, preferred_element_type=f32)
            updated = current + jnp.einsum(
                "hqk,khd->qhd", grad_scores, key_block, preferred_element_type=f32
            )
            return (updated, (key_term, value_term))

        def skip_block(current):
            nothing = jnp.zeros((block_rows, heads_here, head_width), f32)
            return (current, (nothing, nothing))

        return lax.cond(touches(label_block), grad_live_block, skip_block, grad_q)

    grad_queries, (key_terms, value_terms) = lax.scan(
        grad_step, jnp.zeros((row_count, heads_here, head_width), f32), scanned
    )
    grad_keys, grad_values = (
        lax.psum_scatter(
            (key_terms.reshape(key_rows, local_width) * score_scale).astype(jnp.bfloat16),
            "dp",
            scatter_dimension=0,
            tiled=True,
        ).astype(jnp.float32),
        lax.psum_scatter(
            value_terms.reshape(key_rows, local_width).astype(jnp.bfloat16),
            "dp",
            scatter_dimension=0,
            tiled=True,
        ).astype(jnp.float32),
    )
    grad_values_low = grad_values.astype(bf16)
    back_q = rotate(grad_queries * score_scale, cosines, -sines).reshape(row_count, local_width)
    back_k = rotate(grad_keys.reshape(row_count, heads_here, head_width), cosines, -sines).reshape(
        row_count, local_width
    )
    grad_gain_query = jnp.sum(back_q * q_normed, axis=0).reshape(heads_here, head_width)
    grad_gain_key = jnp.sum(back_k * k_normed, axis=0).reshape(heads_here, head_width)
    scaled_q = back_q * g_query
    scaled_k = back_k * g_key
    inner = lax.psum(
        jnp.stack([jnp.sum(scaled_q * q_normed, axis=1), jnp.sum(scaled_k * k_normed, axis=1)]),
        "mp",
    )
    grad_q_raw = (q_factor * (scaled_q - q_normed * inner[0][:, None] / model_width)).astype(bf16)
    grad_k_raw = (k_factor * (scaled_k - k_normed * inner[1][:, None] / model_width)).astype(bf16)
    input_term = (
        jnp.einsum("tc,dc->td", grad_q_raw, w_query, preferred_element_type=f32)
        + jnp.einsum("tc,dc->td", grad_k_raw, w_key, preferred_element_type=f32)
        + jnp.einsum("tc,dc->td", grad_values_low, w_value, preferred_element_type=f32)
    )
    grad_tokens = (
        grad_hidden + lax.psum(input_term.astype(jnp.bfloat16), "mp").astype(jnp.float32)
    ).astype(bf16)
    local_w_query = jnp.einsum("td,tc->dc", tokens, grad_q_raw, preferred_element_type=f32)
    local_w_key = jnp.einsum("td,tc->dc", tokens, grad_k_raw, preferred_element_type=f32)
    local_w_value = jnp.einsum("td,tc->dc", tokens, grad_values_low, preferred_element_type=f32)
    local_w_gate = jnp.einsum("td,tf->df", hidden_low, grad_gate, preferred_element_type=f32)
    local_w_up = jnp.einsum("td,tf->df", hidden_low, grad_up, preferred_element_type=f32)
    grad_w_query, grad_w_key, grad_w_value, grad_w_gate, grad_w_up = (
        lax.psum_scatter(
            local_w_query.astype(jnp.bfloat16), "dp", scatter_dimension=0, tiled=True
        ).astype(jnp.float32),
        lax.psum_scatter(
            local_w_key.astype(jnp.bfloat16), "dp", scatter_dimension=0, tiled=True
        ).astype(jnp.float32),
        lax.psum_scatter(
            local_w_value.astype(jnp.bfloat16), "dp", scatter_dimension=0, tiled=True
        ).astype(jnp.float32),
        lax.psum_scatter(
            local_w_gate.astype(jnp.bfloat16), "dp", scatter_dimension=0, tiled=True
        ).astype(jnp.float32),
        lax.psum_scatter(
            local_w_up.astype(jnp.bfloat16), "dp", scatter_dimension=0, tiled=True
        ).astype(jnp.float32),
    )
    summed_out, summed_down, summed_gq, summed_gk, summed_ga, summed_gm = (
        lax.psum_scatter(
            grad_w_output.astype(jnp.bfloat16), "dp", scatter_dimension=1, tiled=True
        ).astype(jnp.float32),
        lax.psum_scatter(
            grad_w_down.astype(jnp.bfloat16), "dp", scatter_dimension=1, tiled=True
        ).astype(jnp.float32),
        lax.psum_scatter(
            grad_gain_query.astype(jnp.bfloat16), "dp", scatter_dimension=1, tiled=True
        ).astype(jnp.float32),
        lax.psum_scatter(
            grad_gain_key.astype(jnp.bfloat16), "dp", scatter_dimension=1, tiled=True
        ).astype(jnp.float32),
        lax.psum_scatter(
            grad_gain_attn.reshape(gain_attn.shape).astype(jnp.bfloat16),
            "dp",
            scatter_dimension=1,
            tiled=True,
        ).astype(jnp.float32),
        lax.psum_scatter(
            grad_gain_mlp.reshape(gain_mlp.shape).astype(jnp.bfloat16),
            "dp",
            scatter_dimension=1,
            tiled=True,
        ).astype(jnp.float32),
    )
    return (
        output,
        grad_tokens,
        grad_w_query,
        grad_w_key,
        grad_w_value,
        summed_out,
        grad_w_gate,
        grad_w_up,
        summed_down,
        summed_gq,
        summed_gk,
        summed_ga,
        summed_gm,
    )


line = 4
pair = 2
low_score = -1e30
start_max = -1e20
big_vmem = 56 << 20


def line_shift(value, step):
    moves = [
        (z * pair + x, ((z + step) % line) * pair + x) for z in range(line) for x in range(pair)
    ]
    return lax.ppermute(value, "dp", moves)


def line_flip(value, bit):
    return lax.ppermute(
        value, "dp", [(z * pair + x, (z ^ bit) * pair + x) for z in range(line) for x in range(pair)]
    )


def x_swap(value):
    return lax.ppermute(value, "dp", [(i, i ^ 1) for i in range(line * pair)])


def core_swap(value):
    return lax.ppermute(value, "mp", [(i, i ^ 1) for i in range(4)])


def y_swap(value):
    return lax.ppermute(value, "mp", [(i, i ^ 2) for i in range(4)])


def flip_cores(value, axis):
    quarter = value.shape[axis] // 4
    cuts = [lax.slice_in_dim(value, i * quarter, (i + 1) * quarter, axis=axis) for i in (1, 0, 3, 2)]
    return jnp.concatenate(cuts, axis=axis)


def token_sum(value):
    value = value + flip_cores(core_swap(value), 1)
    return value + y_swap(value)


def own_part(value):
    quarter = value.shape[0] // 4
    return jnp.concatenate([value[:quarter], value[2 * quarter : 3 * quarter]], axis=0)


def other_part(value):
    quarter = value.shape[0] // 4
    return jnp.concatenate([value[quarter : 2 * quarter], value[3 * quarter :]], axis=0)


def join_parts(own, other):
    half = own.shape[0] // 2
    return jnp.concatenate([own[:half], other[:half], own[half:], other[half:]], axis=0)


def reduce_own_rows(partial_low):
    f32 = jnp.float32
    arrived = core_swap(other_part(partial_low))
    chip_sum = (own_part(partial_low).astype(f32) + arrived.astype(f32)).astype(jnp.bfloat16)
    return chip_sum.astype(f32) + y_swap(chip_sum).astype(f32)


def dot_t(first, second):
    return lax.dot_general(
        first, second, (((0,), (0,)), ((), ())), preferred_element_type=jnp.float32
    )


def dot_nt(first, second):
    return lax.dot_general(
        first, second, (((1,), (1,)), ((), ())), preferred_element_type=jnp.float32
    )


def vmem_specs(count):
    return [pl.BlockSpec(memory_space=pltpu.VMEM)] * count


def project_kernel(place, own, other, wq, wk, wv, gq, gk, cosines, sines, *refs):
    out_queries, out_pairs = refs[:line], refs[line : 2 * line]
    out_q_raw, out_k_raw, out_squares, turned = refs[2 * line :]
    f32 = jnp.float32
    bf16 = jnp.bfloat16
    width = cosines.shape[1]
    rows = jnp.concatenate([own[...], other[...]], axis=0)

    def keep(raw, gain, slot):
        for h in range(line):
            part = raw[:, h * width : (h + 1) * width] * gain[:, h * width : (h + 1) * width]
            turned[slot, h] = (
                part * cosines[...] + pltpu.roll(part, width // 2, 1) * sines[...]
            ).astype(bf16)

    q_raw = jnp.dot(rows, wq[...], preferred_element_type=f32)
    out_q_raw[...] = q_raw
    out_squares[0:1, :] = jnp.sum((q_raw * q_raw).T, axis=0, keepdims=True)
    keep(q_raw, gq[...], 0)
    k_raw = jnp.dot(rows, wk[...], preferred_element_type=f32)
    out_k_raw[...] = k_raw
    out_squares[1:2, :] = jnp.sum((k_raw * k_raw).T, axis=0, keepdims=True)
    keep(k_raw, gk[...], 1)
    v_raw = jnp.dot(rows, wv[...], preferred_element_type=f32)
    for h in range(line):
        turned[2, h] = v_raw[:, h * width : (h + 1) * width].astype(bf16)
    for d in range(line):
        head = lax.rem(place[1] + d, line)
        out_queries[d][...] = turned[0, head]
        out_pairs[d][0] = turned[1, head]
        out_pairs[d][1] = turned[2, head]


def project(place, tokens, wq, wk, wv, gq, gk, cosines, sines):
    rows, depth = tokens.shape
    columns = wq.shape[1]
    width = columns // line
    half = rows // 2
    f32 = jnp.float32
    bf16 = jnp.bfloat16
    whole = lambda shape: pl.BlockSpec(shape, lambda i, p: (0, 0))
    rows_of = lambda n: pl.BlockSpec((half, n), lambda i, p: (i, 0))
    return pl.pallas_call(
        project_kernel,
        grid_spec=pltpu.PrefetchScalarGridSpec(
            num_scalar_prefetch=1,
            grid=(2,),
            in_specs=[
                pl.BlockSpec((half // 2, depth), lambda i, p: (2 * p[0] + i, 0)),
                pl.BlockSpec((half // 2, depth), lambda i, p: (2 * (1 - p[0]) + i, 0)),
                whole((depth, columns)),
                whole((depth, columns)),
                whole((depth, columns)),
                whole((1, columns)),
                whole((1, columns)),
                rows_of(width),
                rows_of(width),
            ],
            out_specs=[rows_of(width)] * line
            + [pl.BlockSpec((2, half, width), lambda i, p: (0, i, 0))] * line
            + [rows_of(columns)] * 2
            + [pl.BlockSpec((2, half), lambda i, p: (0, i))],
            scratch_shapes=[pltpu.VMEM((3, line, half, width), bf16)],
        ),
        out_shape=[jax.ShapeDtypeStruct((rows, width), bf16)] * line
        + [jax.ShapeDtypeStruct((2, rows, width), bf16)] * line
        + [jax.ShapeDtypeStruct((rows, columns), f32)] * 2
        + [jax.ShapeDtypeStruct((2, rows), f32)],
        compiler_params=pltpu.CompilerParams(vmem_limit_bytes=big_vmem),
        cost_estimate=pl.CostEstimate(
            flops=6 * rows * depth * columns, bytes_accessed=12 << 20, transcendentals=0
        ),
    )(place, tokens, tokens, wq, wk, wv, gq, gk, cosines, sines)


def visible_scores(key, query, key_code, query_code, query_low, factor):
    scores = dot_nt(key, query) * factor
    codes = jnp.concatenate([key_code] * (query.shape[0] // key_code.shape[1]), axis=1)
    return jnp.where((codes <= query_code) & (codes >= query_low), scores, low_score)


def attend_kernel(factor, key_rows, live, notes, *refs):
    query_refs = refs[:line]
    pair_refs = refs[line : 3 * line]
    out_turned, out_log, out_query, out_key, out_codes, out_rows = refs[3 * line : 3 * line + 6]
    out_refs = refs[3 * line + 6 : 4 * line + 6]
    top, total, accum = refs[4 * line + 6 :]
    f32 = jnp.float32
    bf16 = jnp.bfloat16
    count, width = query_refs[0].shape

    def column(row):
        return jnp.broadcast_to(row, (width, count)).T

    for k in range(2 * line):
        out_key[k] = (pair_refs[k][0].astype(f32) * column(notes[k, 1:2, :])).astype(bf16)
        labels = column(notes[k, 2:3, :]).astype(jnp.int32)
        out_codes[k] = labels * key_rows + column(notes[k, 3:4, :]).astype(jnp.int32)
    for q in range(line):
        out_query[q] = (query_refs[q][...].astype(f32) * column(notes[q, 0:1, :])).astype(bf16)
        base = notes[q, 2:3, :].astype(jnp.int32) * key_rows
        out_rows[q : q + 1, :] = base + notes[q, 3:4, :].astype(jnp.int32)
        out_rows[line + q : line + q + 1, :] = base

    for q in range(line):
        top[...] = jnp.full_like(top, start_max)
        total[...] = jnp.zeros_like(total)
        accum[...] = jnp.zeros_like(accum)
        for k in range(2 * line):

            @pl.when(live[q, k] > 0)
            def _(q=q, k=k):
                scores = visible_scores(
                    out_key[k],
                    out_query[q],
                    out_codes[k],
                    out_rows[q : q + 1, :],
                    out_rows[line + q : line + q + 1, :],
                    factor,
                )
                highest = jnp.maximum(top[...], jnp.max(scores, axis=0, keepdims=True))
                weights = jnp.exp2(scores - highest)
                fade = jnp.exp2(top[...] - highest)
                total[...] = total[...] * fade + jnp.sum(weights, axis=0, keepdims=True)
                accum[...] = accum[...] * fade + dot_t(pair_refs[k][1], weights.astype(bf16))
                top[...] = highest

        turned = accum[...] / total[...]
        out_turned[q] = turned
        out_log[q : q + 1, :] = top[...] + jnp.log2(total[...])
        out_refs[q][...] = turned.T.astype(bf16)


def attend_back_kernel(factor, scale, live, codes, rows, queries, keys, *refs):
    pair_refs = refs[: 2 * line]
    turned, log_total = refs[2 * line : 2 * line + 2]
    grad_refs = refs[2 * line + 2 : 3 * line + 2]
    out_query = refs[3 * line + 2 : 4 * line + 2]
    out_pairs = refs[4 * line + 2 : 6 * line + 2]
    key_sum, value_sum, query_sum = refs[6 * line + 2 :]
    f32 = jnp.float32
    bf16 = jnp.bfloat16
    key_sum[...] = jnp.zeros_like(key_sum)
    value_sum[...] = jnp.zeros_like(value_sum)
    for q in range(line):
        query_sum[...] = jnp.zeros_like(query_sum)
        delta = jnp.sum(grad_refs[q][...].astype(f32).T * turned[q], axis=0, keepdims=True)
        for k in range(2 * line):

            @pl.when(live[q, k] > 0)
            def _(q=q, k=k, delta=delta):
                query, key, grad = queries[q], keys[k], grad_refs[q][...]
                scores = visible_scores(
                    key,
                    query,
                    codes[k],
                    rows[q : q + 1, :],
                    rows[line + q : line + q + 1, :],
                    factor,
                )
                probs = jnp.exp2(scores - log_total[q : q + 1, :])
                grad_probs = dot_nt(pair_refs[k][1], grad)
                grad_scores = (probs * (grad_probs - delta)).astype(bf16)
                value_sum[k] += jnp.dot(
                    probs.astype(bf16), grad, preferred_element_type=f32
                )
                key_sum[k] += jnp.dot(grad_scores, query, preferred_element_type=f32)
                query_sum[...] += dot_t(key, grad_scores)

        out_query[q][...] = (query_sum[...] * scale).T.astype(bf16)
    for k in range(2 * line):
        out_pairs[k][0] = (key_sum[k] * scale).astype(bf16)
        out_pairs[k][1] = value_sum[k].astype(bf16)


def attend(key_rows, live, notes, queries, pairs):
    count, width = queries[0].shape
    factor = math.log2(math.e) / math.sqrt(width)
    f32 = jnp.float32
    bf16 = jnp.bfloat16
    return pl.pallas_call(
        functools.partial(attend_kernel, factor, key_rows),
        out_shape=[
            jax.ShapeDtypeStruct((line, width, count), f32),
            jax.ShapeDtypeStruct((2 * line, count), f32),
            jax.ShapeDtypeStruct((line, count, width), bf16),
            jax.ShapeDtypeStruct((2 * line, count, width), bf16),
            jax.ShapeDtypeStruct((2 * line, count, width), jnp.int32),
            jax.ShapeDtypeStruct((2 * line, count), jnp.int32),
        ]
        + [jax.ShapeDtypeStruct((count, width), bf16)] * line,
        in_specs=[pl.BlockSpec(memory_space=pltpu.SMEM)] + vmem_specs(1 + 3 * line),
        out_specs=vmem_specs(6 + line),
        scratch_shapes=[
            pltpu.VMEM((1, count), f32),
            pltpu.VMEM((1, count), f32),
            pltpu.VMEM((width, count), f32),
        ],
        compiler_params=pltpu.CompilerParams(vmem_limit_bytes=40 << 20),
        cost_estimate=pl.CostEstimate(
            flops=10 * 4 * count * count * width,
            bytes_accessed=8 << 20,
            transcendentals=10 * count * count,
        ),
    )(live, notes, *queries, *pairs)


def attend_back(live, codes, rows, queries, keys, pairs, turned, log_total, grads):
    _, count, width = queries.shape
    scale = 1.0 / math.sqrt(width)
    factor = math.log2(math.e) * scale
    f32 = jnp.float32
    return pl.pallas_call(
        functools.partial(attend_back_kernel, factor, scale),
        out_shape=[jax.ShapeDtypeStruct((count, width), jnp.bfloat16)] * line
        + [jax.ShapeDtypeStruct((2, count, width), jnp.bfloat16)] * (2 * line),
        in_specs=[pl.BlockSpec(memory_space=pltpu.SMEM)] + vmem_specs(6 + 3 * line),
        out_specs=vmem_specs(3 * line),
        scratch_shapes=[
            pltpu.VMEM((2 * line, count, width), f32),
            pltpu.VMEM((2 * line, count, width), f32),
            pltpu.VMEM((width, count), f32),
        ],
        compiler_params=pltpu.CompilerParams(vmem_limit_bytes=40 << 20),
        cost_estimate=pl.CostEstimate(
            flops=10 * 10 * count * count * width,
            bytes_accessed=12 << 20,
            transcendentals=10 * count * count,
        ),
    )(live, codes, rows, queries, keys, *pairs, turned, log_total, *grads)


def block_kernel(
    attended,
    w_out,
    own_tokens,
    own_cotangent,
    g_attn,
    g_mlp,
    w_gate_in,
    w_up_in,
    w_down_in,
    out_output,
    out_hidden,
    out_hidden_x,
    out_act,
    out_act_x,
    out_mlp,
    out_mlp_x,
    out_gate,
    out_gate_far,
    out_up,
    out_up_far,
    out_attn,
    out_attended,
    out_grad_hidden,
    out_gain,
    w_gate,
    w_up,
    w_down,
    gate_keep,
    up_keep,
    act_keep,
    hidden_keep,
    mlp_keep,
    attn_keep,
    grad_gate,
    grad_up,
    own_factor,
    own_normed,
    out_keep,
    total,
    part_send,
    part_recv,
    y_send,
    y_recv,
    send_sems,
    recv_sems,
    local_sems,
):
    f32 = jnp.float32
    bf16 = jnp.bfloat16
    depth = w_out.shape[1]
    units = w_gate.shape[1]
    tile = 512
    count = own_tokens.shape[0] // 2
    rows = 2 * count
    mp = lax.axis_index("mp")
    spot = lax.axis_index("dp")
    core = lax.rem(mp, 2)
    x = lax.rem(spot, 2)
    core_peer = {"mp": mp + 1 - 2 * core}
    y_peer = {"mp": lax.rem(mp + 2, 4)}
    x_peer = {"dp": spot + 1 - 2 * x}

    barrier = pltpu.get_barrier_semaphore()
    for peer in (core_peer, y_peer, x_peer):
        pl.semaphore_signal(barrier, inc=1, device_id=peer, device_id_type=pl.DeviceIdType.MESH)
    pl.semaphore_wait(barrier, 3)

    remote, started, local = [], [], []

    def send(source, target, peer):
        index = len(remote)
        copy = pltpu.make_async_remote_copy(
            src_ref=source,
            dst_ref=target,
            send_sem=send_sems.at[index],
            recv_sem=recv_sems.at[index],
            device_id=peer,
            device_id_type=pl.DeviceIdType.MESH,
        )
        remote.append(copy)
        copy.start()
        return copy

    def keep_out(source, target, waited=False):
        copy = pltpu.make_async_copy(source, target, local_sems.at[len(started)])
        started.append(copy)
        if not waited:
            local.append(copy)
        copy.start()
        return copy

    loads = [keep_out(a, b, True) for a, b in ((w_gate_in, w_gate), (w_up_in, w_up), (w_down_in, w_down))]

    own = lambda s: pl.ds(s * rows, count)
    other = lambda s: pl.ds(s * rows + count, count)
    both = lambda s: pl.ds(s * rows, rows)
    mine = lambda s: pl.ds(s * count, count)
    at_home = lambda s: pl.ds(pl.multiple_of(core * rows + s * count, count), count)
    cut = lambda t: pl.ds(pl.multiple_of(t * tile, tile), tile)
    flying = {}

    def reduce_start(stage, s):
        part_send[s] = total[count:, :].astype(bf16)
        copy = send(part_send.at[s], part_recv.at[s], core_peer)
        copy.wait()
        y_send[s] = (total[:count, :] + part_recv[s].astype(f32)).astype(bf16)
        flying[stage, s] = send(y_send.at[s], y_recv.at[stage, s], y_peer)

    def reduced(stage, s):
        flying[stage, s].wait()
        return y_send[s].astype(f32) + y_recv[stage, s].astype(f32)

    def factor_of(value):
        return lax.rsqrt(jnp.mean(value * value, axis=1, keepdims=True) + epsilon)

    def share(keep, s):
        flying["share", s] = send(keep.at[own(s)], keep.at[other(s)], core_peer)

    def project_out(s):
        total[...] = jnp.dot(attended[both(s), :], w_out[...], preferred_element_type=f32)
        reduce_start(0, s)

    def after_attention(s):
        value = reduced(0, s)
        factor = factor_of(value)
        normed = value * factor
        own_factor[mine(s), :] = jnp.broadcast_to(factor, (count, own_factor.shape[1]))
        own_normed[mine(s), :] = normed
        hidden = own_tokens[mine(s), :].astype(f32) + normed * g_attn[...]
        out_grad_hidden[mine(s), :] = hidden
        hidden_keep[own(s), :] = hidden.astype(bf16)
        share(hidden_keep, s)

    def forward(s):
        flying["hidden", s] = send(hidden_keep.at[own(s)], out_hidden_x.at[own(s)], x_peer)
        flying["share", s].wait()
        keep_out(hidden_keep.at[both(s)], out_hidden.at[both(s)])

        def step(t):
            hidden = hidden_keep[both(s), :]
            gate = jnp.dot(hidden, w_gate[:, cut(t)], preferred_element_type=f32)
            up = jnp.dot(hidden, w_up[:, cut(t)], preferred_element_type=f32)
            gate_keep[both(s), cut(t)] = gate.astype(bf16)
            up_keep[both(s), cut(t)] = up.astype(bf16)
            act = (gate * jax.nn.sigmoid(gate) * up).astype(bf16)
            act_keep[both(s), cut(t)] = act
            return jnp.dot(act, w_down[cut(t), :], preferred_element_type=f32)

        total[...] = step(0)

        @pl.loop(1, units // tile)
        def _(t):
            total[...] += step(t)

        reduce_start(1, s)
        keep_out(act_keep.at[both(s)], out_act.at[both(s)])
        half = units // 2
        far = pl.ds(pl.multiple_of((1 - x) * half, half), half)
        flying["act", s] = send(act_keep.at[both(s), far], out_act_x.at[both(s)], x_peer)

    def turn_point(s):
        value = reduced(1, s)
        factor = factor_of(value)
        normed = value * factor
        out_keep[mine(s), :] = (out_grad_hidden[mine(s), :] + normed * g_mlp[...]).astype(bf16)
        keep_out(out_keep.at[mine(s)], out_output.at[at_home(s)])
        flying["output", s] = send(out_keep.at[mine(s)], out_output.at[at_home(s)], core_peer)
        grad = own_cotangent[mine(s), :].astype(f32)
        gain = jnp.sum(grad * normed, axis=0, keepdims=True)
        out_gain[1:2, :] = gain if s == 0 else out_gain[1:2, :] + gain
        mlp_keep[own(s), :] = norm_back(grad * g_mlp[...], normed, factor).astype(bf16)
        share(mlp_keep, s)

    def backward(s):
        flying["mlp", s] = send(mlp_keep.at[own(s)], out_mlp_x.at[own(s)], x_peer)
        flying["share", s].wait()
        keep_out(mlp_keep.at[both(s)], out_mlp.at[both(s)])

        def step(t):
            grad_act = dot_nt(mlp_keep[both(s), :], w_down[cut(t), :])
            gate = gate_keep[both(s), cut(t)].astype(f32)
            up = up_keep[both(s), cut(t)].astype(f32)
            sigmoid = jax.nn.sigmoid(gate)
            to_gate = (grad_act * up * (sigmoid * (1.0 + gate * (1.0 - sigmoid)))).astype(bf16)
            to_up = (grad_act * (gate * sigmoid)).astype(bf16)
            grad_gate[:, cut(t)] = to_gate
            grad_up[:, cut(t)] = to_up
            return dot_nt(to_gate, w_gate[:, cut(t)]) + dot_nt(to_up, w_up[:, cut(t)])

        if s > 0:
            for copy in flying["grads"]:
                copy.wait()
        total[...] = step(0)

        @pl.loop(1, units // tile)
        def _(t):
            total[...] += step(t)

        reduce_start(2, s)
        half = units // 2
        far = pl.ds(pl.multiple_of((1 - x) * half, half), half)
        flying["grads"] = [
            keep_out(source, target.at[both(s)], waited=s == 0)
            for source, target in (
                (grad_gate, out_gate),
                (grad_gate.at[:, far], out_gate_far),
                (grad_up, out_up),
                (grad_up.at[:, far], out_up_far),
            )
        ]

    def to_attention(s):
        value = reduced(2, s)
        grad = own_cotangent[mine(s), :].astype(f32) + value
        out_grad_hidden[mine(s), :] = grad
        normed = own_normed[mine(s), :]
        gain = jnp.sum(grad * normed, axis=0, keepdims=True)
        out_gain[0:1, :] = gain if s == 0 else out_gain[0:1, :] + gain
        factor = own_factor[mine(s), 0:1]
        attn_keep[own(s), :] = norm_back(grad * g_attn[...], normed, factor).astype(bf16)
        share(attn_keep, s)

    def attended_grad(s):
        flying["share", s].wait()
        keep_out(attn_keep.at[both(s)], out_attn.at[both(s)])
        out_attended[both(s), :] = dot_nt(attn_keep[both(s), :], w_out[...]).astype(bf16)

    def forward_core(name, s, array):
        flying[name, s].wait()
        flying[name + "_core", s] = send(array.at[own(s)], array.at[other(s)], core_peer)

    project_out(0)
    project_out(1)
    after_attention(0)
    for load in loads:
        load.wait()
    forward(0)
    after_attention(1)
    forward(1)
    turn_point(0)
    backward(0)
    turn_point(1)
    backward(1)
    for s in range(2):
        forward_core("hidden", s, out_hidden_x)
    to_attention(0)
    attended_grad(0)
    to_attention(1)
    attended_grad(1)
    for s in range(2):
        flying["act", s].wait()
        flying["output", s].wait()
        forward_core("mlp", s, out_mlp_x)
    for s in range(2):
        flying["hidden_core", s].wait()
        flying["mlp_core", s].wait()
    for copy in local:
        copy.wait()


def block(attended, w_out, own_tokens, own_cotangent, g_attn, g_mlp, w_gate, w_up, w_down):
    rows, columns = attended.shape
    depth, units = w_gate.shape
    half = rows // 2
    quarter = rows // 4
    f32 = jnp.float32
    bf16 = jnp.bfloat16
    wide = jax.ShapeDtypeStruct((rows, depth), bf16)
    tall = jax.ShapeDtypeStruct((rows, units), bf16)
    any_spec = pl.BlockSpec(memory_space=pl.ANY)
    return pl.pallas_call(
        block_kernel,
        out_shape=[
            wide,
            wide,
            wide,
            tall,
            jax.ShapeDtypeStruct((rows, units // 2), bf16),
            wide,
            wide,
            tall,
            jax.ShapeDtypeStruct((rows, units // 2), bf16),
            tall,
            jax.ShapeDtypeStruct((rows, units // 2), bf16),
            wide,
            jax.ShapeDtypeStruct((rows, columns), bf16),
            jax.ShapeDtypeStruct((half, depth), f32),
            jax.ShapeDtypeStruct((2, depth), f32),
        ],
        in_specs=vmem_specs(6) + [any_spec] * 3,
        out_specs=[any_spec] * 12 + vmem_specs(3),
        scratch_shapes=[
            pltpu.VMEM((depth, units), bf16),
            pltpu.VMEM((depth, units), bf16),
            pltpu.VMEM((units, depth), bf16),
            pltpu.VMEM((rows, units), bf16),
            pltpu.VMEM((rows, units), bf16),
            pltpu.VMEM((rows, units), bf16),
            pltpu.VMEM((rows, depth), bf16),
            pltpu.VMEM((rows, depth), bf16),
            pltpu.VMEM((rows, depth), bf16),
            pltpu.VMEM((half, units), bf16),
            pltpu.VMEM((half, units), bf16),
            pltpu.VMEM((half, 128), f32),
            pltpu.VMEM((half, depth), f32),
            pltpu.VMEM((half, depth), bf16),
            pltpu.VMEM((half, depth), f32),
            pltpu.VMEM((2, quarter, depth), bf16),
            pltpu.VMEM((2, quarter, depth), bf16),
            pltpu.VMEM((2, quarter, depth), bf16),
            pltpu.VMEM((3, 2, quarter, depth), bf16),
            pltpu.SemaphoreType.DMA((30,)),
            pltpu.SemaphoreType.DMA((30,)),
            pltpu.SemaphoreType.DMA((24,)),
        ],
        compiler_params=pltpu.CompilerParams(
            vmem_limit_bytes=61800 << 10, collective_id=1, has_side_effects=True
        ),
        cost_estimate=pl.CostEstimate(
            flops=12 * rows * depth * units,
            bytes_accessed=60 << 20,
            transcendentals=2 * rows * units,
        ),
    )(attended, w_out, own_tokens, own_cotangent, g_attn, g_mlp, w_gate, w_up, w_down)


def weight_kernel(place, *refs):
    first, second, first_x, second_x = refs[:4]
    total = dot_t(first[...], second[...]) + dot_t(first_x[...], second_x[...])
    if len(refs) == 6:
        total = total + refs[4][...].astype(jnp.float32)
    refs[-1][...] = total.astype(refs[-1].dtype)


def line_block(which):
    if which < 2:
        return lambda p: 2 * which + 1 - p[2]
    if which == 2:
        return lambda p: 2 * (1 - p[3]) + p[2]
    return lambda p: 2 * p[3] + p[2]


def weight_term(place, first, second, cut_first, blocks, extra, kind):
    tokens = first[0].shape[0]
    cut_side, half_side = (first, second) if cut_first else (second, first)
    cut_tile = cut_side[0].shape[1] // line
    half_size = half_side[1].shape[1]
    half_tile = min(half_size, 512)
    while half_size % half_tile:
        half_tile -= 128
    half_count = half_size // half_tile
    own_half = half_count if half_side[0].shape[1] != half_size else 0
    count = len(blocks)

    def cut_map(i, j, p):
        index = line_block(blocks[0])(p)
        if count == 2:
            index = index + i * (line_block(blocks[1])(p) - line_block(blocks[0])(p))
        return (0, index)

    cut_spec = pl.BlockSpec((tokens, cut_tile), cut_map)
    half_own = pl.BlockSpec((tokens, half_tile), lambda i, j, p: (0, j + p[4] * own_half))
    half_far = pl.BlockSpec((tokens, half_tile), lambda i, j, p: (0, j))
    if cut_first:
        in_specs = [cut_spec, half_own, cut_spec, half_far]
        tile_shape = (cut_tile, half_tile)
        out_map = lambda i, j, p: (i, j)
        shape = (count * cut_tile, half_size)
        extra_map = lambda i, j, p: (extra[1](p) + i, j)
    else:
        in_specs = [half_own, cut_spec, half_far, cut_spec]
        tile_shape = (half_tile, cut_tile)
        out_map = lambda i, j, p: (j, i)
        shape = (half_size, count * cut_tile)
        extra_map = lambda i, j, p: (j, extra[1](p) + i)
    args = [first[0], second[0], first[1], second[1]]
    if extra is not None:
        in_specs.append(pl.BlockSpec(tile_shape, extra_map))
        args.append(extra[0])
    return pl.pallas_call(
        weight_kernel,
        grid_spec=pltpu.PrefetchScalarGridSpec(
            num_scalar_prefetch=1,
            grid=(count, half_count),
            in_specs=in_specs,
            out_specs=pl.BlockSpec(tile_shape, out_map),
        ),
        out_shape=jax.ShapeDtypeStruct(shape, kind),
        compiler_params=pltpu.CompilerParams(vmem_limit_bytes=big_vmem),
        cost_estimate=pl.CostEstimate(
            flops=4 * tokens * shape[0] * shape[1],
            bytes_accessed=4 * tokens * (shape[0] + shape[1]) + 4 * shape[0] * shape[1],
            transcendentals=0,
        ),
    )(place, *args)


def after(value, *needed):
    return lax.optimization_barrier((value, needed))[0]


class Spread:
    def __init__(self, place, x, first, second, cut_first):
        self.place, self.x, self.operands, self.cut_first = place, x, (first, second), cut_first
        self.sent = self.make((0, 1), None, jnp.bfloat16)

    def make(self, blocks, extra, kind):
        first, second = self.operands
        return weight_term(self.place, first, second, self.cut_first, blocks, extra, kind)

    def neighbour(self):
        self.arrived = line_flip(self.sent, 1)

    def second(self):
        self.passed = self.make((2,), (self.arrived, lambda p: 1 - p[3]), jnp.bfloat16)
        return self.passed

    def finish(self, *needed):
        own = self.make((3,), (self.arrived, lambda p: p[3]), jnp.float32)
        later = after(line_flip(self.passed, 2), *needed)
        axis = 0 if self.cut_first else 1
        width = own.shape[axis] // pair
        far = lambda value: lax.dynamic_slice_in_dim(value, (1 - self.x) * width, width, axis)
        near = lambda value: lax.dynamic_slice_in_dim(value, self.x * width, width, axis)
        to_x = (far(own) + far(later).astype(jnp.float32)).astype(jnp.bfloat16)
        own_half = near(own) + near(later).astype(jnp.float32)
        return own_half, x_swap(to_x).astype(jnp.float32)


def on_device_lines(
    tokens,
    cotangent,
    doc_ids,
    row_ids,
    offsets,
    w_query,
    w_key,
    w_value,
    w_output,
    w_gate,
    w_up,
    w_down,
    gain_query,
    gain_key,
    gain_attn,
    gain_mlp,
):
    f32 = jnp.float32
    bf16 = jnp.bfloat16
    row_count, model_width = tokens.shape
    heads_here, head_width = gain_query.shape
    local_width = heads_here * head_width
    half_rows = row_count // 2
    key_rows = row_count * line * pair
    spot = lax.axis_index("dp")
    z, x = spot // pair, lax.rem(spot, pair)
    z_high, z_low = z // 2, lax.rem(z, 2)
    core = lax.rem(lax.axis_index("mp"), 2)
    place = jnp.stack([core, z, z_low, z_high, x]).astype(jnp.int32)

    quarter = row_count // 4

    def own_rows(value):
        return lax.dynamic_slice_in_dim(value, core * half_rows, half_rows, 0)

    def other_rows(value):
        return lax.dynamic_slice_in_dim(value, (1 - core) * half_rows, half_rows, 0)

    def reorder(value):
        return join_parts(own_rows(value), other_rows(value))

    def restore(own, other):
        whole = jnp.zeros((row_count,) + own.shape[1:], own.dtype)
        whole = lax.dynamic_update_slice_in_dim(whole, own, core * half_rows, 0)
        return lax.dynamic_update_slice_in_dim(whole, other, (1 - core) * half_rows, 0)

    def half_of(value, x_place):
        width = value.shape[1] // pair
        return lax.dynamic_slice_in_dim(value, x_place * width, width, 1)

    def join_halves(near, far, axis):
        low = jnp.where(x == 0, near, far)
        return jnp.concatenate([low, jnp.where(x == 0, far, near)], axis=axis)

    positions = reorder(offsets[0] + jnp.arange(row_count, dtype=jnp.int32))
    labels = reorder(row_ids[0] * key_rows + doc_ids)
    freqs = rope_base ** (-jnp.arange(0, head_width // 2, dtype=f32) * 2.0 / head_width)
    angles = positions.astype(f32)[:, None] * freqs[None, :]
    cosines, sines = jnp.cos(angles), jnp.sin(angles)
    cosines = jnp.concatenate([cosines, cosines], axis=1)
    sines = jnp.concatenate([-sines, sines], axis=1)
    g_query = gain_query.reshape(1, local_width)
    g_key = gain_key.reshape(1, local_width)

    projected = project(
        place, tokens, w_query, w_key, w_value, g_query, g_key, cosines, sines
    )
    queries, pairs = projected[:line], projected[line : 2 * line]
    q_raw, k_raw, squares = projected[2 * line :]
    pairs = [pairs[0]] + [line_shift(pairs[d], d) for d in range(1, line)]
    queries = [queries[0]] + [line_shift(queries[d], d) for d in range(1, line)]
    pairs = pairs + [x_swap(both) for both in pairs]

    squares = token_sum(squares)
    factors = lax.rsqrt(squares / model_width + epsilon)
    notes = jnp.concatenate(
        [factors, labels.astype(f32)[None, :], positions.astype(f32)[None, :]], axis=0
    )
    notes = jnp.stack([notes] + [line_shift(notes, d) for d in range(1, line)])
    notes = jnp.concatenate([notes, x_swap(notes)], axis=0)
    codes = notes[:, 2, :].astype(jnp.int32) * key_rows + notes[:, 3, :].astype(jnp.int32)
    lows = notes[:line, 2, :].astype(jnp.int32) * key_rows
    live = (
        (jnp.min(codes, axis=1)[None, :] <= jnp.max(codes[:line], axis=1)[:, None])
        & (jnp.max(codes, axis=1)[None, :] >= jnp.min(lows, axis=1)[:, None])
    ).astype(jnp.int32)

    turned, log_total, queries_n, keys_n, code_columns, code_rows, *attended_out = attend(
        key_rows, live, notes, queries, pairs
    )

    def gather_heads(home):
        twice = jnp.concatenate(home + home, axis=1)
        return lax.dynamic_slice_in_dim(
            twice, lax.rem(line - z, line) * head_width, local_width, 1
        )

    def send_home(pieces):
        return [pieces[0]] + [line_shift(pieces[d], line - d) for d in range(1, line)]

    attended_low = gather_heads(send_home(attended_out))
    own_tokens = own_rows(tokens)
    tokens_in = reorder(tokens)
    tokens_own_x = x_swap(after(own_tokens, pairs[-1]))
    tokens_x = join_parts(tokens_own_x, core_swap(tokens_own_x))
    attended_low = after(attended_low, tokens_x)
    g_attn = gain_attn.reshape(1, model_width)
    g_mlp = gain_mlp.reshape(1, model_width)
    (
        output,
        hidden_low,
        hidden_x,
        act_low,
        act_x,
        grad_mlp,
        grad_mlp_x,
        grad_gate,
        grad_gate_far,
        grad_up,
        grad_up_far,
        grad_attn,
        grad_attended,
        grad_hidden,
        wide_gains,
    ) = block(
        attended_low,
        w_output,
        own_tokens,
        own_rows(cotangent),
        g_attn,
        g_mlp,
        w_gate,
        w_up,
        w_down,
    )
    grad_gate_x = x_swap(grad_gate_far)
    grad_up_x = x_swap(grad_up_far)
    down = Spread(place, x, (act_low, act_x), (grad_mlp, grad_mlp_x), False)
    down.neighbour()
    gate = Spread(place, x, (hidden_low, hidden_x), (grad_gate, grad_gate_x), True)
    up = Spread(place, x, (hidden_low, hidden_x), (grad_up, grad_up_x), True)
    gate.neighbour()
    up.neighbour()

    def head_of(value, d):
        return lax.dynamic_slice_in_dim(
            value, lax.rem(z + d, line) * head_width, head_width, 1
        )

    grads = [
        head_of(grad_attended, d) if d == 0 else line_shift(head_of(grad_attended, d), d)
        for d in range(line)
    ]
    attended_far, grad_attn_far = after(
        (half_of(attended_low, 1 - x), own_part(grad_attn)), gate.sent, up.sent
    )
    attended_x = x_swap(attended_far)
    grad_attn_own = x_swap(grad_attn_far)
    grad_attn_x = join_parts(grad_attn_own, core_swap(grad_attn_own))
    out = Spread(place, x, (attended_low, attended_x), (grad_attn, grad_attn_x), False)

    back = attend_back(
        live, code_columns, code_rows, queries_n, keys_n, pairs, turned, log_total, grads
    )
    grad_query_pieces, grad_pairs = back[:line], back[line:]
    far_pairs = [x_swap(grad_pairs[line + d]) for d in range(line)]
    far_pairs = after(far_pairs, gate.sent, up.sent, down.second())
    summed_pairs = [
        (grad_pairs[d].astype(f32) + far_pairs[d].astype(f32)).astype(bf16) for d in range(line)
    ]
    home = send_home(summed_pairs)
    out.neighbour()
    home = after(home, gate.second(), out.sent)
    query_home = after(send_home(grad_query_pieces), gate.sent, up.sent)
    grad_queries = gather_heads(query_home).astype(f32)
    grad_keys = gather_heads([piece[0] for piece in home]).astype(f32)
    grad_values_low = gather_heads([piece[1] for piece in home])

    def turn_back(value):
        parts = []
        for h in range(heads_here):
            part = value[:, h * head_width : (h + 1) * head_width]
            swapped = jnp.concatenate(
                [part[:, head_width // 2 :], part[:, : head_width // 2]], axis=1
            )
            parts.append(part * cosines - swapped * sines)
        return jnp.concatenate(parts, axis=1)

    q_factor = factors[0][:, None]
    k_factor = factors[1][:, None]
    q_normed = q_raw * q_factor
    k_normed = k_raw * k_factor
    back_q = turn_back(grad_queries)
    back_k = turn_back(grad_keys)
    grad_gain_query = jnp.sum(back_q * q_normed, axis=0)
    grad_gain_key = jnp.sum(back_k * k_normed, axis=0)
    scaled_q = back_q * g_query
    scaled_k = back_k * g_key
    inner = token_sum(
        jnp.stack([jnp.sum(scaled_q * q_normed, axis=1), jnp.sum(scaled_k * k_normed, axis=1)])
    )
    grad_q_raw = (q_factor * (scaled_q - q_normed * inner[0][:, None] / model_width)).astype(bf16)
    grad_k_raw = (k_factor * (scaled_k - k_normed * inner[1][:, None] / model_width)).astype(bf16)
    raw_parts = (grad_q_raw, grad_k_raw, grad_values_low)
    grad_raw = jnp.concatenate([half_of(part, x) for part in raw_parts], axis=1)
    grad_raw_x = x_swap(jnp.concatenate([half_of(part, 1 - x) for part in raw_parts], axis=1))
    input_sum = reduce_own_rows(
        (
            dot_nt(grad_q_raw, w_query)
            + dot_nt(grad_k_raw, w_key)
            + dot_nt(grad_values_low, w_value)
        ).astype(bf16)
    )
    grad_raw_x = after(grad_raw_x, up.second(), out.second())
    raw = Spread(place, x, (tokens_in, tokens_x), (grad_raw, grad_raw_x), True)
    raw.neighbour()
    raw.second()
    down_near, down_far = down.finish(raw.sent)
    gate_near, gate_far = gate.finish(raw.sent)
    up_near, up_far = up.finish(raw.sent)
    out_near, out_far = out.finish(raw.sent)
    raw_near, raw_far = raw.finish(raw.sent)
    own_grad_tokens = (grad_hidden + input_sum).astype(bf16)
    grad_tokens = restore(own_grad_tokens, core_swap(own_grad_tokens))

    wide = wide_gains.reshape(2 * model_width)
    wide = wide + core_swap(wide)
    gains = jnp.concatenate([wide, grad_gain_query, grad_gain_key])
    gains = gains + x_swap(gains)
    for bit in (1, 2):
        gains = gains + line_flip(gains, bit)
    piece = head_width // (line * pair)

    def gain_piece(start, rows):
        part = gains[start : start + rows * head_width].reshape(rows, head_width)
        return lax.dynamic_slice_in_dim(part, spot * piece, piece, 1)

    all_heads = model_width // head_width
    part_width = local_width // pair

    def raw_result(index):
        cut = slice(index * part_width, (index + 1) * part_width)
        return join_halves(raw_near[:, cut], raw_far[:, cut], 1)

    return (
        output,
        grad_tokens,
        raw_result(0),
        raw_result(1),
        raw_result(2),
        join_halves(out_near, out_far, 0),
        join_halves(gate_near, gate_far, 1),
        join_halves(up_near, up_far, 1),
        join_halves(down_near, down_far, 0),
        gain_piece(2 * model_width, heads_here),
        gain_piece(2 * model_width + local_width, heads_here),
        gain_piece(0, all_heads),
        gain_piece(model_width, all_heads),
    )


def solution(mesh):
    tuned = mesh.shape["dp"] == line * pair and mesh.shape["mp"] == 4
    body = on_device_lines if tuned else on_device_general
    return jax.shard_map(
        body,
        mesh=mesh,
        in_specs=(
            P("dp", None),
            P("dp", None),
            P("dp"),
            P("dp"),
            P("dp"),
            P(None, "mp"),
            P(None, "mp"),
            P(None, "mp"),
            P("mp", None),
            P(None, "mp"),
            P(None, "mp"),
            P("mp", None),
            P("mp", None),
            P("mp", None),
            P(),
            P(),
        ),
        out_specs=(
            P("dp", None),
            P("dp", None),
            P("dp", "mp"),
            P("dp", "mp"),
            P("dp", "mp"),
            P("mp", "dp"),
            P("dp", "mp"),
            P("dp", "mp"),
            P("mp", "dp"),
            P("mp", "dp"),
            P("mp", "dp"),
            P(None, "dp"),
            P(None, "dp"),
        ),
        check_vma=False,
    )
```

```python
import functools
import math

import jax
import jax.numpy as jnp
from jax import lax
from jax.experimental import pallas as pl
from jax.experimental.pallas import tpu as pltpu
from jax.sharding import PartitionSpec as P

epsilon = 1e-06
rope_base = 500000.0
masked_score = -1e30


def rope_tables(positions, head_width):
    freqs = rope_base ** (-jnp.arange(0, head_width // 2, dtype=jnp.float32) * 2.0 / head_width)
    angles = positions.astype(jnp.float32)[:, None] * freqs[None, :]
    return (jnp.cos(angles)[:, None, :], jnp.sin(angles)[:, None, :])


def rotate(values, cosines, sines):
    half = values.shape[-1] // 2
    first = values[..., :half]
    second = values[..., half:]
    return jnp.concatenate(
        [first * cosines - second * sines, second * cosines + first * sines], axis=-1
    )


def norm_back(grad_normed, normed, factor):
    return factor * (grad_normed - normed * jnp.mean(grad_normed * normed, axis=-1, keepdims=True))


def on_device_general(
    tokens,
    cotangent,
    doc_ids,
    row_ids,
    offsets,
    w_query,
    w_key,
    w_value,
    w_output,
    w_gate,
    w_up,
    w_down,
    gain_query,
    gain_key,
    gain_attn,
    gain_mlp,
):
    f32 = jnp.float32
    bf16 = jnp.bfloat16
    row_count = tokens.shape[0]
    model_width = tokens.shape[1]
    heads_here = gain_query.shape[0]
    head_width = gain_query.shape[1]
    local_width = heads_here * head_width
    groups = lax.axis_size("dp")
    key_rows = row_count * groups
    block_rows = min(key_rows, row_count * max(1, 512 // row_count))
    block_count = key_rows // block_rows
    score_scale = 1.0 / math.sqrt(head_width)
    positions = offsets[0] + jnp.arange(row_count, dtype=jnp.int32)
    labels = row_ids[0] * key_rows + doc_ids
    cosines, sines = rope_tables(positions, head_width)
    q_raw = jnp.dot(tokens, w_query, preferred_element_type=f32)
    k_raw = jnp.dot(tokens, w_key, preferred_element_type=f32)
    v_raw = jnp.dot(tokens, w_value, preferred_element_type=f32)
    squares = lax.psum(
        jnp.stack([jnp.sum(q_raw * q_raw, axis=1), jnp.sum(k_raw * k_raw, axis=1)]), "mp"
    )
    q_factor = lax.rsqrt(squares[0] / model_width + epsilon)[:, None]
    k_factor = lax.rsqrt(squares[1] / model_width + epsilon)[:, None]
    g_query = gain_query.reshape(local_width)
    g_key = gain_key.reshape(local_width)
    q_normed = q_raw * q_factor
    k_normed = k_raw * k_factor
    queries = rotate(
        (q_normed * g_query).reshape(row_count, heads_here, head_width), cosines, sines
    ).astype(bf16)
    keys_low = rotate(
        (k_normed * g_key).reshape(row_count, heads_here, head_width), cosines, sines
    ).astype(bf16)
    values_low = v_raw.astype(bf16)
    all_keys, all_values, all_labels, all_positions = (
        lax.all_gather(keys_low.reshape(row_count, local_width), "dp", axis=0, tiled=True),
        lax.all_gather(values_low, "dp", axis=0, tiled=True),
        lax.all_gather(labels, "dp", axis=0, tiled=True),
        lax.all_gather(positions, "dp", axis=0, tiled=True),
    )
    key_blocks = all_keys.reshape(block_count, block_rows, heads_here, head_width)
    value_blocks = all_values.reshape(block_count, block_rows, heads_here, head_width)
    label_blocks = all_labels.reshape(block_count, block_rows)
    position_blocks = all_positions.reshape(block_count, block_rows)
    scanned = (key_blocks, value_blocks, label_blocks, position_blocks)
    low_label = jnp.min(labels)
    high_label = jnp.max(labels)

    def scores_of(key_block, label_block, position_block):
        scores = (
            jnp.einsum("qhd,khd->hqk", queries, key_block, preferred_element_type=f32) * score_scale
        )
        allowed = (labels[:, None] == label_block[None, :]) & (
            positions[:, None] >= position_block[None, :]
        )
        return (scores, allowed[None])

    def touches(label_block):
        return (jnp.max(label_block) >= low_label) & (jnp.min(label_block) <= high_label)

    def max_step(carry, blocks_in):
        key_block, value_block, label_block, position_block = blocks_in

        def max_live_block(state):
            running, totals = state
            scores, allowed = scores_of(key_block, label_block, position_block)
            highest = jnp.maximum(
                running, jnp.max(jnp.where(allowed, scores, masked_score), axis=2)
            )
            weights = jnp.where(allowed, jnp.exp(scores - highest[:, :, None]), 0.0)
            return (highest, totals * jnp.exp(running - highest) + jnp.sum(weights, axis=2))

        return (lax.cond(touches(label_block), max_live_block, lambda state: state, carry), None)

    start_state = (
        jnp.full((heads_here, row_count), masked_score, f32),
        jnp.zeros((heads_here, row_count), f32),
    )
    (running_max, running_total), _ = lax.scan(max_step, start_state, scanned)
    log_total = running_max + jnp.log(running_total)

    def value_step(accum, blocks_in):
        key_block, value_block, label_block, position_block = blocks_in

        def value_live_block(current):
            scores, allowed = scores_of(key_block, label_block, position_block)
            probs_low = jnp.where(allowed, jnp.exp(scores - log_total[:, :, None]), 0.0).astype(
                bf16
            )
            return current + jnp.einsum(
                "hqk,khd->qhd", probs_low, value_block, preferred_element_type=f32
            )

        return (
            lax.cond(touches(label_block), value_live_block, lambda current: current, accum),
            None,
        )

    attended, _ = lax.scan(value_step, jnp.zeros((row_count, heads_here, head_width), f32), scanned)
    attended_low = attended.reshape(row_count, local_width).astype(bf16)
    attn_sum = lax.psum(
        jnp.dot(attended_low, w_output, preferred_element_type=f32).astype(jnp.bfloat16), "mp"
    ).astype(jnp.float32)
    attn_factor = lax.rsqrt(jnp.mean(attn_sum * attn_sum, axis=1, keepdims=True) + epsilon)
    attn_normed = attn_sum * attn_factor
    g_attn = gain_attn.reshape(model_width)
    hidden = tokens.astype(f32) + attn_normed * g_attn
    hidden_low = hidden.astype(bf16)
    gate_val = jnp.dot(hidden_low, w_gate, preferred_element_type=f32)
    up_val = jnp.dot(hidden_low, w_up, preferred_element_type=f32)
    sigmoid_gate = jax.nn.sigmoid(gate_val)
    silu_gate = gate_val * sigmoid_gate
    act_low = (silu_gate * up_val).astype(bf16)
    mlp_sum = lax.psum(
        jnp.dot(act_low, w_down, preferred_element_type=f32).astype(jnp.bfloat16), "mp"
    ).astype(jnp.float32)
    mlp_factor = lax.rsqrt(jnp.mean(mlp_sum * mlp_sum, axis=1, keepdims=True) + epsilon)
    mlp_normed = mlp_sum * mlp_factor
    g_mlp = gain_mlp.reshape(model_width)
    output = (hidden + mlp_normed * g_mlp).astype(bf16)
    grad_out = cotangent.astype(f32)
    grad_gain_mlp = jnp.sum(grad_out * mlp_normed, axis=0)
    grad_mlp = norm_back(grad_out * g_mlp, mlp_normed, mlp_factor).astype(bf16)
    grad_w_down = jnp.einsum("tf,td->fd", act_low, grad_mlp, preferred_element_type=f32)
    grad_act = jnp.einsum("td,fd->tf", grad_mlp, w_down, preferred_element_type=f32)
    slope = sigmoid_gate * (1.0 + gate_val * (1.0 - sigmoid_gate))
    grad_gate = (grad_act * up_val * slope).astype(bf16)
    grad_up = (grad_act * silu_gate).astype(bf16)
    branch_grad = jnp.einsum(
        "tf,df->td", grad_gate, w_gate, preferred_element_type=f32
    ) + jnp.einsum("tf,df->td", grad_up, w_up, preferred_element_type=f32)
    grad_hidden = grad_out + lax.psum(branch_grad.astype(jnp.bfloat16), "mp").astype(jnp.float32)
    grad_gain_attn = jnp.sum(grad_hidden * attn_normed, axis=0)
    grad_attn = norm_back(grad_hidden * g_attn, attn_normed, attn_factor).astype(bf16)
    grad_w_output = jnp.einsum("tc,td->cd", attended_low, grad_attn, preferred_element_type=f32)
    grad_attended = (
        jnp.einsum("td,cd->tc", grad_attn, w_output, preferred_element_type=f32)
        .astype(bf16)
        .reshape(row_count, heads_here, head_width)
    )
    delta = jnp.sum(grad_attended.astype(f32) * attended, axis=2).T

    def grad_step(grad_q, blocks_in):
        key_block, value_block, label_block, position_block = blocks_in

        def grad_live_block(current):
            scores, allowed = scores_of(key_block, label_block, position_block)
            probs = jnp.where(allowed, jnp.exp(scores - log_total[:, :, None]), 0.0)
            grad_probs = jnp.einsum(
                "qhd,khd->hqk", grad_attended, value_block, preferred_element_type=f32
            )
            grad_scores = (probs * (grad_probs - delta[:, :, None])).astype(bf16)
            value_term = jnp.einsum(
                "hqk,qhd->khd", probs.astype(bf16), grad_attended, preferred_element_type=f32
            )
            key_term = jnp.einsum("hqk,qhd->khd", grad_scores, queries, preferred_element_type=f32)
            updated = current + jnp.einsum(
                "hqk,khd->qhd", grad_scores, key_block, preferred_element_type=f32
            )
            return (updated, (key_term, value_term))

        def skip_block(current):
            nothing = jnp.zeros((block_rows, heads_here, head_width), f32)
            return (current, (nothing, nothing))

        return lax.cond(touches(label_block), grad_live_block, skip_block, grad_q)

    grad_queries, (key_terms, value_terms) = lax.scan(
        grad_step, jnp.zeros((row_count, heads_here, head_width), f32), scanned
    )
    grad_keys, grad_values = (
        lax.psum_scatter(
            (key_terms.reshape(key_rows, local_width) * score_scale).astype(jnp.bfloat16),
            "dp",
            scatter_dimension=0,
            tiled=True,
        ).astype(jnp.float32),
        lax.psum_scatter(
            value_terms.reshape(key_rows, local_width).astype(jnp.bfloat16),
            "dp",
            scatter_dimension=0,
            tiled=True,
        ).astype(jnp.float32),
    )
    grad_values_low = grad_values.astype(bf16)
    back_q = rotate(grad_queries * score_scale, cosines, -sines).reshape(row_count, local_width)
    back_k = rotate(grad_keys.reshape(row_count, heads_here, head_width), cosines, -sines).reshape(
        row_count, local_width
    )
    grad_gain_query = jnp.sum(back_q * q_normed, axis=0).reshape(heads_here, head_width)
    grad_gain_key = jnp.sum(back_k * k_normed, axis=0).reshape(heads_here, head_width)
    scaled_q = back_q * g_query
    scaled_k = back_k * g_key
    inner = lax.psum(
        jnp.stack([jnp.sum(scaled_q * q_normed, axis=1), jnp.sum(scaled_k * k_normed, axis=1)]),
        "mp",
    )
    grad_q_raw = (q_factor * (scaled_q - q_normed * inner[0][:, None] / model_width)).astype(bf16)
    grad_k_raw = (k_factor * (scaled_k - k_normed * inner[1][:, None] / model_width)).astype(bf16)
    input_term = (
        jnp.einsum("tc,dc->td", grad_q_raw, w_query, preferred_element_type=f32)
        + jnp.einsum("tc,dc->td", grad_k_raw, w_key, preferred_element_type=f32)
        + jnp.einsum("tc,dc->td", grad_values_low, w_value, preferred_element_type=f32)
    )
    grad_tokens = (
        grad_hidden + lax.psum(input_term.astype(jnp.bfloat16), "mp").astype(jnp.float32)
    ).astype(bf16)
    local_w_query = jnp.einsum("td,tc->dc", tokens, grad_q_raw, preferred_element_type=f32)
    local_w_key = jnp.einsum("td,tc->dc", tokens, grad_k_raw, preferred_element_type=f32)
    local_w_value = jnp.einsum("td,tc->dc", tokens, grad_values_low, preferred_element_type=f32)
    local_w_gate = jnp.einsum("td,tf->df", hidden_low, grad_gate, preferred_element_type=f32)
    local_w_up = jnp.einsum("td,tf->df", hidden_low, grad_up, preferred_element_type=f32)
    grad_w_query, grad_w_key, grad_w_value, grad_w_gate, grad_w_up = (
        lax.psum_scatter(
            local_w_query.astype(jnp.bfloat16), "dp", scatter_dimension=0, tiled=True
        ).astype(jnp.float32),
        lax.psum_scatter(
            local_w_key.astype(jnp.bfloat16), "dp", scatter_dimension=0, tiled=True
        ).astype(jnp.float32),
        lax.psum_scatter(
            local_w_value.astype(jnp.bfloat16), "dp", scatter_dimension=0, tiled=True
        ).astype(jnp.float32),
        lax.psum_scatter(
            local_w_gate.astype(jnp.bfloat16), "dp", scatter_dimension=0, tiled=True
        ).astype(jnp.float32),
        lax.psum_scatter(
            local_w_up.astype(jnp.bfloat16), "dp", scatter_dimension=0, tiled=True
        ).astype(jnp.float32),
    )
    summed_out, summed_down, summed_gq, summed_gk, summed_ga, summed_gm = (
        lax.psum_scatter(
            grad_w_output.astype(jnp.bfloat16), "dp", scatter_dimension=1, tiled=True
        ).astype(jnp.float32),
        lax.psum_scatter(
            grad_w_down.astype(jnp.bfloat16), "dp", scatter_dimension=1, tiled=True
        ).astype(jnp.float32),
        lax.psum_scatter(
            grad_gain_query.astype(jnp.bfloat16), "dp", scatter_dimension=1, tiled=True
        ).astype(jnp.float32),
        lax.psum_scatter(
            grad_gain_key.astype(jnp.bfloat16), "dp", scatter_dimension=1, tiled=True
        ).astype(jnp.float32),
        lax.psum_scatter(
            grad_gain_attn.reshape(gain_attn.shape).astype(jnp.bfloat16),
            "dp",
            scatter_dimension=1,
            tiled=True,
        ).astype(jnp.float32),
        lax.psum_scatter(
            grad_gain_mlp.reshape(gain_mlp.shape).astype(jnp.bfloat16),
            "dp",
            scatter_dimension=1,
            tiled=True,
        ).astype(jnp.float32),
    )
    return (
        output,
        grad_tokens,
        grad_w_query,
        grad_w_key,
        grad_w_value,
        summed_out,
        grad_w_gate,
        grad_w_up,
        summed_down,
        summed_gq,
        summed_gk,
        summed_ga,
        summed_gm,
    )


line = 4
pair = 2
low_score = -1e30
start_max = -1e20
big_vmem = 56 << 20


def line_shift(value, step):
    moves = [
        (z * pair + x, ((z + step) % line) * pair + x) for z in range(line) for x in range(pair)
    ]
    return lax.ppermute(value, "dp", moves)


def line_flip(value, bit):
    return lax.ppermute(
        value, "dp", [(z * pair + x, (z ^ bit) * pair + x) for z in range(line) for x in range(pair)]
    )


def x_swap(value):
    return lax.ppermute(value, "dp", [(i, i ^ 1) for i in range(line * pair)])


def core_swap(value):
    return lax.ppermute(value, "mp", [(i, i ^ 1) for i in range(4)])


def y_swap(value):
    return lax.ppermute(value, "mp", [(i, i ^ 2) for i in range(4)])


def flip_cores(value, axis):
    quarter = value.shape[axis] // 4
    cuts = [lax.slice_in_dim(value, i * quarter, (i + 1) * quarter, axis=axis) for i in (1, 0, 3, 2)]
    return jnp.concatenate(cuts, axis=axis)


def token_sum(value):
    value = value + flip_cores(core_swap(value), 1)
    return value + y_swap(value)


def own_part(value):
    quarter = value.shape[0] // 4
    return jnp.concatenate([value[:quarter], value[2 * quarter : 3 * quarter]], axis=0)


def other_part(value):
    quarter = value.shape[0] // 4
    return jnp.concatenate([value[quarter : 2 * quarter], value[3 * quarter :]], axis=0)


def join_parts(own, other):
    half = own.shape[0] // 2
    return jnp.concatenate([own[:half], other[:half], own[half:], other[half:]], axis=0)


def reduce_own_rows(partial_low):
    f32 = jnp.float32
    arrived = core_swap(other_part(partial_low))
    chip_sum = (own_part(partial_low).astype(f32) + arrived.astype(f32)).astype(jnp.bfloat16)
    return chip_sum.astype(f32) + y_swap(chip_sum).astype(f32)


def dot_t(first, second):
    return lax.dot_general(
        first, second, (((0,), (0,)), ((), ())), preferred_element_type=jnp.float32
    )


def dot_nt(first, second):
    return lax.dot_general(
        first, second, (((1,), (1,)), ((), ())), preferred_element_type=jnp.float32
    )


def vmem_specs(count):
    return [pl.BlockSpec(memory_space=pltpu.VMEM)] * count


def project_kernel(
    tokens,
    wq,
    wk,
    wv,
    gq,
    gk,
    cosines,
    sines,
    spots,
    out_queries,
    out_pairs,
    out_notes,
    out_q_raw,
    out_k_raw,
    rows_keep,
    query_keep,
    pair_keep,
    squares,
    squares_core,
    squares_y,
    send_sems,
    recv_sems,
    local_sems,
):
    f32 = jnp.float32
    bf16 = jnp.bfloat16
    width = cosines.shape[1]
    depth = wq.shape[0]
    rows = rows_keep.shape[0] // 2
    count = rows // 2
    mp = lax.axis_index("mp")
    spot = lax.axis_index("dp")
    core = lax.rem(mp, 2)
    x = lax.rem(spot, 2)
    z = spot // 2
    core_peer = {"mp": mp + 1 - 2 * core}
    y_peer = {"mp": lax.rem(mp + 2, 4)}
    x_peer = {"dp": spot + 1 - 2 * x}
    ahead = [{"dp": lax.rem(spot + 2 * d, 2 * line)} for d in range(line)]
    head = [lax.rem(z + d, line) for d in range(line)]
    both = lambda s: pl.ds(s * rows, rows)
    remote = []

    def send(source, target, peer):
        index = len(remote)
        copy = pltpu.make_async_remote_copy(
            src_ref=source,
            dst_ref=target,
            send_sem=send_sems.at[index],
            recv_sem=recv_sems.at[index],
            device_id=peer,
            device_id_type=pl.DeviceIdType.MESH,
        )
        remote.append(copy)
        copy.start()
        return copy

    loads = []
    for s in range(2):
        for part, place in ((0, core), (1, 1 - core)):
            start = pl.multiple_of(place * rows + s * count, count)
            copy = pltpu.make_async_copy(
                tokens.at[pl.ds(start, count)],
                rows_keep.at[pl.ds(s * rows + part * count, count)],
                local_sems.at[2 * s + part],
            )
            copy.start()
            loads.append(copy)

    barrier = pltpu.get_barrier_semaphore()
    peers = (core_peer, y_peer, x_peer, ahead[1], ahead[2], ahead[3])
    for peer in peers:
        pl.semaphore_signal(barrier, inc=1, device_id=peer, device_id_type=pl.DeviceIdType.MESH)
    pl.semaphore_wait(barrier, len(peers))

    def turned(raw, gain, s, h):
        part = raw[:, h * width : (h + 1) * width] * gain[:, h * width : (h + 1) * width]
        return (
            part * cosines[both(s), :] + pltpu.roll(part, width // 2, 1) * sines[both(s), :]
        ).astype(bf16)

    flying = {}
    for s in range(2):
        loads[2 * s].wait()
        loads[2 * s + 1].wait()
        k_raw = jnp.dot(rows_keep[both(s), :], wk[...], preferred_element_type=f32)
        out_k_raw[both(s), :] = k_raw
        squares[1:2, both(s)] = jnp.sum((k_raw * k_raw).T, axis=0, keepdims=True)
        v_raw = jnp.dot(rows_keep[both(s), :], wv[...], preferred_element_type=f32)
        for h in range(line):
            pair_keep[h, 0, both(s), :] = turned(k_raw, gk[...], s, h)
            pair_keep[h, 1, both(s), :] = v_raw[:, h * width : (h + 1) * width].astype(bf16)
        for d in (2, 1, 3):
            flying["pair", s, d] = send(
                pair_keep.at[head[d], :, both(s)], out_pairs.at[d, :, both(s)], ahead[d]
            )
        flying["far", s, 0] = send(
            pair_keep.at[z, :, both(s)], out_pairs.at[line, :, both(s)], x_peer
        )
        q_raw = jnp.dot(rows_keep[both(s), :], wq[...], preferred_element_type=f32)
        out_q_raw[both(s), :] = q_raw
        squares[0:1, both(s)] = jnp.sum((q_raw * q_raw).T, axis=0, keepdims=True)
        for h in range(line):
            query_keep[h, both(s), :] = turned(q_raw, gq[...], s, h)

    core_copy = send(squares, squares_core, core_peer)
    core_copy.wait()
    arrived = squares_core[...]
    cuts = [arrived[:, i * count : (i + 1) * count] for i in (1, 0, 3, 2)]
    chip = squares[...] + jnp.concatenate(cuts, axis=1)
    squares[...] = chip
    y_copy = send(squares, squares_y, y_peer)
    y_copy.wait()
    out_notes[0, 0:2, :] = lax.rsqrt((chip + squares_y[...]) / depth + epsilon)
    out_notes[0, 2:4, :] = spots[...]
    for d in range(1, line):
        flying["note", d] = send(out_notes.at[0], out_notes.at[d], ahead[d])
    flying["far_note", 0] = send(out_notes.at[0], out_notes.at[line], x_peer)
    for d in range(1, line):
        flying["query", d] = send(query_keep.at[head[d]], out_queries.at[d], ahead[d])
    out_queries[0] = query_keep[z]
    out_pairs[0] = pair_keep[z]
    for s in range(2):
        for d in (2, 1, 3):
            flying["pair", s, d].wait()
            flying["far", s, d] = send(
                out_pairs.at[d, :, both(s)], out_pairs.at[line + d, :, both(s)], x_peer
            )
    for d in range(1, line):
        flying["note", d].wait()
        flying["far_note", d] = send(out_notes.at[d], out_notes.at[line + d], x_peer)
    for d in range(1, line):
        flying["query", d].wait()
    for d in range(line):
        flying["far_note", d].wait()
        for s in range(2):
            flying["far", s, d].wait()


def project(tokens, wq, wk, wv, gq, gk, cosines, sines, spots):
    rows, depth = tokens.shape
    columns = wq.shape[1]
    width = columns // line
    f32 = jnp.float32
    bf16 = jnp.bfloat16
    return pl.pallas_call(
        project_kernel,
        in_specs=[pl.BlockSpec(memory_space=pl.ANY)] + vmem_specs(8),
        out_specs=vmem_specs(5),
        out_shape=[
            jax.ShapeDtypeStruct((line, rows, width), bf16),
            jax.ShapeDtypeStruct((2 * line, 2, rows, width), bf16),
            jax.ShapeDtypeStruct((2 * line, 4, rows), f32),
            jax.ShapeDtypeStruct((rows, columns), f32),
            jax.ShapeDtypeStruct((rows, columns), f32),
        ],
        scratch_shapes=[
            pltpu.VMEM((rows, depth), bf16),
            pltpu.VMEM((line, rows, width), bf16),
            pltpu.VMEM((line, 2, rows, width), bf16),
            pltpu.VMEM((2, rows), f32),
            pltpu.VMEM((2, rows), f32),
            pltpu.VMEM((2, rows), f32),
            pltpu.SemaphoreType.DMA((28,)),
            pltpu.SemaphoreType.DMA((28,)),
            pltpu.SemaphoreType.DMA((4,)),
        ],
        compiler_params=pltpu.CompilerParams(
            vmem_limit_bytes=48 << 20, collective_id=2, has_side_effects=True
        ),
        cost_estimate=pl.CostEstimate(flops=0, bytes_accessed=0, transcendentals=0),
    )(tokens, wq, wk, wv, gq, gk, cosines, sines, spots)


def visible_scores(key, query, key_code, query_code, query_low, factor):
    scores = dot_nt(key, query) * factor
    codes = jnp.concatenate([key_code] * (query.shape[0] // key_code.shape[1]), axis=1)
    return jnp.where((codes <= query_code) & (codes >= query_low), scores, low_score)


def attend_kernel(factor, key_rows, live, notes, *refs):
    queries, pairs = refs[:2]
    out_turned, out_log, out_query, out_key, out_codes, out_rows, out = refs[2:9]
    top, total, accum = refs[9:]
    f32 = jnp.float32
    bf16 = jnp.bfloat16
    count, width = queries.shape[1:]

    def column(row):
        return jnp.broadcast_to(row, (width, count)).T

    for k in range(2 * line):
        out_key[k] = (pairs[k, 0].astype(f32) * column(notes[k, 1:2, :])).astype(bf16)
        labels = column(notes[k, 2:3, :]).astype(jnp.int32)
        out_codes[k] = labels * key_rows + column(notes[k, 3:4, :]).astype(jnp.int32)
    for q in range(line):
        out_query[q] = (queries[q].astype(f32) * column(notes[q, 0:1, :])).astype(bf16)
        base = notes[q, 2:3, :].astype(jnp.int32) * key_rows
        out_rows[q : q + 1, :] = base + notes[q, 3:4, :].astype(jnp.int32)
        out_rows[line + q : line + q + 1, :] = base

    for q in range(line):
        top[...] = jnp.full_like(top, start_max)
        total[...] = jnp.zeros_like(total)
        accum[...] = jnp.zeros_like(accum)
        for k in range(2 * line):

            @pl.when(live[q, k] > 0)
            def _(q=q, k=k):
                scores = visible_scores(
                    out_key[k],
                    out_query[q],
                    out_codes[k],
                    out_rows[q : q + 1, :],
                    out_rows[line + q : line + q + 1, :],
                    factor,
                )
                highest = jnp.maximum(top[...], jnp.max(scores, axis=0, keepdims=True))
                weights = jnp.exp2(scores - highest)
                fade = jnp.exp2(top[...] - highest)
                total[...] = total[...] * fade + jnp.sum(weights, axis=0, keepdims=True)
                accum[...] = accum[...] * fade + dot_t(pairs[k, 1], weights.astype(bf16))
                top[...] = highest

        turned = accum[...] / total[...]
        out_turned[q] = turned
        out_log[q : q + 1, :] = top[...] + jnp.log2(total[...])
        out[q] = turned.T.astype(bf16)


def attend_back_kernel(factor, scale, live, codes, rows, queries, keys, *refs):
    pairs, turned, log_total, grads = refs[:4]
    out_query = refs[4 : line + 4]
    out_pairs = refs[line + 4 : 3 * line + 4]
    key_sum, value_sum, query_sum = refs[3 * line + 4 :]
    f32 = jnp.float32
    bf16 = jnp.bfloat16
    key_sum[...] = jnp.zeros_like(key_sum)
    value_sum[...] = jnp.zeros_like(value_sum)
    for q in range(line):
        query_sum[...] = jnp.zeros_like(query_sum)
        delta = jnp.sum(grads[q].astype(f32).T * turned[q], axis=0, keepdims=True)
        for k in range(2 * line):

            @pl.when(live[q, k] > 0)
            def _(q=q, k=k, delta=delta):
                query, key, grad = queries[q], keys[k], grads[q]
                scores = visible_scores(
                    key,
                    query,
                    codes[k],
                    rows[q : q + 1, :],
                    rows[line + q : line + q + 1, :],
                    factor,
                )
                probs = jnp.exp2(scores - log_total[q : q + 1, :])
                grad_probs = dot_nt(pairs[k, 1], grad)
                grad_scores = (probs * (grad_probs - delta)).astype(bf16)
                value_sum[k] += jnp.dot(
                    probs.astype(bf16), grad, preferred_element_type=f32
                )
                key_sum[k] += jnp.dot(grad_scores, query, preferred_element_type=f32)
                query_sum[...] += dot_t(key, grad_scores)

        out_query[q][...] = (query_sum[...] * scale).T.astype(bf16)
    for k in range(2 * line):
        out_pairs[k][0] = (key_sum[k] * scale).astype(bf16)
        out_pairs[k][1] = value_sum[k].astype(bf16)


def attend(key_rows, live, notes, queries, pairs):
    _, count, width = queries.shape
    factor = math.log2(math.e) / math.sqrt(width)
    f32 = jnp.float32
    bf16 = jnp.bfloat16
    return pl.pallas_call(
        functools.partial(attend_kernel, factor, key_rows),
        out_shape=[
            jax.ShapeDtypeStruct((line, width, count), f32),
            jax.ShapeDtypeStruct((2 * line, count), f32),
            jax.ShapeDtypeStruct((line, count, width), bf16),
            jax.ShapeDtypeStruct((2 * line, count, width), bf16),
            jax.ShapeDtypeStruct((2 * line, count, width), jnp.int32),
            jax.ShapeDtypeStruct((2 * line, count), jnp.int32),
        ]
        + [jax.ShapeDtypeStruct((line, count, width), bf16)],
        in_specs=[pl.BlockSpec(memory_space=pltpu.SMEM)] + vmem_specs(3),
        out_specs=vmem_specs(7),
        scratch_shapes=[
            pltpu.VMEM((1, count), f32),
            pltpu.VMEM((1, count), f32),
            pltpu.VMEM((width, count), f32),
        ],
        compiler_params=pltpu.CompilerParams(vmem_limit_bytes=40 << 20),
        cost_estimate=pl.CostEstimate(flops=0, bytes_accessed=0, transcendentals=0),
    )(live, notes, queries, pairs)


def attend_back(live, codes, rows, queries, keys, pairs, turned, log_total, grads):
    _, count, width = queries.shape
    scale = 1.0 / math.sqrt(width)
    factor = math.log2(math.e) * scale
    f32 = jnp.float32
    return pl.pallas_call(
        functools.partial(attend_back_kernel, factor, scale),
        out_shape=[jax.ShapeDtypeStruct((count, width), jnp.bfloat16)] * line
        + [jax.ShapeDtypeStruct((2, count, width), jnp.bfloat16)] * (2 * line),
        in_specs=[pl.BlockSpec(memory_space=pltpu.SMEM)] + vmem_specs(8),
        out_specs=vmem_specs(3 * line),
        scratch_shapes=[
            pltpu.VMEM((2 * line, count, width), f32),
            pltpu.VMEM((2 * line, count, width), f32),
            pltpu.VMEM((width, count), f32),
        ],
        compiler_params=pltpu.CompilerParams(vmem_limit_bytes=40 << 20),
        cost_estimate=pl.CostEstimate(
            flops=20 * line * line * count * count * width,
            bytes_accessed=12 << 20,
            transcendentals=2 * line * line * count * count,
        ),
    )(live, codes, rows, queries, keys, pairs, turned, log_total, grads)


def block_kernel(
    pieces,
    w_out,
    g_attn,
    g_mlp,
    tokens,
    cotangent,
    w_gate_in,
    w_up_in,
    w_down_in,
    out_heads,
    out_tokens_x,
    out_output,
    out_hidden,
    out_hidden_x,
    out_act,
    out_act_x,
    out_mlp,
    out_mlp_x,
    out_gate,
    out_gate_far,
    out_up,
    out_up_far,
    out_attn,
    out_grads,
    out_grad_hidden,
    out_gain,
    w_gate,
    w_up,
    w_down,
    gate_keep,
    up_keep,
    act_keep,
    hidden_keep,
    mlp_keep,
    attn_keep,
    grad_gate,
    grad_up,
    own_factor,
    own_normed,
    own_tokens,
    own_cotangent,
    attended,
    heads_keep,
    total,
    part_send,
    part_recv,
    y_send,
    y_recv,
    send_sems,
    recv_sems,
    local_sems,
):
    f32 = jnp.float32
    bf16 = jnp.bfloat16
    depth = w_out.shape[1]
    units = w_gate.shape[1]
    tile = 512
    count = own_tokens.shape[0] // 2
    rows = 2 * count
    mp = lax.axis_index("mp")
    spot = lax.axis_index("dp")
    core = lax.rem(mp, 2)
    x = lax.rem(spot, 2)
    core_peer = {"mp": mp + 1 - 2 * core}
    y_peer = {"mp": lax.rem(mp + 2, 4)}
    x_peer = {"dp": spot + 1 - 2 * x}
    z = spot // 2
    width = pieces.shape[2]
    ahead = [{"dp": lax.rem(spot + 2 * d, 2 * line)} for d in range(line)]
    head = lambda d: pl.ds(pl.multiple_of(lax.rem(z + d, line) * width, width), width)

    remote, started, local = [], [], []

    def send(source, target, peer):
        index = len(remote)
        copy = pltpu.make_async_remote_copy(
            src_ref=source,
            dst_ref=target,
            send_sem=send_sems.at[index],
            recv_sem=recv_sems.at[index],
            device_id=peer,
            device_id_type=pl.DeviceIdType.MESH,
        )
        remote.append(copy)
        copy.start()
        return copy

    def keep_out(source, target, waited=False):
        copy = pltpu.make_async_copy(source, target, local_sems.at[len(started)])
        started.append(copy)
        if not waited:
            local.append(copy)
        copy.start()
        return copy

    own = lambda s: pl.ds(s * rows, count)
    other = lambda s: pl.ds(s * rows + count, count)
    both = lambda s: pl.ds(s * rows, rows)
    mine = lambda s: pl.ds(s * count, count)
    at_home = lambda s: pl.ds(pl.multiple_of(core * rows + s * count, count), count)
    cut = lambda t: pl.ds(pl.multiple_of(t * tile, tile), tile)
    flying = {}

    home_rows = pl.ds(pl.multiple_of(core * rows, rows), rows)
    loads = [
        keep_out(tokens.at[home_rows], own_tokens, True),
        keep_out(cotangent.at[home_rows], own_cotangent, True),
        keep_out(w_gate_in, w_gate, True),
        keep_out(w_up_in, w_up, True),
        keep_out(w_down_in, w_down, True),
    ]
    barrier = pltpu.get_barrier_semaphore()
    peers = (core_peer, y_peer, x_peer, ahead[1], ahead[2], ahead[3])
    for peer in peers:
        pl.semaphore_signal(barrier, inc=1, device_id=peer, device_id_type=pl.DeviceIdType.MESH)
    pl.semaphore_wait(barrier, len(peers))
    for s in range(2):
        for d in range(1, line):
            flying["heads", s, d] = send(
                pieces.at[d, both(s)], attended.at[both(s), head(0)], ahead[line - d]
            )
    attended[:, head(0)] = pieces[0]
    loads[0].wait()
    for s in range(2):
        flying["tokens", s] = send(own_tokens.at[mine(s)], out_tokens_x.at[own(s)], x_peer)

    def forward_core(name, s, array):
        flying[name, s].wait()
        flying[name + "_core", s] = send(array.at[own(s)], array.at[other(s)], core_peer)

    def reduce_start(stage, s):
        part_send[s] = total[count:, :].astype(bf16)
        copy = send(part_send.at[s], part_recv.at[s], core_peer)
        copy.wait()
        y_send[s] = (total[:count, :] + part_recv[s].astype(f32)).astype(bf16)
        flying[stage, s] = send(y_send.at[s], y_recv.at[stage, s], y_peer)

    def reduced(stage, s):
        flying[stage, s].wait()
        return y_send[s].astype(f32) + y_recv[stage, s].astype(f32)

    def factor_of(value):
        return lax.rsqrt(jnp.mean(value * value, axis=1, keepdims=True) + epsilon)

    def share(keep, s):
        flying["share", s] = send(keep.at[own(s)], keep.at[other(s)], core_peer)

    def project_out(s):
        for d in range(1, line):
            flying["heads", s, d].wait()
        keep_out(attended.at[both(s)], out_heads.at[both(s)])
        total[...] = jnp.dot(attended[both(s), :], w_out[...], preferred_element_type=f32)
        reduce_start(0, s)

    def after_attention(s):
        value = reduced(0, s)
        factor = factor_of(value)
        normed = value * factor
        own_factor[mine(s), :] = jnp.broadcast_to(factor, (count, own_factor.shape[1]))
        own_normed[mine(s), :] = normed
        hidden = own_tokens[mine(s), :].astype(f32) + normed * g_attn[...]
        out_grad_hidden[mine(s), :] = hidden
        hidden_keep[own(s), :] = hidden.astype(bf16)
        share(hidden_keep, s)

    def forward(s):
        flying["hidden", s] = send(hidden_keep.at[own(s)], out_hidden_x.at[own(s)], x_peer)
        flying["share", s].wait()
        keep_out(hidden_keep.at[both(s)], out_hidden.at[both(s)])

        def step(t):
            hidden = hidden_keep[both(s), :]
            gate = jnp.dot(hidden, w_gate[:, cut(t)], preferred_element_type=f32)
            up = jnp.dot(hidden, w_up[:, cut(t)], preferred_element_type=f32)
            gate_keep[both(s), cut(t)] = gate.astype(bf16)
            up_keep[both(s), cut(t)] = up.astype(bf16)
            act = (gate * jax.nn.sigmoid(gate) * up).astype(bf16)
            act_keep[both(s), cut(t)] = act
            return jnp.dot(act, w_down[cut(t), :], preferred_element_type=f32)

        total[...] = step(0)

        @pl.loop(1, units // tile)
        def _(t):
            total[...] += step(t)

        reduce_start(1, s)
        keep_out(act_keep.at[both(s)], out_act.at[both(s)])
        half = units // 2
        far = pl.ds(pl.multiple_of((1 - x) * half, half), half)
        flying["act", s] = send(act_keep.at[both(s), far], out_act_x.at[both(s)], x_peer)

    def turn_point(s):
        value = reduced(1, s)
        factor = factor_of(value)
        normed = value * factor
        forward_core("tokens", s, out_tokens_x)
        own_tokens[mine(s), :] = (out_grad_hidden[mine(s), :] + normed * g_mlp[...]).astype(bf16)
        keep_out(own_tokens.at[mine(s)], out_output.at[at_home(s)])
        flying["output", s] = send(own_tokens.at[mine(s)], out_output.at[at_home(s)], core_peer)
        grad = own_cotangent[mine(s), :].astype(f32)
        gain = jnp.sum(grad * normed, axis=0, keepdims=True)
        out_gain[1:2, :] = gain if s == 0 else out_gain[1:2, :] + gain
        mlp_keep[own(s), :] = norm_back(grad * g_mlp[...], normed, factor).astype(bf16)
        share(mlp_keep, s)

    def backward(s):
        flying["mlp", s] = send(mlp_keep.at[own(s)], out_mlp_x.at[own(s)], x_peer)
        flying["share", s].wait()
        keep_out(mlp_keep.at[both(s)], out_mlp.at[both(s)])

        def step(t):
            grad_act = dot_nt(mlp_keep[both(s), :], w_down[cut(t), :])
            gate = gate_keep[both(s), cut(t)].astype(f32)
            up = up_keep[both(s), cut(t)].astype(f32)
            sigmoid = jax.nn.sigmoid(gate)
            to_gate = (grad_act * up * (sigmoid * (1.0 + gate * (1.0 - sigmoid)))).astype(bf16)
            to_up = (grad_act * (gate * sigmoid)).astype(bf16)
            grad_gate[:, cut(t)] = to_gate
            grad_up[:, cut(t)] = to_up
            return dot_nt(to_gate, w_gate[:, cut(t)]) + dot_nt(to_up, w_up[:, cut(t)])

        if s > 0:
            for copy in flying["grads"]:
                copy.wait()
        total[...] = step(0)

        @pl.loop(1, units // tile)
        def _(t):
            total[...] += step(t)

        reduce_start(2, s)
        half = units // 2
        far = pl.ds(pl.multiple_of((1 - x) * half, half), half)
        flying["grads"] = [
            keep_out(source, target.at[both(s)], waited=s == 0)
            for source, target in (
                (grad_gate, out_gate),
                (grad_gate.at[:, far], out_gate_far),
                (grad_up, out_up),
                (grad_up.at[:, far], out_up_far),
            )
        ]

    def to_attention(s):
        value = reduced(2, s)
        grad = own_cotangent[mine(s), :].astype(f32) + value
        out_grad_hidden[mine(s), :] = grad
        normed = own_normed[mine(s), :]
        gain = jnp.sum(grad * normed, axis=0, keepdims=True)
        out_gain[0:1, :] = gain if s == 0 else out_gain[0:1, :] + gain
        factor = own_factor[mine(s), 0:1]
        attn_keep[own(s), :] = norm_back(grad * g_attn[...], normed, factor).astype(bf16)
        share(attn_keep, s)

    def attended_grad(s):
        flying["share", s].wait()
        keep_out(attn_keep.at[both(s)], out_attn.at[both(s)])
        heads_keep[both(s), :] = dot_nt(attn_keep[both(s), :], w_out[...]).astype(bf16)
        for d in range(1, line):
            flying["grads", s, d] = send(
                heads_keep.at[both(s), head(d)], out_grads.at[d, both(s)], ahead[d]
            )
        keep_out(heads_keep.at[both(s), head(0)], out_grads.at[0, both(s)])

    project_out(0)
    project_out(1)
    for load in loads[1:]:
        load.wait()
    after_attention(0)
    forward(0)
    after_attention(1)
    forward(1)
    turn_point(0)
    backward(0)
    turn_point(1)
    backward(1)
    for s in range(2):
        forward_core("hidden", s, out_hidden_x)
    to_attention(0)
    attended_grad(0)
    to_attention(1)
    attended_grad(1)
    for s in range(2):
        flying["act", s].wait()
        flying["output", s].wait()
        forward_core("mlp", s, out_mlp_x)
    for s in range(2):
        flying["tokens_core", s].wait()
        flying["hidden_core", s].wait()
        flying["mlp_core", s].wait()
        for d in range(1, line):
            flying["grads", s, d].wait()
    for copy in local:
        copy.wait()


def block(pieces, w_out, g_attn, g_mlp, tokens, cotangent, w_gate, w_up, w_down):
    _, rows, width = pieces.shape
    columns = line * width
    depth, units = w_gate.shape
    half = rows // 2
    quarter = rows // 4
    f32 = jnp.float32
    bf16 = jnp.bfloat16
    wide = jax.ShapeDtypeStruct((rows, depth), bf16)
    tall = jax.ShapeDtypeStruct((rows, units), bf16)
    any_spec = pl.BlockSpec(memory_space=pl.ANY)
    return pl.pallas_call(
        block_kernel,
        out_shape=[
            jax.ShapeDtypeStruct((rows, columns), bf16),
            wide,
            wide,
            wide,
            wide,
            tall,
            jax.ShapeDtypeStruct((rows, units // 2), bf16),
            wide,
            wide,
            tall,
            jax.ShapeDtypeStruct((rows, units // 2), bf16),
            tall,
            jax.ShapeDtypeStruct((rows, units // 2), bf16),
            wide,
            jax.ShapeDtypeStruct((line, rows, width), bf16),
            jax.ShapeDtypeStruct((half, depth), f32),
            jax.ShapeDtypeStruct((2, depth), f32),
        ],
        in_specs=vmem_specs(4) + [any_spec] * 5,
        out_specs=[any_spec] * 15 + vmem_specs(2),
        scratch_shapes=[
            pltpu.VMEM((depth, units), bf16),
            pltpu.VMEM((depth, units), bf16),
            pltpu.VMEM((units, depth), bf16),
            pltpu.VMEM((rows, units), bf16),
            pltpu.VMEM((rows, units), bf16),
            pltpu.VMEM((rows, units), bf16),
            pltpu.VMEM((rows, depth), bf16),
            pltpu.VMEM((rows, depth), bf16),
            pltpu.VMEM((rows, depth), bf16),
            pltpu.VMEM((half, units), bf16),
            pltpu.VMEM((half, units), bf16),
            pltpu.VMEM((half, 128), f32),
            pltpu.VMEM((half, depth), f32),
            pltpu.VMEM((half, depth), bf16),
            pltpu.VMEM((half, depth), bf16),
            pltpu.VMEM((rows, columns), bf16),
            pltpu.VMEM((rows, columns), bf16),
            pltpu.VMEM((half, depth), f32),
            pltpu.VMEM((2, quarter, depth), bf16),
            pltpu.VMEM((2, quarter, depth), bf16),
            pltpu.VMEM((2, quarter, depth), bf16),
            pltpu.VMEM((3, 2, quarter, depth), bf16),
            pltpu.SemaphoreType.DMA((52,)),
            pltpu.SemaphoreType.DMA((52,)),
            pltpu.SemaphoreType.DMA((32,)),
        ],
        compiler_params=pltpu.CompilerParams(
            vmem_limit_bytes=61800 << 10, collective_id=1, has_side_effects=True
        ),
        cost_estimate=pl.CostEstimate(flops=0, bytes_accessed=0, transcendentals=0),
    )(pieces, w_out, g_attn, g_mlp, tokens, cotangent, w_gate, w_up, w_down)


def weight_kernel(place, *refs):
    first, second, first_x, second_x = refs[:4]
    total = dot_t(first[...], second[...]) + dot_t(first_x[...], second_x[...])
    if len(refs) == 6:
        total = total + refs[4][...].astype(jnp.float32)
    refs[-1][...] = total.astype(refs[-1].dtype)


def line_block(which):
    if which < 2:
        return lambda p: 2 * which + 1 - p[2]
    if which == 2:
        return lambda p: 2 * (1 - p[3]) + p[2]
    return lambda p: 2 * p[3] + p[2]


def weight_term(place, first, second, cut_first, blocks, extra, kind):
    tokens = first[0].shape[0]
    cut_side, half_side = (first, second) if cut_first else (second, first)
    cut_tile = cut_side[0].shape[1] // line
    half_size = half_side[1].shape[1]
    half_tile = min(half_size, 512)
    while half_size % half_tile:
        half_tile -= 128
    half_count = half_size // half_tile
    own_half = half_count if half_side[0].shape[1] != half_size else 0
    count = len(blocks)

    def cut_map(i, j, p):
        index = line_block(blocks[0])(p)
        if count == 2:
            index = index + i * (line_block(blocks[1])(p) - line_block(blocks[0])(p))
        return (0, index)

    cut_spec = pl.BlockSpec((tokens, cut_tile), cut_map)
    half_own = pl.BlockSpec((tokens, half_tile), lambda i, j, p: (0, j + p[4] * own_half))
    half_far = pl.BlockSpec((tokens, half_tile), lambda i, j, p: (0, j))
    if cut_first:
        in_specs = [cut_spec, half_own, cut_spec, half_far]
        tile_shape = (cut_tile, half_tile)
        out_map = lambda i, j, p: (i, j)
        shape = (count * cut_tile, half_size)
        extra_map = lambda i, j, p: (extra[1](p) + i, j)
    else:
        in_specs = [half_own, cut_spec, half_far, cut_spec]
        tile_shape = (half_tile, cut_tile)
        out_map = lambda i, j, p: (j, i)
        shape = (half_size, count * cut_tile)
        extra_map = lambda i, j, p: (j, extra[1](p) + i)
    args = [first[0], second[0], first[1], second[1]]
    if extra is not None:
        in_specs.append(pl.BlockSpec(tile_shape, extra_map))
        args.append(extra[0])
    return pl.pallas_call(
        weight_kernel,
        grid_spec=pltpu.PrefetchScalarGridSpec(
            num_scalar_prefetch=1,
            grid=(count, half_count),
            in_specs=in_specs,
            out_specs=pl.BlockSpec(tile_shape, out_map),
        ),
        out_shape=jax.ShapeDtypeStruct(shape, kind),
        compiler_params=pltpu.CompilerParams(vmem_limit_bytes=big_vmem),
        cost_estimate=pl.CostEstimate(flops=0, bytes_accessed=0, transcendentals=0),
    )(place, *args)


def after(value, *needed):
    return lax.optimization_barrier((value, needed))[0]


class Spread:
    def __init__(self, place, x, first, second, cut_first):
        self.place, self.x, self.operands, self.cut_first = place, x, (first, second), cut_first
        self.sent = self.make((0, 1), None, jnp.bfloat16)

    def make(self, blocks, extra, kind):
        first, second = self.operands
        return weight_term(self.place, first, second, self.cut_first, blocks, extra, kind)

    def neighbour(self, *needed):
        self.arrived = line_flip(after(self.sent, *needed) if needed else self.sent, 1)

    def second(self):
        self.passed = self.make((2,), (self.arrived, lambda p: 1 - p[3]), jnp.bfloat16)
        self.later = line_flip(self.passed, 2)
        return self.passed

    def finish(self, *needed):
        own = self.make((3,), (self.arrived, lambda p: p[3]), jnp.float32)
        later = after(self.later, *needed)
        axis = 0 if self.cut_first else 1
        width = own.shape[axis] // pair
        far = lambda value: lax.dynamic_slice_in_dim(value, (1 - self.x) * width, width, axis)
        near = lambda value: lax.dynamic_slice_in_dim(value, self.x * width, width, axis)
        to_x = (far(own) + far(later).astype(jnp.float32)).astype(jnp.bfloat16)
        own_half = near(own) + near(later).astype(jnp.float32)
        return own_half, x_swap(to_x).astype(jnp.float32)


def on_device_lines(
    tokens,
    cotangent,
    doc_ids,
    row_ids,
    offsets,
    w_query,
    w_key,
    w_value,
    w_output,
    w_gate,
    w_up,
    w_down,
    gain_query,
    gain_key,
    gain_attn,
    gain_mlp,
):
    f32 = jnp.float32
    bf16 = jnp.bfloat16
    row_count, model_width = tokens.shape
    heads_here, head_width = gain_query.shape
    local_width = heads_here * head_width
    half_rows = row_count // 2
    key_rows = row_count * line * pair
    spot = lax.axis_index("dp")
    z, x = spot // pair, lax.rem(spot, pair)
    z_high, z_low = z // 2, lax.rem(z, 2)
    core = lax.rem(lax.axis_index("mp"), 2)
    place = jnp.stack([core, z, z_low, z_high, x]).astype(jnp.int32)

    quarter = row_count // 4

    def own_rows(value):
        return lax.dynamic_slice_in_dim(value, core * half_rows, half_rows, 0)

    def other_rows(value):
        return lax.dynamic_slice_in_dim(value, (1 - core) * half_rows, half_rows, 0)

    def reorder(value):
        return join_parts(own_rows(value), other_rows(value))

    def restore(own, other):
        whole = jnp.zeros((row_count,) + own.shape[1:], own.dtype)
        whole = lax.dynamic_update_slice_in_dim(whole, own, core * half_rows, 0)
        return lax.dynamic_update_slice_in_dim(whole, other, (1 - core) * half_rows, 0)

    def half_of(value, x_place):
        width = value.shape[1] // pair
        return lax.dynamic_slice_in_dim(value, x_place * width, width, 1)

    def join_halves(near, far, axis):
        low = jnp.where(x == 0, near, far)
        return jnp.concatenate([low, jnp.where(x == 0, far, near)], axis=axis)

    positions = reorder(offsets[0] + jnp.arange(row_count, dtype=jnp.int32))
    labels = reorder(row_ids[0] * key_rows + doc_ids)
    freqs = rope_base ** (-jnp.arange(0, head_width // 2, dtype=f32) * 2.0 / head_width)
    angles = positions.astype(f32)[:, None] * freqs[None, :]
    cosines, sines = jnp.cos(angles), jnp.sin(angles)
    cosines = jnp.concatenate([cosines, cosines], axis=1)
    sines = jnp.concatenate([-sines, sines], axis=1)
    g_query = gain_query.reshape(1, local_width)
    g_key = gain_key.reshape(1, local_width)
    spots = jnp.stack([labels, positions]).astype(f32)
    queries, pairs, notes, q_raw, k_raw = project(
        tokens, w_query, w_key, w_value, g_query, g_key, cosines, sines, spots
    )
    factors = notes[0, :2]
    codes = notes[:, 2, :].astype(jnp.int32) * key_rows + notes[:, 3, :].astype(jnp.int32)
    lows = notes[:line, 2, :].astype(jnp.int32) * key_rows
    live = (
        (jnp.min(codes, axis=1)[None, :] <= jnp.max(codes[:line], axis=1)[:, None])
        & (jnp.max(codes, axis=1)[None, :] >= jnp.min(lows, axis=1)[:, None])
    ).astype(jnp.int32)

    turned, log_total, queries_n, keys_n, code_columns, code_rows, attended_out = attend(
        key_rows, live, notes, queries, pairs
    )

    def gather_heads(home):
        twice = jnp.concatenate(home + home, axis=1)
        return lax.dynamic_slice_in_dim(
            twice, lax.rem(line - z, line) * head_width, local_width, 1
        )

    def send_home(pieces):
        return [pieces[0]] + [line_shift(pieces[d], line - d) for d in range(1, line)]

    tokens_in = reorder(tokens)
    g_attn = gain_attn.reshape(1, model_width)
    g_mlp = gain_mlp.reshape(1, model_width)
    (
        attended_low,
        tokens_x,
        output,
        hidden_low,
        hidden_x,
        act_low,
        act_x,
        grad_mlp,
        grad_mlp_x,
        grad_gate,
        grad_gate_far,
        grad_up,
        grad_up_far,
        grad_attn,
        grads,
        grad_hidden,
        wide_gains,
    ) = block(
        attended_out, w_output, g_attn, g_mlp, tokens, cotangent, w_gate, w_up, w_down
    )
    down = Spread(place, x, (act_low, act_x), (grad_mlp, grad_mlp_x), False)
    down.neighbour()
    grad_gate_x = x_swap(grad_gate_far)
    back = attend_back(
        live, code_columns, code_rows, queries_n, keys_n, pairs, turned, log_total, grads
    )
    grad_query_pieces, grad_pairs = back[:line], back[line:]
    far_pairs = after(grad_pairs[line:], grad_gate_x)
    far_pairs = [x_swap(part) for part in far_pairs]
    query_home = send_home(grad_query_pieces)
    summed_pairs = [
        (grad_pairs[d].astype(f32) + far_pairs[d].astype(f32)).astype(bf16) for d in range(line)
    ]
    home = send_home(summed_pairs)
    grad_gate_x = after(grad_gate_x, summed_pairs)
    gate = Spread(place, x, (hidden_low, hidden_x), (grad_gate, grad_gate_x), True)
    gate.neighbour(down.arrived)
    grad_up_x = x_swap(after(grad_up_far, gate.sent))
    up = Spread(place, x, (hidden_low, hidden_x), (grad_up, grad_up_x), True)
    up.neighbour(gate.arrived)
    down.arrived = after(down.arrived, summed_pairs)
    down.second()
    home, query_home = after((home, query_home), gate.sent, down.passed)
    grad_queries = gather_heads(query_home).astype(f32)
    grad_keys = gather_heads([piece[0] for piece in home]).astype(f32)
    grad_values_low = gather_heads([piece[1] for piece in home])

    def turn_back(value):
        parts = []
        for h in range(heads_here):
            part = value[:, h * head_width : (h + 1) * head_width]
            swapped = jnp.concatenate(
                [part[:, head_width // 2 :], part[:, : head_width // 2]], axis=1
            )
            parts.append(part * cosines - swapped * sines)
        return jnp.concatenate(parts, axis=1)

    q_factor = factors[0][:, None]
    k_factor = factors[1][:, None]
    q_normed = q_raw * q_factor
    k_normed = k_raw * k_factor
    back_q = turn_back(grad_queries)
    back_k = turn_back(grad_keys)
    grad_gain_query = jnp.sum(back_q * q_normed, axis=0)
    grad_gain_key = jnp.sum(back_k * k_normed, axis=0)
    scaled_q = back_q * g_query
    scaled_k = back_k * g_key
    inner = token_sum(
        jnp.stack([jnp.sum(scaled_q * q_normed, axis=1), jnp.sum(scaled_k * k_normed, axis=1)])
    )
    inner = after(inner, down.later)
    grad_q_raw = (q_factor * (scaled_q - q_normed * inner[0][:, None] / model_width)).astype(bf16)
    grad_k_raw = (k_factor * (scaled_k - k_normed * inner[1][:, None] / model_width)).astype(bf16)
    raw_parts = (grad_q_raw, grad_k_raw, grad_values_low)
    grad_raw = jnp.concatenate([half_of(part, x) for part in raw_parts], axis=1)
    grad_raw_x = x_swap(jnp.concatenate([half_of(part, 1 - x) for part in raw_parts], axis=1))
    input_sum = reduce_own_rows(
        (
            dot_nt(grad_q_raw, w_query)
            + dot_nt(grad_k_raw, w_key)
            + dot_nt(grad_values_low, w_value)
        ).astype(bf16)
    )
    grad_raw_x = after(grad_raw_x, gate.second(), up.sent)
    raw = Spread(place, x, (tokens_in, tokens_x), (grad_raw, grad_raw_x), True)
    raw.neighbour(up.arrived)
    attended_far, grad_attn_far = after(
        (half_of(attended_low, 1 - x), own_part(grad_attn)), up.sent
    )
    attended_x = x_swap(attended_far)
    grad_attn_own = x_swap(grad_attn_far)
    grad_attn_x = join_parts(grad_attn_own, core_swap(grad_attn_own))
    grad_attn_x = after(grad_attn_x, raw.sent, gate.later)
    out = Spread(place, x, (attended_low, attended_x), (grad_attn, grad_attn_x), False)
    out.neighbour(up.arrived)
    up.arrived = after(up.arrived, out.sent)
    up.second()
    raw.arrived = after(raw.arrived, up.passed)
    raw.second()
    out.arrived = after(out.arrived, raw.passed, up.later)
    out.second()
    down_near, down_far = down.finish(up.passed)
    gate_near, gate_far = gate.finish(raw.passed)
    up_near, up_far = up.finish(raw.passed, out.passed)
    out_near, out_far = out.finish(raw.passed, out.passed)
    raw_near, raw_far = raw.finish(raw.passed, out.passed)
    own_grad_tokens = (grad_hidden + input_sum).astype(bf16)
    grad_tokens = restore(own_grad_tokens, core_swap(own_grad_tokens))

    wide = wide_gains.reshape(2 * model_width)
    wide = wide + core_swap(wide)
    gains = jnp.concatenate([wide, grad_gain_query, grad_gain_key])
    gains = gains + x_swap(gains)
    gains = after(gains, raw.sent)
    for part in [line_shift(gains, d) for d in range(1, line)]:
        gains = gains + after(part, raw.passed, out.passed)
    piece = head_width // (line * pair)

    def gain_piece(start, rows):
        part = gains[start : start + rows * head_width].reshape(rows, head_width)
        return lax.dynamic_slice_in_dim(part, spot * piece, piece, 1)

    all_heads = model_width // head_width
    part_width = local_width // pair

    def raw_result(index):
        cut = slice(index * part_width, (index + 1) * part_width)
        return join_halves(raw_near[:, cut], raw_far[:, cut], 1)

    return (
        output,
        grad_tokens,
        raw_result(0),
        raw_result(1),
        raw_result(2),
        join_halves(out_near, out_far, 0),
        join_halves(gate_near, gate_far, 1),
        join_halves(up_near, up_far, 1),
        join_halves(down_near, down_far, 0),
        gain_piece(2 * model_width, heads_here),
        gain_piece(2 * model_width + local_width, heads_here),
        gain_piece(0, all_heads),
        gain_piece(model_width, all_heads),
    )


def solution(mesh):
    tuned = mesh.shape["dp"] == line * pair and mesh.shape["mp"] == 4
    body = on_device_lines if tuned else on_device_general
    return jax.shard_map(
        body,
        mesh=mesh,
        in_specs=(
            P("dp", None),
            P("dp", None),
            P("dp"),
            P("dp"),
            P("dp"),
            P(None, "mp"),
            P(None, "mp"),
            P(None, "mp"),
            P("mp", None),
            P(None, "mp"),
            P(None, "mp"),
            P("mp", None),
            P("mp", None),
            P("mp", None),
            P(),
            P(),
        ),
        out_specs=(
            P("dp", None),
            P("dp", None),
            P("dp", "mp"),
            P("dp", "mp"),
            P("dp", "mp"),
            P("mp", "dp"),
            P("dp", "mp"),
            P("dp", "mp"),
            P("mp", "dp"),
            P("mp", "dp"),
            P("mp", "dp"),
            P(None, "dp"),
            P(None, "dp"),
        ),
        check_vma=False,
    )
```

```python
import functools
import math

import jax
import jax.numpy as jnp
from jax import lax
from jax.experimental import pallas as pl
from jax.experimental.pallas import tpu as pltpu
from jax.sharding import PartitionSpec as P

epsilon = 1e-06
rope_base = 500000.0
masked_score = -1e30


def rope_tables(positions, head_width):
    freqs = rope_base ** (-jnp.arange(0, head_width // 2, dtype=jnp.float32) * 2.0 / head_width)
    angles = positions.astype(jnp.float32)[:, None] * freqs[None, :]
    return (jnp.cos(angles)[:, None, :], jnp.sin(angles)[:, None, :])


def rotate(values, cosines, sines):
    half = values.shape[-1] // 2
    first = values[..., :half]
    second = values[..., half:]
    return jnp.concatenate(
        [first * cosines - second * sines, second * cosines + first * sines], axis=-1
    )


def norm_back(grad_normed, normed, factor):
    return factor * (grad_normed - normed * jnp.mean(grad_normed * normed, axis=-1, keepdims=True))


def on_device_general(
    tokens,
    cotangent,
    doc_ids,
    row_ids,
    offsets,
    w_query,
    w_key,
    w_value,
    w_output,
    w_gate,
    w_up,
    w_down,
    gain_query,
    gain_key,
    gain_attn,
    gain_mlp,
):
    f32 = jnp.float32
    bf16 = jnp.bfloat16
    row_count = tokens.shape[0]
    model_width = tokens.shape[1]
    heads_here = gain_query.shape[0]
    head_width = gain_query.shape[1]
    local_width = heads_here * head_width
    groups = lax.axis_size("dp")
    key_rows = row_count * groups
    block_rows = min(key_rows, row_count * max(1, 512 // row_count))
    block_count = key_rows // block_rows
    score_scale = 1.0 / math.sqrt(head_width)
    positions = offsets[0] + jnp.arange(row_count, dtype=jnp.int32)
    labels = row_ids[0] * key_rows + doc_ids
    cosines, sines = rope_tables(positions, head_width)
    q_raw = jnp.dot(tokens, w_query, preferred_element_type=f32)
    k_raw = jnp.dot(tokens, w_key, preferred_element_type=f32)
    v_raw = jnp.dot(tokens, w_value, preferred_element_type=f32)
    squares = lax.psum(
        jnp.stack([jnp.sum(q_raw * q_raw, axis=1), jnp.sum(k_raw * k_raw, axis=1)]), "mp"
    )
    q_factor = lax.rsqrt(squares[0] / model_width + epsilon)[:, None]
    k_factor = lax.rsqrt(squares[1] / model_width + epsilon)[:, None]
    g_query = gain_query.reshape(local_width)
    g_key = gain_key.reshape(local_width)
    q_normed = q_raw * q_factor
    k_normed = k_raw * k_factor
    queries = rotate(
        (q_normed * g_query).reshape(row_count, heads_here, head_width), cosines, sines
    ).astype(bf16)
    keys_low = rotate(
        (k_normed * g_key).reshape(row_count, heads_here, head_width), cosines, sines
    ).astype(bf16)
    values_low = v_raw.astype(bf16)
    all_keys, all_values, all_labels, all_positions = (
        lax.all_gather(keys_low.reshape(row_count, local_width), "dp", axis=0, tiled=True),
        lax.all_gather(values_low, "dp", axis=0, tiled=True),
        lax.all_gather(labels, "dp", axis=0, tiled=True),
        lax.all_gather(positions, "dp", axis=0, tiled=True),
    )
    key_blocks = all_keys.reshape(block_count, block_rows, heads_here, head_width)
    value_blocks = all_values.reshape(block_count, block_rows, heads_here, head_width)
    label_blocks = all_labels.reshape(block_count, block_rows)
    position_blocks = all_positions.reshape(block_count, block_rows)
    scanned = (key_blocks, value_blocks, label_blocks, position_blocks)
    low_label = jnp.min(labels)
    high_label = jnp.max(labels)

    def scores_of(key_block, label_block, position_block):
        scores = (
            jnp.einsum("qhd,khd->hqk", queries, key_block, preferred_element_type=f32) * score_scale
        )
        allowed = (labels[:, None] == label_block[None, :]) & (
            positions[:, None] >= position_block[None, :]
        )
        return (scores, allowed[None])

    def touches(label_block):
        return (jnp.max(label_block) >= low_label) & (jnp.min(label_block) <= high_label)

    def max_step(carry, blocks_in):
        key_block, value_block, label_block, position_block = blocks_in

        def max_live_block(state):
            running, totals = state
            scores, allowed = scores_of(key_block, label_block, position_block)
            highest = jnp.maximum(
                running, jnp.max(jnp.where(allowed, scores, masked_score), axis=2)
            )
            weights = jnp.where(allowed, jnp.exp(scores - highest[:, :, None]), 0.0)
            return (highest, totals * jnp.exp(running - highest) + jnp.sum(weights, axis=2))

        return (lax.cond(touches(label_block), max_live_block, lambda state: state, carry), None)

    start_state = (
        jnp.full((heads_here, row_count), masked_score, f32),
        jnp.zeros((heads_here, row_count), f32),
    )
    (running_max, running_total), _ = lax.scan(max_step, start_state, scanned)
    log_total = running_max + jnp.log(running_total)

    def value_step(accum, blocks_in):
        key_block, value_block, label_block, position_block = blocks_in

        def value_live_block(current):
            scores, allowed = scores_of(key_block, label_block, position_block)
            probs_low = jnp.where(allowed, jnp.exp(scores - log_total[:, :, None]), 0.0).astype(
                bf16
            )
            return current + jnp.einsum(
                "hqk,khd->qhd", probs_low, value_block, preferred_element_type=f32
            )

        return (
            lax.cond(touches(label_block), value_live_block, lambda current: current, accum),
            None,
        )

    attended, _ = lax.scan(value_step, jnp.zeros((row_count, heads_here, head_width), f32), scanned)
    attended_low = attended.reshape(row_count, local_width).astype(bf16)
    attn_sum = lax.psum(
        jnp.dot(attended_low, w_output, preferred_element_type=f32).astype(jnp.bfloat16), "mp"
    ).astype(jnp.float32)
    attn_factor = lax.rsqrt(jnp.mean(attn_sum * attn_sum, axis=1, keepdims=True) + epsilon)
    attn_normed = attn_sum * attn_factor
    g_attn = gain_attn.reshape(model_width)
    hidden = tokens.astype(f32) + attn_normed * g_attn
    hidden_low = hidden.astype(bf16)
    gate_val = jnp.dot(hidden_low, w_gate, preferred_element_type=f32)
    up_val = jnp.dot(hidden_low, w_up, preferred_element_type=f32)
    sigmoid_gate = jax.nn.sigmoid(gate_val)
    silu_gate = gate_val * sigmoid_gate
    act_low = (silu_gate * up_val).astype(bf16)
    mlp_sum = lax.psum(
        jnp.dot(act_low, w_down, preferred_element_type=f32).astype(jnp.bfloat16), "mp"
    ).astype(jnp.float32)
    mlp_factor = lax.rsqrt(jnp.mean(mlp_sum * mlp_sum, axis=1, keepdims=True) + epsilon)
    mlp_normed = mlp_sum * mlp_factor
    g_mlp = gain_mlp.reshape(model_width)
    output = (hidden + mlp_normed * g_mlp).astype(bf16)
    grad_out = cotangent.astype(f32)
    grad_gain_mlp = jnp.sum(grad_out * mlp_normed, axis=0)
    grad_mlp = norm_back(grad_out * g_mlp, mlp_normed, mlp_factor).astype(bf16)
    grad_w_down = jnp.einsum("tf,td->fd", act_low, grad_mlp, preferred_element_type=f32)
    grad_act = jnp.einsum("td,fd->tf", grad_mlp, w_down, preferred_element_type=f32)
    slope = sigmoid_gate * (1.0 + gate_val * (1.0 - sigmoid_gate))
    grad_gate = (grad_act * up_val * slope).astype(bf16)
    grad_up = (grad_act * silu_gate).astype(bf16)
    branch_grad = jnp.einsum(
        "tf,df->td", grad_gate, w_gate, preferred_element_type=f32
    ) + jnp.einsum("tf,df->td", grad_up, w_up, preferred_element_type=f32)
    grad_hidden = grad_out + lax.psum(branch_grad.astype(jnp.bfloat16), "mp").astype(jnp.float32)
    grad_gain_attn = jnp.sum(grad_hidden * attn_normed, axis=0)
    grad_attn = norm_back(grad_hidden * g_attn, attn_normed, attn_factor).astype(bf16)
    grad_w_output = jnp.einsum("tc,td->cd", attended_low, grad_attn, preferred_element_type=f32)
    grad_attended = (
        jnp.einsum("td,cd->tc", grad_attn, w_output, preferred_element_type=f32)
        .astype(bf16)
        .reshape(row_count, heads_here, head_width)
    )
    delta = jnp.sum(grad_attended.astype(f32) * attended, axis=2).T

    def grad_step(grad_q, blocks_in):
        key_block, value_block, label_block, position_block = blocks_in

        def grad_live_block(current):
            scores, allowed = scores_of(key_block, label_block, position_block)
            probs = jnp.where(allowed, jnp.exp(scores - log_total[:, :, None]), 0.0)
            grad_probs = jnp.einsum(
                "qhd,khd->hqk", grad_attended, value_block, preferred_element_type=f32
            )
            grad_scores = (probs * (grad_probs - delta[:, :, None])).astype(bf16)
            value_term = jnp.einsum(
                "hqk,qhd->khd", probs.astype(bf16), grad_attended, preferred_element_type=f32
            )
            key_term = jnp.einsum("hqk,qhd->khd", grad_scores, queries, preferred_element_type=f32)
            updated = current + jnp.einsum(
                "hqk,khd->qhd", grad_scores, key_block, preferred_element_type=f32
            )
            return (updated, (key_term, value_term))

        def skip_block(current):
            nothing = jnp.zeros((block_rows, heads_here, head_width), f32)
            return (current, (nothing, nothing))

        return lax.cond(touches(label_block), grad_live_block, skip_block, grad_q)

    grad_queries, (key_terms, value_terms) = lax.scan(
        grad_step, jnp.zeros((row_count, heads_here, head_width), f32), scanned
    )
    grad_keys, grad_values = (
        lax.psum_scatter(
            (key_terms.reshape(key_rows, local_width) * score_scale).astype(jnp.bfloat16),
            "dp",
            scatter_dimension=0,
            tiled=True,
        ).astype(jnp.float32),
        lax.psum_scatter(
            value_terms.reshape(key_rows, local_width).astype(jnp.bfloat16),
            "dp",
            scatter_dimension=0,
            tiled=True,
        ).astype(jnp.float32),
    )
    grad_values_low = grad_values.astype(bf16)
    back_q = rotate(grad_queries * score_scale, cosines, -sines).reshape(row_count, local_width)
    back_k = rotate(grad_keys.reshape(row_count, heads_here, head_width), cosines, -sines).reshape(
        row_count, local_width
    )
    grad_gain_query = jnp.sum(back_q * q_normed, axis=0).reshape(heads_here, head_width)
    grad_gain_key = jnp.sum(back_k * k_normed, axis=0).reshape(heads_here, head_width)
    scaled_q = back_q * g_query
    scaled_k = back_k * g_key
    inner = lax.psum(
        jnp.stack([jnp.sum(scaled_q * q_normed, axis=1), jnp.sum(scaled_k * k_normed, axis=1)]),
        "mp",
    )
    grad_q_raw = (q_factor * (scaled_q - q_normed * inner[0][:, None] / model_width)).astype(bf16)
    grad_k_raw = (k_factor * (scaled_k - k_normed * inner[1][:, None] / model_width)).astype(bf16)
    input_term = (
        jnp.einsum("tc,dc->td", grad_q_raw, w_query, preferred_element_type=f32)
        + jnp.einsum("tc,dc->td", grad_k_raw, w_key, preferred_element_type=f32)
        + jnp.einsum("tc,dc->td", grad_values_low, w_value, preferred_element_type=f32)
    )
    grad_tokens = (
        grad_hidden + lax.psum(input_term.astype(jnp.bfloat16), "mp").astype(jnp.float32)
    ).astype(bf16)
    local_w_query = jnp.einsum("td,tc->dc", tokens, grad_q_raw, preferred_element_type=f32)
    local_w_key = jnp.einsum("td,tc->dc", tokens, grad_k_raw, preferred_element_type=f32)
    local_w_value = jnp.einsum("td,tc->dc", tokens, grad_values_low, preferred_element_type=f32)
    local_w_gate = jnp.einsum("td,tf->df", hidden_low, grad_gate, preferred_element_type=f32)
    local_w_up = jnp.einsum("td,tf->df", hidden_low, grad_up, preferred_element_type=f32)
    grad_w_query, grad_w_key, grad_w_value, grad_w_gate, grad_w_up = (
        lax.psum_scatter(
            local_w_query.astype(jnp.bfloat16), "dp", scatter_dimension=0, tiled=True
        ).astype(jnp.float32),
        lax.psum_scatter(
            local_w_key.astype(jnp.bfloat16), "dp", scatter_dimension=0, tiled=True
        ).astype(jnp.float32),
        lax.psum_scatter(
            local_w_value.astype(jnp.bfloat16), "dp", scatter_dimension=0, tiled=True
        ).astype(jnp.float32),
        lax.psum_scatter(
            local_w_gate.astype(jnp.bfloat16), "dp", scatter_dimension=0, tiled=True
        ).astype(jnp.float32),
        lax.psum_scatter(
            local_w_up.astype(jnp.bfloat16), "dp", scatter_dimension=0, tiled=True
        ).astype(jnp.float32),
    )
    summed_out, summed_down, summed_gq, summed_gk, summed_ga, summed_gm = (
        lax.psum_scatter(
            grad_w_output.astype(jnp.bfloat16), "dp", scatter_dimension=1, tiled=True
        ).astype(jnp.float32),
        lax.psum_scatter(
            grad_w_down.astype(jnp.bfloat16), "dp", scatter_dimension=1, tiled=True
        ).astype(jnp.float32),
        lax.psum_scatter(
            grad_gain_query.astype(jnp.bfloat16), "dp", scatter_dimension=1, tiled=True
        ).astype(jnp.float32),
        lax.psum_scatter(
            grad_gain_key.astype(jnp.bfloat16), "dp", scatter_dimension=1, tiled=True
        ).astype(jnp.float32),
        lax.psum_scatter(
            grad_gain_attn.reshape(gain_attn.shape).astype(jnp.bfloat16),
            "dp",
            scatter_dimension=1,
            tiled=True,
        ).astype(jnp.float32),
        lax.psum_scatter(
            grad_gain_mlp.reshape(gain_mlp.shape).astype(jnp.bfloat16),
            "dp",
            scatter_dimension=1,
            tiled=True,
        ).astype(jnp.float32),
    )
    return (
        output,
        grad_tokens,
        grad_w_query,
        grad_w_key,
        grad_w_value,
        summed_out,
        grad_w_gate,
        grad_w_up,
        summed_down,
        summed_gq,
        summed_gk,
        summed_ga,
        summed_gm,
    )


line = 4
pair = 2
low_score = -1e30
start_max = -1e20
big_vmem = 56 << 20


def line_shift(value, step):
    moves = [
        (z * pair + x, ((z + step) % line) * pair + x) for z in range(line) for x in range(pair)
    ]
    return lax.ppermute(value, "dp", moves)


def line_flip(value, bit):
    return lax.ppermute(
        value, "dp", [(z * pair + x, (z ^ bit) * pair + x) for z in range(line) for x in range(pair)]
    )


def x_swap(value):
    return lax.ppermute(value, "dp", [(i, i ^ 1) for i in range(line * pair)])


def core_swap(value):
    return lax.ppermute(value, "mp", [(i, i ^ 1) for i in range(4)])


def y_swap(value):
    return lax.ppermute(value, "mp", [(i, i ^ 2) for i in range(4)])


def flip_cores(value, axis):
    quarter = value.shape[axis] // 4
    cuts = [lax.slice_in_dim(value, i * quarter, (i + 1) * quarter, axis=axis) for i in (1, 0, 3, 2)]
    return jnp.concatenate(cuts, axis=axis)


def token_sum(value):
    value = value + flip_cores(core_swap(value), 1)
    return value + y_swap(value)


def own_part(value):
    quarter = value.shape[0] // 4
    return jnp.concatenate([value[:quarter], value[2 * quarter : 3 * quarter]], axis=0)


def other_part(value):
    quarter = value.shape[0] // 4
    return jnp.concatenate([value[quarter : 2 * quarter], value[3 * quarter :]], axis=0)


def join_parts(own, other):
    half = own.shape[0] // 2
    return jnp.concatenate([own[:half], other[:half], own[half:], other[half:]], axis=0)


def reduce_own_rows(partial_low):
    f32 = jnp.float32
    arrived = core_swap(other_part(partial_low))
    chip_sum = (own_part(partial_low).astype(f32) + arrived.astype(f32)).astype(jnp.bfloat16)
    return chip_sum.astype(f32) + y_swap(chip_sum).astype(f32)


def dot_t(first, second):
    return lax.dot_general(
        first, second, (((0,), (0,)), ((), ())), preferred_element_type=jnp.float32
    )


def dot_nt(first, second):
    return lax.dot_general(
        first, second, (((1,), (1,)), ((), ())), preferred_element_type=jnp.float32
    )


def vmem_specs(count):
    return [pl.BlockSpec(memory_space=pltpu.VMEM)] * count


def project_kernel(
    tokens,
    wq,
    wk,
    wv,
    gq,
    gk,
    cosines,
    sines,
    spots,
    out_queries,
    out_pairs,
    out_notes,
    out_q_raw,
    out_k_raw,
    rows_keep,
    query_keep,
    pair_keep,
    squares,
    squares_core,
    squares_y,
    send_sems,
    recv_sems,
    local_sems,
):
    f32 = jnp.float32
    bf16 = jnp.bfloat16
    width = cosines.shape[1]
    depth = wq.shape[0]
    rows = rows_keep.shape[0] // 2
    count = rows // 2
    mp = lax.axis_index("mp")
    spot = lax.axis_index("dp")
    core = lax.rem(mp, 2)
    x = lax.rem(spot, 2)
    z = spot // 2
    core_peer = {"mp": mp + 1 - 2 * core}
    y_peer = {"mp": lax.rem(mp + 2, 4)}
    x_peer = {"dp": spot + 1 - 2 * x}
    ahead = [{"dp": lax.rem(spot + 2 * d, 2 * line)} for d in range(line)]
    head = [lax.rem(z + d, line) for d in range(line)]
    both = lambda s: pl.ds(s * rows, rows)
    remote = []

    def send(source, target, peer):
        index = len(remote)
        copy = pltpu.make_async_remote_copy(
            src_ref=source,
            dst_ref=target,
            send_sem=send_sems.at[index],
            recv_sem=recv_sems.at[index],
            device_id=peer,
            device_id_type=pl.DeviceIdType.MESH,
        )
        remote.append(copy)
        copy.start()
        return copy

    loads = []
    for s in range(2):
        for part, place in ((0, core), (1, 1 - core)):
            start = pl.multiple_of(place * rows + s * count, count)
            copy = pltpu.make_async_copy(
                tokens.at[pl.ds(start, count)],
                rows_keep.at[pl.ds(s * rows + part * count, count)],
                local_sems.at[2 * s + part],
            )
            copy.start()
            loads.append(copy)

    barrier = pltpu.get_barrier_semaphore()
    peers = (core_peer, y_peer, x_peer, ahead[1], ahead[2], ahead[3])
    for peer in peers:
        pl.semaphore_signal(barrier, inc=1, device_id=peer, device_id_type=pl.DeviceIdType.MESH)
    pl.semaphore_wait(barrier, len(peers))

    def turned(raw, gain, s, h):
        part = raw[:, h * width : (h + 1) * width] * gain[:, h * width : (h + 1) * width]
        return (
            part * cosines[both(s), :] + pltpu.roll(part, width // 2, 1) * sines[both(s), :]
        ).astype(bf16)

    flying = {}
    for s in range(2):
        loads[2 * s].wait()
        loads[2 * s + 1].wait()
        k_raw = jnp.dot(rows_keep[both(s), :], wk[...], preferred_element_type=f32)
        out_k_raw[both(s), :] = k_raw
        squares[1:2, both(s)] = jnp.sum((k_raw * k_raw).T, axis=0, keepdims=True)
        v_raw = jnp.dot(rows_keep[both(s), :], wv[...], preferred_element_type=f32)
        for h in range(line):
            pair_keep[h, 0, both(s), :] = turned(k_raw, gk[...], s, h)
            pair_keep[h, 1, both(s), :] = v_raw[:, h * width : (h + 1) * width].astype(bf16)
        for d in (2, 1, 3):
            flying["pair", s, d] = send(
                pair_keep.at[head[d], :, both(s)], out_pairs.at[d, :, both(s)], ahead[d]
            )
        flying["far", s, 0] = send(
            pair_keep.at[z, :, both(s)], out_pairs.at[line, :, both(s)], x_peer
        )
        q_raw = jnp.dot(rows_keep[both(s), :], wq[...], preferred_element_type=f32)
        out_q_raw[both(s), :] = q_raw
        squares[0:1, both(s)] = jnp.sum((q_raw * q_raw).T, axis=0, keepdims=True)
        for h in range(line):
            query_keep[h, both(s), :] = turned(q_raw, gq[...], s, h)

    core_copy = send(squares, squares_core, core_peer)
    core_copy.wait()
    arrived = squares_core[...]
    cuts = [arrived[:, i * count : (i + 1) * count] for i in (1, 0, 3, 2)]
    chip = squares[...] + jnp.concatenate(cuts, axis=1)
    squares[...] = chip
    y_copy = send(squares, squares_y, y_peer)
    y_copy.wait()
    out_notes[0, 0:2, :] = lax.rsqrt((chip + squares_y[...]) / depth + epsilon)
    out_notes[0, 2:4, :] = spots[...]
    for d in range(1, line):
        flying["note", d] = send(out_notes.at[0], out_notes.at[d], ahead[d])
    flying["far_note", 0] = send(out_notes.at[0], out_notes.at[line], x_peer)
    for d in range(1, line):
        flying["query", d] = send(query_keep.at[head[d]], out_queries.at[d], ahead[d])
    out_queries[0] = query_keep[z]
    out_pairs[0] = pair_keep[z]
    for s in range(2):
        for d in (2, 1, 3):
            flying["pair", s, d].wait()
            flying["far", s, d] = send(
                out_pairs.at[d, :, both(s)], out_pairs.at[line + d, :, both(s)], x_peer
            )
    for d in range(1, line):
        flying["note", d].wait()
        flying["far_note", d] = send(out_notes.at[d], out_notes.at[line + d], x_peer)
    for d in range(1, line):
        flying["query", d].wait()
    for d in range(line):
        flying["far_note", d].wait()
        for s in range(2):
            flying["far", s, d].wait()


def project(tokens, wq, wk, wv, gq, gk, cosines, sines, spots):
    rows, depth = tokens.shape
    columns = wq.shape[1]
    width = columns // line
    f32 = jnp.float32
    bf16 = jnp.bfloat16
    return pl.pallas_call(
        project_kernel,
        in_specs=[pl.BlockSpec(memory_space=pl.ANY)] + vmem_specs(8),
        out_specs=vmem_specs(5),
        out_shape=[
            jax.ShapeDtypeStruct((line, rows, width), bf16),
            jax.ShapeDtypeStruct((2 * line, 2, rows, width), bf16),
            jax.ShapeDtypeStruct((2 * line, 4, rows), f32),
            jax.ShapeDtypeStruct((rows, columns), f32),
            jax.ShapeDtypeStruct((rows, columns), f32),
        ],
        scratch_shapes=[
            pltpu.VMEM((rows, depth), bf16),
            pltpu.VMEM((line, rows, width), bf16),
            pltpu.VMEM((line, 2, rows, width), bf16),
            pltpu.VMEM((2, rows), f32),
            pltpu.VMEM((2, rows), f32),
            pltpu.VMEM((2, rows), f32),
            pltpu.SemaphoreType.DMA((28,)),
            pltpu.SemaphoreType.DMA((28,)),
            pltpu.SemaphoreType.DMA((4,)),
        ],
        compiler_params=pltpu.CompilerParams(
            vmem_limit_bytes=48 << 20, collective_id=2, has_side_effects=True
        ),
        cost_estimate=pl.CostEstimate(flops=0, bytes_accessed=0, transcendentals=0),
    )(tokens, wq, wk, wv, gq, gk, cosines, sines, spots)


def visible_scores(key, query, key_code, query_code, query_low, factor):
    scores = dot_nt(key, query) * factor
    codes = jnp.concatenate([key_code] * (query.shape[0] // key_code.shape[1]), axis=1)
    return jnp.where((codes <= query_code) & (codes >= query_low), scores, low_score)


def attend_kernel(factor, key_rows, live, notes, *refs):
    queries, pairs = refs[:2]
    out_turned, out_log, out_query, out_key, out_codes, out_rows, out = refs[2:9]
    top, total, accum = refs[9:]
    f32 = jnp.float32
    bf16 = jnp.bfloat16
    count, width = queries.shape[1:]

    def column(row):
        return jnp.broadcast_to(row, (width, count)).T

    for k in range(2 * line):
        out_key[k] = (pairs[k, 0].astype(f32) * column(notes[k, 1:2, :])).astype(bf16)
        labels = column(notes[k, 2:3, :]).astype(jnp.int32)
        out_codes[k] = labels * key_rows + column(notes[k, 3:4, :]).astype(jnp.int32)
    for q in range(line):
        out_query[q] = (queries[q].astype(f32) * column(notes[q, 0:1, :])).astype(bf16)
        base = notes[q, 2:3, :].astype(jnp.int32) * key_rows
        out_rows[q : q + 1, :] = base + notes[q, 3:4, :].astype(jnp.int32)
        out_rows[line + q : line + q + 1, :] = base

    for q in range(line):
        top[...] = jnp.full_like(top, start_max)
        total[...] = jnp.zeros_like(total)
        accum[...] = jnp.zeros_like(accum)
        for k in range(2 * line):

            @pl.when(live[q, k] > 0)
            def _(q=q, k=k):
                scores = visible_scores(
                    out_key[k],
                    out_query[q],
                    out_codes[k],
                    out_rows[q : q + 1, :],
                    out_rows[line + q : line + q + 1, :],
                    factor,
                )
                highest = jnp.maximum(top[...], jnp.max(scores, axis=0, keepdims=True))
                weights = jnp.exp2(scores - highest)
                fade = jnp.exp2(top[...] - highest)
                total[...] = total[...] * fade + jnp.sum(weights, axis=0, keepdims=True)
                accum[...] = accum[...] * fade + dot_t(pairs[k, 1], weights.astype(bf16))
                top[...] = highest

        turned = accum[...] / total[...]
        out_turned[q] = turned
        out_log[q : q + 1, :] = top[...] + jnp.log2(total[...])
        out[q] = turned.T.astype(bf16)


def attend_back_kernel(factor, scale, live, codes, rows, queries, keys, *refs):
    pairs, turned, log_total, grads = refs[:4]
    out_query, out_near, out_far, key_sum, value_sum, query_sum = refs[4:]
    f32 = jnp.float32
    bf16 = jnp.bfloat16
    key_sum[...] = jnp.zeros_like(key_sum)
    value_sum[...] = jnp.zeros_like(value_sum)
    for q in range(line):
        query_sum[...] = jnp.zeros_like(query_sum)
        delta = jnp.sum(grads[q].astype(f32).T * turned[q], axis=0, keepdims=True)
        for k in range(2 * line):

            @pl.when(live[q, k] > 0)
            def _(q=q, k=k, delta=delta):
                query, key, grad = queries[q], keys[k], grads[q]
                scores = visible_scores(
                    key,
                    query,
                    codes[k],
                    rows[q : q + 1, :],
                    rows[line + q : line + q + 1, :],
                    factor,
                )
                probs = jnp.exp2(scores - log_total[q : q + 1, :])
                grad_probs = dot_nt(pairs[k, 1], grad)
                grad_scores = (probs * (grad_probs - delta)).astype(bf16)
                value_sum[k] += jnp.dot(
                    probs.astype(bf16), grad, preferred_element_type=f32
                )
                key_sum[k] += jnp.dot(grad_scores, query, preferred_element_type=f32)
                query_sum[...] += dot_t(key, grad_scores)

        out_query[q] = (query_sum[...] * scale).T.astype(bf16)
    for k in range(line):
        for out, base in ((out_near, 0), (out_far, line)):
            out[k, 0] = (key_sum[base + k] * scale).astype(bf16)
            out[k, 1] = value_sum[base + k].astype(bf16)


def attend(key_rows, live, notes, queries, pairs):
    _, count, width = queries.shape
    factor = math.log2(math.e) / math.sqrt(width)
    f32 = jnp.float32
    bf16 = jnp.bfloat16
    return pl.pallas_call(
        functools.partial(attend_kernel, factor, key_rows),
        out_shape=[
            jax.ShapeDtypeStruct((line, width, count), f32),
            jax.ShapeDtypeStruct((2 * line, count), f32),
            jax.ShapeDtypeStruct((line, count, width), bf16),
            jax.ShapeDtypeStruct((2 * line, count, width), bf16),
            jax.ShapeDtypeStruct((2 * line, count, width), jnp.int32),
            jax.ShapeDtypeStruct((2 * line, count), jnp.int32),
        ]
        + [jax.ShapeDtypeStruct((line, count, width), bf16)],
        in_specs=[pl.BlockSpec(memory_space=pltpu.SMEM)] + vmem_specs(3),
        out_specs=vmem_specs(7),
        scratch_shapes=[
            pltpu.VMEM((1, count), f32),
            pltpu.VMEM((1, count), f32),
            pltpu.VMEM((width, count), f32),
        ],
        compiler_params=pltpu.CompilerParams(vmem_limit_bytes=40 << 20),
        cost_estimate=pl.CostEstimate(flops=0, bytes_accessed=0, transcendentals=0),
    )(live, notes, queries, pairs)


def attend_back(live, codes, rows, queries, keys, pairs, turned, log_total, grads):
    _, count, width = queries.shape
    scale = 1.0 / math.sqrt(width)
    factor = math.log2(math.e) * scale
    f32 = jnp.float32
    return pl.pallas_call(
        functools.partial(attend_back_kernel, factor, scale),
        out_shape=[jax.ShapeDtypeStruct((line, count, width), jnp.bfloat16)]
        + [jax.ShapeDtypeStruct((line, 2, count, width), jnp.bfloat16)] * 2,
        in_specs=[pl.BlockSpec(memory_space=pltpu.SMEM)] + vmem_specs(8),
        out_specs=vmem_specs(3),
        scratch_shapes=[
            pltpu.VMEM((2 * line, count, width), f32),
            pltpu.VMEM((2 * line, count, width), f32),
            pltpu.VMEM((width, count), f32),
        ],
        compiler_params=pltpu.CompilerParams(vmem_limit_bytes=40 << 20),
        cost_estimate=pl.CostEstimate(
            flops=20 * line * line * count * count * width,
            bytes_accessed=12 << 20,
            transcendentals=2 * line * line * count * count,
        ),
    )(live, codes, rows, queries, keys, pairs, turned, log_total, grads)


def block_kernel(
    pieces,
    w_out,
    g_attn,
    g_mlp,
    tokens,
    cotangent,
    w_gate_in,
    w_up_in,
    w_down_in,
    out_heads,
    out_output,
    out_hidden,
    out_hidden_z,
    out_act,
    out_act_z,
    out_mlp,
    out_mlp_z,
    out_gate,
    out_gate_far,
    out_up,
    out_up_far,
    out_attn,
    out_grads,
    out_grad_hidden,
    out_gain,
    w_gate,
    w_up,
    w_down,
    gate_keep,
    up_keep,
    act_keep,
    hidden_keep,
    mlp_keep,
    attn_keep,
    grad_gate,
    grad_up,
    own_factor,
    own_normed,
    own_tokens,
    own_cotangent,
    attended,
    heads_keep,
    total,
    part_send,
    part_recv,
    y_send,
    y_recv,
    send_sems,
    recv_sems,
    local_sems,
):
    f32 = jnp.float32
    bf16 = jnp.bfloat16
    depth = w_out.shape[1]
    units = w_gate.shape[1]
    tile = 512
    count = own_tokens.shape[0] // 2
    rows = 2 * count
    mp = lax.axis_index("mp")
    spot = lax.axis_index("dp")
    core = lax.rem(mp, 2)
    core_peer = {"mp": mp + 1 - 2 * core}
    y_peer = {"mp": lax.rem(mp + 2, 4)}
    z = spot // 2
    z_low = lax.rem(z, 2)
    z_peer = {"dp": spot + 2 - 4 * z_low}
    width = pieces.shape[2]
    ahead = [{"dp": lax.rem(spot + 2 * d, 2 * line)} for d in range(line)]
    head = lambda d: pl.ds(pl.multiple_of(lax.rem(z + d, line) * width, width), width)

    remote, started, local = [], [], []

    def send(source, target, peer):
        index = len(remote)
        copy = pltpu.make_async_remote_copy(
            src_ref=source,
            dst_ref=target,
            send_sem=send_sems.at[index],
            recv_sem=recv_sems.at[index],
            device_id=peer,
            device_id_type=pl.DeviceIdType.MESH,
        )
        remote.append(copy)
        copy.start()
        return copy

    def keep_out(source, target, waited=False):
        copy = pltpu.make_async_copy(source, target, local_sems.at[len(started)])
        started.append(copy)
        if not waited:
            local.append(copy)
        copy.start()
        return copy

    own = lambda s: pl.ds(s * rows, count)
    other = lambda s: pl.ds(s * rows + count, count)
    both = lambda s: pl.ds(s * rows, rows)
    mine = lambda s: pl.ds(s * count, count)
    at_home = lambda s: pl.ds(pl.multiple_of(core * rows + s * count, count), count)
    cut = lambda t: pl.ds(pl.multiple_of(t * tile, tile), tile)
    flying = {}

    home_rows = pl.ds(pl.multiple_of(core * rows, rows), rows)
    loads = [
        keep_out(tokens.at[home_rows], own_tokens, True),
        keep_out(cotangent.at[home_rows], own_cotangent, True),
        keep_out(w_gate_in, w_gate, True),
        keep_out(w_up_in, w_up, True),
        keep_out(w_down_in, w_down, True),
    ]
    barrier = pltpu.get_barrier_semaphore()
    peers = (core_peer, y_peer, ahead[1], ahead[2], ahead[3])
    for peer in peers:
        pl.semaphore_signal(barrier, inc=1, device_id=peer, device_id_type=pl.DeviceIdType.MESH)
    pl.semaphore_wait(barrier, len(peers))
    for s in range(2):
        for d in range(1, line):
            flying["heads", s, d] = send(
                pieces.at[d, both(s)], attended.at[both(s), head(0)], ahead[line - d]
            )
    attended[:, head(0)] = pieces[0]

    def forward_core(name, s, array):
        flying[name, s].wait()
        flying[name + "_core", s] = send(array.at[own(s)], array.at[other(s)], core_peer)

    def reduce_start(stage, s):
        part_send[s] = total[count:, :].astype(bf16)
        copy = send(part_send.at[s], part_recv.at[s], core_peer)
        copy.wait()
        y_send[s] = (total[:count, :] + part_recv[s].astype(f32)).astype(bf16)
        flying[stage, s] = send(y_send.at[s], y_recv.at[stage, s], y_peer)

    def reduced(stage, s):
        flying[stage, s].wait()
        return y_send[s].astype(f32) + y_recv[stage, s].astype(f32)

    def factor_of(value):
        return lax.rsqrt(jnp.mean(value * value, axis=1, keepdims=True) + epsilon)

    def share(keep, s):
        flying["share", s] = send(keep.at[own(s)], keep.at[other(s)], core_peer)

    def project_out(s):
        for d in range(1, line):
            flying["heads", s, d].wait()
        keep_out(attended.at[both(s)], out_heads.at[both(s)])
        total[...] = jnp.dot(attended[both(s), :], w_out[...], preferred_element_type=f32)
        reduce_start(0, s)

    def after_attention(s):
        value = reduced(0, s)
        factor = factor_of(value)
        normed = value * factor
        own_factor[mine(s), :] = jnp.broadcast_to(factor, (count, own_factor.shape[1]))
        own_normed[mine(s), :] = normed
        hidden = own_tokens[mine(s), :].astype(f32) + normed * g_attn[...]
        out_grad_hidden[mine(s), :] = hidden
        hidden_keep[own(s), :] = hidden.astype(bf16)
        share(hidden_keep, s)

    def forward(s):
        flying["hidden", s] = send(hidden_keep.at[own(s)], out_hidden_z.at[own(s)], z_peer)
        flying["share", s].wait()
        keep_out(hidden_keep.at[both(s)], out_hidden.at[both(s)])

        def step(t):
            hidden = hidden_keep[both(s), :]
            gate = jnp.dot(hidden, w_gate[:, cut(t)], preferred_element_type=f32)
            up = jnp.dot(hidden, w_up[:, cut(t)], preferred_element_type=f32)
            gate_keep[both(s), cut(t)] = gate.astype(bf16)
            up_keep[both(s), cut(t)] = up.astype(bf16)
            act = (gate * jax.nn.sigmoid(gate) * up).astype(bf16)
            act_keep[both(s), cut(t)] = act
            return jnp.dot(act, w_down[cut(t), :], preferred_element_type=f32)

        total[...] = step(0)

        @pl.loop(1, units // tile)
        def _(t):
            total[...] += step(t)

        reduce_start(1, s)
        keep_out(act_keep.at[both(s)], out_act.at[both(s)])
        half = units // 2
        far = pl.ds(pl.multiple_of((1 - z_low) * half, half), half)
        flying["act", s] = send(act_keep.at[both(s), far], out_act_z.at[both(s)], z_peer)

    def turn_point(s):
        value = reduced(1, s)
        factor = factor_of(value)
        normed = value * factor
        own_tokens[mine(s), :] = (out_grad_hidden[mine(s), :] + normed * g_mlp[...]).astype(bf16)
        keep_out(own_tokens.at[mine(s)], out_output.at[at_home(s)])
        flying["output", s] = send(own_tokens.at[mine(s)], out_output.at[at_home(s)], core_peer)
        grad = own_cotangent[mine(s), :].astype(f32)
        gain = jnp.sum(grad * normed, axis=0, keepdims=True)
        out_gain[1:2, :] = gain if s == 0 else out_gain[1:2, :] + gain
        mlp_keep[own(s), :] = norm_back(grad * g_mlp[...], normed, factor).astype(bf16)
        share(mlp_keep, s)

    def backward(s):
        flying["mlp", s] = send(mlp_keep.at[own(s)], out_mlp_z.at[own(s)], z_peer)
        flying["share", s].wait()
        keep_out(mlp_keep.at[both(s)], out_mlp.at[both(s)])

        def step(t):
            grad_act = dot_nt(mlp_keep[both(s), :], w_down[cut(t), :])
            gate = gate_keep[both(s), cut(t)].astype(f32)
            up = up_keep[both(s), cut(t)].astype(f32)
            sigmoid = jax.nn.sigmoid(gate)
            to_gate = (grad_act * up * (sigmoid * (1.0 + gate * (1.0 - sigmoid)))).astype(bf16)
            to_up = (grad_act * (gate * sigmoid)).astype(bf16)
            grad_gate[:, cut(t)] = to_gate
            grad_up[:, cut(t)] = to_up
            return dot_nt(to_gate, w_gate[:, cut(t)]) + dot_nt(to_up, w_up[:, cut(t)])

        if s > 0:
            for copy in flying["grads"]:
                copy.wait()
        total[...] = step(0)

        @pl.loop(1, units // tile)
        def _(t):
            total[...] += step(t)

        reduce_start(2, s)
        half = units // 2
        far = pl.ds(pl.multiple_of((1 - z_low) * half, half), half)
        flying["grads"] = [
            keep_out(source, target.at[both(s)], waited=s == 0)
            for source, target in (
                (grad_gate, out_gate),
                (grad_gate.at[:, far], out_gate_far),
                (grad_up, out_up),
                (grad_up.at[:, far], out_up_far),
            )
        ]

    def to_attention(s):
        value = reduced(2, s)
        grad = own_cotangent[mine(s), :].astype(f32) + value
        out_grad_hidden[mine(s), :] = grad
        normed = own_normed[mine(s), :]
        gain = jnp.sum(grad * normed, axis=0, keepdims=True)
        out_gain[0:1, :] = gain if s == 0 else out_gain[0:1, :] + gain
        factor = own_factor[mine(s), 0:1]
        attn_keep[own(s), :] = norm_back(grad * g_attn[...], normed, factor).astype(bf16)
        share(attn_keep, s)

    def attended_grad(s):
        flying["share", s].wait()
        keep_out(attn_keep.at[both(s)], out_attn.at[both(s)])
        heads_keep[both(s), :] = dot_nt(attn_keep[both(s), :], w_out[...]).astype(bf16)
        for d in range(1, line):
            flying["grads", s, d] = send(
                heads_keep.at[both(s), head(d)], out_grads.at[d, both(s)], ahead[d]
            )
        keep_out(heads_keep.at[both(s), head(0)], out_grads.at[0, both(s)])

    project_out(0)
    project_out(1)
    for load in loads:
        load.wait()
    after_attention(0)
    forward(0)
    after_attention(1)
    forward(1)
    turn_point(0)
    backward(0)
    turn_point(1)
    backward(1)
    for s in range(2):
        forward_core("hidden", s, out_hidden_z)
    to_attention(0)
    attended_grad(0)
    to_attention(1)
    attended_grad(1)
    for s in range(2):
        flying["act", s].wait()
        flying["output", s].wait()
        forward_core("mlp", s, out_mlp_z)
    for s in range(2):
        flying["hidden_core", s].wait()
        flying["mlp_core", s].wait()
        for d in range(1, line):
            flying["grads", s, d].wait()
    for copy in local:
        copy.wait()


def block(pieces, w_out, g_attn, g_mlp, tokens, cotangent, w_gate, w_up, w_down):
    _, rows, width = pieces.shape
    columns = line * width
    depth, units = w_gate.shape
    half = rows // 2
    quarter = rows // 4
    f32 = jnp.float32
    bf16 = jnp.bfloat16
    wide = jax.ShapeDtypeStruct((rows, depth), bf16)
    tall = jax.ShapeDtypeStruct((rows, units), bf16)
    any_spec = pl.BlockSpec(memory_space=pl.ANY)
    return pl.pallas_call(
        block_kernel,
        out_shape=[
            jax.ShapeDtypeStruct((rows, columns), bf16),
            wide,
            wide,
            wide,
            tall,
            jax.ShapeDtypeStruct((rows, units // 2), bf16),
            wide,
            wide,
            tall,
            jax.ShapeDtypeStruct((rows, units // 2), bf16),
            tall,
            jax.ShapeDtypeStruct((rows, units // 2), bf16),
            wide,
            jax.ShapeDtypeStruct((line, rows, width), bf16),
            jax.ShapeDtypeStruct((half, depth), f32),
            jax.ShapeDtypeStruct((2, depth), f32),
        ],
        in_specs=vmem_specs(4) + [any_spec] * 5,
        out_specs=[any_spec] * 14 + vmem_specs(2),
        scratch_shapes=[
            pltpu.VMEM((depth, units), bf16),
            pltpu.VMEM((depth, units), bf16),
            pltpu.VMEM((units, depth), bf16),
            pltpu.VMEM((rows, units), bf16),
            pltpu.VMEM((rows, units), bf16),
            pltpu.VMEM((rows, units), bf16),
            pltpu.VMEM((rows, depth), bf16),
            pltpu.VMEM((rows, depth), bf16),
            pltpu.VMEM((rows, depth), bf16),
            pltpu.VMEM((half, units), bf16),
            pltpu.VMEM((half, units), bf16),
            pltpu.VMEM((half, 128), f32),
            pltpu.VMEM((half, depth), f32),
            pltpu.VMEM((half, depth), bf16),
            pltpu.VMEM((half, depth), bf16),
            pltpu.VMEM((rows, columns), bf16),
            pltpu.VMEM((rows, columns), bf16),
            pltpu.VMEM((half, depth), f32),
            pltpu.VMEM((2, quarter, depth), bf16),
            pltpu.VMEM((2, quarter, depth), bf16),
            pltpu.VMEM((2, quarter, depth), bf16),
            pltpu.VMEM((3, 2, quarter, depth), bf16),
            pltpu.SemaphoreType.DMA((48,)),
            pltpu.SemaphoreType.DMA((48,)),
            pltpu.SemaphoreType.DMA((32,)),
        ],
        compiler_params=pltpu.CompilerParams(
            vmem_limit_bytes=61800 << 10, collective_id=1, has_side_effects=True
        ),
        cost_estimate=pl.CostEstimate(flops=0, bytes_accessed=0, transcendentals=0),
    )(pieces, w_out, g_attn, g_mlp, tokens, cotangent, w_gate, w_up, w_down)


class Courier:
    def __init__(self, send_sems, recv_sems, local_sems):
        self.send_sems, self.recv_sems, self.local_sems = send_sems, recv_sems, local_sems
        self.remote, self.local = 0, 0

    def send(self, source, target, peer):
        copy = pltpu.make_async_remote_copy(
            src_ref=source,
            dst_ref=target,
            send_sem=self.send_sems.at[self.remote],
            recv_sem=self.recv_sems.at[self.remote],
            device_id=peer,
            device_id_type=pl.DeviceIdType.MESH,
        )
        self.remote += 1
        copy.start()
        return copy

    def move(self, source, target):
        copy = pltpu.make_async_copy(source, target, self.local_sems.at[self.local])
        self.local += 1
        copy.start()
        return copy


def greet(peers):
    barrier = pltpu.get_barrier_semaphore()
    for peer in peers:
        pl.semaphore_signal(barrier, inc=1, device_id=peer, device_id_type=pl.DeviceIdType.MESH)
    pl.semaphore_wait(barrier, len(peers))


class Spot:
    def __init__(self):
        mp = lax.axis_index("mp")
        spot = lax.axis_index("dp")
        self.core = lax.rem(mp, 2)
        self.x = lax.rem(spot, 2)
        self.z = spot // 2
        self.z_low = lax.rem(self.z, 2)
        self.z_high = self.z // 2
        self.core_peer = {"mp": mp + 1 - 2 * self.core}
        self.y_peer = {"mp": lax.rem(mp + 2, 4)}
        self.x_peer = {"dp": spot + 1 - 2 * self.x}
        self.z_peer = {"dp": spot + 2 - 4 * self.z_low}
        self.far_peer = {"dp": lax.rem(spot + 4, 8)}
        self.ahead = [{"dp": lax.rem(spot + 2 * d, 2 * line)} for d in range(line)]
        self.all = (self.core_peer, self.y_peer, self.x_peer) + tuple(self.ahead[1:])


class Job:
    def __init__(self, first, first_z, second, second_z, cut_first):
        self.operands, self.cut_first = (first, first_z, second, second_z), cut_first
        self.tile = (first if cut_first else second).shape[1] // (line * pair)

    def at(self, ref, index):
        block = pl.ds(pl.multiple_of(index * self.tile, self.tile), self.tile)
        return ref.at[block, :] if self.cut_first else ref.at[:, block]

    def span(self, ref, index):
        block = pl.ds(pl.multiple_of(index * 2 * self.tile, 2 * self.tile), 2 * self.tile)
        return ref.at[block, :] if self.cut_first else ref.at[:, block]

    def term(self, index):
        first, first_z, second, second_z = self.operands
        block = pl.ds(pl.multiple_of(index * self.tile, self.tile), self.tile)
        if self.cut_first:
            return dot_t(first[:, block], second[...]) + dot_t(first_z[:, block], second_z[...])
        return dot_t(first[...], second[:, block]) + dot_t(first_z[...], second_z[:, block])

    def send_terms(self, spot, target):
        @pl.loop(0, line)
        def _(i):
            self.at(target, i)[...] = self.term(i * pair + 1 - spot.x).astype(jnp.bfloat16)

    def second_terms(self, spot, arrived, target):
        @pl.loop(0, 2)
        def _(i):
            total = self.term((2 * (1 - spot.z_high) + i) * pair + spot.x)
            total = total + self.at(arrived, i)[...].astype(jnp.float32)
            self.at(target, i)[...] = total.astype(jnp.bfloat16)

    def own_term(self, spot, side, arrived):
        total = self.term((2 * spot.z_high + side) * pair + spot.x)
        return total + self.at(arrived, side)[...].astype(jnp.float32)


def middle_kernel(
    grad_queries,
    near,
    far,
    q_raw,
    k_raw,
    factors,
    cosines,
    sines,
    gq,
    gk,
    act,
    act_z,
    mlp,
    mlp_z,
    hidden,
    hidden_z,
    gate,
    gate_far,
    up_far,
    out_own_down,
    out_r2_down,
    out_r1_gate,
    out_gate_z,
    out_up_z,
    out_raw_z,
    r1_down,
    out_raw,
    out_raw_own,
    out_gain,
    act_v,
    act_zv,
    mlp_v,
    mlp_zv,
    hidden_v,
    hidden_zv,
    gate_v,
    gate_zv,
    send_down,
    send_gate,
    r1_v,
    r1_own,
    s2_v,
    own_v,
    far_in,
    sums,
    query_home,
    pair_home,
    scaled,
    raw_far,
    inner,
    inner_core,
    inner_y,
    send_sems,
    recv_sems,
    local_sems,
):
    f32 = jnp.float32
    bf16 = jnp.bfloat16
    spot = Spot()
    mail = Courier(send_sems, recv_sems, local_sems)
    count, width = cosines.shape
    columns = line * width
    depth = mlp_v.shape[1]
    half = act_v.shape[1]
    own_half = pl.ds(pl.multiple_of(spot.z_low * half, half), half)
    loads = [
        mail.move(act.at[:, own_half], act_v),
        mail.move(act_z, act_zv),
        mail.move(mlp, mlp_v),
        mail.move(mlp_z, mlp_zv),
        mail.move(hidden, hidden_v),
        mail.move(hidden_z, hidden_zv),
        mail.move(gate.at[:, own_half], gate_v),
    ]
    greet(spot.all)
    far_copy = mail.send(far, far_in, spot.x_peer)
    my_head = pl.ds(pl.multiple_of(spot.z * width, width), width)
    query_copies = [
        mail.send(grad_queries.at[d], query_home.at[:, my_head], spot.ahead[line - d])
        for d in range(1, line)
    ]
    gate_copy = mail.send(gate_far, gate_zv, spot.z_peer)
    query_home[:, my_head] = grad_queries[0]
    for load in loads:
        load.wait()
    down = Job(act_v, act_zv, mlp_v, mlp_zv, False)
    down.send_terms(spot, send_down)
    down_copy = mail.send(send_down, r1_down, spot.x_peer)

    far_copy.wait()
    sums[...] = (near[...].astype(f32) + far_in[...].astype(f32)).astype(bf16)
    pair_copies = [
        mail.send(sums.at[d], pair_home.at[:, :, my_head], spot.ahead[line - d])
        for d in range(1, line)
    ]
    pair_home[:, :, my_head] = sums[0]
    gate_copy.wait()
    up_copy = mail.send(up_far, out_up_z, spot.z_peer)
    keep_gate = mail.move(gate_zv, out_gate_z)
    gates = Job(hidden_v, hidden_zv, gate_v, gate_zv, True)
    gates.send_terms(spot, send_gate)
    gate_terms = mail.send(send_gate, out_r1_gate, spot.x_peer)

    for copy in query_copies + pair_copies:
        copy.wait()

    def column(row):
        return jnp.broadcast_to(row, (width, count)).T

    sources = ((query_home, None, q_raw, gq), (pair_home, 0, k_raw, gk))
    factor_columns = [column(factors[which : which + 1, :]) for which in range(2)]
    for which, (home, slot, raw, gain) in enumerate(sources):
        inner_sum = jnp.zeros((count, width), f32)
        for h in range(line):
            cut = slice(h * width, (h + 1) * width)
            part = (home[:, cut] if slot is None else home[slot, :, cut]).astype(f32)
            back = part * cosines[...] - pltpu.roll(part, width // 2, 1) * sines[...]
            normed = raw[:, cut] * factor_columns[which]
            out_gain[which : which + 1, cut] = jnp.sum(back * normed, axis=0, keepdims=True)
            value = back * gain[:, cut]
            scaled[which, :, cut] = value
            inner_sum = inner_sum + value * normed
        inner[which : which + 1, :] = jnp.sum(inner_sum.T, axis=0, keepdims=True)
    core_copy = mail.send(inner, inner_core, spot.core_peer)
    core_copy.wait()
    arrived = inner_core[...]
    quarter = count // 4
    cuts = [arrived[:, i * quarter : (i + 1) * quarter] for i in (1, 0, 3, 2)]
    chip = inner[...] + jnp.concatenate(cuts, axis=1)
    inner[...] = chip
    y_copy = mail.send(inner, inner_y, spot.y_peer)
    y_copy.wait()
    inner_all = (chip + inner_y[...]) / depth
    for which, (home, slot, raw, gain) in enumerate(sources):
        inner_column = column(inner_all[which : which + 1, :])
        for h in range(line):
            cut = slice(h * width, (h + 1) * width)
            normed = raw[:, cut] * factor_columns[which]
            value = factor_columns[which] * (scaled[which, :, cut] - normed * inner_column)
            base = which * columns + h * width
            out_raw[:, base : base + width] = value.astype(bf16)
    out_raw[:, 2 * columns :] = pair_home[1]
    part_width = columns // 2
    for which in range(3):
        cut = slice(which * part_width, (which + 1) * part_width)
        base = which * columns

        def side(index):
            start = pl.multiple_of(base + index * part_width, part_width)
            return out_raw[:, pl.ds(start, part_width)]

        out_raw_own[:, cut] = side(spot.z_low)
        raw_far[:, cut] = side(1 - spot.z_low)
    raw_copy = mail.send(raw_far, out_raw_z, spot.z_peer)

    down_copy.wait()
    loads = [
        mail.move(down.span(r1_down, 1 - spot.z_high), r1_v),
        mail.move(down.span(r1_down, spot.z_high), r1_own),
    ]
    loads[0].wait()
    down.second_terms(spot, r1_v, s2_v)
    second_copy = mail.send(s2_v, out_r2_down, spot.far_peer)
    loads[1].wait()

    @pl.loop(0, 2)
    def _(i):
        down.at(own_v, i)[...] = down.own_term(spot, i, r1_own)

    keep_own = mail.move(own_v, out_own_down)
    for copy in (up_copy, gate_terms, raw_copy, second_copy, keep_gate, keep_own):
        copy.wait()


def middle(small, large):
    f32 = jnp.float32
    bf16 = jnp.bfloat16
    grad_queries, near, far, q_raw = small[:4]
    act, act_z, grad_mlp = large[:3]
    _, count, width = grad_queries.shape
    columns = line * width
    depth = grad_mlp.shape[1]
    units = act.shape[1]
    half = units // 2
    cut = depth // 2
    any_spec = pl.BlockSpec(memory_space=pl.ANY)
    shape = jax.ShapeDtypeStruct
    return pl.pallas_call(
        middle_kernel,
        in_specs=vmem_specs(10) + [any_spec] * 9,
        out_specs=[any_spec] * 7 + vmem_specs(3),
        out_shape=[
            shape((half, cut // 2), f32),
            shape((half, cut // 2), bf16),
            shape((cut, half), bf16),
            shape((count, half), bf16),
            shape((count, half), bf16),
            shape((count, 3 * columns // 2), bf16),
            shape((half, cut), bf16),
            shape((count, 3 * columns), bf16),
            shape((count, 3 * columns // 2), bf16),
            shape((2, columns), f32),
        ],
        scratch_shapes=[
            pltpu.VMEM((count, half), bf16),
            pltpu.VMEM((count, half), bf16),
            pltpu.VMEM((count, depth), bf16),
            pltpu.VMEM((count, depth), bf16),
            pltpu.VMEM((count, depth), bf16),
            pltpu.VMEM((count, depth), bf16),
            pltpu.VMEM((count, half), bf16),
            pltpu.VMEM((count, half), bf16),
            pltpu.VMEM((half, cut), bf16),
            pltpu.VMEM((cut, half), bf16),
            pltpu.VMEM((half, cut // 2), bf16),
            pltpu.VMEM((half, cut // 2), bf16),
            pltpu.VMEM((half, cut // 2), bf16),
            pltpu.VMEM((half, cut // 2), f32),
            pltpu.VMEM(near.shape, bf16),
            pltpu.VMEM(near.shape, bf16),
            pltpu.VMEM((count, columns), bf16),
            pltpu.VMEM((2, count, columns), bf16),
            pltpu.VMEM((2, count, columns), f32),
            pltpu.VMEM((count, 3 * columns // 2), bf16),
            pltpu.VMEM((2, count), f32),
            pltpu.VMEM((2, count), f32),
            pltpu.VMEM((2, count), f32),
            pltpu.SemaphoreType.DMA((16,)),
            pltpu.SemaphoreType.DMA((16,)),
            pltpu.SemaphoreType.DMA((16,)),
        ],
        compiler_params=pltpu.CompilerParams(
            vmem_limit_bytes=big_vmem, collective_id=3, has_side_effects=True
        ),
    )(*small, *large)


def last_kernel(
    raw,
    raw_own,
    raw_z,
    wide,
    narrow,
    attended,
    hidden,
    hidden_z,
    gate,
    gate_z,
    up,
    up_z,
    attn,
    tokens,
    own_down,
    r2_down,
    r1_gate,
    w_query,
    w_key,
    w_value,
    grad_hidden,
    *refs,
):
    outs, refs = refs[:14], refs[14:]
    near_down, near_gate, near_up, near_raw, near_out = outs[:5]
    far_down, far_gate, far_up, far_raw, far_out = outs[5:10]
    out_tokens, r1_up, r1_raw, r1_out = outs[10:]
    out_wide, out_narrow = refs[:2]
    (
        hidden_v,
        hidden_zv,
        gate_v,
        gate_zv,
        up_v,
        up_zv,
        tokens_v,
        tokens_zv,
        attn_v,
        attn_zv,
        heads_v,
        heads_far,
        heads_zv,
        send_up,
        send_raw,
        send_out,
        r1_wide,
        r1_raw_v,
        r1_out_v,
        s2_gate,
        s2_up,
        s2_raw,
        s2_out,
        r2_gate,
        r2_up,
        r2_raw,
        r2_out,
        own_down_v,
        r2_down_v,
        fin_down,
        fin_gate,
        fin_up,
        fin_raw,
        fin_out,
        keep_down,
        keep_gate,
        keep_up,
        keep_raw,
        keep_out,
        weight_v,
        total,
        part_send,
        part_recv,
        y_send,
        y_recv,
        hidden_own,
        token_keep,
        wide_core,
        wide_x,
        narrow_x,
        wide_z,
        narrow_z,
        send_sems,
        recv_sems,
        local_sems,
    ) = refs[2:]
    f32 = jnp.float32
    bf16 = jnp.bfloat16
    spot = Spot()
    mail = Courier(send_sems, recv_sems, local_sems)
    rows_all = tokens_v.shape[0]
    rows = rows_all // 2
    count = rows // 2
    half = gate_v.shape[1]
    own_half = pl.ds(pl.multiple_of(spot.z_low * half, half), half)
    heads_half = heads_v.shape[1]
    side_heads = lambda side: pl.ds(pl.multiple_of(side * heads_half, heads_half), heads_half)
    own = lambda s: pl.ds(s * rows, count)
    other = lambda s: pl.ds(s * rows + count, count)
    both = lambda s: pl.ds(s * rows, rows)
    mine = lambda s: pl.ds(s * count, count)

    first_loads = [
        mail.move(hidden, hidden_v),
        mail.move(hidden_z, hidden_zv),
        mail.move(up.at[:, own_half], up_v),
        mail.move(up_z, up_zv),
    ]
    token_loads, attn_loads = [], []
    for s in range(2):
        for part, place in ((0, spot.core), (1, 1 - spot.core)):
            start = pl.multiple_of(place * rows + s * count, count)
            target = tokens_v.at[pl.ds(s * rows + part * count, count)]
            token_loads.append(mail.move(tokens.at[pl.ds(start, count)], target))
    attn_load = mail.move(attn, attn_v)
    later_loads = [
        mail.move(gate.at[:, own_half], gate_v),
        mail.move(gate_z, gate_zv),
    ]
    greet(spot.all)
    wide_copy = mail.send(wide, wide_core, spot.core_peer)
    for load in first_loads:
        load.wait()
    ups = Job(hidden_v, hidden_zv, up_v, up_zv, True)
    gates = Job(hidden_v, hidden_zv, gate_v, gate_zv, True)
    raws = Job(tokens_v, tokens_zv, raw_own, raw_z, True)
    outs_job = Job(heads_v, heads_zv, attn_v, attn_zv, False)
    for load in token_loads:
        load.wait()
    token_copies = [
        mail.send(tokens_v.at[own(s)], tokens_zv.at[own(s)], spot.z_peer) for s in range(2)
    ]
    heads_far[...] = attended[:, side_heads(1 - spot.z_low)]
    heads_v[...] = attended[:, side_heads(spot.z_low)]
    heads_copy = mail.send(heads_far, heads_zv, spot.z_peer)
    ups.send_terms(spot, send_up)
    wide_copy.wait()
    out_wide[...] = wide[...] + wide_core[...]
    out_narrow[...] = narrow[...]
    wide_x_copy = mail.send(out_wide, wide_x, spot.x_peer)
    narrow_x_copy = mail.send(out_narrow, narrow_x, spot.x_peer)
    up_copy = mail.send(send_up, r1_up, spot.x_peer)

    r1_load = mail.move(gates.span(r1_gate, 1 - spot.z_high), r1_wide.at[0])
    r1_gate_own = mail.move(gates.span(r1_gate, spot.z_high), r1_wide.at[1])
    for load in later_loads:
        load.wait()
    r1_load.wait()
    gates.second_terms(spot, r1_wide.at[0], s2_gate)
    gate_copy = mail.send(s2_gate, r2_gate, spot.far_peer)
    attn_load.wait()
    attn_copies = [
        mail.send(attn_v.at[own(s)], attn_zv.at[own(s)], spot.z_peer) for s in range(2)
    ]

    input_weights = (w_query, w_key, w_value)
    columns = w_query.shape[1]
    flying = {}
    for which, source in enumerate(input_weights):
        load = mail.move(source, weight_v)
        load.wait()
        for s in range(2):
            term = dot_nt(raw[both(s), which * columns : (which + 1) * columns], weight_v[...])
            total[both(s), :] = term if which == 0 else total[both(s), :] + term
    for s in range(2):
        part_send[s] = total[other(s), :].astype(bf16)
        flying["core", s] = mail.send(part_send.at[s], part_recv.at[s], spot.core_peer)
    hidden_load = mail.move(grad_hidden, hidden_own)
    for s in range(2):
        flying["core", s].wait()
        y_send[s] = (total[own(s), :] + part_recv[s].astype(f32)).astype(bf16)
        flying["y", s] = mail.send(y_send.at[s], y_recv.at[s], spot.y_peer)

    near_copies, far_copies = [], []

    def finish(job, value_of, fin, far, keep, target):
        fin[...] = value_of(1 - spot.z_low).astype(bf16)
        far_copies.append(mail.send(fin, far, spot.z_peer))
        keep[...] = value_of(spot.z_low)
        near_copies.append(mail.move(keep, target))

    down_loads = [mail.move(own_down, own_down_v), mail.move(r2_down, r2_down_v)]
    for load in down_loads:
        load.wait()
    down = Job(heads_v, heads_zv, attn_v, attn_zv, False)
    finish(
        down,
        lambda side: down.at(own_down_v, side)[...] + down.at(r2_down_v, side)[...].astype(f32),
        fin_down,
        far_down,
        keep_down,
        near_down,
    )

    for s in range(2):
        token_copies[s].wait()
    token_core = [
        mail.send(tokens_zv.at[own(s)], tokens_zv.at[other(s)], spot.core_peer) for s in range(2)
    ]
    for copy in token_core:
        copy.wait()
    raws.send_terms(spot, send_raw)
    wide_x_copy.wait()
    narrow_x_copy.wait()
    out_wide[...] = out_wide[...] + wide_x[...]
    out_narrow[...] = out_narrow[...] + narrow_x[...]
    raw_copy = mail.send(send_raw, r1_raw, spot.x_peer)
    for s in range(2):
        attn_copies[s].wait()
    attn_core = [
        mail.send(attn_zv.at[own(s)], attn_zv.at[other(s)], spot.core_peer) for s in range(2)
    ]
    for copy in attn_core:
        copy.wait()
    heads_copy.wait()
    outs_job.send_terms(spot, send_out)
    out_copy = mail.send(send_out, r1_out, spot.x_peer)

    hidden_load.wait()
    for s in range(2):
        flying["y", s].wait()
        value = y_send[s].astype(f32) + y_recv[s].astype(f32)
        token_keep[mine(s), :] = (hidden_own[mine(s), :] + value).astype(bf16)
        home = pl.ds(pl.multiple_of(spot.core * rows + s * count, count), count)
        flying["keep", s] = mail.move(token_keep.at[mine(s)], out_tokens.at[home])
        flying["tokens", s] = mail.send(
            token_keep.at[mine(s)], out_tokens.at[home], spot.core_peer
        )
    gain_copies = []
    for d in range(1, line):
        gain_copies.append(mail.send(out_wide, wide_z.at[d - 1], spot.ahead[d]))
        gain_copies.append(mail.send(out_narrow, narrow_z.at[d - 1], spot.ahead[d]))

    up_copy.wait()
    r1_up_second = mail.move(ups.span(r1_up, 1 - spot.z_high), r1_wide.at[2])
    r1_up_own = mail.move(ups.span(r1_up, spot.z_high), r1_wide.at[3])
    r1_up_second.wait()
    ups.second_terms(spot, r1_wide.at[2], s2_up)
    second_up = mail.send(s2_up, r2_up, spot.far_peer)

    def final_of(job, r1_own, r2):
        return lambda side: job.own_term(spot, side, r1_own) + job.at(r2, side)[...].astype(f32)

    r1_gate_own.wait()
    gate_copy.wait()
    finish(gates, final_of(gates, r1_wide.at[1], r2_gate), fin_gate, far_gate, keep_gate, near_gate)

    raw_copy.wait()
    raw_loads = [
        mail.move(raws.span(r1_raw, 1 - spot.z_high), r1_raw_v.at[0]),
        mail.move(raws.span(r1_raw, spot.z_high), r1_raw_v.at[1]),
    ]
    for load in raw_loads:
        load.wait()
    raws.second_terms(spot, r1_raw_v.at[0], s2_raw)
    second_raw = mail.send(s2_raw, r2_raw, spot.far_peer)
    out_copy.wait()
    out_loads = [
        mail.move(outs_job.span(r1_out, 1 - spot.z_high), r1_out_v.at[0]),
        mail.move(outs_job.span(r1_out, spot.z_high), r1_out_v.at[1]),
    ]
    for load in out_loads:
        load.wait()
    outs_job.second_terms(spot, r1_out_v.at[0], s2_out)
    second_out = mail.send(s2_out, r2_out, spot.far_peer)
    r1_up_own.wait()
    second_up.wait()
    finish(ups, final_of(ups, r1_wide.at[3], r2_up), fin_up, far_up, keep_up, near_up)
    second_raw.wait()
    finish(raws, final_of(raws, r1_raw_v.at[1], r2_raw), fin_raw, far_raw, keep_raw, near_raw)
    second_out.wait()
    finish(
        outs_job, final_of(outs_job, r1_out_v.at[1], r2_out), fin_out, far_out, keep_out, near_out
    )
    for copy in gain_copies:
        copy.wait()
    for d in range(1, line):
        out_wide[...] = out_wide[...] + wide_z[d - 1]
        out_narrow[...] = out_narrow[...] + narrow_z[d - 1]
    for s in range(2):
        flying["keep", s].wait()
        flying["tokens", s].wait()
    for copy in near_copies + far_copies:
        copy.wait()


def last(small, large):
    f32 = jnp.float32
    bf16 = jnp.bfloat16
    raw, raw_own, raw_z, wide, narrow, attended = small
    hidden, gate = large[0], large[2]
    count, depth = hidden.shape
    units = gate.shape[1]
    half = units // 2
    block = depth // (line * pair)
    columns = attended.shape[1]
    heads_half = columns // 2
    raw_half = raw_own.shape[1]
    rows = count // 2
    any_spec = pl.BlockSpec(memory_space=pl.ANY)
    shape = jax.ShapeDtypeStruct
    vmem = lambda *size: pltpu.VMEM(size, bf16)
    wide_vmem = lambda *size: pltpu.VMEM(size, f32)
    return pl.pallas_call(
        last_kernel,
        in_specs=vmem_specs(6) + [any_spec] * len(large),
        out_specs=[any_spec] * 14 + vmem_specs(2),
        out_shape=[
            shape((half, block), f32),
            shape((block, half), f32),
            shape((block, half), f32),
            shape((block, raw_half), f32),
            shape((heads_half, block), f32),
            shape((half, block), bf16),
            shape((block, half), bf16),
            shape((block, half), bf16),
            shape((block, raw_half), bf16),
            shape((heads_half, block), bf16),
            shape((count, depth), bf16),
            shape((line * block, half), bf16),
            shape((line * block, raw_half), bf16),
            shape((heads_half, line * block), bf16),
            shape(wide.shape, f32),
            shape(narrow.shape, f32),
        ],
        scratch_shapes=[
            vmem(count, depth),
            vmem(count, depth),
            vmem(count, half),
            vmem(count, half),
            vmem(count, half),
            vmem(count, half),
            vmem(count, depth),
            vmem(count, depth),
            vmem(count, depth),
            vmem(count, depth),
            vmem(count, heads_half),
            vmem(count, heads_half),
            vmem(count, heads_half),
            vmem(line * block, half),
            vmem(line * block, raw_half),
            vmem(heads_half, line * block),
            vmem(4, 2 * block, half),
            vmem(2, 2 * block, raw_half),
            vmem(2, heads_half, 2 * block),
            vmem(2 * block, half),
            vmem(2 * block, half),
            vmem(2 * block, raw_half),
            vmem(heads_half, 2 * block),
            vmem(2 * block, half),
            vmem(2 * block, half),
            vmem(2 * block, raw_half),
            vmem(heads_half, 2 * block),
            wide_vmem(half, 2 * block),
            vmem(half, 2 * block),
            vmem(half, block),
            vmem(block, half),
            vmem(block, half),
            vmem(block, raw_half),
            vmem(heads_half, block),
            wide_vmem(half, block),
            wide_vmem(block, half),
            wide_vmem(block, half),
            wide_vmem(block, raw_half),
            wide_vmem(heads_half, block),
            vmem(depth, columns),
            wide_vmem(count, depth),
            vmem(2, rows // 2, depth),
            vmem(2, rows // 2, depth),
            vmem(2, rows // 2, depth),
            vmem(2, rows // 2, depth),
            wide_vmem(rows, depth),
            vmem(rows, depth),
            wide_vmem(*wide.shape),
            wide_vmem(*wide.shape),
            wide_vmem(*narrow.shape),
            wide_vmem(line - 1, *wide.shape),
            wide_vmem(line - 1, *narrow.shape),
            pltpu.SemaphoreType.DMA((48,)),
            pltpu.SemaphoreType.DMA((48,)),
            pltpu.SemaphoreType.DMA((40,)),
        ],
        compiler_params=pltpu.CompilerParams(
            vmem_limit_bytes=61800 << 10, collective_id=4, has_side_effects=True
        ),
    )(*small, *large)


def on_device_lines(
    tokens,
    cotangent,
    doc_ids,
    row_ids,
    offsets,
    w_query,
    w_key,
    w_value,
    w_output,
    w_gate,
    w_up,
    w_down,
    gain_query,
    gain_key,
    gain_attn,
    gain_mlp,
):
    f32 = jnp.float32
    bf16 = jnp.bfloat16
    row_count, model_width = tokens.shape
    heads_here, head_width = gain_query.shape
    local_width = heads_here * head_width
    half_rows = row_count // 2
    key_rows = row_count * line * pair
    spot = lax.axis_index("dp")
    z, x = spot // pair, lax.rem(spot, pair)
    z_high, z_low = z // 2, lax.rem(z, 2)
    core = lax.rem(lax.axis_index("mp"), 2)
    place = jnp.stack([core, z, z_low, z_high, x]).astype(jnp.int32)

    quarter = row_count // 4

    def own_rows(value):
        return lax.dynamic_slice_in_dim(value, core * half_rows, half_rows, 0)

    def other_rows(value):
        return lax.dynamic_slice_in_dim(value, (1 - core) * half_rows, half_rows, 0)

    def reorder(value):
        return join_parts(own_rows(value), other_rows(value))

    def restore(own, other):
        whole = jnp.zeros((row_count,) + own.shape[1:], own.dtype)
        whole = lax.dynamic_update_slice_in_dim(whole, own, core * half_rows, 0)
        return lax.dynamic_update_slice_in_dim(whole, other, (1 - core) * half_rows, 0)

    def half_of(value, side):
        width = value.shape[1] // 2
        return lax.dynamic_slice_in_dim(value, side * width, width, 1)

    def join_halves(near, far, axis):
        low = jnp.where(z_low == 0, near, far)
        return jnp.concatenate([low, jnp.where(z_low == 0, far, near)], axis=axis)

    positions = reorder(offsets[0] + jnp.arange(row_count, dtype=jnp.int32))
    labels = reorder(row_ids[0] * key_rows + doc_ids)
    freqs = rope_base ** (-jnp.arange(0, head_width // 2, dtype=f32) * 2.0 / head_width)
    angles = positions.astype(f32)[:, None] * freqs[None, :]
    cosines, sines = jnp.cos(angles), jnp.sin(angles)
    cosines = jnp.concatenate([cosines, cosines], axis=1)
    sines = jnp.concatenate([-sines, sines], axis=1)
    g_query = gain_query.reshape(1, local_width)
    g_key = gain_key.reshape(1, local_width)
    spots = jnp.stack([labels, positions]).astype(f32)
    queries, pairs, notes, q_raw, k_raw = project(
        tokens, w_query, w_key, w_value, g_query, g_key, cosines, sines, spots
    )
    factors = notes[0, :2]
    codes = notes[:, 2, :].astype(jnp.int32) * key_rows + notes[:, 3, :].astype(jnp.int32)
    lows = notes[:line, 2, :].astype(jnp.int32) * key_rows
    live = (
        (jnp.min(codes, axis=1)[None, :] <= jnp.max(codes[:line], axis=1)[:, None])
        & (jnp.max(codes, axis=1)[None, :] >= jnp.min(lows, axis=1)[:, None])
    ).astype(jnp.int32)

    turned, log_total, queries_n, keys_n, code_columns, code_rows, attended_out = attend(
        key_rows, live, notes, queries, pairs
    )

    def gather_heads(home):
        twice = jnp.concatenate(home + home, axis=1)
        return lax.dynamic_slice_in_dim(
            twice, lax.rem(line - z, line) * head_width, local_width, 1
        )

    def send_home(pieces):
        return [pieces[0]] + [line_shift(pieces[d], line - d) for d in range(1, line)]

    tokens_in = reorder(tokens)
    g_attn = gain_attn.reshape(1, model_width)
    g_mlp = gain_mlp.reshape(1, model_width)
    (
        attended_low,
        output,
        hidden_low,
        hidden_z,
        act_low,
        act_z,
        grad_mlp,
        grad_mlp_z,
        grad_gate,
        grad_gate_far,
        grad_up,
        grad_up_far,
        grad_attn,
        grads,
        grad_hidden,
        wide_gains,
    ) = block(
        attended_out, w_output, g_attn, g_mlp, tokens, cotangent, w_gate, w_up, w_down
    )
    back = attend_back(
        live, code_columns, code_rows, queries_n, keys_n, pairs, turned, log_total, grads
    )
    (
        own_down,
        r2_down,
        r1_gate,
        grad_gate_z,
        grad_up_z,
        raw_z,
        _,
        raw,
        raw_own,
        narrow_gains,
    ) = middle(
        (*back, q_raw, k_raw, factors, cosines, sines, g_query, g_key),
        (
            act_low,
            act_z,
            grad_mlp,
            grad_mlp_z,
            hidden_low,
            hidden_z,
            grad_gate,
            grad_gate_far,
            grad_up_far,
        ),
    )
    results = last(
        (raw, raw_own, raw_z, wide_gains, narrow_gains, attended_low),
        (
            hidden_low,
            hidden_z,
            grad_gate,
            grad_gate_z,
            grad_up,
            grad_up_z,
            grad_attn,
            tokens,
            own_down,
            r2_down,
            r1_gate,
            w_query,
            w_key,
            w_value,
            grad_hidden,
        ),
    )
    down_near, gate_near, up_near, raw_near, out_near = results[:5]
    down_far, gate_far, up_far, raw_far, out_far = [part.astype(f32) for part in results[5:10]]
    grad_tokens = results[10]
    wide, narrow = results[14:]
    gains = jnp.concatenate([wide.reshape(2 * model_width), narrow.reshape(2 * local_width)])
    piece = head_width // (line * pair)

    def gain_piece(start, rows):
        part = gains[start : start + rows * head_width].reshape(rows, head_width)
        return lax.dynamic_slice_in_dim(part, spot * piece, piece, 1)

    all_heads = model_width // head_width
    part_width = local_width // pair

    def raw_result(index):
        cut = slice(index * part_width, (index + 1) * part_width)
        return join_halves(raw_near[:, cut], raw_far[:, cut], 1)

    return (
        output,
        grad_tokens,
        raw_result(0),
        raw_result(1),
        raw_result(2),
        join_halves(out_near, out_far, 0),
        join_halves(gate_near, gate_far, 1),
        join_halves(up_near, up_far, 1),
        join_halves(down_near, down_far, 0),
        gain_piece(2 * model_width, heads_here),
        gain_piece(2 * model_width + local_width, heads_here),
        gain_piece(0, all_heads),
        gain_piece(model_width, all_heads),
    )


def solution(mesh):
    tuned = mesh.shape["dp"] == line * pair and mesh.shape["mp"] == 4
    body = on_device_lines if tuned else on_device_general
    return jax.shard_map(
        body,
        mesh=mesh,
        in_specs=(
            P("dp", None),
            P("dp", None),
            P("dp"),
            P("dp"),
            P("dp"),
            P(None, "mp"),
            P(None, "mp"),
            P(None, "mp"),
            P("mp", None),
            P(None, "mp"),
            P(None, "mp"),
            P("mp", None),
            P("mp", None),
            P("mp", None),
            P(),
            P(),
        ),
        out_specs=(
            P("dp", None),
            P("dp", None),
            P("dp", "mp"),
            P("dp", "mp"),
            P("dp", "mp"),
            P("mp", "dp"),
            P("dp", "mp"),
            P("dp", "mp"),
            P("mp", "dp"),
            P("mp", "dp"),
            P("mp", "dp"),
            P(None, "dp"),
            P(None, "dp"),
        ),
        check_vma=False,
    )
```

```python
import functools
import math

import jax
import jax.numpy as jnp
from jax import lax
from jax.experimental import pallas as pl
from jax.experimental.pallas import tpu as pltpu
from jax.sharding import PartitionSpec as P

epsilon = 1e-06
rope_base = 500000.0
masked_score = -1e30


def rope_tables(positions, head_width):
    freqs = rope_base ** (-jnp.arange(0, head_width // 2, dtype=jnp.float32) * 2.0 / head_width)
    angles = positions.astype(jnp.float32)[:, None] * freqs[None, :]
    return (jnp.cos(angles)[:, None, :], jnp.sin(angles)[:, None, :])


def rotate(values, cosines, sines):
    half = values.shape[-1] // 2
    first = values[..., :half]
    second = values[..., half:]
    return jnp.concatenate(
        [first * cosines - second * sines, second * cosines + first * sines], axis=-1
    )


def norm_back(grad_normed, normed, factor):
    return factor * (grad_normed - normed * jnp.mean(grad_normed * normed, axis=-1, keepdims=True))


def on_device_general(
    tokens,
    cotangent,
    doc_ids,
    row_ids,
    offsets,
    w_query,
    w_key,
    w_value,
    w_output,
    w_gate,
    w_up,
    w_down,
    gain_query,
    gain_key,
    gain_attn,
    gain_mlp,
):
    f32 = jnp.float32
    bf16 = jnp.bfloat16
    row_count = tokens.shape[0]
    model_width = tokens.shape[1]
    heads_here = gain_query.shape[0]
    head_width = gain_query.shape[1]
    local_width = heads_here * head_width
    groups = lax.axis_size("dp")
    key_rows = row_count * groups
    block_rows = min(key_rows, row_count * max(1, 512 // row_count))
    block_count = key_rows // block_rows
    score_scale = 1.0 / math.sqrt(head_width)
    positions = offsets[0] + jnp.arange(row_count, dtype=jnp.int32)
    labels = row_ids[0] * key_rows + doc_ids
    cosines, sines = rope_tables(positions, head_width)
    q_raw = jnp.dot(tokens, w_query, preferred_element_type=f32)
    k_raw = jnp.dot(tokens, w_key, preferred_element_type=f32)
    v_raw = jnp.dot(tokens, w_value, preferred_element_type=f32)
    squares = lax.psum(
        jnp.stack([jnp.sum(q_raw * q_raw, axis=1), jnp.sum(k_raw * k_raw, axis=1)]), "mp"
    )
    q_factor = lax.rsqrt(squares[0] / model_width + epsilon)[:, None]
    k_factor = lax.rsqrt(squares[1] / model_width + epsilon)[:, None]
    g_query = gain_query.reshape(local_width)
    g_key = gain_key.reshape(local_width)
    q_normed = q_raw * q_factor
    k_normed = k_raw * k_factor
    queries = rotate(
        (q_normed * g_query).reshape(row_count, heads_here, head_width), cosines, sines
    ).astype(bf16)
    keys_low = rotate(
        (k_normed * g_key).reshape(row_count, heads_here, head_width), cosines, sines
    ).astype(bf16)
    values_low = v_raw.astype(bf16)
    all_keys, all_values, all_labels, all_positions = (
        lax.all_gather(keys_low.reshape(row_count, local_width), "dp", axis=0, tiled=True),
        lax.all_gather(values_low, "dp", axis=0, tiled=True),
        lax.all_gather(labels, "dp", axis=0, tiled=True),
        lax.all_gather(positions, "dp", axis=0, tiled=True),
    )
    key_blocks = all_keys.reshape(block_count, block_rows, heads_here, head_width)
    value_blocks = all_values.reshape(block_count, block_rows, heads_here, head_width)
    label_blocks = all_labels.reshape(block_count, block_rows)
    position_blocks = all_positions.reshape(block_count, block_rows)
    scanned = (key_blocks, value_blocks, label_blocks, position_blocks)
    low_label = jnp.min(labels)
    high_label = jnp.max(labels)

    def scores_of(key_block, label_block, position_block):
        scores = (
            jnp.einsum("qhd,khd->hqk", queries, key_block, preferred_element_type=f32) * score_scale
        )
        allowed = (labels[:, None] == label_block[None, :]) & (
            positions[:, None] >= position_block[None, :]
        )
        return (scores, allowed[None])

    def touches(label_block):
        return (jnp.max(label_block) >= low_label) & (jnp.min(label_block) <= high_label)

    def max_step(carry, blocks_in):
        key_block, value_block, label_block, position_block = blocks_in

        def max_live_block(state):
            running, totals = state
            scores, allowed = scores_of(key_block, label_block, position_block)
            highest = jnp.maximum(
                running, jnp.max(jnp.where(allowed, scores, masked_score), axis=2)
            )
            weights = jnp.where(allowed, jnp.exp(scores - highest[:, :, None]), 0.0)
            return (highest, totals * jnp.exp(running - highest) + jnp.sum(weights, axis=2))

        return (lax.cond(touches(label_block), max_live_block, lambda state: state, carry), None)

    start_state = (
        jnp.full((heads_here, row_count), masked_score, f32),
        jnp.zeros((heads_here, row_count), f32),
    )
    (running_max, running_total), _ = lax.scan(max_step, start_state, scanned)
    log_total = running_max + jnp.log(running_total)

    def value_step(accum, blocks_in):
        key_block, value_block, label_block, position_block = blocks_in

        def value_live_block(current):
            scores, allowed = scores_of(key_block, label_block, position_block)
            probs_low = jnp.where(allowed, jnp.exp(scores - log_total[:, :, None]), 0.0).astype(
                bf16
            )
            return current + jnp.einsum(
                "hqk,khd->qhd", probs_low, value_block, preferred_element_type=f32
            )

        return (
            lax.cond(touches(label_block), value_live_block, lambda current: current, accum),
            None,
        )

    attended, _ = lax.scan(value_step, jnp.zeros((row_count, heads_here, head_width), f32), scanned)
    attended_low = attended.reshape(row_count, local_width).astype(bf16)
    attn_sum = lax.psum(
        jnp.dot(attended_low, w_output, preferred_element_type=f32).astype(jnp.bfloat16), "mp"
    ).astype(jnp.float32)
    attn_factor = lax.rsqrt(jnp.mean(attn_sum * attn_sum, axis=1, keepdims=True) + epsilon)
    attn_normed = attn_sum * attn_factor
    g_attn = gain_attn.reshape(model_width)
    hidden = tokens.astype(f32) + attn_normed * g_attn
    hidden_low = hidden.astype(bf16)
    gate_val = jnp.dot(hidden_low, w_gate, preferred_element_type=f32)
    up_val = jnp.dot(hidden_low, w_up, preferred_element_type=f32)
    sigmoid_gate = jax.nn.sigmoid(gate_val)
    silu_gate = gate_val * sigmoid_gate
    act_low = (silu_gate * up_val).astype(bf16)
    mlp_sum = lax.psum(
        jnp.dot(act_low, w_down, preferred_element_type=f32).astype(jnp.bfloat16), "mp"
    ).astype(jnp.float32)
    mlp_factor = lax.rsqrt(jnp.mean(mlp_sum * mlp_sum, axis=1, keepdims=True) + epsilon)
    mlp_normed = mlp_sum * mlp_factor
    g_mlp = gain_mlp.reshape(model_width)
    output = (hidden + mlp_normed * g_mlp).astype(bf16)
    grad_out = cotangent.astype(f32)
    grad_gain_mlp = jnp.sum(grad_out * mlp_normed, axis=0)
    grad_mlp = norm_back(grad_out * g_mlp, mlp_normed, mlp_factor).astype(bf16)
    grad_w_down = jnp.einsum("tf,td->fd", act_low, grad_mlp, preferred_element_type=f32)
    grad_act = jnp.einsum("td,fd->tf", grad_mlp, w_down, preferred_element_type=f32)
    slope = sigmoid_gate * (1.0 + gate_val * (1.0 - sigmoid_gate))
    grad_gate = (grad_act * up_val * slope).astype(bf16)
    grad_up = (grad_act * silu_gate).astype(bf16)
    branch_grad = jnp.einsum(
        "tf,df->td", grad_gate, w_gate, preferred_element_type=f32
    ) + jnp.einsum("tf,df->td", grad_up, w_up, preferred_element_type=f32)
    grad_hidden = grad_out + lax.psum(branch_grad.astype(jnp.bfloat16), "mp").astype(jnp.float32)
    grad_gain_attn = jnp.sum(grad_hidden * attn_normed, axis=0)
    grad_attn = norm_back(grad_hidden * g_attn, attn_normed, attn_factor).astype(bf16)
    grad_w_output = jnp.einsum("tc,td->cd", attended_low, grad_attn, preferred_element_type=f32)
    grad_attended = (
        jnp.einsum("td,cd->tc", grad_attn, w_output, preferred_element_type=f32)
        .astype(bf16)
        .reshape(row_count, heads_here, head_width)
    )
    delta = jnp.sum(grad_attended.astype(f32) * attended, axis=2).T

    def grad_step(grad_q, blocks_in):
        key_block, value_block, label_block, position_block = blocks_in

        def grad_live_block(current):
            scores, allowed = scores_of(key_block, label_block, position_block)
            probs = jnp.where(allowed, jnp.exp(scores - log_total[:, :, None]), 0.0)
            grad_probs = jnp.einsum(
                "qhd,khd->hqk", grad_attended, value_block, preferred_element_type=f32
            )
            grad_scores = (probs * (grad_probs - delta[:, :, None])).astype(bf16)
            value_term = jnp.einsum(
                "hqk,qhd->khd", probs.astype(bf16), grad_attended, preferred_element_type=f32
            )
            key_term = jnp.einsum("hqk,qhd->khd", grad_scores, queries, preferred_element_type=f32)
            updated = current + jnp.einsum(
                "hqk,khd->qhd", grad_scores, key_block, preferred_element_type=f32
            )
            return (updated, (key_term, value_term))

        def skip_block(current):
            nothing = jnp.zeros((block_rows, heads_here, head_width), f32)
            return (current, (nothing, nothing))

        return lax.cond(touches(label_block), grad_live_block, skip_block, grad_q)

    grad_queries, (key_terms, value_terms) = lax.scan(
        grad_step, jnp.zeros((row_count, heads_here, head_width), f32), scanned
    )
    grad_keys, grad_values = (
        lax.psum_scatter(
            (key_terms.reshape(key_rows, local_width) * score_scale).astype(jnp.bfloat16),
            "dp",
            scatter_dimension=0,
            tiled=True,
        ).astype(jnp.float32),
        lax.psum_scatter(
            value_terms.reshape(key_rows, local_width).astype(jnp.bfloat16),
            "dp",
            scatter_dimension=0,
            tiled=True,
        ).astype(jnp.float32),
    )
    grad_values_low = grad_values.astype(bf16)
    back_q = rotate(grad_queries * score_scale, cosines, -sines).reshape(row_count, local_width)
    back_k = rotate(grad_keys.reshape(row_count, heads_here, head_width), cosines, -sines).reshape(
        row_count, local_width
    )
    grad_gain_query = jnp.sum(back_q * q_normed, axis=0).reshape(heads_here, head_width)
    grad_gain_key = jnp.sum(back_k * k_normed, axis=0).reshape(heads_here, head_width)
    scaled_q = back_q * g_query
    scaled_k = back_k * g_key
    inner = lax.psum(
        jnp.stack([jnp.sum(scaled_q * q_normed, axis=1), jnp.sum(scaled_k * k_normed, axis=1)]),
        "mp",
    )
    grad_q_raw = (q_factor * (scaled_q - q_normed * inner[0][:, None] / model_width)).astype(bf16)
    grad_k_raw = (k_factor * (scaled_k - k_normed * inner[1][:, None] / model_width)).astype(bf16)
    input_term = (
        jnp.einsum("tc,dc->td", grad_q_raw, w_query, preferred_element_type=f32)
        + jnp.einsum("tc,dc->td", grad_k_raw, w_key, preferred_element_type=f32)
        + jnp.einsum("tc,dc->td", grad_values_low, w_value, preferred_element_type=f32)
    )
    grad_tokens = (
        grad_hidden + lax.psum(input_term.astype(jnp.bfloat16), "mp").astype(jnp.float32)
    ).astype(bf16)
    local_w_query = jnp.einsum("td,tc->dc", tokens, grad_q_raw, preferred_element_type=f32)
    local_w_key = jnp.einsum("td,tc->dc", tokens, grad_k_raw, preferred_element_type=f32)
    local_w_value = jnp.einsum("td,tc->dc", tokens, grad_values_low, preferred_element_type=f32)
    local_w_gate = jnp.einsum("td,tf->df", hidden_low, grad_gate, preferred_element_type=f32)
    local_w_up = jnp.einsum("td,tf->df", hidden_low, grad_up, preferred_element_type=f32)
    grad_w_query, grad_w_key, grad_w_value, grad_w_gate, grad_w_up = (
        lax.psum_scatter(
            local_w_query.astype(jnp.bfloat16), "dp", scatter_dimension=0, tiled=True
        ).astype(jnp.float32),
        lax.psum_scatter(
            local_w_key.astype(jnp.bfloat16), "dp", scatter_dimension=0, tiled=True
        ).astype(jnp.float32),
        lax.psum_scatter(
            local_w_value.astype(jnp.bfloat16), "dp", scatter_dimension=0, tiled=True
        ).astype(jnp.float32),
        lax.psum_scatter(
            local_w_gate.astype(jnp.bfloat16), "dp", scatter_dimension=0, tiled=True
        ).astype(jnp.float32),
        lax.psum_scatter(
            local_w_up.astype(jnp.bfloat16), "dp", scatter_dimension=0, tiled=True
        ).astype(jnp.float32),
    )
    summed_out, summed_down, summed_gq, summed_gk, summed_ga, summed_gm = (
        lax.psum_scatter(
            grad_w_output.astype(jnp.bfloat16), "dp", scatter_dimension=1, tiled=True
        ).astype(jnp.float32),
        lax.psum_scatter(
            grad_w_down.astype(jnp.bfloat16), "dp", scatter_dimension=1, tiled=True
        ).astype(jnp.float32),
        lax.psum_scatter(
            grad_gain_query.astype(jnp.bfloat16), "dp", scatter_dimension=1, tiled=True
        ).astype(jnp.float32),
        lax.psum_scatter(
            grad_gain_key.astype(jnp.bfloat16), "dp", scatter_dimension=1, tiled=True
        ).astype(jnp.float32),
        lax.psum_scatter(
            grad_gain_attn.reshape(gain_attn.shape).astype(jnp.bfloat16),
            "dp",
            scatter_dimension=1,
            tiled=True,
        ).astype(jnp.float32),
        lax.psum_scatter(
            grad_gain_mlp.reshape(gain_mlp.shape).astype(jnp.bfloat16),
            "dp",
            scatter_dimension=1,
            tiled=True,
        ).astype(jnp.float32),
    )
    return (
        output,
        grad_tokens,
        grad_w_query,
        grad_w_key,
        grad_w_value,
        summed_out,
        grad_w_gate,
        grad_w_up,
        summed_down,
        summed_gq,
        summed_gk,
        summed_ga,
        summed_gm,
    )


line = 4
pair = 2
low_score = -1e30
start_max = -1e20
big_vmem = 56 << 20


def line_shift(value, step):
    moves = [
        (z * pair + x, ((z + step) % line) * pair + x) for z in range(line) for x in range(pair)
    ]
    return lax.ppermute(value, "dp", moves)


def line_flip(value, bit):
    return lax.ppermute(
        value, "dp", [(z * pair + x, (z ^ bit) * pair + x) for z in range(line) for x in range(pair)]
    )


def x_swap(value):
    return lax.ppermute(value, "dp", [(i, i ^ 1) for i in range(line * pair)])


def core_swap(value):
    return lax.ppermute(value, "mp", [(i, i ^ 1) for i in range(4)])


def y_swap(value):
    return lax.ppermute(value, "mp", [(i, i ^ 2) for i in range(4)])


def flip_cores(value, axis):
    quarter = value.shape[axis] // 4
    cuts = [lax.slice_in_dim(value, i * quarter, (i + 1) * quarter, axis=axis) for i in (1, 0, 3, 2)]
    return jnp.concatenate(cuts, axis=axis)


def token_sum(value):
    value = value + flip_cores(core_swap(value), 1)
    return value + y_swap(value)


def own_part(value):
    quarter = value.shape[0] // 4
    return jnp.concatenate([value[:quarter], value[2 * quarter : 3 * quarter]], axis=0)


def other_part(value):
    quarter = value.shape[0] // 4
    return jnp.concatenate([value[quarter : 2 * quarter], value[3 * quarter :]], axis=0)


def join_parts(own, other):
    half = own.shape[0] // 2
    return jnp.concatenate([own[:half], other[:half], own[half:], other[half:]], axis=0)


def reduce_own_rows(partial_low):
    f32 = jnp.float32
    arrived = core_swap(other_part(partial_low))
    chip_sum = (own_part(partial_low).astype(f32) + arrived.astype(f32)).astype(jnp.bfloat16)
    return chip_sum.astype(f32) + y_swap(chip_sum).astype(f32)


def dot_t(first, second):
    return lax.dot_general(
        first, second, (((0,), (0,)), ((), ())), preferred_element_type=jnp.float32
    )


def dot_nt(first, second):
    return lax.dot_general(
        first, second, (((1,), (1,)), ((), ())), preferred_element_type=jnp.float32
    )


def vmem_specs(count):
    return [pl.BlockSpec(memory_space=pltpu.VMEM)] * count


def project_kernel(
    tokens,
    wq,
    wk,
    wv,
    gq,
    gk,
    cosines,
    sines,
    spots,
    out_queries,
    out_pairs,
    out_notes,
    out_q_raw,
    out_k_raw,
    rows_keep,
    query_keep,
    pair_keep,
    squares,
    squares_core,
    squares_y,
    send_sems,
    recv_sems,
    local_sems,
):
    f32 = jnp.float32
    bf16 = jnp.bfloat16
    width = cosines.shape[1]
    depth = wq.shape[0]
    rows = rows_keep.shape[0] // 2
    count = rows // 2
    mp = lax.axis_index("mp")
    spot = lax.axis_index("dp")
    core = lax.rem(mp, 2)
    x = lax.rem(spot, 2)
    z = spot // 2
    core_peer = {"mp": mp + 1 - 2 * core}
    y_peer = {"mp": lax.rem(mp + 2, 4)}
    x_peer = {"dp": spot + 1 - 2 * x}
    ahead = [{"dp": lax.rem(spot + 2 * d, 2 * line)} for d in range(line)]
    head = [lax.rem(z + d, line) for d in range(line)]
    both = lambda s: pl.ds(s * rows, rows)
    remote = []

    def send(source, target, peer):
        index = len(remote)
        copy = pltpu.make_async_remote_copy(
            src_ref=source,
            dst_ref=target,
            send_sem=send_sems.at[index],
            recv_sem=recv_sems.at[index],
            device_id=peer,
            device_id_type=pl.DeviceIdType.MESH,
        )
        remote.append(copy)
        copy.start()
        return copy

    loads = []
    for s in range(2):
        for part, place in ((0, core), (1, 1 - core)):
            start = pl.multiple_of(place * rows + s * count, count)
            copy = pltpu.make_async_copy(
                tokens.at[pl.ds(start, count)],
                rows_keep.at[pl.ds(s * rows + part * count, count)],
                local_sems.at[2 * s + part],
            )
            copy.start()
            loads.append(copy)

    barrier = pltpu.get_barrier_semaphore()
    peers = (core_peer, y_peer, x_peer, ahead[1], ahead[2], ahead[3])
    for peer in peers:
        pl.semaphore_signal(barrier, inc=1, device_id=peer, device_id_type=pl.DeviceIdType.MESH)
    pl.semaphore_wait(barrier, len(peers))

    def turned(raw, gain, s, h):
        part = raw[:, h * width : (h + 1) * width] * gain[:, h * width : (h + 1) * width]
        return (
            part * cosines[both(s), :] + pltpu.roll(part, width // 2, 1) * sines[both(s), :]
        ).astype(bf16)

    flying = {}
    for s in range(2):
        loads[2 * s].wait()
        loads[2 * s + 1].wait()
        k_raw = jnp.dot(rows_keep[both(s), :], wk[...], preferred_element_type=f32)
        out_k_raw[both(s), :] = k_raw
        squares[1:2, both(s)] = jnp.sum((k_raw * k_raw).T, axis=0, keepdims=True)
        v_raw = jnp.dot(rows_keep[both(s), :], wv[...], preferred_element_type=f32)
        for h in range(line):
            pair_keep[h, 0, both(s), :] = turned(k_raw, gk[...], s, h)
            pair_keep[h, 1, both(s), :] = v_raw[:, h * width : (h + 1) * width].astype(bf16)
        for d in (2, 1, 3):
            flying["pair", s, d] = send(
                pair_keep.at[head[d], :, both(s)], out_pairs.at[d, :, both(s)], ahead[d]
            )
        flying["far", s, 0] = send(
            pair_keep.at[z, :, both(s)], out_pairs.at[line, :, both(s)], x_peer
        )
        q_raw = jnp.dot(rows_keep[both(s), :], wq[...], preferred_element_type=f32)
        out_q_raw[both(s), :] = q_raw
        squares[0:1, both(s)] = jnp.sum((q_raw * q_raw).T, axis=0, keepdims=True)
        for h in range(line):
            query_keep[h, both(s), :] = turned(q_raw, gq[...], s, h)

    core_copy = send(squares, squares_core, core_peer)
    core_copy.wait()
    arrived = squares_core[...]
    cuts = [arrived[:, i * count : (i + 1) * count] for i in (1, 0, 3, 2)]
    chip = squares[...] + jnp.concatenate(cuts, axis=1)
    squares[...] = chip
    y_copy = send(squares, squares_y, y_peer)
    y_copy.wait()
    out_notes[0, 0:2, :] = lax.rsqrt((chip + squares_y[...]) / depth + epsilon)
    out_notes[0, 2:4, :] = spots[...]
    for d in range(1, line):
        flying["note", d] = send(out_notes.at[0], out_notes.at[d], ahead[d])
    flying["far_note", 0] = send(out_notes.at[0], out_notes.at[line], x_peer)
    for d in range(1, line):
        flying["query", d] = send(query_keep.at[head[d]], out_queries.at[d], ahead[d])
    out_queries[0] = query_keep[z]
    out_pairs[0] = pair_keep[z]
    for s in range(2):
        for d in (2, 1, 3):
            flying["pair", s, d].wait()
            flying["far", s, d] = send(
                out_pairs.at[d, :, both(s)], out_pairs.at[line + d, :, both(s)], x_peer
            )
    for d in range(1, line):
        flying["note", d].wait()
        flying["far_note", d] = send(out_notes.at[d], out_notes.at[line + d], x_peer)
    for d in range(1, line):
        flying["query", d].wait()
    for d in range(line):
        flying["far_note", d].wait()
        for s in range(2):
            flying["far", s, d].wait()


def project(tokens, wq, wk, wv, gq, gk, cosines, sines, spots):
    rows, depth = tokens.shape
    columns = wq.shape[1]
    width = columns // line
    f32 = jnp.float32
    bf16 = jnp.bfloat16
    return pl.pallas_call(
        project_kernel,
        in_specs=[pl.BlockSpec(memory_space=pl.ANY)] + vmem_specs(8),
        out_specs=vmem_specs(5),
        out_shape=[
            jax.ShapeDtypeStruct((line, rows, width), bf16),
            jax.ShapeDtypeStruct((2 * line, 2, rows, width), bf16),
            jax.ShapeDtypeStruct((2 * line, 4, rows), f32),
            jax.ShapeDtypeStruct((rows, columns), f32),
            jax.ShapeDtypeStruct((rows, columns), f32),
        ],
        scratch_shapes=[
            pltpu.VMEM((rows, depth), bf16),
            pltpu.VMEM((line, rows, width), bf16),
            pltpu.VMEM((line, 2, rows, width), bf16),
            pltpu.VMEM((2, rows), f32),
            pltpu.VMEM((2, rows), f32),
            pltpu.VMEM((2, rows), f32),
            pltpu.SemaphoreType.DMA((28,)),
            pltpu.SemaphoreType.DMA((28,)),
            pltpu.SemaphoreType.DMA((4,)),
        ],
        compiler_params=pltpu.CompilerParams(
            vmem_limit_bytes=48 << 20, collective_id=2, has_side_effects=True
        ),
        cost_estimate=pl.CostEstimate(flops=0, bytes_accessed=0, transcendentals=0),
    )(tokens, wq, wk, wv, gq, gk, cosines, sines, spots)


def visible_scores(key, query, key_code, query_code, query_low, factor):
    scores = dot_nt(key, query) * factor
    codes = jnp.concatenate([key_code] * (query.shape[0] // key_code.shape[1]), axis=1)
    return jnp.where((codes <= query_code) & (codes >= query_low), scores, low_score)


def attend_kernel(factor, key_rows, live, notes, *refs):
    queries, pairs = refs[:2]
    out_turned, out_log, out_query, out_key, out_codes, out_rows, out = refs[2:9]
    top, total, accum = refs[9:]
    f32 = jnp.float32
    bf16 = jnp.bfloat16
    count, width = queries.shape[1:]

    def column(row):
        return jnp.broadcast_to(row, (width, count)).T

    for k in range(2 * line):
        out_key[k] = (pairs[k, 0].astype(f32) * column(notes[k, 1:2, :])).astype(bf16)
        labels = column(notes[k, 2:3, :]).astype(jnp.int32)
        out_codes[k] = labels * key_rows + column(notes[k, 3:4, :]).astype(jnp.int32)
    for q in range(line):
        out_query[q] = (queries[q].astype(f32) * column(notes[q, 0:1, :])).astype(bf16)
        base = notes[q, 2:3, :].astype(jnp.int32) * key_rows
        out_rows[q : q + 1, :] = base + notes[q, 3:4, :].astype(jnp.int32)
        out_rows[line + q : line + q + 1, :] = base

    for q in range(line):
        top[...] = jnp.full_like(top, start_max)
        total[...] = jnp.zeros_like(total)
        accum[...] = jnp.zeros_like(accum)
        for k in range(2 * line):

            @pl.when(live[q, k] > 0)
            def _(q=q, k=k):
                scores = visible_scores(
                    out_key[k],
                    out_query[q],
                    out_codes[k],
                    out_rows[q : q + 1, :],
                    out_rows[line + q : line + q + 1, :],
                    factor,
                )
                highest = jnp.maximum(top[...], jnp.max(scores, axis=0, keepdims=True))
                weights = jnp.exp2(scores - highest)
                fade = jnp.exp2(top[...] - highest)
                total[...] = total[...] * fade + jnp.sum(weights, axis=0, keepdims=True)
                accum[...] = accum[...] * fade + dot_t(pairs[k, 1], weights.astype(bf16))
                top[...] = highest

        turned = accum[...] / total[...]
        out_turned[q] = turned
        out_log[q : q + 1, :] = top[...] + jnp.log2(total[...])
        out[q] = turned.T.astype(bf16)


def attend_back_kernel(factor, scale, live, codes, rows, queries, keys, *refs):
    pairs, turned, log_total, grads = refs[:4]
    out_query, out_near, out_far, key_sum, value_sum, query_sum = refs[4:]
    f32 = jnp.float32
    bf16 = jnp.bfloat16
    key_sum[...] = jnp.zeros_like(key_sum)
    value_sum[...] = jnp.zeros_like(value_sum)
    for q in range(line):
        query_sum[...] = jnp.zeros_like(query_sum)
        delta = jnp.sum(grads[q].astype(f32).T * turned[q], axis=0, keepdims=True)
        for k in range(2 * line):

            @pl.when(live[q, k] > 0)
            def _(q=q, k=k, delta=delta):
                query, key, grad = queries[q], keys[k], grads[q]
                scores = visible_scores(
                    key,
                    query,
                    codes[k],
                    rows[q : q + 1, :],
                    rows[line + q : line + q + 1, :],
                    factor,
                )
                probs = jnp.exp2(scores - log_total[q : q + 1, :])
                grad_probs = dot_nt(pairs[k, 1], grad)
                grad_scores = (probs * (grad_probs - delta)).astype(bf16)
                value_sum[k] += jnp.dot(
                    probs.astype(bf16), grad, preferred_element_type=f32
                )
                key_sum[k] += jnp.dot(grad_scores, query, preferred_element_type=f32)
                query_sum[...] += dot_t(key, grad_scores)

        out_query[q] = (query_sum[...] * scale).T.astype(bf16)
    for k in range(line):
        for out, base in ((out_near, 0), (out_far, line)):
            out[k, 0] = (key_sum[base + k] * scale).astype(bf16)
            out[k, 1] = value_sum[base + k].astype(bf16)


def attend(key_rows, live, notes, queries, pairs):
    _, count, width = queries.shape
    factor = math.log2(math.e) / math.sqrt(width)
    f32 = jnp.float32
    bf16 = jnp.bfloat16
    return pl.pallas_call(
        functools.partial(attend_kernel, factor, key_rows),
        out_shape=[
            jax.ShapeDtypeStruct((line, width, count), f32),
            jax.ShapeDtypeStruct((2 * line, count), f32),
            jax.ShapeDtypeStruct((line, count, width), bf16),
            jax.ShapeDtypeStruct((2 * line, count, width), bf16),
            jax.ShapeDtypeStruct((2 * line, count, width), jnp.int32),
            jax.ShapeDtypeStruct((2 * line, count), jnp.int32),
        ]
        + [jax.ShapeDtypeStruct((line, count, width), bf16)],
        in_specs=[pl.BlockSpec(memory_space=pltpu.SMEM)] + vmem_specs(3),
        out_specs=vmem_specs(7),
        scratch_shapes=[
            pltpu.VMEM((1, count), f32),
            pltpu.VMEM((1, count), f32),
            pltpu.VMEM((width, count), f32),
        ],
        compiler_params=pltpu.CompilerParams(vmem_limit_bytes=40 << 20),
        cost_estimate=pl.CostEstimate(flops=0, bytes_accessed=0, transcendentals=0),
    )(live, notes, queries, pairs)


def attend_back(live, codes, rows, queries, keys, pairs, turned, log_total, grads):
    _, count, width = queries.shape
    scale = 1.0 / math.sqrt(width)
    factor = math.log2(math.e) * scale
    f32 = jnp.float32
    return pl.pallas_call(
        functools.partial(attend_back_kernel, factor, scale),
        out_shape=[jax.ShapeDtypeStruct((line, count, width), jnp.bfloat16)]
        + [jax.ShapeDtypeStruct((line, 2, count, width), jnp.bfloat16)] * 2,
        in_specs=[pl.BlockSpec(memory_space=pltpu.SMEM)] + vmem_specs(8),
        out_specs=vmem_specs(3),
        scratch_shapes=[
            pltpu.VMEM((2 * line, count, width), f32),
            pltpu.VMEM((2 * line, count, width), f32),
            pltpu.VMEM((width, count), f32),
        ],
        compiler_params=pltpu.CompilerParams(vmem_limit_bytes=40 << 20),
        cost_estimate=pl.CostEstimate(
            flops=20 * line * line * count * count * width,
            bytes_accessed=12 << 20,
            transcendentals=2 * line * line * count * count,
        ),
    )(live, codes, rows, queries, keys, pairs, turned, log_total, grads)


def block_kernel(
    pieces,
    w_out,
    g_attn,
    g_mlp,
    tokens,
    cotangent,
    w_gate_in,
    w_up_in,
    w_down_in,
    out_heads,
    out_tokens_x,
    out_output,
    out_hidden,
    out_hidden_z,
    out_act,
    out_act_x,
    out_mlp,
    out_mlp_x,
    out_gate,
    out_gate_far,
    out_gate_z,
    out_up,
    out_up_far,
    out_attn,
    out_grads,
    out_grad_hidden,
    out_gain,
    w_gate,
    w_up,
    w_down,
    gate_keep,
    up_keep,
    act_keep,
    hidden_keep,
    mlp_keep,
    attn_keep,
    grad_gate,
    grad_up,
    own_factor,
    own_normed,
    own_tokens,
    own_cotangent,
    attended,
    heads_keep,
    total,
    part_send,
    part_recv,
    y_send,
    y_recv,
    send_sems,
    recv_sems,
    local_sems,
):
    f32 = jnp.float32
    bf16 = jnp.bfloat16
    depth = w_out.shape[1]
    units = w_gate.shape[1]
    tile = 512
    count = own_tokens.shape[0] // 2
    rows = 2 * count
    mp = lax.axis_index("mp")
    spot = lax.axis_index("dp")
    core = lax.rem(mp, 2)
    core_peer = {"mp": mp + 1 - 2 * core}
    y_peer = {"mp": lax.rem(mp + 2, 4)}
    z = spot // 2
    z_low = lax.rem(z, 2)
    z_peer = {"dp": spot + 2 - 4 * z_low}
    x = lax.rem(spot, 2)
    x_peer = {"dp": spot + 1 - 2 * x}
    width = pieces.shape[2]
    ahead = [{"dp": lax.rem(spot + 2 * d, 2 * line)} for d in range(line)]
    head = lambda d: pl.ds(pl.multiple_of(lax.rem(z + d, line) * width, width), width)

    remote, started, local = [], [], []

    def send(source, target, peer):
        index = len(remote)
        copy = pltpu.make_async_remote_copy(
            src_ref=source,
            dst_ref=target,
            send_sem=send_sems.at[index],
            recv_sem=recv_sems.at[index],
            device_id=peer,
            device_id_type=pl.DeviceIdType.MESH,
        )
        remote.append(copy)
        copy.start()
        return copy

    def keep_out(source, target, waited=False):
        copy = pltpu.make_async_copy(source, target, local_sems.at[len(started)])
        started.append(copy)
        if not waited:
            local.append(copy)
        copy.start()
        return copy

    own = lambda s: pl.ds(s * rows, count)
    other = lambda s: pl.ds(s * rows + count, count)
    both = lambda s: pl.ds(s * rows, rows)
    mine = lambda s: pl.ds(s * count, count)
    at_home = lambda s: pl.ds(pl.multiple_of(core * rows + s * count, count), count)
    cut = lambda t: pl.ds(pl.multiple_of(t * tile, tile), tile)
    flying = {}

    home_rows = pl.ds(pl.multiple_of(core * rows, rows), rows)
    loads = [
        keep_out(tokens.at[home_rows], own_tokens, True),
        keep_out(cotangent.at[home_rows], own_cotangent, True),
        keep_out(w_gate_in, w_gate, True),
        keep_out(w_up_in, w_up, True),
        keep_out(w_down_in, w_down, True),
    ]
    barrier = pltpu.get_barrier_semaphore()
    peers = (core_peer, y_peer, x_peer, ahead[1], ahead[2], ahead[3])
    for peer in peers:
        pl.semaphore_signal(barrier, inc=1, device_id=peer, device_id_type=pl.DeviceIdType.MESH)
    pl.semaphore_wait(barrier, len(peers))
    for s in range(2):
        for d in range(1, line):
            flying["heads", s, d] = send(
                pieces.at[d, both(s)], attended.at[both(s), head(0)], ahead[line - d]
            )
    attended[:, head(0)] = pieces[0]

    loads[0].wait()
    for s in range(2):
        flying["tokens", s] = send(own_tokens.at[mine(s)], out_tokens_x.at[own(s)], x_peer)

    def forward_core(name, s, array):
        flying[name, s].wait()
        flying[name + "_core", s] = send(array.at[own(s)], array.at[other(s)], core_peer)

    def reduce_start(stage, s):
        part_send[s] = total[count:, :].astype(bf16)
        copy = send(part_send.at[s], part_recv.at[s], core_peer)
        copy.wait()
        y_send[s] = (total[:count, :] + part_recv[s].astype(f32)).astype(bf16)
        flying[stage, s] = send(y_send.at[s], y_recv.at[stage, s], y_peer)

    def reduced(stage, s):
        flying[stage, s].wait()
        return y_send[s].astype(f32) + y_recv[stage, s].astype(f32)

    def factor_of(value):
        return lax.rsqrt(jnp.mean(value * value, axis=1, keepdims=True) + epsilon)

    def share(keep, s):
        flying["share", s] = send(keep.at[own(s)], keep.at[other(s)], core_peer)

    def project_out(s):
        for d in range(1, line):
            flying["heads", s, d].wait()
        keep_out(attended.at[both(s)], out_heads.at[both(s)])
        total[...] = jnp.dot(attended[both(s), :], w_out[...], preferred_element_type=f32)
        reduce_start(0, s)

    def after_attention(s):
        value = reduced(0, s)
        factor = factor_of(value)
        normed = value * factor
        own_factor[mine(s), :] = jnp.broadcast_to(factor, (count, own_factor.shape[1]))
        own_normed[mine(s), :] = normed
        hidden = own_tokens[mine(s), :].astype(f32) + normed * g_attn[...]
        out_grad_hidden[mine(s), :] = hidden
        hidden_keep[own(s), :] = hidden.astype(bf16)
        share(hidden_keep, s)

    def forward(s):
        flying["hidden", s] = send(hidden_keep.at[own(s)], out_hidden_z.at[own(s)], z_peer)
        flying["share", s].wait()
        keep_out(hidden_keep.at[both(s)], out_hidden.at[both(s)])

        def step(t):
            hidden = hidden_keep[both(s), :]
            gate = jnp.dot(hidden, w_gate[:, cut(t)], preferred_element_type=f32)
            up = jnp.dot(hidden, w_up[:, cut(t)], preferred_element_type=f32)
            gate_keep[both(s), cut(t)] = gate.astype(bf16)
            up_keep[both(s), cut(t)] = up.astype(bf16)
            act = (gate * jax.nn.sigmoid(gate) * up).astype(bf16)
            act_keep[both(s), cut(t)] = act
            return jnp.dot(act, w_down[cut(t), :], preferred_element_type=f32)

        total[...] = step(0)

        @pl.loop(1, units // tile)
        def _(t):
            total[...] += step(t)

        reduce_start(1, s)
        keep_out(act_keep.at[both(s)], out_act.at[both(s)])
        half = units // 2
        far = pl.ds(pl.multiple_of((1 - x) * half, half), half)
        flying["act", s] = send(act_keep.at[both(s), far], out_act_x.at[both(s)], x_peer)

    def turn_point(s):
        value = reduced(1, s)
        factor = factor_of(value)
        normed = value * factor
        forward_core("tokens", s, out_tokens_x)
        own_tokens[mine(s), :] = (out_grad_hidden[mine(s), :] + normed * g_mlp[...]).astype(bf16)
        keep_out(own_tokens.at[mine(s)], out_output.at[at_home(s)])
        flying["output", s] = send(own_tokens.at[mine(s)], out_output.at[at_home(s)], core_peer)
        grad = own_cotangent[mine(s), :].astype(f32)
        gain = jnp.sum(grad * normed, axis=0, keepdims=True)
        out_gain[1:2, :] = gain if s == 0 else out_gain[1:2, :] + gain
        mlp_keep[own(s), :] = norm_back(grad * g_mlp[...], normed, factor).astype(bf16)
        share(mlp_keep, s)

    def backward(s):
        flying["mlp", s] = send(mlp_keep.at[own(s)], out_mlp_x.at[own(s)], x_peer)
        flying["share", s].wait()
        keep_out(mlp_keep.at[both(s)], out_mlp.at[both(s)])

        def step(t):
            grad_act = dot_nt(mlp_keep[both(s), :], w_down[cut(t), :])
            gate = gate_keep[both(s), cut(t)].astype(f32)
            up = up_keep[both(s), cut(t)].astype(f32)
            sigmoid = jax.nn.sigmoid(gate)
            to_gate = (grad_act * up * (sigmoid * (1.0 + gate * (1.0 - sigmoid)))).astype(bf16)
            to_up = (grad_act * (gate * sigmoid)).astype(bf16)
            grad_gate[:, cut(t)] = to_gate
            grad_up[:, cut(t)] = to_up
            return dot_nt(to_gate, w_gate[:, cut(t)]) + dot_nt(to_up, w_up[:, cut(t)])

        if s > 0:
            gate_to_z(0)
        total[...] = step(0)

        @pl.loop(1, units // tile)
        def _(t):
            total[...] += step(t)

        reduce_start(2, s)
        half = units // 2
        far = pl.ds(pl.multiple_of((1 - z_low) * half, half), half)
        flying["grads"] = [
            keep_out(source, target.at[both(s)], waited=True)
            for source, target in (
                (grad_gate, out_gate),
                (grad_gate.at[:, far], out_gate_far),
                (grad_up, out_up),
                (grad_up.at[:, far], out_up_far),
            )
        ]

    def gate_to_z(s):
        for copy in flying["grads"]:
            copy.wait()
        flying["gate_z", s] = send(out_gate_far.at[both(s)], out_gate_z.at[both(s)], z_peer)

    def to_attention(s):
        value = reduced(2, s)
        grad = own_cotangent[mine(s), :].astype(f32) + value
        out_grad_hidden[mine(s), :] = grad
        normed = own_normed[mine(s), :]
        gain = jnp.sum(grad * normed, axis=0, keepdims=True)
        out_gain[0:1, :] = gain if s == 0 else out_gain[0:1, :] + gain
        factor = own_factor[mine(s), 0:1]
        attn_keep[own(s), :] = norm_back(grad * g_attn[...], normed, factor).astype(bf16)
        share(attn_keep, s)

    def attended_grad(s):
        flying["share", s].wait()
        keep_out(attn_keep.at[both(s)], out_attn.at[both(s)])
        heads_keep[both(s), :] = dot_nt(attn_keep[both(s), :], w_out[...]).astype(bf16)
        for d in range(1, line):
            flying["grads", s, d] = send(
                heads_keep.at[both(s), head(d)], out_grads.at[d, both(s)], ahead[d]
            )
        keep_out(heads_keep.at[both(s), head(0)], out_grads.at[0, both(s)])

    project_out(0)
    project_out(1)
    for load in loads[1:]:
        load.wait()
    after_attention(0)
    forward(0)
    after_attention(1)
    forward(1)
    turn_point(0)
    backward(0)
    turn_point(1)
    backward(1)
    gate_to_z(1)
    for s in range(2):
        forward_core("hidden", s, out_hidden_z)
    to_attention(0)
    attended_grad(0)
    to_attention(1)
    attended_grad(1)
    for s in range(2):
        flying["act", s].wait()
        flying["output", s].wait()
        forward_core("mlp", s, out_mlp_x)
    for s in range(2):
        flying["tokens_core", s].wait()
        flying["gate_z", s].wait()
        flying["hidden_core", s].wait()
        flying["mlp_core", s].wait()
        for d in range(1, line):
            flying["grads", s, d].wait()
    for copy in local:
        copy.wait()


def block(pieces, w_out, g_attn, g_mlp, tokens, cotangent, w_gate, w_up, w_down):
    _, rows, width = pieces.shape
    columns = line * width
    depth, units = w_gate.shape
    half = rows // 2
    quarter = rows // 4
    f32 = jnp.float32
    bf16 = jnp.bfloat16
    wide = jax.ShapeDtypeStruct((rows, depth), bf16)
    tall = jax.ShapeDtypeStruct((rows, units), bf16)
    any_spec = pl.BlockSpec(memory_space=pl.ANY)
    return pl.pallas_call(
        block_kernel,
        out_shape=[
            jax.ShapeDtypeStruct((rows, columns), bf16),
            wide,
            wide,
            wide,
            wide,
            tall,
            jax.ShapeDtypeStruct((rows, units // 2), bf16),
            wide,
            wide,
            tall,
            jax.ShapeDtypeStruct((rows, units // 2), bf16),
            jax.ShapeDtypeStruct((rows, units // 2), bf16),
            tall,
            jax.ShapeDtypeStruct((rows, units // 2), bf16),
            wide,
            jax.ShapeDtypeStruct((line, rows, width), bf16),
            jax.ShapeDtypeStruct((half, depth), f32),
            jax.ShapeDtypeStruct((2, depth), f32),
        ],
        in_specs=vmem_specs(4) + [any_spec] * 5,
        out_specs=[any_spec] * 16 + vmem_specs(2),
        scratch_shapes=[
            pltpu.VMEM((depth, units), bf16),
            pltpu.VMEM((depth, units), bf16),
            pltpu.VMEM((units, depth), bf16),
            pltpu.VMEM((rows, units), bf16),
            pltpu.VMEM((rows, units), bf16),
            pltpu.VMEM((rows, units), bf16),
            pltpu.VMEM((rows, depth), bf16),
            pltpu.VMEM((rows, depth), bf16),
            pltpu.VMEM((rows, depth), bf16),
            pltpu.VMEM((half, units), bf16),
            pltpu.VMEM((half, units), bf16),
            pltpu.VMEM((half, 128), f32),
            pltpu.VMEM((half, depth), f32),
            pltpu.VMEM((half, depth), bf16),
            pltpu.VMEM((half, depth), bf16),
            pltpu.VMEM((rows, columns), bf16),
            pltpu.VMEM((rows, columns), bf16),
            pltpu.VMEM((half, depth), f32),
            pltpu.VMEM((2, quarter, depth), bf16),
            pltpu.VMEM((2, quarter, depth), bf16),
            pltpu.VMEM((2, quarter, depth), bf16),
            pltpu.VMEM((3, 2, quarter, depth), bf16),
            pltpu.SemaphoreType.DMA((56,)),
            pltpu.SemaphoreType.DMA((56,)),
            pltpu.SemaphoreType.DMA((32,)),
        ],
        compiler_params=pltpu.CompilerParams(
            vmem_limit_bytes=61800 << 10, collective_id=1, has_side_effects=True
        ),
        cost_estimate=pl.CostEstimate(flops=0, bytes_accessed=0, transcendentals=0),
    )(pieces, w_out, g_attn, g_mlp, tokens, cotangent, w_gate, w_up, w_down)


class Courier:
    def __init__(self, send_sems, recv_sems, local_sems):
        self.send_sems, self.recv_sems, self.local_sems = send_sems, recv_sems, local_sems
        self.remote, self.local = 0, 0

    def send(self, source, target, peer):
        copy = pltpu.make_async_remote_copy(
            src_ref=source,
            dst_ref=target,
            send_sem=self.send_sems.at[self.remote],
            recv_sem=self.recv_sems.at[self.remote],
            device_id=peer,
            device_id_type=pl.DeviceIdType.MESH,
        )
        self.remote += 1
        copy.start()
        return copy

    def move(self, source, target):
        copy = pltpu.make_async_copy(source, target, self.local_sems.at[self.local])
        self.local += 1
        copy.start()
        return copy


def greet(peers):
    barrier = pltpu.get_barrier_semaphore()
    for peer in peers:
        pl.semaphore_signal(barrier, inc=1, device_id=peer, device_id_type=pl.DeviceIdType.MESH)
    pl.semaphore_wait(barrier, len(peers))


class Spot:
    def __init__(self):
        mp = lax.axis_index("mp")
        spot = lax.axis_index("dp")
        self.core = lax.rem(mp, 2)
        self.x = lax.rem(spot, 2)
        self.z = spot // 2
        self.z_low = lax.rem(self.z, 2)
        self.z_high = self.z // 2
        self.core_peer = {"mp": mp + 1 - 2 * self.core}
        self.y_peer = {"mp": lax.rem(mp + 2, 4)}
        self.x_peer = {"dp": spot + 1 - 2 * self.x}
        self.z_peer = {"dp": spot + 2 - 4 * self.z_low}
        self.far_peer = {"dp": lax.rem(spot + 4, 8)}
        self.ahead = [{"dp": lax.rem(spot + 2 * d, 2 * line)} for d in range(line)]
        self.all = (self.core_peer, self.y_peer, self.x_peer) + tuple(self.ahead[1:])


class Job:
    def __init__(self, spot, over_x, first, first_far, second, second_far, cut_first):
        self.operands, self.cut_first = (first, first_far, second, second_far), cut_first
        self.tile = (first if cut_first else second).shape[1] // (line * pair)
        self.spot, self.over_x = spot, over_x
        self.side = spot.x if over_x else spot.z_low
        self.partner = spot.x_peer if over_x else spot.z_peer
        self.first_peer = spot.z_peer if over_x else spot.x_peer

    def at(self, ref, index):
        block = pl.ds(pl.multiple_of(index * self.tile, self.tile), self.tile)
        return ref.at[block, :] if self.cut_first else ref.at[:, block]

    def span(self, ref, index):
        block = pl.ds(pl.multiple_of(index * 2 * self.tile, 2 * self.tile), 2 * self.tile)
        return ref.at[block, :] if self.cut_first else ref.at[:, block]

    def term(self, index):
        first, first_far, second, second_far = self.operands
        block = pl.ds(pl.multiple_of(index * self.tile, self.tile), self.tile)
        if self.cut_first:
            return dot_t(first[:, block], second[...]) + dot_t(first_far[:, block], second_far[...])
        return dot_t(first[...], second[:, block]) + dot_t(first_far[...], second_far[:, block])

    def block_of(self, high, index):
        if self.over_x:
            return (2 * high + self.spot.z_low) * pair + index
        return (2 * high + index) * pair + self.spot.x

    def send_terms(self, target):
        @pl.loop(0, line)
        def _(i):
            if self.over_x:
                index = (i // 2) * 4 + (1 - self.spot.z_low) * 2 + lax.rem(i, 2)
            else:
                index = i * pair + 1 - self.spot.x
            self.at(target, i)[...] = self.term(index).astype(jnp.bfloat16)

    def second_terms(self, arrived, target):
        @pl.loop(0, 2)
        def _(i):
            total = self.term(self.block_of(1 - self.spot.z_high, i))
            total = total + self.at(arrived, i)[...].astype(jnp.float32)
            self.at(target, i)[...] = total.astype(jnp.bfloat16)

    def own_term(self, side, arrived):
        total = self.term(self.block_of(self.spot.z_high, side))
        return total + self.at(arrived, side)[...].astype(jnp.float32)


def middle_kernel(
    grad_queries,
    near,
    far,
    q_raw,
    k_raw,
    factors,
    cosines,
    sines,
    gq,
    gk,
    act,
    act_x,
    mlp,
    mlp_x,
    hidden,
    hidden_z,
    gate,
    gate_z,
    up,
    up_far,
    out_own_down,
    out_r2_down,
    out_r1_gate,
    out_r1_up,
    out_up_z,
    out_raw_x,
    r1_down,
    out_raw,
    out_raw_own,
    out_gain,
    act_v,
    act_zv,
    mlp_v,
    mlp_zv,
    hidden_v,
    hidden_zv,
    gate_v,
    gate_zv,
    up_v,
    up_zv,
    send_down,
    send_gate,
    send_up,
    r1_v,
    r1_own,
    s2_v,
    own_v,
    far_in,
    sums,
    query_home,
    pair_home,
    scaled,
    raw_far,
    inner,
    inner_core,
    inner_y,
    send_sems,
    recv_sems,
    local_sems,
):
    f32 = jnp.float32
    bf16 = jnp.bfloat16
    spot = Spot()
    mail = Courier(send_sems, recv_sems, local_sems)
    count, width = cosines.shape
    columns = line * width
    depth = mlp_v.shape[1]
    half = act_v.shape[1]
    own_half = pl.ds(pl.multiple_of(spot.z_low * half, half), half)
    x_half = pl.ds(pl.multiple_of(spot.x * half, half), half)
    loads = [
        mail.move(act.at[:, x_half], act_v),
        mail.move(act_x, act_zv),
        mail.move(mlp, mlp_v),
        mail.move(mlp_x, mlp_zv),
        mail.move(hidden, hidden_v),
        mail.move(hidden_z, hidden_zv),
        mail.move(gate.at[:, own_half], gate_v),
        mail.move(gate_z, gate_zv),
        mail.move(up.at[:, own_half], up_v),
    ]
    greet(spot.all)
    far_copy = mail.send(far, far_in, spot.x_peer)
    my_head = pl.ds(pl.multiple_of(spot.z * width, width), width)
    query_copies = [
        mail.send(grad_queries.at[d], query_home.at[:, my_head], spot.ahead[line - d])
        for d in range(1, line)
    ]
    up_copy = mail.send(up_far, up_zv, spot.z_peer)
    query_home[:, my_head] = grad_queries[0]
    for load in loads[:4]:
        load.wait()
    down = Job(spot, True, act_v, act_zv, mlp_v, mlp_zv, False)
    down.send_terms(send_down)
    down_copy = mail.send(send_down, r1_down, down.first_peer)
    for load in loads[4:]:
        load.wait()
    gates = Job(spot, False, hidden_v, hidden_zv, gate_v, gate_zv, True)
    gates.send_terms(send_gate)
    far_copy.wait()
    gate_terms = mail.send(send_gate, out_r1_gate, gates.first_peer)
    sums[...] = (near[...].astype(f32) + far_in[...].astype(f32)).astype(bf16)
    pair_copies = [
        mail.send(sums.at[d], pair_home.at[:, :, my_head], spot.ahead[line - d])
        for d in range(1, line)
    ]
    pair_home[:, :, my_head] = sums[0]
    up_copy.wait()
    keep_up = mail.move(up_zv, out_up_z)
    ups = Job(spot, False, hidden_v, hidden_zv, up_v, up_zv, True)
    ups.send_terms(send_up)
    up_terms = mail.send(send_up, out_r1_up, ups.first_peer)

    for copy in query_copies + pair_copies:
        copy.wait()

    def column(row):
        return jnp.broadcast_to(row, (width, count)).T

    sources = ((query_home, None, q_raw, gq), (pair_home, 0, k_raw, gk))
    factor_columns = [column(factors[which : which + 1, :]) for which in range(2)]
    for which, (home, slot, raw, gain) in enumerate(sources):
        inner_sum = jnp.zeros((count, width), f32)
        for h in range(line):
            cut = slice(h * width, (h + 1) * width)
            part = (home[:, cut] if slot is None else home[slot, :, cut]).astype(f32)
            back = part * cosines[...] - pltpu.roll(part, width // 2, 1) * sines[...]
            normed = raw[:, cut] * factor_columns[which]
            out_gain[which : which + 1, cut] = jnp.sum(back * normed, axis=0, keepdims=True)
            value = back * gain[:, cut]
            scaled[which, :, cut] = value
            inner_sum = inner_sum + value * normed
        inner[which : which + 1, :] = jnp.sum(inner_sum.T, axis=0, keepdims=True)
    core_copy = mail.send(inner, inner_core, spot.core_peer)
    core_copy.wait()
    arrived = inner_core[...]
    quarter = count // 4
    cuts = [arrived[:, i * quarter : (i + 1) * quarter] for i in (1, 0, 3, 2)]
    chip = inner[...] + jnp.concatenate(cuts, axis=1)
    inner[...] = chip
    y_copy = mail.send(inner, inner_y, spot.y_peer)
    y_copy.wait()
    inner_all = (chip + inner_y[...]) / depth
    for which, (home, slot, raw, gain) in enumerate(sources):
        inner_column = column(inner_all[which : which + 1, :])
        for h in range(line):
            cut = slice(h * width, (h + 1) * width)
            normed = raw[:, cut] * factor_columns[which]
            value = factor_columns[which] * (scaled[which, :, cut] - normed * inner_column)
            base = which * columns + h * width
            out_raw[:, base : base + width] = value.astype(bf16)
    out_raw[:, 2 * columns :] = pair_home[1]
    part_width = columns // 2
    for which in range(3):
        cut = slice(which * part_width, (which + 1) * part_width)
        base = which * columns

        def side(index):
            start = pl.multiple_of(base + index * part_width, part_width)
            return out_raw[:, pl.ds(start, part_width)]

        out_raw_own[:, cut] = side(spot.x)
        raw_far[:, cut] = side(1 - spot.x)
    raw_copy = mail.send(raw_far, out_raw_x, spot.x_peer)

    down_copy.wait()
    loads = [
        mail.move(down.span(r1_down, 1 - spot.z_high), r1_v),
        mail.move(down.span(r1_down, spot.z_high), r1_own),
    ]
    loads[0].wait()
    down.second_terms(r1_v, s2_v)
    second_copy = mail.send(s2_v, out_r2_down, spot.far_peer)
    loads[1].wait()

    @pl.loop(0, 2)
    def _(i):
        down.at(own_v, i)[...] = down.own_term(i, r1_own)

    keep_own = mail.move(own_v, out_own_down)
    for copy in (gate_terms, up_terms, raw_copy, second_copy, keep_up, keep_own):
        copy.wait()


def middle(small, large):
    f32 = jnp.float32
    bf16 = jnp.bfloat16
    grad_queries, near, far, q_raw = small[:4]
    act, act_x, grad_mlp = large[:3]
    _, count, width = grad_queries.shape
    columns = line * width
    depth = grad_mlp.shape[1]
    units = act.shape[1]
    half = units // 2
    cut = depth // 2
    any_spec = pl.BlockSpec(memory_space=pl.ANY)
    shape = jax.ShapeDtypeStruct
    return pl.pallas_call(
        middle_kernel,
        in_specs=vmem_specs(10) + [any_spec] * 10,
        out_specs=[any_spec] * 7 + vmem_specs(3),
        out_shape=[
            shape((half, cut // 2), f32),
            shape((half, cut // 2), bf16),
            shape((cut, half), bf16),
            shape((cut, half), bf16),
            shape((count, half), bf16),
            shape((count, 3 * columns // 2), bf16),
            shape((half, cut), bf16),
            shape((count, 3 * columns), bf16),
            shape((count, 3 * columns // 2), bf16),
            shape((2, columns), f32),
        ],
        scratch_shapes=[
            pltpu.VMEM((count, half), bf16),
            pltpu.VMEM((count, half), bf16),
            pltpu.VMEM((count, depth), bf16),
            pltpu.VMEM((count, depth), bf16),
            pltpu.VMEM((count, depth), bf16),
            pltpu.VMEM((count, depth), bf16),
            pltpu.VMEM((count, half), bf16),
            pltpu.VMEM((count, half), bf16),
            pltpu.VMEM((count, half), bf16),
            pltpu.VMEM((count, half), bf16),
            pltpu.VMEM((half, cut), bf16),
            pltpu.VMEM((cut, half), bf16),
            pltpu.VMEM((cut, half), bf16),
            pltpu.VMEM((half, cut // 2), bf16),
            pltpu.VMEM((half, cut // 2), bf16),
            pltpu.VMEM((half, cut // 2), bf16),
            pltpu.VMEM((half, cut // 2), f32),
            pltpu.VMEM(near.shape, bf16),
            pltpu.VMEM(near.shape, bf16),
            pltpu.VMEM((count, columns), bf16),
            pltpu.VMEM((2, count, columns), bf16),
            pltpu.VMEM((2, count, columns), f32),
            pltpu.VMEM((count, 3 * columns // 2), bf16),
            pltpu.VMEM((2, count), f32),
            pltpu.VMEM((2, count), f32),
            pltpu.VMEM((2, count), f32),
            pltpu.SemaphoreType.DMA((16,)),
            pltpu.SemaphoreType.DMA((16,)),
            pltpu.SemaphoreType.DMA((16,)),
        ],
        compiler_params=pltpu.CompilerParams(
            vmem_limit_bytes=60 << 20, collective_id=3, has_side_effects=True
        ),
    )(*small, *large)


def last_kernel(
    raw,
    raw_own,
    raw_x,
    wide,
    narrow,
    attended,
    hidden,
    hidden_z,
    gate,
    gate_z,
    up,
    up_z,
    attn,
    tokens,
    tokens_x,
    own_down,
    r2_down,
    r1_gate,
    r1_up,
    w_query,
    w_key,
    w_value,
    grad_hidden,
    *refs,
):
    outs, refs = refs[:13], refs[13:]
    near_down, near_gate, near_up, near_raw, near_out = outs[:5]
    far_down, far_gate, far_up, far_raw, far_out = outs[5:10]
    out_tokens, r1_raw, r1_out = outs[10:]
    out_wide, out_narrow = refs[:2]
    (
        hidden_v,
        hidden_zv,
        gate_v,
        gate_zv,
        up_v,
        up_zv,
        tokens_v,
        tokens_xv,
        attn_v,
        attn_xv,
        heads_v,
        heads_far,
        heads_xv,
        send_raw,
        send_out,
        r1_wide,
        r1_raw_v,
        r1_out_v,
        s2_gate,
        s2_up,
        s2_raw,
        s2_out,
        r2_gate,
        r2_up,
        r2_raw,
        r2_out,
        own_down_v,
        r2_down_v,
        fin_down,
        fin_gate,
        fin_up,
        fin_raw,
        fin_out,
        keep_down,
        keep_gate,
        keep_up,
        keep_raw,
        keep_out,
        weight_v,
        total,
        part_send,
        part_recv,
        y_send,
        y_recv,
        hidden_own,
        token_keep,
        wide_core,
        wide_x,
        narrow_x,
        wide_z,
        narrow_z,
        send_sems,
        recv_sems,
        local_sems,
    ) = refs[2:]
    f32 = jnp.float32
    bf16 = jnp.bfloat16
    spot = Spot()
    mail = Courier(send_sems, recv_sems, local_sems)
    rows_all = tokens_v.shape[0]
    rows = rows_all // 2
    count = rows // 2
    half = gate_v.shape[1]
    own_half = pl.ds(pl.multiple_of(spot.z_low * half, half), half)
    heads_half = heads_v.shape[1]
    side_heads = lambda side: pl.ds(pl.multiple_of(side * heads_half, heads_half), heads_half)
    own = lambda s: pl.ds(s * rows, count)
    other = lambda s: pl.ds(s * rows + count, count)
    both = lambda s: pl.ds(s * rows, rows)
    mine = lambda s: pl.ds(s * count, count)

    token_loads = [mail.move(tokens_x, tokens_xv)]
    for s in range(2):
        for part, place in ((0, spot.core), (1, 1 - spot.core)):
            start = pl.multiple_of(place * rows + s * count, count)
            target = tokens_v.at[pl.ds(s * rows + part * count, count)]
            token_loads.append(mail.move(tokens.at[pl.ds(start, count)], target))
    attn_load = mail.move(attn, attn_v)
    r1_loads = []
    first_loads = [mail.move(hidden, hidden_v), mail.move(hidden_z, hidden_zv)]
    gate_loads = [mail.move(gate.at[:, own_half], gate_v), mail.move(gate_z, gate_zv)]
    up_loads = [mail.move(up.at[:, own_half], up_v), mail.move(up_z, up_zv)]
    ups = Job(spot, False, hidden_v, hidden_zv, up_v, up_zv, True)
    gates = Job(spot, False, hidden_v, hidden_zv, gate_v, gate_zv, True)
    raws = Job(spot, True, tokens_v, tokens_xv, raw_own, raw_x, True)
    outs_job = Job(spot, True, heads_v, heads_xv, attn_v, attn_xv, False)
    gate_second = mail.move(gates.span(r1_gate, 1 - spot.z_high), r1_wide.at[0])
    gate_own = mail.move(gates.span(r1_gate, spot.z_high), r1_wide.at[1])
    up_second = mail.move(ups.span(r1_up, 1 - spot.z_high), r1_wide.at[2])
    up_own = mail.move(ups.span(r1_up, spot.z_high), r1_wide.at[3])
    greet(spot.all)
    wide_copy = mail.send(wide, wide_core, spot.core_peer)
    attn_load.wait()
    attn_copies = [
        mail.send(attn_v.at[own(s)], attn_xv.at[own(s)], spot.x_peer) for s in range(2)
    ]
    heads_far[...] = attended[:, side_heads(1 - spot.x)]
    heads_v[...] = attended[:, side_heads(spot.x)]
    heads_copy = mail.send(heads_far, heads_xv, spot.x_peer)
    for load in token_loads:
        load.wait()
    raws.send_terms(send_raw)
    raw_copy = mail.send(send_raw, r1_raw, raws.first_peer)
    wide_copy.wait()
    out_wide[...] = wide[...] + wide_core[...]
    out_narrow[...] = narrow[...]
    wide_x_copy = mail.send(out_wide, wide_x, spot.x_peer)
    narrow_x_copy = mail.send(out_narrow, narrow_x, spot.x_peer)

    for load in (*first_loads, *gate_loads, gate_second):
        load.wait()
    gates.second_terms(r1_wide.at[0], s2_gate)
    gate_copy = mail.send(s2_gate, r2_gate, spot.far_peer)
    for load in (*up_loads, up_second):
        load.wait()
    ups.second_terms(r1_wide.at[2], s2_up)
    second_up = mail.send(s2_up, r2_up, spot.far_peer)

    input_weights = (w_query, w_key, w_value)
    columns = w_query.shape[1]
    flying = {}
    for which, source in enumerate(input_weights):
        load = mail.move(source, weight_v)
        load.wait()
        for s in range(2):
            term = dot_nt(raw[both(s), which * columns : (which + 1) * columns], weight_v[...])
            total[both(s), :] = term if which == 0 else total[both(s), :] + term
    for s in range(2):
        part_send[s] = total[other(s), :].astype(bf16)
        flying["core", s] = mail.send(part_send.at[s], part_recv.at[s], spot.core_peer)
    hidden_load = mail.move(grad_hidden, hidden_own)
    for s in range(2):
        flying["core", s].wait()
        y_send[s] = (total[own(s), :] + part_recv[s].astype(f32)).astype(bf16)
        flying["y", s] = mail.send(y_send.at[s], y_recv.at[s], spot.y_peer)

    near_copies, far_copies = [], []

    def finish(job, value_of, fin, far, keep, target):
        fin[...] = value_of(1 - job.side).astype(bf16)
        far_copies.append(mail.send(fin, far, job.partner))
        keep[...] = value_of(job.side)
        near_copies.append(mail.move(keep, target))

    down_loads = [mail.move(own_down, own_down_v), mail.move(r2_down, r2_down_v)]
    for load in down_loads:
        load.wait()
    down = outs_job
    finish(
        down,
        lambda side: down.at(own_down_v, side)[...] + down.at(r2_down_v, side)[...].astype(f32),
        fin_down,
        far_down,
        keep_down,
        near_down,
    )

    wide_x_copy.wait()
    narrow_x_copy.wait()
    out_wide[...] = out_wide[...] + wide_x[...]
    out_narrow[...] = out_narrow[...] + narrow_x[...]
    for s in range(2):
        attn_copies[s].wait()
    attn_core = [
        mail.send(attn_xv.at[own(s)], attn_xv.at[other(s)], spot.core_peer) for s in range(2)
    ]
    for copy in attn_core:
        copy.wait()
    heads_copy.wait()
    outs_job.send_terms(send_out)
    out_copy = mail.send(send_out, r1_out, outs_job.first_peer)

    hidden_load.wait()
    for s in range(2):
        flying["y", s].wait()
        value = y_send[s].astype(f32) + y_recv[s].astype(f32)
        token_keep[mine(s), :] = (hidden_own[mine(s), :] + value).astype(bf16)
        home = pl.ds(pl.multiple_of(spot.core * rows + s * count, count), count)
        flying["keep", s] = mail.move(token_keep.at[mine(s)], out_tokens.at[home])
        flying["tokens", s] = mail.send(
            token_keep.at[mine(s)], out_tokens.at[home], spot.core_peer
        )
    gain_copies = []
    for d in range(1, line):
        gain_copies.append(mail.send(out_wide, wide_z.at[d - 1], spot.ahead[d]))
        gain_copies.append(mail.send(out_narrow, narrow_z.at[d - 1], spot.ahead[d]))

    def final_of(job, r1_own, r2):
        return lambda side: job.own_term(side, r1_own) + job.at(r2, side)[...].astype(f32)

    raw_copy.wait()
    raw_loads = [
        mail.move(raws.span(r1_raw, 1 - spot.z_high), r1_raw_v.at[0]),
        mail.move(raws.span(r1_raw, spot.z_high), r1_raw_v.at[1]),
    ]
    for load in raw_loads:
        load.wait()
    raws.second_terms(r1_raw_v.at[0], s2_raw)
    second_raw = mail.send(s2_raw, r2_raw, spot.far_peer)
    out_copy.wait()
    out_loads = [
        mail.move(outs_job.span(r1_out, 1 - spot.z_high), r1_out_v.at[0]),
        mail.move(outs_job.span(r1_out, spot.z_high), r1_out_v.at[1]),
    ]
    for load in out_loads:
        load.wait()
    outs_job.second_terms(r1_out_v.at[0], s2_out)
    second_out = mail.send(s2_out, r2_out, spot.far_peer)
    gate_own.wait()
    gate_copy.wait()
    finish(gates, final_of(gates, r1_wide.at[1], r2_gate), fin_gate, far_gate, keep_gate, near_gate)

    up_own.wait()
    second_up.wait()
    finish(ups, final_of(ups, r1_wide.at[3], r2_up), fin_up, far_up, keep_up, near_up)
    second_raw.wait()
    finish(raws, final_of(raws, r1_raw_v.at[1], r2_raw), fin_raw, far_raw, keep_raw, near_raw)
    second_out.wait()
    finish(
        outs_job, final_of(outs_job, r1_out_v.at[1], r2_out), fin_out, far_out, keep_out, near_out
    )
    for copy in gain_copies:
        copy.wait()
    for d in range(1, line):
        out_wide[...] = out_wide[...] + wide_z[d - 1]
        out_narrow[...] = out_narrow[...] + narrow_z[d - 1]
    for s in range(2):
        flying["keep", s].wait()
        flying["tokens", s].wait()
    for copy in near_copies + far_copies:
        copy.wait()


def last(small, large):
    f32 = jnp.float32
    bf16 = jnp.bfloat16
    raw, raw_own, raw_x, wide, narrow, attended = small
    hidden, gate = large[0], large[2]
    count, depth = hidden.shape
    units = gate.shape[1]
    half = units // 2
    block = depth // (line * pair)
    columns = attended.shape[1]
    heads_half = columns // 2
    raw_half = raw_own.shape[1]
    rows = count // 2
    any_spec = pl.BlockSpec(memory_space=pl.ANY)
    shape = jax.ShapeDtypeStruct
    vmem = lambda *size: pltpu.VMEM(size, bf16)
    wide_vmem = lambda *size: pltpu.VMEM(size, f32)
    return pl.pallas_call(
        last_kernel,
        in_specs=vmem_specs(6) + [any_spec] * len(large),
        out_specs=[any_spec] * 13 + vmem_specs(2),
        out_shape=[
            shape((half, block), f32),
            shape((block, half), f32),
            shape((block, half), f32),
            shape((block, raw_half), f32),
            shape((heads_half, block), f32),
            shape((half, block), bf16),
            shape((block, half), bf16),
            shape((block, half), bf16),
            shape((block, raw_half), bf16),
            shape((heads_half, block), bf16),
            shape((count, depth), bf16),
            shape((line * block, raw_half), bf16),
            shape((heads_half, line * block), bf16),
            shape(wide.shape, f32),
            shape(narrow.shape, f32),
        ],
        scratch_shapes=[
            vmem(count, depth),
            vmem(count, depth),
            vmem(count, half),
            vmem(count, half),
            vmem(count, half),
            vmem(count, half),
            vmem(count, depth),
            vmem(count, depth),
            vmem(count, depth),
            vmem(count, depth),
            vmem(count, heads_half),
            vmem(count, heads_half),
            vmem(count, heads_half),
            vmem(line * block, raw_half),
            vmem(heads_half, line * block),
            vmem(4, 2 * block, half),
            vmem(2, 2 * block, raw_half),
            vmem(2, heads_half, 2 * block),
            vmem(2 * block, half),
            vmem(2 * block, half),
            vmem(2 * block, raw_half),
            vmem(heads_half, 2 * block),
            vmem(2 * block, half),
            vmem(2 * block, half),
            vmem(2 * block, raw_half),
            vmem(heads_half, 2 * block),
            wide_vmem(half, 2 * block),
            vmem(half, 2 * block),
            vmem(half, block),
            vmem(block, half),
            vmem(block, half),
            vmem(block, raw_half),
            vmem(heads_half, block),
            wide_vmem(half, block),
            wide_vmem(block, half),
            wide_vmem(block, half),
            wide_vmem(block, raw_half),
            wide_vmem(heads_half, block),
            vmem(depth, columns),
            wide_vmem(count, depth),
            vmem(2, rows // 2, depth),
            vmem(2, rows // 2, depth),
            vmem(2, rows // 2, depth),
            vmem(2, rows // 2, depth),
            wide_vmem(rows, depth),
            vmem(rows, depth),
            wide_vmem(*wide.shape),
            wide_vmem(*wide.shape),
            wide_vmem(*narrow.shape),
            wide_vmem(line - 1, *wide.shape),
            wide_vmem(line - 1, *narrow.shape),
            pltpu.SemaphoreType.DMA((48,)),
            pltpu.SemaphoreType.DMA((48,)),
            pltpu.SemaphoreType.DMA((40,)),
        ],
        compiler_params=pltpu.CompilerParams(
            vmem_limit_bytes=61800 << 10, collective_id=4, has_side_effects=True
        ),
    )(*small, *large)


def on_device_lines(
    tokens,
    cotangent,
    doc_ids,
    row_ids,
    offsets,
    w_query,
    w_key,
    w_value,
    w_output,
    w_gate,
    w_up,
    w_down,
    gain_query,
    gain_key,
    gain_attn,
    gain_mlp,
):
    f32 = jnp.float32
    bf16 = jnp.bfloat16
    row_count, model_width = tokens.shape
    heads_here, head_width = gain_query.shape
    local_width = heads_here * head_width
    half_rows = row_count // 2
    key_rows = row_count * line * pair
    spot = lax.axis_index("dp")
    z, x = spot // pair, lax.rem(spot, pair)
    z_high, z_low = z // 2, lax.rem(z, 2)
    core = lax.rem(lax.axis_index("mp"), 2)
    place = jnp.stack([core, z, z_low, z_high, x]).astype(jnp.int32)

    quarter = row_count // 4

    def own_rows(value):
        return lax.dynamic_slice_in_dim(value, core * half_rows, half_rows, 0)

    def other_rows(value):
        return lax.dynamic_slice_in_dim(value, (1 - core) * half_rows, half_rows, 0)

    def reorder(value):
        return join_parts(own_rows(value), other_rows(value))

    def restore(own, other):
        whole = jnp.zeros((row_count,) + own.shape[1:], own.dtype)
        whole = lax.dynamic_update_slice_in_dim(whole, own, core * half_rows, 0)
        return lax.dynamic_update_slice_in_dim(whole, other, (1 - core) * half_rows, 0)

    def half_of(value, side):
        width = value.shape[1] // 2
        return lax.dynamic_slice_in_dim(value, side * width, width, 1)

    def join_halves(near, far, axis, side):
        low = jnp.where(side == 0, near, far)
        return jnp.concatenate([low, jnp.where(side == 0, far, near)], axis=axis)

    positions = reorder(offsets[0] + jnp.arange(row_count, dtype=jnp.int32))
    labels = reorder(row_ids[0] * key_rows + doc_ids)
    freqs = rope_base ** (-jnp.arange(0, head_width // 2, dtype=f32) * 2.0 / head_width)
    angles = positions.astype(f32)[:, None] * freqs[None, :]
    cosines, sines = jnp.cos(angles), jnp.sin(angles)
    cosines = jnp.concatenate([cosines, cosines], axis=1)
    sines = jnp.concatenate([-sines, sines], axis=1)
    g_query = gain_query.reshape(1, local_width)
    g_key = gain_key.reshape(1, local_width)
    spots = jnp.stack([labels, positions]).astype(f32)
    queries, pairs, notes, q_raw, k_raw = project(
        tokens, w_query, w_key, w_value, g_query, g_key, cosines, sines, spots
    )
    factors = notes[0, :2]
    codes = notes[:, 2, :].astype(jnp.int32) * key_rows + notes[:, 3, :].astype(jnp.int32)
    lows = notes[:line, 2, :].astype(jnp.int32) * key_rows
    live = (
        (jnp.min(codes, axis=1)[None, :] <= jnp.max(codes[:line], axis=1)[:, None])
        & (jnp.max(codes, axis=1)[None, :] >= jnp.min(lows, axis=1)[:, None])
    ).astype(jnp.int32)

    turned, log_total, queries_n, keys_n, code_columns, code_rows, attended_out = attend(
        key_rows, live, notes, queries, pairs
    )

    def gather_heads(home):
        twice = jnp.concatenate(home + home, axis=1)
        return lax.dynamic_slice_in_dim(
            twice, lax.rem(line - z, line) * head_width, local_width, 1
        )

    def send_home(pieces):
        return [pieces[0]] + [line_shift(pieces[d], line - d) for d in range(1, line)]

    tokens_in = reorder(tokens)
    g_attn = gain_attn.reshape(1, model_width)
    g_mlp = gain_mlp.reshape(1, model_width)
    (
        attended_low,
        tokens_x,
        output,
        hidden_low,
        hidden_z,
        act_low,
        act_x,
        grad_mlp,
        grad_mlp_x,
        grad_gate,
        _,
        grad_gate_z,
        grad_up,
        grad_up_far,
        grad_attn,
        grads,
        grad_hidden,
        wide_gains,
    ) = block(
        attended_out, w_output, g_attn, g_mlp, tokens, cotangent, w_gate, w_up, w_down
    )
    back = attend_back(
        live, code_columns, code_rows, queries_n, keys_n, pairs, turned, log_total, grads
    )
    (
        own_down,
        r2_down,
        r1_gate,
        r1_up,
        grad_up_z,
        raw_x,
        _,
        raw,
        raw_own,
        narrow_gains,
    ) = middle(
        (*back, q_raw, k_raw, factors, cosines, sines, g_query, g_key),
        (
            act_low,
            act_x,
            grad_mlp,
            grad_mlp_x,
            hidden_low,
            hidden_z,
            grad_gate,
            grad_gate_z,
            grad_up,
            grad_up_far,
        ),
    )
    results = last(
        (raw, raw_own, raw_x, wide_gains, narrow_gains, attended_low),
        (
            hidden_low,
            hidden_z,
            grad_gate,
            grad_gate_z,
            grad_up,
            grad_up_z,
            grad_attn,
            tokens,
            tokens_x,
            own_down,
            r2_down,
            r1_gate,
            r1_up,
            w_query,
            w_key,
            w_value,
            grad_hidden,
        ),
    )
    down_near, gate_near, up_near, raw_near, out_near = results[:5]
    down_far, gate_far, up_far, raw_far, out_far = [part.astype(f32) for part in results[5:10]]
    grad_tokens = results[10]
    wide, narrow = results[13:]
    gains = jnp.concatenate([wide.reshape(2 * model_width), narrow.reshape(2 * local_width)])
    piece = head_width // (line * pair)

    def gain_piece(start, rows):
        part = gains[start : start + rows * head_width].reshape(rows, head_width)
        return lax.dynamic_slice_in_dim(part, spot * piece, piece, 1)

    all_heads = model_width // head_width
    part_width = local_width // pair

    def raw_result(index):
        cut = slice(index * part_width, (index + 1) * part_width)
        return join_halves(raw_near[:, cut], raw_far[:, cut], 1, x)

    return (
        output,
        grad_tokens,
        raw_result(0),
        raw_result(1),
        raw_result(2),
        join_halves(out_near, out_far, 0, x),
        join_halves(gate_near, gate_far, 1, z_low),
        join_halves(up_near, up_far, 1, z_low),
        join_halves(down_near, down_far, 0, x),
        gain_piece(2 * model_width, heads_here),
        gain_piece(2 * model_width + local_width, heads_here),
        gain_piece(0, all_heads),
        gain_piece(model_width, all_heads),
    )


def solution(mesh):
    tuned = mesh.shape["dp"] == line * pair and mesh.shape["mp"] == 4
    body = on_device_lines if tuned else on_device_general
    return jax.shard_map(
        body,
        mesh=mesh,
        in_specs=(
            P("dp", None),
            P("dp", None),
            P("dp"),
            P("dp"),
            P("dp"),
            P(None, "mp"),
            P(None, "mp"),
            P(None, "mp"),
            P("mp", None),
            P(None, "mp"),
            P(None, "mp"),
            P("mp", None),
            P("mp", None),
            P("mp", None),
            P(),
            P(),
        ),
        out_specs=(
            P("dp", None),
            P("dp", None),
            P("dp", "mp"),
            P("dp", "mp"),
            P("dp", "mp"),
            P("mp", "dp"),
            P("dp", "mp"),
            P("dp", "mp"),
            P("mp", "dp"),
            P("mp", "dp"),
            P("mp", "dp"),
            P(None, "dp"),
            P(None, "dp"),
        ),
        check_vma=False,
    )
```

```python
import functools
import math

import jax
import jax.numpy as jnp
from jax import lax
from jax.experimental import pallas as pl
from jax.experimental.pallas import tpu as pltpu
from jax.sharding import PartitionSpec as P

epsilon = 1e-06
rope_base = 500000.0
masked_score = -1e30


def rope_tables(positions, head_width):
    freqs = rope_base ** (-jnp.arange(0, head_width // 2, dtype=jnp.float32) * 2.0 / head_width)
    angles = positions.astype(jnp.float32)[:, None] * freqs[None, :]
    return (jnp.cos(angles)[:, None, :], jnp.sin(angles)[:, None, :])


def rotate(values, cosines, sines):
    half = values.shape[-1] // 2
    first = values[..., :half]
    second = values[..., half:]
    return jnp.concatenate(
        [first * cosines - second * sines, second * cosines + first * sines], axis=-1
    )


def norm_back(grad_normed, normed, factor):
    return factor * (grad_normed - normed * jnp.mean(grad_normed * normed, axis=-1, keepdims=True))


def on_device_general(
    tokens,
    cotangent,
    doc_ids,
    row_ids,
    offsets,
    w_query,
    w_key,
    w_value,
    w_output,
    w_gate,
    w_up,
    w_down,
    gain_query,
    gain_key,
    gain_attn,
    gain_mlp,
):
    f32 = jnp.float32
    bf16 = jnp.bfloat16
    row_count = tokens.shape[0]
    model_width = tokens.shape[1]
    heads_here = gain_query.shape[0]
    head_width = gain_query.shape[1]
    local_width = heads_here * head_width
    groups = lax.axis_size("dp")
    key_rows = row_count * groups
    block_rows = min(key_rows, row_count * max(1, 512 // row_count))
    block_count = key_rows // block_rows
    score_scale = 1.0 / math.sqrt(head_width)
    positions = offsets[0] + jnp.arange(row_count, dtype=jnp.int32)
    labels = row_ids[0] * key_rows + doc_ids
    cosines, sines = rope_tables(positions, head_width)
    q_raw = jnp.dot(tokens, w_query, preferred_element_type=f32)
    k_raw = jnp.dot(tokens, w_key, preferred_element_type=f32)
    v_raw = jnp.dot(tokens, w_value, preferred_element_type=f32)
    squares = lax.psum(
        jnp.stack([jnp.sum(q_raw * q_raw, axis=1), jnp.sum(k_raw * k_raw, axis=1)]), "mp"
    )
    q_factor = lax.rsqrt(squares[0] / model_width + epsilon)[:, None]
    k_factor = lax.rsqrt(squares[1] / model_width + epsilon)[:, None]
    g_query = gain_query.reshape(local_width)
    g_key = gain_key.reshape(local_width)
    q_normed = q_raw * q_factor
    k_normed = k_raw * k_factor
    queries = rotate(
        (q_normed * g_query).reshape(row_count, heads_here, head_width), cosines, sines
    ).astype(bf16)
    keys_low = rotate(
        (k_normed * g_key).reshape(row_count, heads_here, head_width), cosines, sines
    ).astype(bf16)
    values_low = v_raw.astype(bf16)
    all_keys, all_values, all_labels, all_positions = (
        lax.all_gather(keys_low.reshape(row_count, local_width), "dp", axis=0, tiled=True),
        lax.all_gather(values_low, "dp", axis=0, tiled=True),
        lax.all_gather(labels, "dp", axis=0, tiled=True),
        lax.all_gather(positions, "dp", axis=0, tiled=True),
    )
    key_blocks = all_keys.reshape(block_count, block_rows, heads_here, head_width)
    value_blocks = all_values.reshape(block_count, block_rows, heads_here, head_width)
    label_blocks = all_labels.reshape(block_count, block_rows)
    position_blocks = all_positions.reshape(block_count, block_rows)
    scanned = (key_blocks, value_blocks, label_blocks, position_blocks)
    low_label = jnp.min(labels)
    high_label = jnp.max(labels)

    def scores_of(key_block, label_block, position_block):
        scores = (
            jnp.einsum("qhd,khd->hqk", queries, key_block, preferred_element_type=f32) * score_scale
        )
        allowed = (labels[:, None] == label_block[None, :]) & (
            positions[:, None] >= position_block[None, :]
        )
        return (scores, allowed[None])

    def touches(label_block):
        return (jnp.max(label_block) >= low_label) & (jnp.min(label_block) <= high_label)

    def max_step(carry, blocks_in):
        key_block, value_block, label_block, position_block = blocks_in

        def max_live_block(state):
            running, totals = state
            scores, allowed = scores_of(key_block, label_block, position_block)
            highest = jnp.maximum(
                running, jnp.max(jnp.where(allowed, scores, masked_score), axis=2)
            )
            weights = jnp.where(allowed, jnp.exp(scores - highest[:, :, None]), 0.0)
            return (highest, totals * jnp.exp(running - highest) + jnp.sum(weights, axis=2))

        return (lax.cond(touches(label_block), max_live_block, lambda state: state, carry), None)

    start_state = (
        jnp.full((heads_here, row_count), masked_score, f32),
        jnp.zeros((heads_here, row_count), f32),
    )
    (running_max, running_total), _ = lax.scan(max_step, start_state, scanned)
    log_total = running_max + jnp.log(running_total)

    def value_step(accum, blocks_in):
        key_block, value_block, label_block, position_block = blocks_in

        def value_live_block(current):
            scores, allowed = scores_of(key_block, label_block, position_block)
            probs_low = jnp.where(allowed, jnp.exp(scores - log_total[:, :, None]), 0.0).astype(
                bf16
            )
            return current + jnp.einsum(
                "hqk,khd->qhd", probs_low, value_block, preferred_element_type=f32
            )

        return (
            lax.cond(touches(label_block), value_live_block, lambda current: current, accum),
            None,
        )

    attended, _ = lax.scan(value_step, jnp.zeros((row_count, heads_here, head_width), f32), scanned)
    attended_low = attended.reshape(row_count, local_width).astype(bf16)
    attn_sum = lax.psum(
        jnp.dot(attended_low, w_output, preferred_element_type=f32).astype(jnp.bfloat16), "mp"
    ).astype(jnp.float32)
    attn_factor = lax.rsqrt(jnp.mean(attn_sum * attn_sum, axis=1, keepdims=True) + epsilon)
    attn_normed = attn_sum * attn_factor
    g_attn = gain_attn.reshape(model_width)
    hidden = tokens.astype(f32) + attn_normed * g_attn
    hidden_low = hidden.astype(bf16)
    gate_val = jnp.dot(hidden_low, w_gate, preferred_element_type=f32)
    up_val = jnp.dot(hidden_low, w_up, preferred_element_type=f32)
    sigmoid_gate = jax.nn.sigmoid(gate_val)
    silu_gate = gate_val * sigmoid_gate
    act_low = (silu_gate * up_val).astype(bf16)
    mlp_sum = lax.psum(
        jnp.dot(act_low, w_down, preferred_element_type=f32).astype(jnp.bfloat16), "mp"
    ).astype(jnp.float32)
    mlp_factor = lax.rsqrt(jnp.mean(mlp_sum * mlp_sum, axis=1, keepdims=True) + epsilon)
    mlp_normed = mlp_sum * mlp_factor
    g_mlp = gain_mlp.reshape(model_width)
    output = (hidden + mlp_normed * g_mlp).astype(bf16)
    grad_out = cotangent.astype(f32)
    grad_gain_mlp = jnp.sum(grad_out * mlp_normed, axis=0)
    grad_mlp = norm_back(grad_out * g_mlp, mlp_normed, mlp_factor).astype(bf16)
    grad_w_down = jnp.einsum("tf,td->fd", act_low, grad_mlp, preferred_element_type=f32)
    grad_act = jnp.einsum("td,fd->tf", grad_mlp, w_down, preferred_element_type=f32)
    slope = sigmoid_gate * (1.0 + gate_val * (1.0 - sigmoid_gate))
    grad_gate = (grad_act * up_val * slope).astype(bf16)
    grad_up = (grad_act * silu_gate).astype(bf16)
    branch_grad = jnp.einsum(
        "tf,df->td", grad_gate, w_gate, preferred_element_type=f32
    ) + jnp.einsum("tf,df->td", grad_up, w_up, preferred_element_type=f32)
    grad_hidden = grad_out + lax.psum(branch_grad.astype(jnp.bfloat16), "mp").astype(jnp.float32)
    grad_gain_attn = jnp.sum(grad_hidden * attn_normed, axis=0)
    grad_attn = norm_back(grad_hidden * g_attn, attn_normed, attn_factor).astype(bf16)
    grad_w_output = jnp.einsum("tc,td->cd", attended_low, grad_attn, preferred_element_type=f32)
    grad_attended = (
        jnp.einsum("td,cd->tc", grad_attn, w_output, preferred_element_type=f32)
        .astype(bf16)
        .reshape(row_count, heads_here, head_width)
    )
    delta = jnp.sum(grad_attended.astype(f32) * attended, axis=2).T

    def grad_step(grad_q, blocks_in):
        key_block, value_block, label_block, position_block = blocks_in

        def grad_live_block(current):
            scores, allowed = scores_of(key_block, label_block, position_block)
            probs = jnp.where(allowed, jnp.exp(scores - log_total[:, :, None]), 0.0)
            grad_probs = jnp.einsum(
                "qhd,khd->hqk", grad_attended, value_block, preferred_element_type=f32
            )
            grad_scores = (probs * (grad_probs - delta[:, :, None])).astype(bf16)
            value_term = jnp.einsum(
                "hqk,qhd->khd", probs.astype(bf16), grad_attended, preferred_element_type=f32
            )
            key_term = jnp.einsum("hqk,qhd->khd", grad_scores, queries, preferred_element_type=f32)
            updated = current + jnp.einsum(
                "hqk,khd->qhd", grad_scores, key_block, preferred_element_type=f32
            )
            return (updated, (key_term, value_term))

        def skip_block(current):
            nothing = jnp.zeros((block_rows, heads_here, head_width), f32)
            return (current, (nothing, nothing))

        return lax.cond(touches(label_block), grad_live_block, skip_block, grad_q)

    grad_queries, (key_terms, value_terms) = lax.scan(
        grad_step, jnp.zeros((row_count, heads_here, head_width), f32), scanned
    )
    grad_keys, grad_values = (
        lax.psum_scatter(
            (key_terms.reshape(key_rows, local_width) * score_scale).astype(jnp.bfloat16),
            "dp",
            scatter_dimension=0,
            tiled=True,
        ).astype(jnp.float32),
        lax.psum_scatter(
            value_terms.reshape(key_rows, local_width).astype(jnp.bfloat16),
            "dp",
            scatter_dimension=0,
            tiled=True,
        ).astype(jnp.float32),
    )
    grad_values_low = grad_values.astype(bf16)
    back_q = rotate(grad_queries * score_scale, cosines, -sines).reshape(row_count, local_width)
    back_k = rotate(grad_keys.reshape(row_count, heads_here, head_width), cosines, -sines).reshape(
        row_count, local_width
    )
    grad_gain_query = jnp.sum(back_q * q_normed, axis=0).reshape(heads_here, head_width)
    grad_gain_key = jnp.sum(back_k * k_normed, axis=0).reshape(heads_here, head_width)
    scaled_q = back_q * g_query
    scaled_k = back_k * g_key
    inner = lax.psum(
        jnp.stack([jnp.sum(scaled_q * q_normed, axis=1), jnp.sum(scaled_k * k_normed, axis=1)]),
        "mp",
    )
    grad_q_raw = (q_factor * (scaled_q - q_normed * inner[0][:, None] / model_width)).astype(bf16)
    grad_k_raw = (k_factor * (scaled_k - k_normed * inner[1][:, None] / model_width)).astype(bf16)
    input_term = (
        jnp.einsum("tc,dc->td", grad_q_raw, w_query, preferred_element_type=f32)
        + jnp.einsum("tc,dc->td", grad_k_raw, w_key, preferred_element_type=f32)
        + jnp.einsum("tc,dc->td", grad_values_low, w_value, preferred_element_type=f32)
    )
    grad_tokens = (
        grad_hidden + lax.psum(input_term.astype(jnp.bfloat16), "mp").astype(jnp.float32)
    ).astype(bf16)
    local_w_query = jnp.einsum("td,tc->dc", tokens, grad_q_raw, preferred_element_type=f32)
    local_w_key = jnp.einsum("td,tc->dc", tokens, grad_k_raw, preferred_element_type=f32)
    local_w_value = jnp.einsum("td,tc->dc", tokens, grad_values_low, preferred_element_type=f32)
    local_w_gate = jnp.einsum("td,tf->df", hidden_low, grad_gate, preferred_element_type=f32)
    local_w_up = jnp.einsum("td,tf->df", hidden_low, grad_up, preferred_element_type=f32)
    grad_w_query, grad_w_key, grad_w_value, grad_w_gate, grad_w_up = (
        lax.psum_scatter(
            local_w_query.astype(jnp.bfloat16), "dp", scatter_dimension=0, tiled=True
        ).astype(jnp.float32),
        lax.psum_scatter(
            local_w_key.astype(jnp.bfloat16), "dp", scatter_dimension=0, tiled=True
        ).astype(jnp.float32),
        lax.psum_scatter(
            local_w_value.astype(jnp.bfloat16), "dp", scatter_dimension=0, tiled=True
        ).astype(jnp.float32),
        lax.psum_scatter(
            local_w_gate.astype(jnp.bfloat16), "dp", scatter_dimension=0, tiled=True
        ).astype(jnp.float32),
        lax.psum_scatter(
            local_w_up.astype(jnp.bfloat16), "dp", scatter_dimension=0, tiled=True
        ).astype(jnp.float32),
    )
    summed_out, summed_down, summed_gq, summed_gk, summed_ga, summed_gm = (
        lax.psum_scatter(
            grad_w_output.astype(jnp.bfloat16), "dp", scatter_dimension=1, tiled=True
        ).astype(jnp.float32),
        lax.psum_scatter(
            grad_w_down.astype(jnp.bfloat16), "dp", scatter_dimension=1, tiled=True
        ).astype(jnp.float32),
        lax.psum_scatter(
            grad_gain_query.astype(jnp.bfloat16), "dp", scatter_dimension=1, tiled=True
        ).astype(jnp.float32),
        lax.psum_scatter(
            grad_gain_key.astype(jnp.bfloat16), "dp", scatter_dimension=1, tiled=True
        ).astype(jnp.float32),
        lax.psum_scatter(
            grad_gain_attn.reshape(gain_attn.shape).astype(jnp.bfloat16),
            "dp",
            scatter_dimension=1,
            tiled=True,
        ).astype(jnp.float32),
        lax.psum_scatter(
            grad_gain_mlp.reshape(gain_mlp.shape).astype(jnp.bfloat16),
            "dp",
            scatter_dimension=1,
            tiled=True,
        ).astype(jnp.float32),
    )
    return (
        output,
        grad_tokens,
        grad_w_query,
        grad_w_key,
        grad_w_value,
        summed_out,
        grad_w_gate,
        grad_w_up,
        summed_down,
        summed_gq,
        summed_gk,
        summed_ga,
        summed_gm,
    )


line = 4
pair = 2
low_score = -1e30
start_max = -1e20
big_vmem = 56 << 20


def line_shift(value, step):
    moves = [
        (z * pair + x, ((z + step) % line) * pair + x) for z in range(line) for x in range(pair)
    ]
    return lax.ppermute(value, "dp", moves)


def line_flip(value, bit):
    return lax.ppermute(
        value, "dp", [(z * pair + x, (z ^ bit) * pair + x) for z in range(line) for x in range(pair)]
    )


def x_swap(value):
    return lax.ppermute(value, "dp", [(i, i ^ 1) for i in range(line * pair)])


def core_swap(value):
    return lax.ppermute(value, "mp", [(i, i ^ 1) for i in range(4)])


def y_swap(value):
    return lax.ppermute(value, "mp", [(i, i ^ 2) for i in range(4)])


def flip_cores(value, axis):
    quarter = value.shape[axis] // 4
    cuts = [lax.slice_in_dim(value, i * quarter, (i + 1) * quarter, axis=axis) for i in (1, 0, 3, 2)]
    return jnp.concatenate(cuts, axis=axis)


def token_sum(value):
    value = value + flip_cores(core_swap(value), 1)
    return value + y_swap(value)


def own_part(value):
    quarter = value.shape[0] // 4
    return jnp.concatenate([value[:quarter], value[2 * quarter : 3 * quarter]], axis=0)


def other_part(value):
    quarter = value.shape[0] // 4
    return jnp.concatenate([value[quarter : 2 * quarter], value[3 * quarter :]], axis=0)


def join_parts(own, other):
    half = own.shape[0] // 2
    return jnp.concatenate([own[:half], other[:half], own[half:], other[half:]], axis=0)


def reduce_own_rows(partial_low):
    f32 = jnp.float32
    arrived = core_swap(other_part(partial_low))
    chip_sum = (own_part(partial_low).astype(f32) + arrived.astype(f32)).astype(jnp.bfloat16)
    return chip_sum.astype(f32) + y_swap(chip_sum).astype(f32)


def dot_t(first, second):
    return lax.dot_general(
        first, second, (((0,), (0,)), ((), ())), preferred_element_type=jnp.float32
    )


def dot_nt(first, second):
    return lax.dot_general(
        first, second, (((1,), (1,)), ((), ())), preferred_element_type=jnp.float32
    )


def vmem_specs(count):
    return [pl.BlockSpec(memory_space=pltpu.VMEM)] * count


def project_kernel(
    tokens,
    wq,
    wk,
    wv,
    gq,
    gk,
    cosines,
    sines,
    spots,
    out_queries,
    out_pairs,
    out_notes,
    out_q_raw,
    out_k_raw,
    rows_keep,
    query_keep,
    pair_keep,
    squares,
    squares_core,
    squares_y,
    send_sems,
    recv_sems,
    local_sems,
):
    f32 = jnp.float32
    bf16 = jnp.bfloat16
    width = cosines.shape[1]
    depth = wq.shape[0]
    rows = rows_keep.shape[0] // 2
    count = rows // 2
    mp = lax.axis_index("mp")
    spot = lax.axis_index("dp")
    core = lax.rem(mp, 2)
    x = lax.rem(spot, 2)
    z = spot // 2
    core_peer = {"mp": mp + 1 - 2 * core}
    y_peer = {"mp": lax.rem(mp + 2, 4)}
    x_peer = {"dp": spot + 1 - 2 * x}
    ahead = [{"dp": lax.rem(spot + 2 * d, 2 * line)} for d in range(line)]
    head = [lax.rem(z + d, line) for d in range(line)]
    both = lambda s: pl.ds(s * rows, rows)
    remote = []

    def send(source, target, peer):
        index = len(remote)
        copy = pltpu.make_async_remote_copy(
            src_ref=source,
            dst_ref=target,
            send_sem=send_sems.at[index],
            recv_sem=recv_sems.at[index],
            device_id=peer,
            device_id_type=pl.DeviceIdType.MESH,
        )
        remote.append(copy)
        copy.start()
        return copy

    loads = []
    for s in range(2):
        for part, place in ((0, core), (1, 1 - core)):
            start = pl.multiple_of(place * rows + s * count, count)
            copy = pltpu.make_async_copy(
                tokens.at[pl.ds(start, count)],
                rows_keep.at[pl.ds(s * rows + part * count, count)],
                local_sems.at[2 * s + part],
            )
            copy.start()
            loads.append(copy)

    barrier = pltpu.get_barrier_semaphore()
    peers = (core_peer, y_peer, x_peer, ahead[1], ahead[2], ahead[3])
    for peer in peers:
        pl.semaphore_signal(barrier, inc=1, device_id=peer, device_id_type=pl.DeviceIdType.MESH)
    pl.semaphore_wait(barrier, len(peers))

    def turned(raw, gain, s, h):
        part = raw[:, h * width : (h + 1) * width] * gain[:, h * width : (h + 1) * width]
        return (
            part * cosines[both(s), :] + pltpu.roll(part, width // 2, 1) * sines[both(s), :]
        ).astype(bf16)

    flying = {}
    for s in range(2):
        loads[2 * s].wait()
        loads[2 * s + 1].wait()
        k_raw = jnp.dot(rows_keep[both(s), :], wk[...], preferred_element_type=f32)
        out_k_raw[both(s), :] = k_raw
        squares[1:2, both(s)] = jnp.sum((k_raw * k_raw).T, axis=0, keepdims=True)
        v_raw = jnp.dot(rows_keep[both(s), :], wv[...], preferred_element_type=f32)
        for h in range(line):
            pair_keep[h, 0, both(s), :] = turned(k_raw, gk[...], s, h)
            pair_keep[h, 1, both(s), :] = v_raw[:, h * width : (h + 1) * width].astype(bf16)
        for d in (2, 1, 3):
            flying["pair", s, d] = send(
                pair_keep.at[head[d], :, both(s)], out_pairs.at[d, :, both(s)], ahead[d]
            )
        flying["far", s, 0] = send(
            pair_keep.at[z, :, both(s)], out_pairs.at[line, :, both(s)], x_peer
        )
        q_raw = jnp.dot(rows_keep[both(s), :], wq[...], preferred_element_type=f32)
        out_q_raw[both(s), :] = q_raw
        squares[0:1, both(s)] = jnp.sum((q_raw * q_raw).T, axis=0, keepdims=True)
        for h in range(line):
            query_keep[h, both(s), :] = turned(q_raw, gq[...], s, h)

    core_copy = send(squares, squares_core, core_peer)
    core_copy.wait()
    arrived = squares_core[...]
    cuts = [arrived[:, i * count : (i + 1) * count] for i in (1, 0, 3, 2)]
    chip = squares[...] + jnp.concatenate(cuts, axis=1)
    squares[...] = chip
    y_copy = send(squares, squares_y, y_peer)
    y_copy.wait()
    out_notes[0, 0:2, :] = lax.rsqrt((chip + squares_y[...]) / depth + epsilon)
    out_notes[0, 2:4, :] = spots[...]
    for d in range(1, line):
        flying["note", d] = send(out_notes.at[0], out_notes.at[d], ahead[d])
    flying["far_note", 0] = send(out_notes.at[0], out_notes.at[line], x_peer)
    for d in range(1, line):
        flying["query", d] = send(query_keep.at[head[d]], out_queries.at[d], ahead[d])
    out_queries[0] = query_keep[z]
    out_pairs[0] = pair_keep[z]
    for s in range(2):
        for d in (2, 1, 3):
            flying["pair", s, d].wait()
            flying["far", s, d] = send(
                out_pairs.at[d, :, both(s)], out_pairs.at[line + d, :, both(s)], x_peer
            )
    for d in range(1, line):
        flying["note", d].wait()
        flying["far_note", d] = send(out_notes.at[d], out_notes.at[line + d], x_peer)
    for d in range(1, line):
        flying["query", d].wait()
    for d in range(line):
        flying["far_note", d].wait()
        for s in range(2):
            flying["far", s, d].wait()


def project(tokens, wq, wk, wv, gq, gk, cosines, sines, spots):
    rows, depth = tokens.shape
    columns = wq.shape[1]
    width = columns // line
    f32 = jnp.float32
    bf16 = jnp.bfloat16
    return pl.pallas_call(
        project_kernel,
        in_specs=[pl.BlockSpec(memory_space=pl.ANY)] + vmem_specs(8),
        out_specs=vmem_specs(5),
        out_shape=[
            jax.ShapeDtypeStruct((line, rows, width), bf16),
            jax.ShapeDtypeStruct((2 * line, 2, rows, width), bf16),
            jax.ShapeDtypeStruct((2 * line, 4, rows), f32),
            jax.ShapeDtypeStruct((rows, columns), f32),
            jax.ShapeDtypeStruct((rows, columns), f32),
        ],
        scratch_shapes=[
            pltpu.VMEM((rows, depth), bf16),
            pltpu.VMEM((line, rows, width), bf16),
            pltpu.VMEM((line, 2, rows, width), bf16),
            pltpu.VMEM((2, rows), f32),
            pltpu.VMEM((2, rows), f32),
            pltpu.VMEM((2, rows), f32),
            pltpu.SemaphoreType.DMA((28,)),
            pltpu.SemaphoreType.DMA((28,)),
            pltpu.SemaphoreType.DMA((4,)),
        ],
        compiler_params=pltpu.CompilerParams(
            vmem_limit_bytes=48 << 20, collective_id=2, has_side_effects=True
        ),
        cost_estimate=pl.CostEstimate(flops=0, bytes_accessed=0, transcendentals=0),
    )(tokens, wq, wk, wv, gq, gk, cosines, sines, spots)


def visible_scores(key, query, key_code, query_code, query_low, factor):
    scores = dot_nt(key, query) * factor
    codes = jnp.concatenate([key_code] * (query.shape[0] // key_code.shape[1]), axis=1)
    return jnp.where((codes <= query_code) & (codes >= query_low), scores, low_score)


def attend_kernel(factor, key_rows, live, notes, *refs):
    queries, pairs = refs[:2]
    out_turned, out_log, out_query, out_key, out_codes, out_rows, out = refs[2:9]
    top, total, accum = refs[9:]
    f32 = jnp.float32
    bf16 = jnp.bfloat16
    count, width = queries.shape[1:]

    def column(row):
        return jnp.broadcast_to(row, (width, count)).T

    for k in range(2 * line):
        out_key[k] = (pairs[k, 0].astype(f32) * column(notes[k, 1:2, :])).astype(bf16)
        labels = column(notes[k, 2:3, :]).astype(jnp.int32)
        out_codes[k] = labels * key_rows + column(notes[k, 3:4, :]).astype(jnp.int32)
    for q in range(line):
        out_query[q] = (queries[q].astype(f32) * column(notes[q, 0:1, :])).astype(bf16)
        base = notes[q, 2:3, :].astype(jnp.int32) * key_rows
        out_rows[q : q + 1, :] = base + notes[q, 3:4, :].astype(jnp.int32)
        out_rows[line + q : line + q + 1, :] = base

    for q in range(line):
        top[...] = jnp.full_like(top, start_max)
        total[...] = jnp.zeros_like(total)
        accum[...] = jnp.zeros_like(accum)
        for k in range(2 * line):

            @pl.when(live[q, k] > 0)
            def _(q=q, k=k):
                scores = visible_scores(
                    out_key[k],
                    out_query[q],
                    out_codes[k],
                    out_rows[q : q + 1, :],
                    out_rows[line + q : line + q + 1, :],
                    factor,
                )
                highest = jnp.maximum(top[...], jnp.max(scores, axis=0, keepdims=True))
                weights = jnp.exp2(scores - highest)
                fade = jnp.exp2(top[...] - highest)
                total[...] = total[...] * fade + jnp.sum(weights, axis=0, keepdims=True)
                accum[...] = accum[...] * fade + dot_t(pairs[k, 1], weights.astype(bf16))
                top[...] = highest

        turned = accum[...] / total[...]
        out_turned[q] = turned
        out_log[q : q + 1, :] = top[...] + jnp.log2(total[...])
        out[q] = turned.T.astype(bf16)


def attend_back_kernel(factor, scale, live, codes, rows, queries, keys, *refs):
    pairs, turned, log_total, grads = refs[:4]
    out_query, out_near, out_far, key_sum, value_sum, query_sum = refs[4:]
    f32 = jnp.float32
    bf16 = jnp.bfloat16
    key_sum[...] = jnp.zeros_like(key_sum)
    value_sum[...] = jnp.zeros_like(value_sum)
    for q in range(line):
        query_sum[...] = jnp.zeros_like(query_sum)
        delta = jnp.sum(grads[q].astype(f32).T * turned[q], axis=0, keepdims=True)
        for k in range(2 * line):

            @pl.when(live[q, k] > 0)
            def _(q=q, k=k, delta=delta):
                query, key, grad = queries[q], keys[k], grads[q]
                scores = visible_scores(
                    key,
                    query,
                    codes[k],
                    rows[q : q + 1, :],
                    rows[line + q : line + q + 1, :],
                    factor,
                )
                probs = jnp.exp2(scores - log_total[q : q + 1, :])
                grad_probs = dot_nt(pairs[k, 1], grad)
                grad_scores = (probs * (grad_probs - delta)).astype(bf16)
                value_sum[k] += jnp.dot(
                    probs.astype(bf16), grad, preferred_element_type=f32
                )
                key_sum[k] += jnp.dot(grad_scores, query, preferred_element_type=f32)
                query_sum[...] += dot_t(key, grad_scores)

        out_query[q] = (query_sum[...] * scale).T.astype(bf16)
    for k in range(line):
        for out, base in ((out_near, 0), (out_far, line)):
            out[k, 0] = (key_sum[base + k] * scale).astype(bf16)
            out[k, 1] = value_sum[base + k].astype(bf16)


def attend(key_rows, live, notes, queries, pairs):
    _, count, width = queries.shape
    factor = math.log2(math.e) / math.sqrt(width)
    f32 = jnp.float32
    bf16 = jnp.bfloat16
    return pl.pallas_call(
        functools.partial(attend_kernel, factor, key_rows),
        out_shape=[
            jax.ShapeDtypeStruct((line, width, count), f32),
            jax.ShapeDtypeStruct((2 * line, count), f32),
            jax.ShapeDtypeStruct((line, count, width), bf16),
            jax.ShapeDtypeStruct((2 * line, count, width), bf16),
            jax.ShapeDtypeStruct((2 * line, count, width), jnp.int32),
            jax.ShapeDtypeStruct((2 * line, count), jnp.int32),
        ]
        + [jax.ShapeDtypeStruct((line, count, width), bf16)],
        in_specs=[pl.BlockSpec(memory_space=pltpu.SMEM)] + vmem_specs(3),
        out_specs=vmem_specs(7),
        scratch_shapes=[
            pltpu.VMEM((1, count), f32),
            pltpu.VMEM((1, count), f32),
            pltpu.VMEM((width, count), f32),
        ],
        compiler_params=pltpu.CompilerParams(vmem_limit_bytes=40 << 20),
        cost_estimate=pl.CostEstimate(flops=0, bytes_accessed=0, transcendentals=0),
    )(live, notes, queries, pairs)


def attend_back(live, codes, rows, queries, keys, pairs, turned, log_total, grads):
    _, count, width = queries.shape
    scale = 1.0 / math.sqrt(width)
    factor = math.log2(math.e) * scale
    f32 = jnp.float32
    return pl.pallas_call(
        functools.partial(attend_back_kernel, factor, scale),
        out_shape=[jax.ShapeDtypeStruct((line, count, width), jnp.bfloat16)]
        + [jax.ShapeDtypeStruct((line, 2, count, width), jnp.bfloat16)] * 2,
        in_specs=[pl.BlockSpec(memory_space=pltpu.SMEM)] + vmem_specs(8),
        out_specs=vmem_specs(3),
        scratch_shapes=[
            pltpu.VMEM((2 * line, count, width), f32),
            pltpu.VMEM((2 * line, count, width), f32),
            pltpu.VMEM((width, count), f32),
        ],
        compiler_params=pltpu.CompilerParams(vmem_limit_bytes=40 << 20),
        cost_estimate=pl.CostEstimate(
            flops=20 * line * line * count * count * width,
            bytes_accessed=12 << 20,
            transcendentals=2 * line * line * count * count,
        ),
    )(live, codes, rows, queries, keys, pairs, turned, log_total, grads)


def block_kernel(
    pieces,
    w_out,
    g_attn,
    g_mlp,
    tokens,
    cotangent,
    w_gate_in,
    w_up_in,
    w_down_in,
    out_heads,
    out_tokens_x,
    out_output,
    out_hidden,
    out_hidden_z,
    out_act,
    out_act_x,
    out_mlp,
    out_mlp_x,
    out_gate,
    out_gate_far,
    out_gate_z,
    out_up,
    out_up_far,
    out_attn,
    out_grads,
    out_grad_hidden,
    out_gain,
    w_gate,
    w_up,
    w_down,
    gate_keep,
    up_keep,
    act_keep,
    hidden_keep,
    mlp_keep,
    attn_keep,
    grad_gate,
    grad_up,
    own_factor,
    own_normed,
    own_tokens,
    own_cotangent,
    attended,
    heads_keep,
    total,
    part_send,
    part_recv,
    y_send,
    y_recv,
    send_sems,
    recv_sems,
    local_sems,
):
    f32 = jnp.float32
    bf16 = jnp.bfloat16
    depth = w_out.shape[1]
    units = w_gate.shape[1]
    tile = 512
    count = own_tokens.shape[0] // 2
    rows = 2 * count
    mp = lax.axis_index("mp")
    spot = lax.axis_index("dp")
    core = lax.rem(mp, 2)
    core_peer = {"mp": mp + 1 - 2 * core}
    y_peer = {"mp": lax.rem(mp + 2, 4)}
    z = spot // 2
    z_low = lax.rem(z, 2)
    z_peer = {"dp": spot + 2 - 4 * z_low}
    x = lax.rem(spot, 2)
    x_peer = {"dp": spot + 1 - 2 * x}
    width = pieces.shape[2]
    ahead = [{"dp": lax.rem(spot + 2 * d, 2 * line)} for d in range(line)]
    head = lambda d: pl.ds(pl.multiple_of(lax.rem(z + d, line) * width, width), width)

    remote, started, local = [], [], []

    def send(source, target, peer):
        index = len(remote)
        copy = pltpu.make_async_remote_copy(
            src_ref=source,
            dst_ref=target,
            send_sem=send_sems.at[index],
            recv_sem=recv_sems.at[index],
            device_id=peer,
            device_id_type=pl.DeviceIdType.MESH,
        )
        remote.append(copy)
        copy.start()
        return copy

    def keep_out(source, target, waited=False):
        copy = pltpu.make_async_copy(source, target, local_sems.at[len(started)])
        started.append(copy)
        if not waited:
            local.append(copy)
        copy.start()
        return copy

    own = lambda s: pl.ds(s * rows, count)
    other = lambda s: pl.ds(s * rows + count, count)
    both = lambda s: pl.ds(s * rows, rows)
    mine = lambda s: pl.ds(s * count, count)
    at_home = lambda s: pl.ds(pl.multiple_of(core * rows + s * count, count), count)
    cut = lambda t: pl.ds(pl.multiple_of(t * tile, tile), tile)
    flying = {}

    home_rows = pl.ds(pl.multiple_of(core * rows, rows), rows)
    loads = [
        keep_out(tokens.at[home_rows], own_tokens, True),
        keep_out(cotangent.at[home_rows], own_cotangent, True),
        keep_out(w_gate_in, w_gate, True),
        keep_out(w_up_in, w_up, True),
        keep_out(w_down_in, w_down, True),
    ]
    barrier = pltpu.get_barrier_semaphore()
    peers = (core_peer, y_peer, x_peer, ahead[1], ahead[2], ahead[3])
    for peer in peers:
        pl.semaphore_signal(barrier, inc=1, device_id=peer, device_id_type=pl.DeviceIdType.MESH)
    pl.semaphore_wait(barrier, len(peers))
    for s in range(2):
        for d in range(1, line):
            flying["heads", s, d] = send(
                pieces.at[d, both(s)], attended.at[both(s), head(0)], ahead[line - d]
            )
    attended[:, head(0)] = pieces[0]

    loads[0].wait()
    for s in range(2):
        flying["tokens", s] = send(own_tokens.at[mine(s)], out_tokens_x.at[own(s)], x_peer)

    def forward_core(name, s, array):
        flying[name, s].wait()
        flying[name + "_core", s] = send(array.at[own(s)], array.at[other(s)], core_peer)

    def reduce_start(stage, s):
        part_send[s] = total[count:, :].astype(bf16)
        copy = send(part_send.at[s], part_recv.at[s], core_peer)
        copy.wait()
        y_send[s] = (total[:count, :] + part_recv[s].astype(f32)).astype(bf16)
        flying[stage, s] = send(y_send.at[s], y_recv.at[stage, s], y_peer)

    def reduced(stage, s):
        flying[stage, s].wait()
        return y_send[s].astype(f32) + y_recv[stage, s].astype(f32)

    def factor_of(value):
        return lax.rsqrt(jnp.mean(value * value, axis=1, keepdims=True) + epsilon)

    def share(keep, s):
        flying["share", s] = send(keep.at[own(s)], keep.at[other(s)], core_peer)

    def project_out(s):
        for d in range(1, line):
            flying["heads", s, d].wait()
        keep_out(attended.at[both(s)], out_heads.at[both(s)])
        total[...] = jnp.dot(attended[both(s), :], w_out[...], preferred_element_type=f32)
        reduce_start(0, s)

    def after_attention(s):
        value = reduced(0, s)
        factor = factor_of(value)
        normed = value * factor
        own_factor[mine(s), :] = jnp.broadcast_to(factor, (count, own_factor.shape[1]))
        own_normed[mine(s), :] = normed
        hidden = own_tokens[mine(s), :].astype(f32) + normed * g_attn[...]
        out_grad_hidden[mine(s), :] = hidden
        hidden_keep[own(s), :] = hidden.astype(bf16)
        share(hidden_keep, s)

    def forward(s):
        flying["hidden", s] = send(hidden_keep.at[own(s)], out_hidden_z.at[own(s)], z_peer)
        flying["share", s].wait()
        keep_out(hidden_keep.at[both(s)], out_hidden.at[both(s)])

        def step(t):
            hidden = hidden_keep[both(s), :]
            gate = jnp.dot(hidden, w_gate[:, cut(t)], preferred_element_type=f32)
            up = jnp.dot(hidden, w_up[:, cut(t)], preferred_element_type=f32)
            gate_keep[both(s), cut(t)] = gate.astype(bf16)
            up_keep[both(s), cut(t)] = up.astype(bf16)
            act = (gate * jax.nn.sigmoid(gate) * up).astype(bf16)
            act_keep[both(s), cut(t)] = act
            return jnp.dot(act, w_down[cut(t), :], preferred_element_type=f32)

        total[...] = step(0)

        @pl.loop(1, units // tile)
        def _(t):
            total[...] += step(t)

        reduce_start(1, s)
        keep_out(act_keep.at[both(s)], out_act.at[both(s)])
        half = units // 2
        far = pl.ds(pl.multiple_of((1 - x) * half, half), half)
        flying["act", s] = send(act_keep.at[both(s), far], out_act_x.at[both(s)], x_peer)

    def turn_point(s):
        value = reduced(1, s)
        factor = factor_of(value)
        normed = value * factor
        forward_core("tokens", s, out_tokens_x)
        own_tokens[mine(s), :] = (out_grad_hidden[mine(s), :] + normed * g_mlp[...]).astype(bf16)
        keep_out(own_tokens.at[mine(s)], out_output.at[at_home(s)])
        flying["output", s] = send(own_tokens.at[mine(s)], out_output.at[at_home(s)], core_peer)
        grad = own_cotangent[mine(s), :].astype(f32)
        gain = jnp.sum(grad * normed, axis=0, keepdims=True)
        out_gain[1:2, :] = gain if s == 0 else out_gain[1:2, :] + gain
        mlp_keep[own(s), :] = norm_back(grad * g_mlp[...], normed, factor).astype(bf16)
        share(mlp_keep, s)

    def backward(s):
        flying["mlp", s] = send(mlp_keep.at[own(s)], out_mlp_x.at[own(s)], x_peer)
        flying["share", s].wait()
        keep_out(mlp_keep.at[both(s)], out_mlp.at[both(s)])

        def step(t):
            grad_act = dot_nt(mlp_keep[both(s), :], w_down[cut(t), :])
            gate = gate_keep[both(s), cut(t)].astype(f32)
            up = up_keep[both(s), cut(t)].astype(f32)
            sigmoid = jax.nn.sigmoid(gate)
            to_gate = (grad_act * up * (sigmoid * (1.0 + gate * (1.0 - sigmoid)))).astype(bf16)
            to_up = (grad_act * (gate * sigmoid)).astype(bf16)
            grad_gate[:, cut(t)] = to_gate
            grad_up[:, cut(t)] = to_up
            return dot_nt(to_gate, w_gate[:, cut(t)]) + dot_nt(to_up, w_up[:, cut(t)])

        if s > 0:
            gate_to_z(0)
        total[...] = step(0)

        @pl.loop(1, units // tile)
        def _(t):
            total[...] += step(t)

        reduce_start(2, s)
        half = units // 2
        far = pl.ds(pl.multiple_of((1 - z_low) * half, half), half)
        flying["grads"] = [
            keep_out(source, target.at[both(s)], waited=True)
            for source, target in (
                (grad_gate, out_gate),
                (grad_gate.at[:, far], out_gate_far),
                (grad_up, out_up),
                (grad_up.at[:, far], out_up_far),
            )
        ]

    def gate_to_z(s):
        for copy in flying["grads"]:
            copy.wait()
        flying["gate_z", s] = send(out_gate_far.at[both(s)], out_gate_z.at[both(s)], z_peer)

    def to_attention(s):
        value = reduced(2, s)
        grad = own_cotangent[mine(s), :].astype(f32) + value
        out_grad_hidden[mine(s), :] = grad
        normed = own_normed[mine(s), :]
        gain = jnp.sum(grad * normed, axis=0, keepdims=True)
        out_gain[0:1, :] = gain if s == 0 else out_gain[0:1, :] + gain
        factor = own_factor[mine(s), 0:1]
        attn_keep[own(s), :] = norm_back(grad * g_attn[...], normed, factor).astype(bf16)
        share(attn_keep, s)

    def attended_grad(s):
        flying["share", s].wait()
        keep_out(attn_keep.at[both(s)], out_attn.at[both(s)])
        heads_keep[both(s), :] = dot_nt(attn_keep[both(s), :], w_out[...]).astype(bf16)
        for d in range(1, line):
            flying["grads", s, d] = send(
                heads_keep.at[both(s), head(d)], out_grads.at[d, both(s)], ahead[d]
            )
        keep_out(heads_keep.at[both(s), head(0)], out_grads.at[0, both(s)])

    project_out(0)
    project_out(1)
    for load in loads[1:]:
        load.wait()
    after_attention(0)
    forward(0)
    after_attention(1)
    forward(1)
    turn_point(0)
    backward(0)
    turn_point(1)
    backward(1)
    gate_to_z(1)
    for s in range(2):
        forward_core("hidden", s, out_hidden_z)
    to_attention(0)
    attended_grad(0)
    to_attention(1)
    attended_grad(1)
    for s in range(2):
        flying["act", s].wait()
        flying["output", s].wait()
        forward_core("mlp", s, out_mlp_x)
    for s in range(2):
        flying["tokens_core", s].wait()
        flying["gate_z", s].wait()
        flying["hidden_core", s].wait()
        flying["mlp_core", s].wait()
        for d in range(1, line):
            flying["grads", s, d].wait()
    for copy in local:
        copy.wait()


def block(pieces, w_out, g_attn, g_mlp, tokens, cotangent, w_gate, w_up, w_down):
    _, rows, width = pieces.shape
    columns = line * width
    depth, units = w_gate.shape
    half = rows // 2
    quarter = rows // 4
    f32 = jnp.float32
    bf16 = jnp.bfloat16
    wide = jax.ShapeDtypeStruct((rows, depth), bf16)
    tall = jax.ShapeDtypeStruct((rows, units), bf16)
    any_spec = pl.BlockSpec(memory_space=pl.ANY)
    return pl.pallas_call(
        block_kernel,
        out_shape=[
            jax.ShapeDtypeStruct((rows, columns), bf16),
            wide,
            wide,
            wide,
            wide,
            tall,
            jax.ShapeDtypeStruct((rows, units // 2), bf16),
            wide,
            wide,
            tall,
            jax.ShapeDtypeStruct((rows, units // 2), bf16),
            jax.ShapeDtypeStruct((rows, units // 2), bf16),
            tall,
            jax.ShapeDtypeStruct((rows, units // 2), bf16),
            wide,
            jax.ShapeDtypeStruct((line, rows, width), bf16),
            jax.ShapeDtypeStruct((half, depth), f32),
            jax.ShapeDtypeStruct((2, depth), f32),
        ],
        in_specs=vmem_specs(4) + [any_spec] * 5,
        out_specs=[any_spec] * 16 + vmem_specs(2),
        scratch_shapes=[
            pltpu.VMEM((depth, units), bf16),
            pltpu.VMEM((depth, units), bf16),
            pltpu.VMEM((units, depth), bf16),
            pltpu.VMEM((rows, units), bf16),
            pltpu.VMEM((rows, units), bf16),
            pltpu.VMEM((rows, units), bf16),
            pltpu.VMEM((rows, depth), bf16),
            pltpu.VMEM((rows, depth), bf16),
            pltpu.VMEM((rows, depth), bf16),
            pltpu.VMEM((half, units), bf16),
            pltpu.VMEM((half, units), bf16),
            pltpu.VMEM((half, 128), f32),
            pltpu.VMEM((half, depth), f32),
            pltpu.VMEM((half, depth), bf16),
            pltpu.VMEM((half, depth), bf16),
            pltpu.VMEM((rows, columns), bf16),
            pltpu.VMEM((rows, columns), bf16),
            pltpu.VMEM((half, depth), f32),
            pltpu.VMEM((2, quarter, depth), bf16),
            pltpu.VMEM((2, quarter, depth), bf16),
            pltpu.VMEM((2, quarter, depth), bf16),
            pltpu.VMEM((3, 2, quarter, depth), bf16),
            pltpu.SemaphoreType.DMA((56,)),
            pltpu.SemaphoreType.DMA((56,)),
            pltpu.SemaphoreType.DMA((32,)),
        ],
        compiler_params=pltpu.CompilerParams(
            vmem_limit_bytes=61800 << 10, collective_id=1, has_side_effects=True
        ),
        cost_estimate=pl.CostEstimate(flops=0, bytes_accessed=0, transcendentals=0),
    )(pieces, w_out, g_attn, g_mlp, tokens, cotangent, w_gate, w_up, w_down)


class Courier:
    def __init__(self, send_sems, recv_sems, local_sems):
        self.send_sems, self.recv_sems, self.local_sems = send_sems, recv_sems, local_sems
        self.remote, self.local = 0, 0

    def send(self, source, target, peer):
        copy = pltpu.make_async_remote_copy(
            src_ref=source,
            dst_ref=target,
            send_sem=self.send_sems.at[self.remote],
            recv_sem=self.recv_sems.at[self.remote],
            device_id=peer,
            device_id_type=pl.DeviceIdType.MESH,
        )
        self.remote += 1
        copy.start()
        return copy

    def move(self, source, target):
        copy = pltpu.make_async_copy(source, target, self.local_sems.at[self.local])
        self.local += 1
        copy.start()
        return copy


def greet(peers):
    barrier = pltpu.get_barrier_semaphore()
    for peer in peers:
        pl.semaphore_signal(barrier, inc=1, device_id=peer, device_id_type=pl.DeviceIdType.MESH)
    pl.semaphore_wait(barrier, len(peers))


class Spot:
    def __init__(self):
        mp = lax.axis_index("mp")
        spot = lax.axis_index("dp")
        self.core = lax.rem(mp, 2)
        self.x = lax.rem(spot, 2)
        self.z = spot // 2
        self.z_low = lax.rem(self.z, 2)
        self.z_high = self.z // 2
        self.core_peer = {"mp": mp + 1 - 2 * self.core}
        self.y_peer = {"mp": lax.rem(mp + 2, 4)}
        self.x_peer = {"dp": spot + 1 - 2 * self.x}
        self.z_peer = {"dp": spot + 2 - 4 * self.z_low}
        self.far_peer = {"dp": lax.rem(spot + 4, 8)}
        self.ahead = [{"dp": lax.rem(spot + 2 * d, 2 * line)} for d in range(line)]
        self.all = (self.core_peer, self.y_peer, self.x_peer) + tuple(self.ahead[1:])


class Job:
    def __init__(self, spot, over_x, first, first_far, second, second_far, cut_first):
        self.operands, self.cut_first = (first, first_far, second, second_far), cut_first
        self.tile = (first if cut_first else second).shape[1] // (line * pair)
        self.spot, self.over_x = spot, over_x
        self.side = spot.x if over_x else spot.z_low
        self.partner = spot.x_peer if over_x else spot.z_peer
        self.first_peer = spot.z_peer if over_x else spot.x_peer

    def at(self, ref, index):
        block = pl.ds(pl.multiple_of(index * self.tile, self.tile), self.tile)
        return ref.at[block, :] if self.cut_first else ref.at[:, block]

    def span(self, ref, index):
        block = pl.ds(pl.multiple_of(index * 2 * self.tile, 2 * self.tile), 2 * self.tile)
        return ref.at[block, :] if self.cut_first else ref.at[:, block]

    def term(self, index):
        first, first_far, second, second_far = self.operands
        block = pl.ds(pl.multiple_of(index * self.tile, self.tile), self.tile)
        if self.cut_first:
            return dot_t(first[:, block], second[...]) + dot_t(first_far[:, block], second_far[...])
        return dot_t(first[...], second[:, block]) + dot_t(first_far[...], second_far[:, block])

    def block_of(self, high, index):
        if self.over_x:
            return (2 * high + self.spot.z_low) * pair + index
        return (2 * high + index) * pair + self.spot.x

    def send_terms(self, target):
        @pl.loop(0, line)
        def _(i):
            if self.over_x:
                index = (i // 2) * 4 + (1 - self.spot.z_low) * 2 + lax.rem(i, 2)
            else:
                index = i * pair + 1 - self.spot.x
            self.at(target, i)[...] = self.term(index).astype(jnp.bfloat16)

    def second_term(self, arrived, target, i):
        total = self.term(self.block_of(1 - self.spot.z_high, i))
        total = total + self.at(arrived, i)[...].astype(jnp.float32)
        self.at(target, i)[...] = total.astype(jnp.bfloat16)

    def second_terms(self, arrived, target):
        @pl.loop(0, 2)
        def _(i):
            self.second_term(arrived, target, i)

    def own_term(self, side, arrived):
        total = self.term(self.block_of(self.spot.z_high, side))
        return total + self.at(arrived, side)[...].astype(jnp.float32)


def middle_kernel(
    grad_queries_in,
    near_in,
    far,
    q_raw,
    k_raw,
    factors,
    cosines,
    sines,
    gq,
    gk,
    act,
    act_x,
    mlp,
    mlp_x,
    hidden,
    hidden_z,
    gate,
    gate_z,
    up,
    up_z,
    out_own_down,
    out_r2_down,
    out_r1_gate,
    out_r1_up,
    out_r2_gate,
    out_raw_x,
    r1_down,
    out_raw,
    out_raw_own,
    out_gain,
    act_v,
    act_zv,
    mlp_v,
    mlp_zv,
    hidden_v,
    hidden_zv,
    gate_v,
    gate_zv,
    up_v,
    up_zv,
    send_down,
    send_gate,
    send_up,
    r1_v,
    r1_own,
    s2_v,
    own_v,
    r1_gate_v,
    s2_gate,
    grad_queries,
    near,
    far_in,
    sums,
    query_home,
    pair_home,
    scaled,
    raw_far,
    inner,
    inner_core,
    inner_y,
    send_sems,
    recv_sems,
    local_sems,
):
    f32 = jnp.float32
    bf16 = jnp.bfloat16
    spot = Spot()
    mail = Courier(send_sems, recv_sems, local_sems)
    count, width = cosines.shape
    columns = line * width
    depth = mlp_v.shape[1]
    half = act_v.shape[1]
    own_half = pl.ds(pl.multiple_of(spot.z_low * half, half), half)
    x_half = pl.ds(pl.multiple_of(spot.x * half, half), half)
    loads = [
        mail.move(act.at[:, x_half], act_v),
        mail.move(act_x, act_zv),
        mail.move(mlp, mlp_v),
        mail.move(mlp_x, mlp_zv),
        mail.move(hidden, hidden_v),
        mail.move(hidden_z, hidden_zv),
        mail.move(gate.at[:, own_half], gate_v),
        mail.move(gate_z, gate_zv),
        mail.move(up.at[:, own_half], up_v),
        mail.move(up_z, up_zv),
    ]
    small_loads = [mail.move(grad_queries_in, grad_queries), mail.move(near_in, near)]
    greet(spot.all)
    far_copy = mail.send(far, far_in, spot.x_peer)
    my_head = pl.ds(pl.multiple_of(spot.z * width, width), width)
    for load in small_loads:
        load.wait()
    query_copies = [
        mail.send(grad_queries.at[d], query_home.at[:, my_head], spot.ahead[line - d])
        for d in range(1, line)
    ]
    query_home[:, my_head] = grad_queries[0]
    for load in loads[:4]:
        load.wait()
    down = Job(spot, True, act_v, act_zv, mlp_v, mlp_zv, False)
    down.send_terms(send_down)
    down_copy = mail.send(send_down, r1_down, down.first_peer)
    for load in loads[4:]:
        load.wait()
    gates = Job(spot, False, hidden_v, hidden_zv, gate_v, gate_zv, True)
    gates.send_terms(send_gate)
    far_copy.wait()
    gate_terms = mail.send(send_gate, out_r1_gate, gates.first_peer)
    sums[...] = (near[...].astype(f32) + far_in[...].astype(f32)).astype(bf16)
    pair_copies = [
        mail.send(sums.at[d], pair_home.at[:, :, my_head], spot.ahead[line - d])
        for d in range(1, line)
    ]
    pair_home[:, :, my_head] = sums[0]
    ups = Job(spot, False, hidden_v, hidden_zv, up_v, up_zv, True)
    ups.send_terms(send_up)
    up_terms = mail.send(send_up, out_r1_up, ups.first_peer)

    down_copy.wait()
    loads = [
        mail.move(down.span(r1_down, 1 - spot.z_high), r1_v),
        mail.move(down.span(r1_down, spot.z_high), r1_own),
    ]
    loads[0].wait()
    down.second_terms(r1_v, s2_v)
    second_copy = mail.send(s2_v, out_r2_down, spot.far_peer)
    gate_terms.wait()
    gate_load = mail.move(gates.span(out_r1_gate, 1 - spot.z_high), r1_gate_v)
    gate_load.wait()
    gates.second_term(r1_gate_v, s2_gate, 0)
    gate_second = mail.send(gates.at(s2_gate, 0), out_r2_gate, spot.far_peer)
    for copy in query_copies + pair_copies:
        copy.wait()

    def column(row):
        return jnp.broadcast_to(row, (width, count)).T

    sources = ((query_home, None, q_raw, gq), (pair_home, 0, k_raw, gk))
    factor_columns = [column(factors[which : which + 1, :]) for which in range(2)]
    for which, (home, slot, raw, gain) in enumerate(sources):
        inner_sum = jnp.zeros((count, width), f32)
        for h in range(line):
            cut = slice(h * width, (h + 1) * width)
            part = (home[:, cut] if slot is None else home[slot, :, cut]).astype(f32)
            back = part * cosines[...] - pltpu.roll(part, width // 2, 1) * sines[...]
            normed = raw[:, cut] * factor_columns[which]
            out_gain[which : which + 1, cut] = jnp.sum(back * normed, axis=0, keepdims=True)
            value = back * gain[:, cut]
            scaled[which, :, cut] = value
            inner_sum = inner_sum + value * normed
        inner[which : which + 1, :] = jnp.sum(inner_sum.T, axis=0, keepdims=True)
    core_copy = mail.send(inner, inner_core, spot.core_peer)
    core_copy.wait()
    arrived = inner_core[...]
    quarter = count // 4
    cuts = [arrived[:, i * quarter : (i + 1) * quarter] for i in (1, 0, 3, 2)]
    chip = inner[...] + jnp.concatenate(cuts, axis=1)
    inner[...] = chip
    y_copy = mail.send(inner, inner_y, spot.y_peer)
    y_copy.wait()
    inner_all = (chip + inner_y[...]) / depth
    for which, (home, slot, raw, gain) in enumerate(sources):
        inner_column = column(inner_all[which : which + 1, :])
        for h in range(line):
            cut = slice(h * width, (h + 1) * width)
            normed = raw[:, cut] * factor_columns[which]
            value = factor_columns[which] * (scaled[which, :, cut] - normed * inner_column)
            base = which * columns + h * width
            out_raw[:, base : base + width] = value.astype(bf16)
    out_raw[:, 2 * columns :] = pair_home[1]
    part_width = columns // 2
    for which in range(3):
        cut = slice(which * part_width, (which + 1) * part_width)
        base = which * columns

        def side(index):
            start = pl.multiple_of(base + index * part_width, part_width)
            return out_raw[:, pl.ds(start, part_width)]

        out_raw_own[:, cut] = side(spot.x)
        raw_far[:, cut] = side(1 - spot.x)
    raw_copy = mail.send(raw_far, out_raw_x, spot.x_peer)

    loads[1].wait()

    @pl.loop(0, 2)
    def _(i):
        down.at(own_v, i)[...] = down.own_term(i, r1_own)

    keep_own = mail.move(own_v, out_own_down)
    for copy in (gate_second, up_terms, raw_copy, second_copy, keep_own):
        copy.wait()


def middle(small, large):
    f32 = jnp.float32
    bf16 = jnp.bfloat16
    grad_queries, near, far, q_raw = small[:4]
    act, act_x, grad_mlp = large[:3]
    _, count, width = grad_queries.shape
    columns = line * width
    depth = grad_mlp.shape[1]
    units = act.shape[1]
    half = units // 2
    cut = depth // 2
    any_spec = pl.BlockSpec(memory_space=pl.ANY)
    shape = jax.ShapeDtypeStruct
    return pl.pallas_call(
        middle_kernel,
        in_specs=[pl.BlockSpec(memory_space=pltpu.HBM)] * 3 + vmem_specs(7) + [any_spec] * 10,
        out_specs=[any_spec] * 7 + vmem_specs(3),
        out_shape=[
            shape((half, cut // 2), f32),
            shape((half, cut // 2), bf16),
            shape((cut, half), bf16),
            shape((cut, half), bf16),
            shape((cut // 4, half), bf16),
            shape((count, 3 * columns // 2), bf16),
            shape((half, cut), bf16),
            shape((count, 3 * columns), bf16),
            shape((count, 3 * columns // 2), bf16),
            shape((2, columns), f32),
        ],
        scratch_shapes=[
            pltpu.VMEM((count, half), bf16),
            pltpu.VMEM((count, half), bf16),
            pltpu.VMEM((count, depth), bf16),
            pltpu.VMEM((count, depth), bf16),
            pltpu.VMEM((count, depth), bf16),
            pltpu.VMEM((count, depth), bf16),
            pltpu.VMEM((count, half), bf16),
            pltpu.VMEM((count, half), bf16),
            pltpu.VMEM((count, half), bf16),
            pltpu.VMEM((count, half), bf16),
            pltpu.VMEM((half, cut), bf16),
            pltpu.VMEM((cut, half), bf16),
            pltpu.VMEM((cut, half), bf16),
            pltpu.VMEM((half, cut // 2), bf16),
            pltpu.VMEM((half, cut // 2), bf16),
            pltpu.VMEM((half, cut // 2), bf16),
            pltpu.VMEM((half, cut // 2), f32),
            pltpu.VMEM((cut // 2, half), bf16),
            pltpu.VMEM((cut // 2, half), bf16),
            pltpu.VMEM(grad_queries.shape, bf16),
            pltpu.VMEM(near.shape, bf16),
            pltpu.VMEM(near.shape, bf16),
            pltpu.VMEM(near.shape, bf16),
            pltpu.VMEM((count, columns), bf16),
            pltpu.VMEM((2, count, columns), bf16),
            pltpu.VMEM((2, count, columns), f32),
            pltpu.VMEM((count, 3 * columns // 2), bf16),
            pltpu.VMEM((2, count), f32),
            pltpu.VMEM((2, count), f32),
            pltpu.VMEM((2, count), f32),
            pltpu.SemaphoreType.DMA((16,)),
            pltpu.SemaphoreType.DMA((16,)),
            pltpu.SemaphoreType.DMA((16,)),
        ],
        compiler_params=pltpu.CompilerParams(
            vmem_limit_bytes=60 << 20, collective_id=3, has_side_effects=True
        ),
    )(*small, *large)


def last_kernel(
    raw,
    raw_own,
    raw_x,
    wide,
    narrow,
    attended,
    hidden,
    hidden_z,
    gate,
    gate_z,
    up,
    up_z,
    attn,
    tokens,
    tokens_x,
    own_down,
    r2_down,
    r1_gate,
    r1_up,
    r2_gate_in,
    w_query,
    w_key,
    w_value,
    grad_hidden,
    *refs,
):
    outs, refs = refs[:13], refs[13:]
    near_down, near_gate, near_up, near_raw, near_out = outs[:5]
    far_down, far_gate, far_up, far_raw, far_out = outs[5:10]
    out_tokens, r1_raw, r1_out = outs[10:]
    out_wide, out_narrow = refs[:2]
    (
        hidden_v,
        hidden_zv,
        gate_v,
        gate_zv,
        up_v,
        up_zv,
        tokens_v,
        tokens_xv,
        attn_v,
        attn_xv,
        heads_v,
        heads_far,
        heads_xv,
        send_raw,
        send_out,
        r1_wide,
        r1_raw_v,
        r1_out_v,
        s2_gate,
        s2_up,
        s2_raw,
        s2_out,
        r2_gate,
        r2_up,
        r2_raw,
        r2_out,
        own_down_v,
        r2_down_v,
        fin_down,
        fin_gate,
        fin_up,
        fin_raw,
        fin_out,
        keep_down,
        keep_gate,
        keep_up,
        keep_raw,
        keep_out,
        weight_v,
        total,
        part_send,
        part_recv,
        y_send,
        y_recv,
        hidden_own,
        token_keep,
        wide_core,
        wide_x,
        narrow_x,
        wide_z,
        narrow_z,
        send_sems,
        recv_sems,
        local_sems,
    ) = refs[2:]
    f32 = jnp.float32
    bf16 = jnp.bfloat16
    spot = Spot()
    mail = Courier(send_sems, recv_sems, local_sems)
    rows_all = tokens_v.shape[0]
    rows = rows_all // 2
    count = rows // 2
    half = gate_v.shape[1]
    own_half = pl.ds(pl.multiple_of(spot.z_low * half, half), half)
    heads_half = heads_v.shape[1]
    side_heads = lambda side: pl.ds(pl.multiple_of(side * heads_half, heads_half), heads_half)
    own = lambda s: pl.ds(s * rows, count)
    other = lambda s: pl.ds(s * rows + count, count)
    both = lambda s: pl.ds(s * rows, rows)
    mine = lambda s: pl.ds(s * count, count)

    token_loads = [mail.move(tokens_x, tokens_xv)]
    for s in range(2):
        for part, place in ((0, spot.core), (1, 1 - spot.core)):
            start = pl.multiple_of(place * rows + s * count, count)
            target = tokens_v.at[pl.ds(s * rows + part * count, count)]
            token_loads.append(mail.move(tokens.at[pl.ds(start, count)], target))
    attn_load = mail.move(attn, attn_v)
    r1_loads = []
    first_loads = [mail.move(hidden, hidden_v), mail.move(hidden_z, hidden_zv)]
    gate_loads = [mail.move(gate.at[:, own_half], gate_v), mail.move(gate_z, gate_zv)]
    up_loads = [mail.move(up.at[:, own_half], up_v), mail.move(up_z, up_zv)]
    ups = Job(spot, False, hidden_v, hidden_zv, up_v, up_zv, True)
    gates = Job(spot, False, hidden_v, hidden_zv, gate_v, gate_zv, True)
    raws = Job(spot, True, tokens_v, tokens_xv, raw_own, raw_x, True)
    outs_job = Job(spot, True, heads_v, heads_xv, attn_v, attn_xv, False)
    gate_arrived = mail.move(r2_gate_in, gates.at(r2_gate, 0))
    gate_second = mail.move(gates.span(r1_gate, 1 - spot.z_high), r1_wide.at[0])
    gate_own = mail.move(gates.span(r1_gate, spot.z_high), r1_wide.at[1])
    up_second = mail.move(ups.span(r1_up, 1 - spot.z_high), r1_wide.at[2])
    up_own = mail.move(ups.span(r1_up, spot.z_high), r1_wide.at[3])
    greet(spot.all)
    wide_copy = mail.send(wide, wide_core, spot.core_peer)
    attn_load.wait()
    attn_copies = [
        mail.send(attn_v.at[own(s)], attn_xv.at[own(s)], spot.x_peer) for s in range(2)
    ]
    heads_far[...] = attended[:, side_heads(1 - spot.x)]
    heads_v[...] = attended[:, side_heads(spot.x)]
    heads_copy = mail.send(heads_far, heads_xv, spot.x_peer)
    for load in token_loads:
        load.wait()
    raws.send_terms(send_raw)
    raw_copy = mail.send(send_raw, r1_raw, raws.first_peer)
    wide_copy.wait()
    out_wide[...] = wide[...] + wide_core[...]
    out_narrow[...] = narrow[...]
    wide_x_copy = mail.send(out_wide, wide_x, spot.x_peer)
    narrow_x_copy = mail.send(out_narrow, narrow_x, spot.x_peer)

    for load in (*first_loads, *gate_loads, gate_second):
        load.wait()
    gates.second_term(r1_wide.at[0], s2_gate, 1)
    gate_copy = mail.send(gates.at(s2_gate, 1), gates.at(r2_gate, 1), spot.far_peer)
    for load in (*up_loads, up_second):
        load.wait()
    ups.second_terms(r1_wide.at[2], s2_up)
    second_up = mail.send(s2_up, r2_up, spot.far_peer)

    input_weights = (w_query, w_key, w_value)
    columns = w_query.shape[1]
    flying = {}
    for which, source in enumerate(input_weights):
        load = mail.move(source, weight_v)
        load.wait()
        for s in range(2):
            term = dot_nt(raw[both(s), which * columns : (which + 1) * columns], weight_v[...])
            total[both(s), :] = term if which == 0 else total[both(s), :] + term
    for s in range(2):
        part_send[s] = total[other(s), :].astype(bf16)
        flying["core", s] = mail.send(part_send.at[s], part_recv.at[s], spot.core_peer)
    hidden_load = mail.move(grad_hidden, hidden_own)
    for s in range(2):
        flying["core", s].wait()
        y_send[s] = (total[own(s), :] + part_recv[s].astype(f32)).astype(bf16)
        flying["y", s] = mail.send(y_send.at[s], y_recv.at[s], spot.y_peer)

    near_copies, far_copies = [], []

    def finish(job, value_of, fin, far, keep, target):
        fin[...] = value_of(1 - job.side).astype(bf16)
        far_copies.append(mail.send(fin, far, job.partner))
        keep[...] = value_of(job.side)
        near_copies.append(mail.move(keep, target))

    down_loads = [mail.move(own_down, own_down_v), mail.move(r2_down, r2_down_v)]
    for load in down_loads:
        load.wait()
    down = outs_job
    finish(
        down,
        lambda side: down.at(own_down_v, side)[...] + down.at(r2_down_v, side)[...].astype(f32),
        fin_down,
        far_down,
        keep_down,
        near_down,
    )

    wide_x_copy.wait()
    narrow_x_copy.wait()
    out_wide[...] = out_wide[...] + wide_x[...]
    out_narrow[...] = out_narrow[...] + narrow_x[...]
    for s in range(2):
        attn_copies[s].wait()
    attn_core = [
        mail.send(attn_xv.at[own(s)], attn_xv.at[other(s)], spot.core_peer) for s in range(2)
    ]
    for copy in attn_core:
        copy.wait()
    heads_copy.wait()
    outs_job.send_terms(send_out)
    out_copy = mail.send(send_out, r1_out, outs_job.first_peer)

    def final_of(job, r1_own, r2):
        return lambda side: job.own_term(side, r1_own) + job.at(r2, side)[...].astype(f32)

    for load in (gate_own, gate_arrived):
        load.wait()
    gate_copy.wait()
    finish(gates, final_of(gates, r1_wide.at[1], r2_gate), fin_gate, far_gate, keep_gate, near_gate)

    hidden_load.wait()
    for s in range(2):
        flying["y", s].wait()
        value = y_send[s].astype(f32) + y_recv[s].astype(f32)
        token_keep[mine(s), :] = (hidden_own[mine(s), :] + value).astype(bf16)
        home = pl.ds(pl.multiple_of(spot.core * rows + s * count, count), count)
        flying["keep", s] = mail.move(token_keep.at[mine(s)], out_tokens.at[home])
        flying["tokens", s] = mail.send(
            token_keep.at[mine(s)], out_tokens.at[home], spot.core_peer
        )
    gain_copies = []
    for d in range(1, line):
        gain_copies.append(mail.send(out_wide, wide_z.at[d - 1], spot.ahead[d]))
        gain_copies.append(mail.send(out_narrow, narrow_z.at[d - 1], spot.ahead[d]))

    raw_copy.wait()
    raw_loads = [
        mail.move(raws.span(r1_raw, 1 - spot.z_high), r1_raw_v.at[0]),
        mail.move(raws.span(r1_raw, spot.z_high), r1_raw_v.at[1]),
    ]
    for load in raw_loads:
        load.wait()
    raws.second_terms(r1_raw_v.at[0], s2_raw)
    second_raw = mail.send(s2_raw, r2_raw, spot.far_peer)
    out_copy.wait()
    out_loads = [
        mail.move(outs_job.span(r1_out, 1 - spot.z_high), r1_out_v.at[0]),
        mail.move(outs_job.span(r1_out, spot.z_high), r1_out_v.at[1]),
    ]
    for load in out_loads:
        load.wait()
    outs_job.second_terms(r1_out_v.at[0], s2_out)
    second_out = mail.send(s2_out, r2_out, spot.far_peer)
    up_own.wait()
    second_up.wait()
    finish(ups, final_of(ups, r1_wide.at[3], r2_up), fin_up, far_up, keep_up, near_up)
    second_raw.wait()
    finish(raws, final_of(raws, r1_raw_v.at[1], r2_raw), fin_raw, far_raw, keep_raw, near_raw)
    second_out.wait()
    finish(
        outs_job, final_of(outs_job, r1_out_v.at[1], r2_out), fin_out, far_out, keep_out, near_out
    )
    for copy in gain_copies:
        copy.wait()
    for d in range(1, line):
        out_wide[...] = out_wide[...] + wide_z[d - 1]
        out_narrow[...] = out_narrow[...] + narrow_z[d - 1]
    for s in range(2):
        flying["keep", s].wait()
        flying["tokens", s].wait()
    for copy in near_copies + far_copies:
        copy.wait()


def last(small, large):
    f32 = jnp.float32
    bf16 = jnp.bfloat16
    raw, raw_own, raw_x, wide, narrow, attended = small
    hidden, gate = large[0], large[2]
    count, depth = hidden.shape
    units = gate.shape[1]
    half = units // 2
    block = depth // (line * pair)
    columns = attended.shape[1]
    heads_half = columns // 2
    raw_half = raw_own.shape[1]
    rows = count // 2
    any_spec = pl.BlockSpec(memory_space=pl.ANY)
    shape = jax.ShapeDtypeStruct
    vmem = lambda *size: pltpu.VMEM(size, bf16)
    wide_vmem = lambda *size: pltpu.VMEM(size, f32)
    return pl.pallas_call(
        last_kernel,
        in_specs=vmem_specs(6) + [any_spec] * len(large),
        out_specs=[any_spec] * 13 + vmem_specs(2),
        out_shape=[
            shape((half, block), f32),
            shape((block, half), f32),
            shape((block, half), f32),
            shape((block, raw_half), f32),
            shape((heads_half, block), f32),
            shape((half, block), bf16),
            shape((block, half), bf16),
            shape((block, half), bf16),
            shape((block, raw_half), bf16),
            shape((heads_half, block), bf16),
            shape((count, depth), bf16),
            shape((line * block, raw_half), bf16),
            shape((heads_half, line * block), bf16),
            shape(wide.shape, f32),
            shape(narrow.shape, f32),
        ],
        scratch_shapes=[
            vmem(count, depth),
            vmem(count, depth),
            vmem(count, half),
            vmem(count, half),
            vmem(count, half),
            vmem(count, half),
            vmem(count, depth),
            vmem(count, depth),
            vmem(count, depth),
            vmem(count, depth),
            vmem(count, heads_half),
            vmem(count, heads_half),
            vmem(count, heads_half),
            vmem(line * block, raw_half),
            vmem(heads_half, line * block),
            vmem(4, 2 * block, half),
            vmem(2, 2 * block, raw_half),
            vmem(2, heads_half, 2 * block),
            vmem(2 * block, half),
            vmem(2 * block, half),
            vmem(2 * block, raw_half),
            vmem(heads_half, 2 * block),
            vmem(2 * block, half),
            vmem(2 * block, half),
            vmem(2 * block, raw_half),
            vmem(heads_half, 2 * block),
            wide_vmem(half, 2 * block),
            vmem(half, 2 * block),
            vmem(half, block),
            vmem(block, half),
            vmem(block, half),
            vmem(block, raw_half),
            vmem(heads_half, block),
            wide_vmem(half, block),
            wide_vmem(block, half),
            wide_vmem(block, half),
            wide_vmem(block, raw_half),
            wide_vmem(heads_half, block),
            vmem(depth, columns),
            wide_vmem(count, depth),
            vmem(2, rows // 2, depth),
            vmem(2, rows // 2, depth),
            vmem(2, rows // 2, depth),
            vmem(2, rows // 2, depth),
            wide_vmem(rows, depth),
            vmem(rows, depth),
            wide_vmem(*wide.shape),
            wide_vmem(*wide.shape),
            wide_vmem(*narrow.shape),
            wide_vmem(line - 1, *wide.shape),
            wide_vmem(line - 1, *narrow.shape),
            pltpu.SemaphoreType.DMA((48,)),
            pltpu.SemaphoreType.DMA((48,)),
            pltpu.SemaphoreType.DMA((40,)),
        ],
        compiler_params=pltpu.CompilerParams(
            vmem_limit_bytes=61800 << 10, collective_id=4, has_side_effects=True
        ),
    )(*small, *large)


def join_kernel(*refs):
    sources, out_output, out_tokens = refs[:12], refs[12], refs[13]
    outs, parts, sems = refs[14:21], refs[21:33], refs[33]
    nears, fars = parts[:5], parts[5:10]
    loads = [
        pltpu.make_async_copy(source, part, sems.at[i])
        for i, (source, part) in enumerate(zip(sources, parts))
    ]
    for load in loads[10:] + loads[:10]:
        load.start()
    copies = []
    for i, target in ((10, out_output), (11, out_tokens)):
        loads[i].wait()
        copies.append(pltpu.make_async_copy(parts[i], target, sems.at[i + 2]))
        copies[-1].start()
    for load in loads[:10]:
        load.wait()
    spot = lax.axis_index("dp")
    x = lax.rem(spot, 2)
    z_low = lax.rem(spot // 2, 2)

    def place(out, near, far, side, axis):
        size = near.shape[axis]
        for value, index in ((near, side), (far.astype(jnp.float32), 1 - side)):
            cut = pl.ds(pl.multiple_of(index * size, size), size)
            if axis == 0:
                out[cut, :] = value
            else:
                out[:, cut] = value

    place(outs[6], nears[0][...], fars[0][...], x, 0)
    place(outs[4], nears[1][...], fars[1][...], z_low, 1)
    place(outs[5], nears[2][...], fars[2][...], z_low, 1)
    width = nears[3].shape[1] // 3
    for which in range(3):
        cut = slice(which * width, (which + 1) * width)
        place(outs[which], nears[3][:, cut], fars[3][:, cut], x, 1)
    place(outs[3], nears[4][...], fars[4][...], x, 0)
    for copy in copies:
        copy.wait()


def join(nears, fars, output, tokens):
    f32 = jnp.float32
    shape = jax.ShapeDtypeStruct
    any_spec = pl.BlockSpec(memory_space=pl.ANY)
    far_spec = pl.BlockSpec(memory_space=pltpu.HBM)
    down, gate, up, raw, out = [part.shape for part in nears]
    third = shape((raw[0], 2 * raw[1] // 3), f32)
    return pl.pallas_call(
        join_kernel,
        in_specs=[far_spec] * 12,
        out_specs=[any_spec] * 2 + vmem_specs(7),
        out_shape=[
            shape(output.shape, output.dtype),
            shape(tokens.shape, tokens.dtype),
            third,
            third,
            third,
            shape((2 * out[0], out[1]), f32),
            shape((gate[0], 2 * gate[1]), f32),
            shape((up[0], 2 * up[1]), f32),
            shape((2 * down[0], down[1]), f32),
        ],
        scratch_shapes=[pltpu.VMEM(part.shape, part.dtype) for part in (*nears, *fars, output, tokens)]
        + [pltpu.SemaphoreType.DMA((14,))],
        compiler_params=pltpu.CompilerParams(vmem_limit_bytes=60 << 20),
    )(*nears, *fars, output, tokens)


def on_device_lines(
    tokens,
    cotangent,
    doc_ids,
    row_ids,
    offsets,
    w_query,
    w_key,
    w_value,
    w_output,
    w_gate,
    w_up,
    w_down,
    gain_query,
    gain_key,
    gain_attn,
    gain_mlp,
):
    f32 = jnp.float32
    bf16 = jnp.bfloat16
    row_count, model_width = tokens.shape
    heads_here, head_width = gain_query.shape
    local_width = heads_here * head_width
    half_rows = row_count // 2
    key_rows = row_count * line * pair
    spot = lax.axis_index("dp")
    z, x = spot // pair, lax.rem(spot, pair)
    z_high, z_low = z // 2, lax.rem(z, 2)
    core = lax.rem(lax.axis_index("mp"), 2)
    place = jnp.stack([core, z, z_low, z_high, x]).astype(jnp.int32)

    quarter = row_count // 4

    def own_rows(value):
        return lax.dynamic_slice_in_dim(value, core * half_rows, half_rows, 0)

    def other_rows(value):
        return lax.dynamic_slice_in_dim(value, (1 - core) * half_rows, half_rows, 0)

    def reorder(value):
        return join_parts(own_rows(value), other_rows(value))

    def restore(own, other):
        whole = jnp.zeros((row_count,) + own.shape[1:], own.dtype)
        whole = lax.dynamic_update_slice_in_dim(whole, own, core * half_rows, 0)
        return lax.dynamic_update_slice_in_dim(whole, other, (1 - core) * half_rows, 0)

    def half_of(value, side):
        width = value.shape[1] // 2
        return lax.dynamic_slice_in_dim(value, side * width, width, 1)

    positions = reorder(offsets[0] + jnp.arange(row_count, dtype=jnp.int32))
    labels = reorder(row_ids[0] * key_rows + doc_ids)
    freqs = rope_base ** (-jnp.arange(0, head_width // 2, dtype=f32) * 2.0 / head_width)
    angles = positions.astype(f32)[:, None] * freqs[None, :]
    cosines, sines = jnp.cos(angles), jnp.sin(angles)
    cosines = jnp.concatenate([cosines, cosines], axis=1)
    sines = jnp.concatenate([-sines, sines], axis=1)
    g_query = gain_query.reshape(1, local_width)
    g_key = gain_key.reshape(1, local_width)
    spots = jnp.stack([labels, positions]).astype(f32)
    queries, pairs, notes, q_raw, k_raw = project(
        tokens, w_query, w_key, w_value, g_query, g_key, cosines, sines, spots
    )
    factors = notes[0, :2]
    codes = notes[:, 2, :].astype(jnp.int32) * key_rows + notes[:, 3, :].astype(jnp.int32)
    lows = notes[:line, 2, :].astype(jnp.int32) * key_rows
    live = (
        (jnp.min(codes, axis=1)[None, :] <= jnp.max(codes[:line], axis=1)[:, None])
        & (jnp.max(codes, axis=1)[None, :] >= jnp.min(lows, axis=1)[:, None])
    ).astype(jnp.int32)

    turned, log_total, queries_n, keys_n, code_columns, code_rows, attended_out = attend(
        key_rows, live, notes, queries, pairs
    )

    def gather_heads(home):
        twice = jnp.concatenate(home + home, axis=1)
        return lax.dynamic_slice_in_dim(
            twice, lax.rem(line - z, line) * head_width, local_width, 1
        )

    def send_home(pieces):
        return [pieces[0]] + [line_shift(pieces[d], line - d) for d in range(1, line)]

    tokens_in = reorder(tokens)
    g_attn = gain_attn.reshape(1, model_width)
    g_mlp = gain_mlp.reshape(1, model_width)
    (
        attended_low,
        tokens_x,
        output,
        hidden_low,
        hidden_z,
        act_low,
        act_x,
        grad_mlp,
        grad_mlp_x,
        grad_gate,
        _,
        grad_gate_z,
        grad_up,
        grad_up_far,
        grad_attn,
        grads,
        grad_hidden,
        wide_gains,
    ) = block(
        attended_out, w_output, g_attn, g_mlp, tokens, cotangent, w_gate, w_up, w_down
    )
    grad_up_z = line_flip(grad_up_far, 1)
    back = attend_back(
        live, code_columns, code_rows, queries_n, keys_n, pairs, turned, log_total, grads
    )
    (
        own_down,
        r2_down,
        r1_gate,
        r1_up,
        r2_gate,
        raw_x,
        _,
        raw,
        raw_own,
        narrow_gains,
    ) = middle(
        (*back, q_raw, k_raw, factors, cosines, sines, g_query, g_key),
        (
            act_low,
            act_x,
            grad_mlp,
            grad_mlp_x,
            hidden_low,
            hidden_z,
            grad_gate,
            grad_gate_z,
            grad_up,
            grad_up_z,
        ),
    )
    results = last(
        (raw, raw_own, raw_x, wide_gains, narrow_gains, attended_low),
        (
            hidden_low,
            hidden_z,
            grad_gate,
            grad_gate_z,
            grad_up,
            grad_up_z,
            grad_attn,
            tokens,
            tokens_x,
            own_down,
            r2_down,
            r1_gate,
            r1_up,
            r2_gate,
            w_query,
            w_key,
            w_value,
            grad_hidden,
        ),
    )
    joined = join(results[:5], results[5:10], output, results[10])
    wide, narrow = results[13:]
    gains = jnp.concatenate([wide.reshape(2 * model_width), narrow.reshape(2 * local_width)])
    piece = head_width // (line * pair)

    def gain_piece(start, rows):
        part = gains[start : start + rows * head_width].reshape(rows, head_width)
        return lax.dynamic_slice_in_dim(part, spot * piece, piece, 1)

    all_heads = model_width // head_width
    return (
        *joined,
        gain_piece(2 * model_width, heads_here),
        gain_piece(2 * model_width + local_width, heads_here),
        gain_piece(0, all_heads),
        gain_piece(model_width, all_heads),
    )


def solution(mesh):
    tuned = mesh.shape["dp"] == line * pair and mesh.shape["mp"] == 4
    body = on_device_lines if tuned else on_device_general
    return jax.shard_map(
        body,
        mesh=mesh,
        in_specs=(
            P("dp", None),
            P("dp", None),
            P("dp"),
            P("dp"),
            P("dp"),
            P(None, "mp"),
            P(None, "mp"),
            P(None, "mp"),
            P("mp", None),
            P(None, "mp"),
            P(None, "mp"),
            P("mp", None),
            P("mp", None),
            P("mp", None),
            P(),
            P(),
        ),
        out_specs=(
            P("dp", None),
            P("dp", None),
            P("dp", "mp"),
            P("dp", "mp"),
            P("dp", "mp"),
            P("mp", "dp"),
            P("dp", "mp"),
            P("dp", "mp"),
            P("mp", "dp"),
            P("mp", "dp"),
            P("mp", "dp"),
            P(None, "dp"),
            P(None, "dp"),
        ),
        check_vma=False,
    )
```

```python
import functools
import math

import jax
import jax.numpy as jnp
from jax import lax
from jax.experimental import pallas as pl
from jax.experimental.pallas import tpu as pltpu
from jax.sharding import PartitionSpec as P

epsilon = 1e-06
rope_base = 500000.0
masked_score = -1e30


def rope_tables(positions, head_width):
    freqs = rope_base ** (-jnp.arange(0, head_width // 2, dtype=jnp.float32) * 2.0 / head_width)
    angles = positions.astype(jnp.float32)[:, None] * freqs[None, :]
    return (jnp.cos(angles)[:, None, :], jnp.sin(angles)[:, None, :])


def rotate(values, cosines, sines):
    half = values.shape[-1] // 2
    first = values[..., :half]
    second = values[..., half:]
    return jnp.concatenate(
        [first * cosines - second * sines, second * cosines + first * sines], axis=-1
    )


def norm_back(grad_normed, normed, factor):
    return factor * (grad_normed - normed * jnp.mean(grad_normed * normed, axis=-1, keepdims=True))


def on_device_general(
    tokens,
    cotangent,
    doc_ids,
    row_ids,
    offsets,
    w_query,
    w_key,
    w_value,
    w_output,
    w_gate,
    w_up,
    w_down,
    gain_query,
    gain_key,
    gain_attn,
    gain_mlp,
):
    f32 = jnp.float32
    bf16 = jnp.bfloat16
    row_count = tokens.shape[0]
    model_width = tokens.shape[1]
    heads_here = gain_query.shape[0]
    head_width = gain_query.shape[1]
    local_width = heads_here * head_width
    groups = lax.axis_size("dp")
    key_rows = row_count * groups
    block_rows = min(key_rows, row_count * max(1, 512 // row_count))
    block_count = key_rows // block_rows
    score_scale = 1.0 / math.sqrt(head_width)
    positions = offsets[0] + jnp.arange(row_count, dtype=jnp.int32)
    labels = row_ids[0] * key_rows + doc_ids
    cosines, sines = rope_tables(positions, head_width)
    q_raw = jnp.dot(tokens, w_query, preferred_element_type=f32)
    k_raw = jnp.dot(tokens, w_key, preferred_element_type=f32)
    v_raw = jnp.dot(tokens, w_value, preferred_element_type=f32)
    squares = lax.psum(
        jnp.stack([jnp.sum(q_raw * q_raw, axis=1), jnp.sum(k_raw * k_raw, axis=1)]), "mp"
    )
    q_factor = lax.rsqrt(squares[0] / model_width + epsilon)[:, None]
    k_factor = lax.rsqrt(squares[1] / model_width + epsilon)[:, None]
    g_query = gain_query.reshape(local_width)
    g_key = gain_key.reshape(local_width)
    q_normed = q_raw * q_factor
    k_normed = k_raw * k_factor
    queries = rotate(
        (q_normed * g_query).reshape(row_count, heads_here, head_width), cosines, sines
    ).astype(bf16)
    keys_low = rotate(
        (k_normed * g_key).reshape(row_count, heads_here, head_width), cosines, sines
    ).astype(bf16)
    values_low = v_raw.astype(bf16)
    all_keys, all_values, all_labels, all_positions = (
        lax.all_gather(keys_low.reshape(row_count, local_width), "dp", axis=0, tiled=True),
        lax.all_gather(values_low, "dp", axis=0, tiled=True),
        lax.all_gather(labels, "dp", axis=0, tiled=True),
        lax.all_gather(positions, "dp", axis=0, tiled=True),
    )
    key_blocks = all_keys.reshape(block_count, block_rows, heads_here, head_width)
    value_blocks = all_values.reshape(block_count, block_rows, heads_here, head_width)
    label_blocks = all_labels.reshape(block_count, block_rows)
    position_blocks = all_positions.reshape(block_count, block_rows)
    scanned = (key_blocks, value_blocks, label_blocks, position_blocks)
    low_label = jnp.min(labels)
    high_label = jnp.max(labels)

    def scores_of(key_block, label_block, position_block):
        scores = (
            jnp.einsum("qhd,khd->hqk", queries, key_block, preferred_element_type=f32) * score_scale
        )
        allowed = (labels[:, None] == label_block[None, :]) & (
            positions[:, None] >= position_block[None, :]
        )
        return (scores, allowed[None])

    def touches(label_block):
        return (jnp.max(label_block) >= low_label) & (jnp.min(label_block) <= high_label)

    def max_step(carry, blocks_in):
        key_block, value_block, label_block, position_block = blocks_in

        def max_live_block(state):
            running, totals = state
            scores, allowed = scores_of(key_block, label_block, position_block)
            highest = jnp.maximum(
                running, jnp.max(jnp.where(allowed, scores, masked_score), axis=2)
            )
            weights = jnp.where(allowed, jnp.exp(scores - highest[:, :, None]), 0.0)
            return (highest, totals * jnp.exp(running - highest) + jnp.sum(weights, axis=2))

        return (lax.cond(touches(label_block), max_live_block, lambda state: state, carry), None)

    start_state = (
        jnp.full((heads_here, row_count), masked_score, f32),
        jnp.zeros((heads_here, row_count), f32),
    )
    (running_max, running_total), _ = lax.scan(max_step, start_state, scanned)
    log_total = running_max + jnp.log(running_total)

    def value_step(accum, blocks_in):
        key_block, value_block, label_block, position_block = blocks_in

        def value_live_block(current):
            scores, allowed = scores_of(key_block, label_block, position_block)
            probs_low = jnp.where(allowed, jnp.exp(scores - log_total[:, :, None]), 0.0).astype(
                bf16
            )
            return current + jnp.einsum(
                "hqk,khd->qhd", probs_low, value_block, preferred_element_type=f32
            )

        return (
            lax.cond(touches(label_block), value_live_block, lambda current: current, accum),
            None,
        )

    attended, _ = lax.scan(value_step, jnp.zeros((row_count, heads_here, head_width), f32), scanned)
    attended_low = attended.reshape(row_count, local_width).astype(bf16)
    attn_sum = lax.psum(
        jnp.dot(attended_low, w_output, preferred_element_type=f32).astype(jnp.bfloat16), "mp"
    ).astype(jnp.float32)
    attn_factor = lax.rsqrt(jnp.mean(attn_sum * attn_sum, axis=1, keepdims=True) + epsilon)
    attn_normed = attn_sum * attn_factor
    g_attn = gain_attn.reshape(model_width)
    hidden = tokens.astype(f32) + attn_normed * g_attn
    hidden_low = hidden.astype(bf16)
    gate_val = jnp.dot(hidden_low, w_gate, preferred_element_type=f32)
    up_val = jnp.dot(hidden_low, w_up, preferred_element_type=f32)
    sigmoid_gate = jax.nn.sigmoid(gate_val)
    silu_gate = gate_val * sigmoid_gate
    act_low = (silu_gate * up_val).astype(bf16)
    mlp_sum = lax.psum(
        jnp.dot(act_low, w_down, preferred_element_type=f32).astype(jnp.bfloat16), "mp"
    ).astype(jnp.float32)
    mlp_factor = lax.rsqrt(jnp.mean(mlp_sum * mlp_sum, axis=1, keepdims=True) + epsilon)
    mlp_normed = mlp_sum * mlp_factor
    g_mlp = gain_mlp.reshape(model_width)
    output = (hidden + mlp_normed * g_mlp).astype(bf16)
    grad_out = cotangent.astype(f32)
    grad_gain_mlp = jnp.sum(grad_out * mlp_normed, axis=0)
    grad_mlp = norm_back(grad_out * g_mlp, mlp_normed, mlp_factor).astype(bf16)
    grad_w_down = jnp.einsum("tf,td->fd", act_low, grad_mlp, preferred_element_type=f32)
    grad_act = jnp.einsum("td,fd->tf", grad_mlp, w_down, preferred_element_type=f32)
    slope = sigmoid_gate * (1.0 + gate_val * (1.0 - sigmoid_gate))
    grad_gate = (grad_act * up_val * slope).astype(bf16)
    grad_up = (grad_act * silu_gate).astype(bf16)
    branch_grad = jnp.einsum(
        "tf,df->td", grad_gate, w_gate, preferred_element_type=f32
    ) + jnp.einsum("tf,df->td", grad_up, w_up, preferred_element_type=f32)
    grad_hidden = grad_out + lax.psum(branch_grad.astype(jnp.bfloat16), "mp").astype(jnp.float32)
    grad_gain_attn = jnp.sum(grad_hidden * attn_normed, axis=0)
    grad_attn = norm_back(grad_hidden * g_attn, attn_normed, attn_factor).astype(bf16)
    grad_w_output = jnp.einsum("tc,td->cd", attended_low, grad_attn, preferred_element_type=f32)
    grad_attended = (
        jnp.einsum("td,cd->tc", grad_attn, w_output, preferred_element_type=f32)
        .astype(bf16)
        .reshape(row_count, heads_here, head_width)
    )
    delta = jnp.sum(grad_attended.astype(f32) * attended, axis=2).T

    def grad_step(grad_q, blocks_in):
        key_block, value_block, label_block, position_block = blocks_in

        def grad_live_block(current):
            scores, allowed = scores_of(key_block, label_block, position_block)
            probs = jnp.where(allowed, jnp.exp(scores - log_total[:, :, None]), 0.0)
            grad_probs = jnp.einsum(
                "qhd,khd->hqk", grad_attended, value_block, preferred_element_type=f32
            )
            grad_scores = (probs * (grad_probs - delta[:, :, None])).astype(bf16)
            value_term = jnp.einsum(
                "hqk,qhd->khd", probs.astype(bf16), grad_attended, preferred_element_type=f32
            )
            key_term = jnp.einsum("hqk,qhd->khd", grad_scores, queries, preferred_element_type=f32)
            updated = current + jnp.einsum(
                "hqk,khd->qhd", grad_scores, key_block, preferred_element_type=f32
            )
            return (updated, (key_term, value_term))

        def skip_block(current):
            nothing = jnp.zeros((block_rows, heads_here, head_width), f32)
            return (current, (nothing, nothing))

        return lax.cond(touches(label_block), grad_live_block, skip_block, grad_q)

    grad_queries, (key_terms, value_terms) = lax.scan(
        grad_step, jnp.zeros((row_count, heads_here, head_width), f32), scanned
    )
    grad_keys, grad_values = (
        lax.psum_scatter(
            (key_terms.reshape(key_rows, local_width) * score_scale).astype(jnp.bfloat16),
            "dp",
            scatter_dimension=0,
            tiled=True,
        ).astype(jnp.float32),
        lax.psum_scatter(
            value_terms.reshape(key_rows, local_width).astype(jnp.bfloat16),
            "dp",
            scatter_dimension=0,
            tiled=True,
        ).astype(jnp.float32),
    )
    grad_values_low = grad_values.astype(bf16)
    back_q = rotate(grad_queries * score_scale, cosines, -sines).reshape(row_count, local_width)
    back_k = rotate(grad_keys.reshape(row_count, heads_here, head_width), cosines, -sines).reshape(
        row_count, local_width
    )
    grad_gain_query = jnp.sum(back_q * q_normed, axis=0).reshape(heads_here, head_width)
    grad_gain_key = jnp.sum(back_k * k_normed, axis=0).reshape(heads_here, head_width)
    scaled_q = back_q * g_query
    scaled_k = back_k * g_key
    inner = lax.psum(
        jnp.stack([jnp.sum(scaled_q * q_normed, axis=1), jnp.sum(scaled_k * k_normed, axis=1)]),
        "mp",
    )
    grad_q_raw = (q_factor * (scaled_q - q_normed * inner[0][:, None] / model_width)).astype(bf16)
    grad_k_raw = (k_factor * (scaled_k - k_normed * inner[1][:, None] / model_width)).astype(bf16)
    input_term = (
        jnp.einsum("tc,dc->td", grad_q_raw, w_query, preferred_element_type=f32)
        + jnp.einsum("tc,dc->td", grad_k_raw, w_key, preferred_element_type=f32)
        + jnp.einsum("tc,dc->td", grad_values_low, w_value, preferred_element_type=f32)
    )
    grad_tokens = (
        grad_hidden + lax.psum(input_term.astype(jnp.bfloat16), "mp").astype(jnp.float32)
    ).astype(bf16)
    local_w_query = jnp.einsum("td,tc->dc", tokens, grad_q_raw, preferred_element_type=f32)
    local_w_key = jnp.einsum("td,tc->dc", tokens, grad_k_raw, preferred_element_type=f32)
    local_w_value = jnp.einsum("td,tc->dc", tokens, grad_values_low, preferred_element_type=f32)
    local_w_gate = jnp.einsum("td,tf->df", hidden_low, grad_gate, preferred_element_type=f32)
    local_w_up = jnp.einsum("td,tf->df", hidden_low, grad_up, preferred_element_type=f32)
    grad_w_query, grad_w_key, grad_w_value, grad_w_gate, grad_w_up = (
        lax.psum_scatter(
            local_w_query.astype(jnp.bfloat16), "dp", scatter_dimension=0, tiled=True
        ).astype(jnp.float32),
        lax.psum_scatter(
            local_w_key.astype(jnp.bfloat16), "dp", scatter_dimension=0, tiled=True
        ).astype(jnp.float32),
        lax.psum_scatter(
            local_w_value.astype(jnp.bfloat16), "dp", scatter_dimension=0, tiled=True
        ).astype(jnp.float32),
        lax.psum_scatter(
            local_w_gate.astype(jnp.bfloat16), "dp", scatter_dimension=0, tiled=True
        ).astype(jnp.float32),
        lax.psum_scatter(
            local_w_up.astype(jnp.bfloat16), "dp", scatter_dimension=0, tiled=True
        ).astype(jnp.float32),
    )
    summed_out, summed_down, summed_gq, summed_gk, summed_ga, summed_gm = (
        lax.psum_scatter(
            grad_w_output.astype(jnp.bfloat16), "dp", scatter_dimension=1, tiled=True
        ).astype(jnp.float32),
        lax.psum_scatter(
            grad_w_down.astype(jnp.bfloat16), "dp", scatter_dimension=1, tiled=True
        ).astype(jnp.float32),
        lax.psum_scatter(
            grad_gain_query.astype(jnp.bfloat16), "dp", scatter_dimension=1, tiled=True
        ).astype(jnp.float32),
        lax.psum_scatter(
            grad_gain_key.astype(jnp.bfloat16), "dp", scatter_dimension=1, tiled=True
        ).astype(jnp.float32),
        lax.psum_scatter(
            grad_gain_attn.reshape(gain_attn.shape).astype(jnp.bfloat16),
            "dp",
            scatter_dimension=1,
            tiled=True,
        ).astype(jnp.float32),
        lax.psum_scatter(
            grad_gain_mlp.reshape(gain_mlp.shape).astype(jnp.bfloat16),
            "dp",
            scatter_dimension=1,
            tiled=True,
        ).astype(jnp.float32),
    )
    return (
        output,
        grad_tokens,
        grad_w_query,
        grad_w_key,
        grad_w_value,
        summed_out,
        grad_w_gate,
        grad_w_up,
        summed_down,
        summed_gq,
        summed_gk,
        summed_ga,
        summed_gm,
    )


line = 4
pair = 2
low_score = -1e30
start_max = -1e20
big_vmem = 56 << 20


def line_shift(value, step):
    moves = [
        (z * pair + x, ((z + step) % line) * pair + x) for z in range(line) for x in range(pair)
    ]
    return lax.ppermute(value, "dp", moves)


def line_flip(value, bit):
    return lax.ppermute(
        value, "dp", [(z * pair + x, (z ^ bit) * pair + x) for z in range(line) for x in range(pair)]
    )


def x_swap(value):
    return lax.ppermute(value, "dp", [(i, i ^ 1) for i in range(line * pair)])


def core_swap(value):
    return lax.ppermute(value, "mp", [(i, i ^ 1) for i in range(4)])


def y_swap(value):
    return lax.ppermute(value, "mp", [(i, i ^ 2) for i in range(4)])


def flip_cores(value, axis):
    quarter = value.shape[axis] // 4
    cuts = [lax.slice_in_dim(value, i * quarter, (i + 1) * quarter, axis=axis) for i in (1, 0, 3, 2)]
    return jnp.concatenate(cuts, axis=axis)


def token_sum(value):
    value = value + flip_cores(core_swap(value), 1)
    return value + y_swap(value)


def own_part(value):
    quarter = value.shape[0] // 4
    return jnp.concatenate([value[:quarter], value[2 * quarter : 3 * quarter]], axis=0)


def other_part(value):
    quarter = value.shape[0] // 4
    return jnp.concatenate([value[quarter : 2 * quarter], value[3 * quarter :]], axis=0)


def join_parts(own, other):
    half = own.shape[0] // 2
    return jnp.concatenate([own[:half], other[:half], own[half:], other[half:]], axis=0)


def reduce_own_rows(partial_low):
    f32 = jnp.float32
    arrived = core_swap(other_part(partial_low))
    chip_sum = (own_part(partial_low).astype(f32) + arrived.astype(f32)).astype(jnp.bfloat16)
    return chip_sum.astype(f32) + y_swap(chip_sum).astype(f32)


def dot_t(first, second):
    return lax.dot_general(
        first, second, (((0,), (0,)), ((), ())), preferred_element_type=jnp.float32
    )


def dot_nt(first, second):
    return lax.dot_general(
        first, second, (((1,), (1,)), ((), ())), preferred_element_type=jnp.float32
    )


def vmem_specs(count):
    return [pl.BlockSpec(memory_space=pltpu.VMEM)] * count


def project_kernel(
    tokens,
    wq,
    wk,
    wv,
    gq,
    gk,
    cosines,
    sines,
    spots,
    out_queries,
    out_pairs,
    out_notes,
    out_q_raw,
    out_k_raw,
    rows_keep,
    query_keep,
    pair_keep,
    squares,
    squares_core,
    squares_y,
    send_sems,
    recv_sems,
    local_sems,
):
    f32 = jnp.float32
    bf16 = jnp.bfloat16
    width = cosines.shape[1]
    depth = wq.shape[0]
    rows = rows_keep.shape[0] // 2
    count = rows // 2
    mp = lax.axis_index("mp")
    spot = lax.axis_index("dp")
    core = lax.rem(mp, 2)
    x = lax.rem(spot, 2)
    z = spot // 2
    core_peer = {"mp": mp + 1 - 2 * core}
    y_peer = {"mp": lax.rem(mp + 2, 4)}
    x_peer = {"dp": spot + 1 - 2 * x}
    ahead = [{"dp": lax.rem(spot + 2 * d, 2 * line)} for d in range(line)]
    head = [lax.rem(z + d, line) for d in range(line)]
    both = lambda s: pl.ds(s * rows, rows)
    remote = []

    def send(source, target, peer):
        index = len(remote)
        copy = pltpu.make_async_remote_copy(
            src_ref=source,
            dst_ref=target,
            send_sem=send_sems.at[index],
            recv_sem=recv_sems.at[index],
            device_id=peer,
            device_id_type=pl.DeviceIdType.MESH,
        )
        remote.append(copy)
        copy.start()
        return copy

    loads = []
    for s in range(2):
        for part, place in ((0, core), (1, 1 - core)):
            start = pl.multiple_of(place * rows + s * count, count)
            copy = pltpu.make_async_copy(
                tokens.at[pl.ds(start, count)],
                rows_keep.at[pl.ds(s * rows + part * count, count)],
                local_sems.at[2 * s + part],
            )
            copy.start()
            loads.append(copy)

    barrier = pltpu.get_barrier_semaphore()
    peers = (core_peer, y_peer, x_peer, ahead[1], ahead[2], ahead[3])
    for peer in peers:
        pl.semaphore_signal(barrier, inc=1, device_id=peer, device_id_type=pl.DeviceIdType.MESH)
    pl.semaphore_wait(barrier, len(peers))

    def turned(raw, gain, s, h):
        part = raw[:, h * width : (h + 1) * width] * gain[:, h * width : (h + 1) * width]
        return (
            part * cosines[both(s), :] + pltpu.roll(part, width // 2, 1) * sines[both(s), :]
        ).astype(bf16)

    flying = {}
    for s in range(2):
        loads[2 * s].wait()
        loads[2 * s + 1].wait()
        k_raw = jnp.dot(rows_keep[both(s), :], wk[...], preferred_element_type=f32)
        out_k_raw[both(s), :] = k_raw
        squares[1:2, both(s)] = jnp.sum((k_raw * k_raw).T, axis=0, keepdims=True)
        v_raw = jnp.dot(rows_keep[both(s), :], wv[...], preferred_element_type=f32)
        for h in range(line):
            pair_keep[h, 0, both(s), :] = turned(k_raw, gk[...], s, h)
            pair_keep[h, 1, both(s), :] = v_raw[:, h * width : (h + 1) * width].astype(bf16)
        for d in (2, 1, 3):
            flying["pair", s, d] = send(
                pair_keep.at[head[d], :, both(s)], out_pairs.at[d, :, both(s)], ahead[d]
            )
        flying["far", s, 0] = send(
            pair_keep.at[z, :, both(s)], out_pairs.at[line, :, both(s)], x_peer
        )
        q_raw = jnp.dot(rows_keep[both(s), :], wq[...], preferred_element_type=f32)
        out_q_raw[both(s), :] = q_raw
        squares[0:1, both(s)] = jnp.sum((q_raw * q_raw).T, axis=0, keepdims=True)
        for h in range(line):
            query_keep[h, both(s), :] = turned(q_raw, gq[...], s, h)

    core_copy = send(squares, squares_core, core_peer)
    core_copy.wait()
    arrived = squares_core[...]
    cuts = [arrived[:, i * count : (i + 1) * count] for i in (1, 0, 3, 2)]
    chip = squares[...] + jnp.concatenate(cuts, axis=1)
    squares[...] = chip
    y_copy = send(squares, squares_y, y_peer)
    y_copy.wait()
    out_notes[0, 0:2, :] = lax.rsqrt((chip + squares_y[...]) / depth + epsilon)
    out_notes[0, 2:4, :] = spots[...]
    for d in range(1, line):
        flying["note", d] = send(out_notes.at[0], out_notes.at[d], ahead[d])
    flying["far_note", 0] = send(out_notes.at[0], out_notes.at[line], x_peer)
    for d in range(1, line):
        flying["query", d] = send(query_keep.at[head[d]], out_queries.at[d], ahead[d])
    out_queries[0] = query_keep[z]
    out_pairs[0] = pair_keep[z]
    for s in range(2):
        for d in (2, 1, 3):
            flying["pair", s, d].wait()
            flying["far", s, d] = send(
                out_pairs.at[d, :, both(s)], out_pairs.at[line + d, :, both(s)], x_peer
            )
    for d in range(1, line):
        flying["note", d].wait()
        flying["far_note", d] = send(out_notes.at[d], out_notes.at[line + d], x_peer)
    for d in range(1, line):
        flying["query", d].wait()
    for d in range(line):
        flying["far_note", d].wait()
        for s in range(2):
            flying["far", s, d].wait()


def project(tokens, wq, wk, wv, gq, gk, cosines, sines, spots):
    rows, depth = tokens.shape
    columns = wq.shape[1]
    width = columns // line
    f32 = jnp.float32
    bf16 = jnp.bfloat16
    return pl.pallas_call(
        project_kernel,
        in_specs=[pl.BlockSpec(memory_space=pl.ANY)] + vmem_specs(8),
        out_specs=vmem_specs(5),
        out_shape=[
            jax.ShapeDtypeStruct((line, rows, width), bf16),
            jax.ShapeDtypeStruct((2 * line, 2, rows, width), bf16),
            jax.ShapeDtypeStruct((2 * line, 4, rows), f32),
            jax.ShapeDtypeStruct((rows, columns), f32),
            jax.ShapeDtypeStruct((rows, columns), f32),
        ],
        scratch_shapes=[
            pltpu.VMEM((rows, depth), bf16),
            pltpu.VMEM((line, rows, width), bf16),
            pltpu.VMEM((line, 2, rows, width), bf16),
            pltpu.VMEM((2, rows), f32),
            pltpu.VMEM((2, rows), f32),
            pltpu.VMEM((2, rows), f32),
            pltpu.SemaphoreType.DMA((28,)),
            pltpu.SemaphoreType.DMA((28,)),
            pltpu.SemaphoreType.DMA((4,)),
        ],
        compiler_params=pltpu.CompilerParams(
            vmem_limit_bytes=48 << 20, collective_id=2, has_side_effects=True
        ),
        cost_estimate=pl.CostEstimate(flops=0, bytes_accessed=0, transcendentals=0),
    )(tokens, wq, wk, wv, gq, gk, cosines, sines, spots)


def visible_scores(key, query, key_code, query_code, query_low, factor):
    scores = dot_nt(key, query) * factor
    codes = jnp.concatenate([key_code] * (query.shape[0] // key_code.shape[1]), axis=1)
    return jnp.where((codes <= query_code) & (codes >= query_low), scores, low_score)


def attend_kernel(factor, key_rows, live, notes, *refs):
    queries, pairs = refs[:2]
    out_turned, out_log, out_query, out_key, out_codes, out_rows, out = refs[2:9]
    top, total, accum = refs[9:]
    f32 = jnp.float32
    bf16 = jnp.bfloat16
    count, width = queries.shape[1:]

    def column(row):
        return jnp.broadcast_to(row, (width, count)).T

    for k in range(2 * line):
        out_key[k] = (pairs[k, 0].astype(f32) * column(notes[k, 1:2, :])).astype(bf16)
        labels = column(notes[k, 2:3, :]).astype(jnp.int32)
        out_codes[k] = labels * key_rows + column(notes[k, 3:4, :]).astype(jnp.int32)
    for q in range(line):
        out_query[q] = (queries[q].astype(f32) * column(notes[q, 0:1, :])).astype(bf16)
        base = notes[q, 2:3, :].astype(jnp.int32) * key_rows
        out_rows[q : q + 1, :] = base + notes[q, 3:4, :].astype(jnp.int32)
        out_rows[line + q : line + q + 1, :] = base

    for q in range(line):
        top[...] = jnp.full_like(top, start_max)
        total[...] = jnp.zeros_like(total)
        accum[...] = jnp.zeros_like(accum)
        @pl.loop(0, 2 * line)
        def _(k, q=q):
            @pl.when(live[q, k] > 0)
            def _():
                scores = visible_scores(
                    out_key[k],
                    out_query[q],
                    out_codes[k],
                    out_rows[q : q + 1, :],
                    out_rows[line + q : line + q + 1, :],
                    factor,
                )
                highest = jnp.maximum(top[...], jnp.max(scores, axis=0, keepdims=True))
                weights = jnp.exp2(scores - highest)
                fade = jnp.exp2(top[...] - highest)
                total[...] = total[...] * fade + jnp.sum(weights, axis=0, keepdims=True)
                accum[...] = accum[...] * fade + dot_t(pairs[k, 1], weights.astype(bf16))
                top[...] = highest

        turned = accum[...] / total[...]
        out_turned[q] = turned
        out_log[q : q + 1, :] = top[...] + jnp.log2(total[...])
        out[q] = turned.T.astype(bf16)


def attend_back_kernel(factor, scale, live, codes, rows, queries, keys, *refs):
    pairs, turned, log_total, grads = refs[:4]
    out_query, out_near, out_far, key_sum, value_sum, query_sum = refs[4:]
    f32 = jnp.float32
    bf16 = jnp.bfloat16
    key_sum[...] = jnp.zeros_like(key_sum)
    value_sum[...] = jnp.zeros_like(value_sum)
    for q in range(line):
        query_sum[...] = jnp.zeros_like(query_sum)
        delta = jnp.sum(grads[q].astype(f32).T * turned[q], axis=0, keepdims=True)
        @pl.loop(0, 2 * line)
        def _(k, q=q, delta=delta):
            @pl.when(live[q, k] > 0)
            def _():
                query, key, grad = queries[q], keys[k], grads[q]
                scores = visible_scores(
                    key,
                    query,
                    codes[k],
                    rows[q : q + 1, :],
                    rows[line + q : line + q + 1, :],
                    factor,
                )
                probs = jnp.exp2(scores - log_total[q : q + 1, :])
                grad_probs = dot_nt(pairs[k, 1], grad)
                grad_scores = (probs * (grad_probs - delta)).astype(bf16)
                value_sum[k] += jnp.dot(
                    probs.astype(bf16), grad, preferred_element_type=f32
                )
                key_sum[k] += jnp.dot(grad_scores, query, preferred_element_type=f32)
                query_sum[...] += dot_t(key, grad_scores)

        out_query[q] = (query_sum[...] * scale).T.astype(bf16)
    for k in range(line):
        for out, base in ((out_near, 0), (out_far, line)):
            out[k, 0] = (key_sum[base + k] * scale).astype(bf16)
            out[k, 1] = value_sum[base + k].astype(bf16)


def attend(key_rows, live, notes, queries, pairs):
    _, count, width = queries.shape
    factor = math.log2(math.e) / math.sqrt(width)
    f32 = jnp.float32
    bf16 = jnp.bfloat16
    return pl.pallas_call(
        functools.partial(attend_kernel, factor, key_rows),
        out_shape=[
            jax.ShapeDtypeStruct((line, width, count), f32),
            jax.ShapeDtypeStruct((2 * line, count), f32),
            jax.ShapeDtypeStruct((line, count, width), bf16),
            jax.ShapeDtypeStruct((2 * line, count, width), bf16),
            jax.ShapeDtypeStruct((2 * line, count, width), jnp.int32),
            jax.ShapeDtypeStruct((2 * line, count), jnp.int32),
        ]
        + [jax.ShapeDtypeStruct((line, count, width), bf16)],
        in_specs=[pl.BlockSpec(memory_space=pltpu.SMEM)] + vmem_specs(3),
        out_specs=vmem_specs(7),
        scratch_shapes=[
            pltpu.VMEM((1, count), f32),
            pltpu.VMEM((1, count), f32),
            pltpu.VMEM((width, count), f32),
        ],
        compiler_params=pltpu.CompilerParams(vmem_limit_bytes=40 << 20),
        cost_estimate=pl.CostEstimate(flops=0, bytes_accessed=0, transcendentals=0),
    )(live, notes, queries, pairs)


def attend_back(live, codes, rows, queries, keys, pairs, turned, log_total, grads):
    _, count, width = queries.shape
    scale = 1.0 / math.sqrt(width)
    factor = math.log2(math.e) * scale
    f32 = jnp.float32
    return pl.pallas_call(
        functools.partial(attend_back_kernel, factor, scale),
        out_shape=[jax.ShapeDtypeStruct((line, count, width), jnp.bfloat16)]
        + [jax.ShapeDtypeStruct((line, 2, count, width), jnp.bfloat16)] * 2,
        in_specs=[pl.BlockSpec(memory_space=pltpu.SMEM)] + vmem_specs(8),
        out_specs=vmem_specs(3),
        scratch_shapes=[
            pltpu.VMEM((2 * line, count, width), f32),
            pltpu.VMEM((2 * line, count, width), f32),
            pltpu.VMEM((width, count), f32),
        ],
        compiler_params=pltpu.CompilerParams(vmem_limit_bytes=40 << 20),
        cost_estimate=pl.CostEstimate(
            flops=20 * line * line * count * count * width,
            bytes_accessed=12 << 20,
            transcendentals=2 * line * line * count * count,
        ),
    )(live, codes, rows, queries, keys, pairs, turned, log_total, grads)


def block_kernel(
    pieces,
    w_out,
    g_attn,
    g_mlp,
    tokens,
    cotangent,
    w_gate_in,
    w_up_in,
    w_down_in,
    out_heads,
    out_tokens_x,
    out_output,
    out_hidden,
    out_hidden_z,
    out_act,
    out_act_x,
    out_mlp,
    out_mlp_x,
    out_gate,
    out_gate_far,
    out_gate_z,
    out_up,
    out_up_far,
    out_attn,
    out_grads,
    out_grad_hidden,
    out_gain,
    w_gate,
    w_up,
    w_down,
    gate_keep,
    up_keep,
    act_keep,
    hidden_keep,
    mlp_keep,
    attn_keep,
    grad_gate,
    grad_up,
    own_factor,
    own_normed,
    own_tokens,
    own_cotangent,
    attended,
    heads_keep,
    total,
    part_send,
    part_recv,
    y_send,
    y_recv,
    send_sems,
    recv_sems,
    local_sems,
):
    f32 = jnp.float32
    bf16 = jnp.bfloat16
    depth = w_out.shape[1]
    units = w_gate.shape[1]
    tile = 512
    count = own_tokens.shape[0] // 2
    rows = 2 * count
    mp = lax.axis_index("mp")
    spot = lax.axis_index("dp")
    core = lax.rem(mp, 2)
    core_peer = {"mp": mp + 1 - 2 * core}
    y_peer = {"mp": lax.rem(mp + 2, 4)}
    z = spot // 2
    z_low = lax.rem(z, 2)
    z_peer = {"dp": spot + 2 - 4 * z_low}
    x = lax.rem(spot, 2)
    x_peer = {"dp": spot + 1 - 2 * x}
    width = pieces.shape[2]
    ahead = [{"dp": lax.rem(spot + 2 * d, 2 * line)} for d in range(line)]
    head = lambda d: pl.ds(pl.multiple_of(lax.rem(z + d, line) * width, width), width)

    remote, started, local = [], [], []

    def send(source, target, peer):
        index = len(remote)
        copy = pltpu.make_async_remote_copy(
            src_ref=source,
            dst_ref=target,
            send_sem=send_sems.at[index],
            recv_sem=recv_sems.at[index],
            device_id=peer,
            device_id_type=pl.DeviceIdType.MESH,
        )
        remote.append(copy)
        copy.start()
        return copy

    def keep_out(source, target, waited=False):
        copy = pltpu.make_async_copy(source, target, local_sems.at[len(started)])
        started.append(copy)
        if not waited:
            local.append(copy)
        copy.start()
        return copy

    own = lambda s: pl.ds(s * rows, count)
    other = lambda s: pl.ds(s * rows + count, count)
    both = lambda s: pl.ds(s * rows, rows)
    mine = lambda s: pl.ds(s * count, count)
    at_home = lambda s: pl.ds(pl.multiple_of(core * rows + s * count, count), count)
    cut = lambda t: pl.ds(pl.multiple_of(t * tile, tile), tile)
    flying = {}

    home_rows = pl.ds(pl.multiple_of(core * rows, rows), rows)
    loads = [
        keep_out(tokens.at[home_rows], own_tokens, True),
        keep_out(cotangent.at[home_rows], own_cotangent, True),
        keep_out(w_gate_in, w_gate, True),
        keep_out(w_up_in, w_up, True),
        keep_out(w_down_in, w_down, True),
    ]
    barrier = pltpu.get_barrier_semaphore()
    peers = (core_peer, y_peer, x_peer, ahead[1], ahead[2], ahead[3])
    for peer in peers:
        pl.semaphore_signal(barrier, inc=1, device_id=peer, device_id_type=pl.DeviceIdType.MESH)
    pl.semaphore_wait(barrier, len(peers))
    for s in range(2):
        for d in range(1, line):
            flying["heads", s, d] = send(
                pieces.at[d, both(s)], attended.at[both(s), head(0)], ahead[line - d]
            )
    attended[:, head(0)] = pieces[0]

    loads[0].wait()
    for s in range(2):
        flying["tokens", s] = send(own_tokens.at[mine(s)], out_tokens_x.at[own(s)], x_peer)

    def forward_core(name, s, array):
        flying[name, s].wait()
        flying[name + "_core", s] = send(array.at[own(s)], array.at[other(s)], core_peer)

    def reduce_start(stage, s):
        part_send[s] = total[count:, :].astype(bf16)
        copy = send(part_send.at[s], part_recv.at[s], core_peer)
        copy.wait()
        y_send[s] = (total[:count, :] + part_recv[s].astype(f32)).astype(bf16)
        flying[stage, s] = send(y_send.at[s], y_recv.at[stage, s], y_peer)

    def reduced(stage, s):
        flying[stage, s].wait()
        return y_send[s].astype(f32) + y_recv[stage, s].astype(f32)

    def factor_of(value):
        return lax.rsqrt(jnp.mean(value * value, axis=1, keepdims=True) + epsilon)

    def share(keep, s):
        flying["share", s] = send(keep.at[own(s)], keep.at[other(s)], core_peer)

    def project_out(s):
        for d in range(1, line):
            flying["heads", s, d].wait()
        keep_out(attended.at[both(s)], out_heads.at[both(s)])
        total[...] = jnp.dot(attended[both(s), :], w_out[...], preferred_element_type=f32)
        reduce_start(0, s)

    def after_attention(s):
        value = reduced(0, s)
        factor = factor_of(value)
        normed = value * factor
        own_factor[mine(s), :] = jnp.broadcast_to(factor, (count, own_factor.shape[1]))
        own_normed[mine(s), :] = normed
        hidden = own_tokens[mine(s), :].astype(f32) + normed * g_attn[...]
        out_grad_hidden[mine(s), :] = hidden
        hidden_keep[own(s), :] = hidden.astype(bf16)
        share(hidden_keep, s)

    def forward(s):
        flying["hidden", s] = send(hidden_keep.at[own(s)], out_hidden_z.at[own(s)], z_peer)
        flying["share", s].wait()
        keep_out(hidden_keep.at[both(s)], out_hidden.at[both(s)])

        def step(t):
            hidden = hidden_keep[both(s), :]
            gate = jnp.dot(hidden, w_gate[:, cut(t)], preferred_element_type=f32)
            up = jnp.dot(hidden, w_up[:, cut(t)], preferred_element_type=f32)
            gate_keep[both(s), cut(t)] = gate.astype(bf16)
            up_keep[both(s), cut(t)] = up.astype(bf16)
            act = (gate * jax.nn.sigmoid(gate) * up).astype(bf16)
            act_keep[both(s), cut(t)] = act
            return jnp.dot(act, w_down[cut(t), :], preferred_element_type=f32)

        total[...] = step(0)

        @pl.loop(1, units // tile)
        def _(t):
            total[...] += step(t)

        reduce_start(1, s)
        keep_out(act_keep.at[both(s)], out_act.at[both(s)])
        half = units // 2
        far = pl.ds(pl.multiple_of((1 - x) * half, half), half)
        flying["act", s] = send(act_keep.at[both(s), far], out_act_x.at[both(s)], x_peer)

    def turn_point(s):
        value = reduced(1, s)
        factor = factor_of(value)
        normed = value * factor
        forward_core("tokens", s, out_tokens_x)
        own_tokens[mine(s), :] = (out_grad_hidden[mine(s), :] + normed * g_mlp[...]).astype(bf16)
        keep_out(own_tokens.at[mine(s)], out_output.at[at_home(s)])
        flying["output", s] = send(own_tokens.at[mine(s)], out_output.at[at_home(s)], core_peer)
        grad = own_cotangent[mine(s), :].astype(f32)
        gain = jnp.sum(grad * normed, axis=0, keepdims=True)
        out_gain[1:2, :] = gain if s == 0 else out_gain[1:2, :] + gain
        mlp_keep[own(s), :] = norm_back(grad * g_mlp[...], normed, factor).astype(bf16)
        share(mlp_keep, s)

    def backward(s):
        flying["mlp", s] = send(mlp_keep.at[own(s)], out_mlp_x.at[own(s)], x_peer)
        flying["share", s].wait()
        keep_out(mlp_keep.at[both(s)], out_mlp.at[both(s)])

        def step(t):
            grad_act = dot_nt(mlp_keep[both(s), :], w_down[cut(t), :])
            gate = gate_keep[both(s), cut(t)].astype(f32)
            up = up_keep[both(s), cut(t)].astype(f32)
            sigmoid = jax.nn.sigmoid(gate)
            to_gate = (grad_act * up * (sigmoid * (1.0 + gate * (1.0 - sigmoid)))).astype(bf16)
            to_up = (grad_act * (gate * sigmoid)).astype(bf16)
            grad_gate[:, cut(t)] = to_gate
            grad_up[:, cut(t)] = to_up
            return dot_nt(to_gate, w_gate[:, cut(t)]) + dot_nt(to_up, w_up[:, cut(t)])

        if s > 0:
            gate_to_z(0)
        total[...] = step(0)

        @pl.loop(1, units // tile)
        def _(t):
            total[...] += step(t)

        reduce_start(2, s)
        half = units // 2
        far = pl.ds(pl.multiple_of((1 - z_low) * half, half), half)
        flying["grads"] = [
            keep_out(source, target.at[both(s)], waited=True)
            for source, target in (
                (grad_gate, out_gate),
                (grad_gate.at[:, far], out_gate_far),
                (grad_up, out_up),
                (grad_up.at[:, far], out_up_far),
            )
        ]

    def gate_to_z(s):
        for copy in flying["grads"]:
            copy.wait()
        flying["gate_z", s] = send(out_gate_far.at[both(s)], out_gate_z.at[both(s)], z_peer)

    def to_attention(s):
        value = reduced(2, s)
        grad = own_cotangent[mine(s), :].astype(f32) + value
        out_grad_hidden[mine(s), :] = grad
        normed = own_normed[mine(s), :]
        gain = jnp.sum(grad * normed, axis=0, keepdims=True)
        out_gain[0:1, :] = gain if s == 0 else out_gain[0:1, :] + gain
        factor = own_factor[mine(s), 0:1]
        attn_keep[own(s), :] = norm_back(grad * g_attn[...], normed, factor).astype(bf16)
        share(attn_keep, s)

    def attended_grad(s):
        flying["share", s].wait()
        keep_out(attn_keep.at[both(s)], out_attn.at[both(s)])
        heads_keep[both(s), :] = dot_nt(attn_keep[both(s), :], w_out[...]).astype(bf16)
        for d in range(1, line):
            flying["grads", s, d] = send(
                heads_keep.at[both(s), head(d)], out_grads.at[d, both(s)], ahead[d]
            )
        keep_out(heads_keep.at[both(s), head(0)], out_grads.at[0, both(s)])

    project_out(0)
    project_out(1)
    for load in loads[1:]:
        load.wait()
    after_attention(0)
    forward(0)
    after_attention(1)
    forward(1)
    turn_point(0)
    backward(0)
    turn_point(1)
    backward(1)
    gate_to_z(1)
    for s in range(2):
        forward_core("hidden", s, out_hidden_z)
    to_attention(0)
    attended_grad(0)
    to_attention(1)
    attended_grad(1)
    for s in range(2):
        flying["act", s].wait()
        flying["output", s].wait()
        forward_core("mlp", s, out_mlp_x)
    for s in range(2):
        flying["tokens_core", s].wait()
        flying["gate_z", s].wait()
        flying["hidden_core", s].wait()
        flying["mlp_core", s].wait()
        for d in range(1, line):
            flying["grads", s, d].wait()
    for copy in local:
        copy.wait()


def block(pieces, w_out, g_attn, g_mlp, tokens, cotangent, w_gate, w_up, w_down):
    _, rows, width = pieces.shape
    columns = line * width
    depth, units = w_gate.shape
    half = rows // 2
    quarter = rows // 4
    f32 = jnp.float32
    bf16 = jnp.bfloat16
    wide = jax.ShapeDtypeStruct((rows, depth), bf16)
    tall = jax.ShapeDtypeStruct((rows, units), bf16)
    any_spec = pl.BlockSpec(memory_space=pl.ANY)
    return pl.pallas_call(
        block_kernel,
        out_shape=[
            jax.ShapeDtypeStruct((rows, columns), bf16),
            wide,
            wide,
            wide,
            wide,
            tall,
            jax.ShapeDtypeStruct((rows, units // 2), bf16),
            wide,
            wide,
            tall,
            jax.ShapeDtypeStruct((rows, units // 2), bf16),
            jax.ShapeDtypeStruct((rows, units // 2), bf16),
            tall,
            jax.ShapeDtypeStruct((rows, units // 2), bf16),
            wide,
            jax.ShapeDtypeStruct((line, rows, width), bf16),
            jax.ShapeDtypeStruct((half, depth), f32),
            jax.ShapeDtypeStruct((2, depth), f32),
        ],
        in_specs=vmem_specs(4) + [any_spec] * 5,
        out_specs=[any_spec] * 16 + vmem_specs(2),
        scratch_shapes=[
            pltpu.VMEM((depth, units), bf16),
            pltpu.VMEM((depth, units), bf16),
            pltpu.VMEM((units, depth), bf16),
            pltpu.VMEM((rows, units), bf16),
            pltpu.VMEM((rows, units), bf16),
            pltpu.VMEM((rows, units), bf16),
            pltpu.VMEM((rows, depth), bf16),
            pltpu.VMEM((rows, depth), bf16),
            pltpu.VMEM((rows, depth), bf16),
            pltpu.VMEM((half, units), bf16),
            pltpu.VMEM((half, units), bf16),
            pltpu.VMEM((half, 128), f32),
            pltpu.VMEM((half, depth), f32),
            pltpu.VMEM((half, depth), bf16),
            pltpu.VMEM((half, depth), bf16),
            pltpu.VMEM((rows, columns), bf16),
            pltpu.VMEM((rows, columns), bf16),
            pltpu.VMEM((half, depth), f32),
            pltpu.VMEM((2, quarter, depth), bf16),
            pltpu.VMEM((2, quarter, depth), bf16),
            pltpu.VMEM((2, quarter, depth), bf16),
            pltpu.VMEM((3, 2, quarter, depth), bf16),
            pltpu.SemaphoreType.DMA((56,)),
            pltpu.SemaphoreType.DMA((56,)),
            pltpu.SemaphoreType.DMA((32,)),
        ],
        compiler_params=pltpu.CompilerParams(
            vmem_limit_bytes=61800 << 10, collective_id=1, has_side_effects=True
        ),
        cost_estimate=pl.CostEstimate(flops=0, bytes_accessed=0, transcendentals=0),
    )(pieces, w_out, g_attn, g_mlp, tokens, cotangent, w_gate, w_up, w_down)


class Courier:
    def __init__(self, send_sems, recv_sems, local_sems):
        self.send_sems, self.recv_sems, self.local_sems = send_sems, recv_sems, local_sems
        self.remote, self.local = 0, 0

    def send(self, source, target, peer):
        copy = pltpu.make_async_remote_copy(
            src_ref=source,
            dst_ref=target,
            send_sem=self.send_sems.at[self.remote],
            recv_sem=self.recv_sems.at[self.remote],
            device_id=peer,
            device_id_type=pl.DeviceIdType.MESH,
        )
        self.remote += 1
        copy.start()
        return copy

    def move(self, source, target):
        copy = pltpu.make_async_copy(source, target, self.local_sems.at[self.local])
        self.local += 1
        copy.start()
        return copy


def greet(peers):
    barrier = pltpu.get_barrier_semaphore()
    for peer in peers:
        pl.semaphore_signal(barrier, inc=1, device_id=peer, device_id_type=pl.DeviceIdType.MESH)
    pl.semaphore_wait(barrier, len(peers))


class Spot:
    def __init__(self):
        mp = lax.axis_index("mp")
        spot = lax.axis_index("dp")
        self.core = lax.rem(mp, 2)
        self.x = lax.rem(spot, 2)
        self.z = spot // 2
        self.z_low = lax.rem(self.z, 2)
        self.z_high = self.z // 2
        self.core_peer = {"mp": mp + 1 - 2 * self.core}
        self.y_peer = {"mp": lax.rem(mp + 2, 4)}
        self.x_peer = {"dp": spot + 1 - 2 * self.x}
        self.z_peer = {"dp": spot + 2 - 4 * self.z_low}
        self.far_peer = {"dp": lax.rem(spot + 4, 8)}
        self.ahead = [{"dp": lax.rem(spot + 2 * d, 2 * line)} for d in range(line)]
        self.all = (self.core_peer, self.y_peer, self.x_peer) + tuple(self.ahead[1:])


class Job:
    def __init__(self, spot, over_x, first, first_far, second, second_far, cut_first):
        self.operands, self.cut_first = (first, first_far, second, second_far), cut_first
        self.tile = (first if cut_first else second).shape[1] // (line * pair)
        self.spot, self.over_x = spot, over_x
        self.side = spot.x if over_x else spot.z_low
        self.partner = spot.x_peer if over_x else spot.z_peer
        self.first_peer = spot.z_peer if over_x else spot.x_peer

    def at(self, ref, index):
        block = pl.ds(pl.multiple_of(index * self.tile, self.tile), self.tile)
        return ref.at[block, :] if self.cut_first else ref.at[:, block]

    def span(self, ref, index):
        block = pl.ds(pl.multiple_of(index * 2 * self.tile, 2 * self.tile), 2 * self.tile)
        return ref.at[block, :] if self.cut_first else ref.at[:, block]

    def term(self, index):
        first, first_far, second, second_far = self.operands
        block = pl.ds(pl.multiple_of(index * self.tile, self.tile), self.tile)
        if self.cut_first:
            return dot_t(first[:, block], second[...]) + dot_t(first_far[:, block], second_far[...])
        return dot_t(first[...], second[:, block]) + dot_t(first_far[...], second_far[:, block])

    def block_of(self, high, index):
        if self.over_x:
            return (2 * high + self.spot.z_low) * pair + index
        return (2 * high + index) * pair + self.spot.x

    def make_half(self, target, high):
        @pl.loop(0, 2)
        def _(i):
            if self.over_x:
                index = (2 * high + 1 - self.spot.z_low) * pair + i
            else:
                index = (2 * high + i) * pair + 1 - self.spot.x
            self.at(target, 2 * high + i)[...] = self.term(index).astype(jnp.bfloat16)

    def send_half(self, mail, target, remote, high):
        return mail.send(self.span(target, high), self.span(remote, high), self.first_peer)

    def start_first(self, mail, target, remote):
        copies = []
        for high in (1 - self.spot.z_high, self.spot.z_high):
            self.make_half(target, high)
            copies.append(self.send_half(mail, target, remote, high))
        return copies

    def second_term(self, arrived, target, i):
        total = self.term(self.block_of(1 - self.spot.z_high, i))
        total = total + self.at(arrived, i)[...].astype(jnp.float32)
        self.at(target, i)[...] = total.astype(jnp.bfloat16)

    def second_terms(self, arrived, target):
        @pl.loop(0, 2)
        def _(i):
            self.second_term(arrived, target, i)

    def own_term(self, side, arrived):
        total = self.term(self.block_of(self.spot.z_high, side))
        return total + self.at(arrived, side)[...].astype(jnp.float32)


def middle_kernel(
    grad_queries_in,
    near_in,
    far,
    q_raw,
    k_raw,
    factors,
    cosines,
    sines,
    gq,
    gk,
    act,
    act_x,
    mlp,
    mlp_x,
    hidden,
    hidden_z,
    gate,
    gate_z,
    up,
    up_z,
    out_own_down,
    out_r2_down,
    out_r1_gate,
    out_r1_up,
    out_r2_gate,
    out_raw_x,
    r1_down,
    out_raw,
    out_raw_own,
    out_gain,
    act_v,
    act_zv,
    mlp_v,
    mlp_zv,
    hidden_v,
    hidden_zv,
    gate_v,
    gate_zv,
    up_v,
    up_zv,
    send_down,
    send_gate,
    send_up,
    r1_v,
    r1_own,
    s2_v,
    own_v,
    r1_gate_v,
    s2_gate,
    grad_queries,
    near,
    far_in,
    sums,
    query_home,
    pair_home,
    scaled,
    raw_far,
    inner,
    inner_core,
    inner_y,
    send_sems,
    recv_sems,
    local_sems,
):
    f32 = jnp.float32
    bf16 = jnp.bfloat16
    spot = Spot()
    mail = Courier(send_sems, recv_sems, local_sems)
    count, width = cosines.shape
    columns = line * width
    depth = mlp_v.shape[1]
    half = act_v.shape[1]
    own_half = pl.ds(pl.multiple_of(spot.z_low * half, half), half)
    x_half = pl.ds(pl.multiple_of(spot.x * half, half), half)
    loads = [
        mail.move(act.at[:, x_half], act_v),
        mail.move(act_x, act_zv),
        mail.move(mlp, mlp_v),
        mail.move(mlp_x, mlp_zv),
        mail.move(hidden, hidden_v),
        mail.move(hidden_z, hidden_zv),
        mail.move(gate.at[:, own_half], gate_v),
        mail.move(gate_z, gate_zv),
        mail.move(up.at[:, own_half], up_v),
        mail.move(up_z, up_zv),
    ]
    small_loads = [mail.move(grad_queries_in, grad_queries), mail.move(near_in, near)]
    greet(spot.all)
    far_copy = mail.send(far, far_in, spot.x_peer)
    my_head = pl.ds(pl.multiple_of(spot.z * width, width), width)
    for load in small_loads:
        load.wait()
    query_copies = [
        mail.send(grad_queries.at[d], query_home.at[:, my_head], spot.ahead[line - d])
        for d in range(1, line)
    ]
    query_home[:, my_head] = grad_queries[0]
    for load in loads[:4]:
        load.wait()
    down = Job(spot, True, act_v, act_zv, mlp_v, mlp_zv, False)
    down_first = down.start_first(mail, send_down, r1_down)
    for load in loads[4:]:
        load.wait()
    gates = Job(spot, False, hidden_v, hidden_zv, gate_v, gate_zv, True)
    both = (1 - spot.z_high, spot.z_high)
    for high in both:
        gates.make_half(send_gate, high)
    far_copy.wait()
    gate_first = [gates.send_half(mail, send_gate, out_r1_gate, high) for high in both]
    sums[...] = (near[...].astype(f32) + far_in[...].astype(f32)).astype(bf16)
    pair_copies = [
        mail.send(sums.at[d], pair_home.at[:, :, my_head], spot.ahead[line - d])
        for d in range(1, line)
    ]
    pair_home[:, :, my_head] = sums[0]
    ups = Job(spot, False, hidden_v, hidden_zv, up_v, up_zv, True)
    up_first = ups.start_first(mail, send_up, out_r1_up)

    down_first[0].wait()
    down_load = mail.move(down.span(r1_down, 1 - spot.z_high), r1_v)
    down_load.wait()
    down.second_terms(r1_v, s2_v)
    second_copy = mail.send(s2_v, out_r2_down, spot.far_peer)
    gate_first[0].wait()
    gate_load = mail.move(gates.span(out_r1_gate, 1 - spot.z_high), r1_gate_v)
    gate_load.wait()
    gates.second_terms(r1_gate_v, s2_gate)
    gate_second = mail.send(s2_gate, out_r2_gate, spot.far_peer)
    for copy in query_copies + pair_copies:
        copy.wait()

    def column(row):
        return jnp.broadcast_to(row, (width, count)).T

    sources = ((query_home, None, q_raw, gq), (pair_home, 0, k_raw, gk))
    factor_columns = [column(factors[which : which + 1, :]) for which in range(2)]
    for which, (home, slot, raw, gain) in enumerate(sources):
        inner_sum = jnp.zeros((count, width), f32)
        for h in range(line):
            cut = slice(h * width, (h + 1) * width)
            part = (home[:, cut] if slot is None else home[slot, :, cut]).astype(f32)
            back = part * cosines[...] - pltpu.roll(part, width // 2, 1) * sines[...]
            normed = raw[:, cut] * factor_columns[which]
            out_gain[which : which + 1, cut] = jnp.sum(back * normed, axis=0, keepdims=True)
            value = back * gain[:, cut]
            scaled[which, :, cut] = value
            inner_sum = inner_sum + value * normed
        inner[which : which + 1, :] = jnp.sum(inner_sum.T, axis=0, keepdims=True)
    core_copy = mail.send(inner, inner_core, spot.core_peer)
    core_copy.wait()
    arrived = inner_core[...]
    quarter = count // 4
    cuts = [arrived[:, i * quarter : (i + 1) * quarter] for i in (1, 0, 3, 2)]
    chip = inner[...] + jnp.concatenate(cuts, axis=1)
    inner[...] = chip
    y_copy = mail.send(inner, inner_y, spot.y_peer)
    y_copy.wait()
    inner_all = (chip + inner_y[...]) / depth
    for which, (home, slot, raw, gain) in enumerate(sources):
        inner_column = column(inner_all[which : which + 1, :])
        for h in range(line):
            cut = slice(h * width, (h + 1) * width)
            normed = raw[:, cut] * factor_columns[which]
            value = factor_columns[which] * (scaled[which, :, cut] - normed * inner_column)
            base = which * columns + h * width
            out_raw[:, base : base + width] = value.astype(bf16)
    out_raw[:, 2 * columns :] = pair_home[1]
    part_width = columns // 2
    for which in range(3):
        cut = slice(which * part_width, (which + 1) * part_width)
        base = which * columns

        def side(index):
            start = pl.multiple_of(base + index * part_width, part_width)
            return out_raw[:, pl.ds(start, part_width)]

        out_raw_own[:, cut] = side(spot.x)
        raw_far[:, cut] = side(1 - spot.x)
    raw_copy = mail.send(raw_far, out_raw_x, spot.x_peer)

    down_first[1].wait()
    own_load = mail.move(down.span(r1_down, spot.z_high), r1_own)
    own_load.wait()

    @pl.loop(0, 2)
    def _(i):
        down.at(own_v, i)[...] = down.own_term(i, r1_own)

    keep_own = mail.move(own_v, out_own_down)
    for copy in (gate_second, gate_first[1], *up_first, raw_copy, second_copy, keep_own):
        copy.wait()


def middle(small, large):
    f32 = jnp.float32
    bf16 = jnp.bfloat16
    grad_queries, near, far, q_raw = small[:4]
    act, act_x, grad_mlp = large[:3]
    _, count, width = grad_queries.shape
    columns = line * width
    depth = grad_mlp.shape[1]
    units = act.shape[1]
    half = units // 2
    cut = depth // 2
    any_spec = pl.BlockSpec(memory_space=pl.ANY)
    shape = jax.ShapeDtypeStruct
    return pl.pallas_call(
        middle_kernel,
        in_specs=[pl.BlockSpec(memory_space=pltpu.HBM)] * 3 + vmem_specs(7) + [any_spec] * 10,
        out_specs=[any_spec] * 7 + vmem_specs(3),
        out_shape=[
            shape((half, cut // 2), f32),
            shape((half, cut // 2), bf16),
            shape((cut, half), bf16),
            shape((cut, half), bf16),
            shape((cut // 2, half), bf16),
            shape((count, 3 * columns // 2), bf16),
            shape((half, cut), bf16),
            shape((count, 3 * columns), bf16),
            shape((count, 3 * columns // 2), bf16),
            shape((2, columns), f32),
        ],
        scratch_shapes=[
            pltpu.VMEM((count, half), bf16),
            pltpu.VMEM((count, half), bf16),
            pltpu.VMEM((count, depth), bf16),
            pltpu.VMEM((count, depth), bf16),
            pltpu.VMEM((count, depth), bf16),
            pltpu.VMEM((count, depth), bf16),
            pltpu.VMEM((count, half), bf16),
            pltpu.VMEM((count, half), bf16),
            pltpu.VMEM((count, half), bf16),
            pltpu.VMEM((count, half), bf16),
            pltpu.VMEM((half, cut), bf16),
            pltpu.VMEM((cut, half), bf16),
            pltpu.VMEM((cut, half), bf16),
            pltpu.VMEM((half, cut // 2), bf16),
            pltpu.VMEM((half, cut // 2), bf16),
            pltpu.VMEM((half, cut // 2), bf16),
            pltpu.VMEM((half, cut // 2), f32),
            pltpu.VMEM((cut // 2, half), bf16),
            pltpu.VMEM((cut // 2, half), bf16),
            pltpu.VMEM(grad_queries.shape, bf16),
            pltpu.VMEM(near.shape, bf16),
            pltpu.VMEM(near.shape, bf16),
            pltpu.VMEM(near.shape, bf16),
            pltpu.VMEM((count, columns), bf16),
            pltpu.VMEM((2, count, columns), bf16),
            pltpu.VMEM((2, count, columns), f32),
            pltpu.VMEM((count, 3 * columns // 2), bf16),
            pltpu.VMEM((2, count), f32),
            pltpu.VMEM((2, count), f32),
            pltpu.VMEM((2, count), f32),
            pltpu.SemaphoreType.DMA((28,)),
            pltpu.SemaphoreType.DMA((28,)),
            pltpu.SemaphoreType.DMA((28,)),
        ],
        compiler_params=pltpu.CompilerParams(
            vmem_limit_bytes=60 << 20, collective_id=3, has_side_effects=True
        ),
    )(*small, *large)


def last_kernel(
    raw,
    raw_own,
    raw_x,
    wide,
    narrow,
    attended,
    hidden,
    hidden_z,
    gate,
    gate_z,
    up,
    up_z,
    attn,
    tokens,
    tokens_x,
    own_down,
    r2_down,
    r1_gate,
    r1_up,
    r2_gate_in,
    w_query,
    w_key,
    w_value,
    grad_hidden,
    *refs,
):
    outs, refs = refs[:13], refs[13:]
    near_down, near_gate, near_up, near_raw, near_out = outs[:5]
    far_down, far_gate, far_up, far_raw, far_out = outs[5:10]
    out_tokens, r1_raw, r1_out = outs[10:]
    out_wide, out_narrow = refs[:2]
    (
        hidden_v,
        hidden_zv,
        gate_v,
        gate_zv,
        up_v,
        up_zv,
        tokens_v,
        tokens_xv,
        attn_v,
        attn_xv,
        heads_v,
        heads_far,
        heads_xv,
        send_raw,
        send_out,
        r1_wide,
        r1_raw_v,
        r1_out_v,
        s2_up,
        s2_raw,
        s2_out,
        r2_gate,
        r2_up,
        r2_raw,
        r2_out,
        own_down_v,
        r2_down_v,
        fin_down,
        fin_gate,
        fin_up,
        fin_raw,
        fin_out,
        keep_down,
        keep_gate,
        keep_up,
        keep_raw,
        keep_out,
        weight_v,
        total,
        part_send,
        part_recv,
        y_send,
        y_recv,
        hidden_own,
        token_keep,
        wide_core,
        wide_x,
        narrow_x,
        wide_z,
        narrow_z,
        send_sems,
        recv_sems,
        local_sems,
    ) = refs[2:]
    f32 = jnp.float32
    bf16 = jnp.bfloat16
    spot = Spot()
    mail = Courier(send_sems, recv_sems, local_sems)
    rows_all = tokens_v.shape[0]
    rows = rows_all // 2
    count = rows // 2
    half = gate_v.shape[1]
    own_half = pl.ds(pl.multiple_of(spot.z_low * half, half), half)
    heads_half = heads_v.shape[1]
    side_heads = lambda side: pl.ds(pl.multiple_of(side * heads_half, heads_half), heads_half)
    own = lambda s: pl.ds(s * rows, count)
    other = lambda s: pl.ds(s * rows + count, count)
    both = lambda s: pl.ds(s * rows, rows)
    mine = lambda s: pl.ds(s * count, count)

    token_loads = [mail.move(tokens_x, tokens_xv)]
    for s in range(2):
        for part, place in ((0, spot.core), (1, 1 - spot.core)):
            start = pl.multiple_of(place * rows + s * count, count)
            target = tokens_v.at[pl.ds(s * rows + part * count, count)]
            token_loads.append(mail.move(tokens.at[pl.ds(start, count)], target))
    attn_load = mail.move(attn, attn_v)
    r1_loads = []
    first_loads = [mail.move(hidden, hidden_v), mail.move(hidden_z, hidden_zv)]
    gate_loads = [mail.move(gate.at[:, own_half], gate_v), mail.move(gate_z, gate_zv)]
    up_loads = [mail.move(up.at[:, own_half], up_v), mail.move(up_z, up_zv)]
    ups = Job(spot, False, hidden_v, hidden_zv, up_v, up_zv, True)
    gates = Job(spot, False, hidden_v, hidden_zv, gate_v, gate_zv, True)
    raws = Job(spot, True, tokens_v, tokens_xv, raw_own, raw_x, True)
    outs_job = Job(spot, True, heads_v, heads_xv, attn_v, attn_xv, False)
    gate_second = mail.move(r2_gate_in, r2_gate)
    gate_own = mail.move(gates.span(r1_gate, spot.z_high), r1_wide.at[1])
    up_second = mail.move(ups.span(r1_up, 1 - spot.z_high), r1_wide.at[2])
    up_own = mail.move(ups.span(r1_up, spot.z_high), r1_wide.at[3])
    greet(spot.all)
    wide_copy = mail.send(wide, wide_core, spot.core_peer)
    attn_load.wait()
    attn_copies = [
        mail.send(attn_v.at[own(s)], attn_xv.at[own(s)], spot.x_peer) for s in range(2)
    ]
    heads_far[...] = attended[:, side_heads(1 - spot.x)]
    heads_v[...] = attended[:, side_heads(spot.x)]
    heads_copy = mail.send(heads_far, heads_xv, spot.x_peer)
    for load in token_loads:
        load.wait()
    raw_first = raws.start_first(mail, send_raw, r1_raw)
    wide_copy.wait()
    out_wide[...] = wide[...] + wide_core[...]
    out_narrow[...] = narrow[...]
    wide_x_copy = mail.send(out_wide, wide_x, spot.x_peer)
    narrow_x_copy = mail.send(out_narrow, narrow_x, spot.x_peer)

    for load in (*first_loads, *up_loads, up_second):
        load.wait()
    ups.second_terms(r1_wide.at[2], s2_up)
    second_up = mail.send(s2_up, r2_up, spot.far_peer)

    for s in range(2):
        attn_copies[s].wait()
    attn_core = [
        mail.send(attn_xv.at[own(s)], attn_xv.at[other(s)], spot.core_peer) for s in range(2)
    ]
    for copy in attn_core:
        copy.wait()
    heads_copy.wait()
    out_first = outs_job.start_first(mail, send_out, r1_out)

    raw_first[0].wait()
    raw_load = mail.move(raws.span(r1_raw, 1 - spot.z_high), r1_raw_v.at[0])
    raw_load.wait()
    raws.second_terms(r1_raw_v.at[0], s2_raw)
    second_raw = mail.send(s2_raw, r2_raw, spot.far_peer)
    input_weights = (w_query, w_key, w_value)
    columns = w_query.shape[1]
    flying = {}
    for which, source in enumerate(input_weights):
        load = mail.move(source, weight_v)
        load.wait()
        for s in range(2):
            term = dot_nt(raw[both(s), which * columns : (which + 1) * columns], weight_v[...])
            total[both(s), :] = term if which == 0 else total[both(s), :] + term
    for s in range(2):
        part_send[s] = total[other(s), :].astype(bf16)
        flying["core", s] = mail.send(part_send.at[s], part_recv.at[s], spot.core_peer)
    hidden_load = mail.move(grad_hidden, hidden_own)
    for s in range(2):
        flying["core", s].wait()
        y_send[s] = (total[own(s), :] + part_recv[s].astype(f32)).astype(bf16)
        flying["y", s] = mail.send(y_send.at[s], y_recv.at[s], spot.y_peer)

    wide_x_copy.wait()
    narrow_x_copy.wait()
    out_wide[...] = out_wide[...] + wide_x[...]
    out_narrow[...] = out_narrow[...] + narrow_x[...]
    near_copies, far_copies = [], []

    def finish(job, value_of, fin, far, keep, target):
        fin[...] = value_of(1 - job.side).astype(bf16)
        far_copies.append(mail.send(fin, far, job.partner))
        keep[...] = value_of(job.side)
        near_copies.append(mail.move(keep, target))

    down_loads = [mail.move(own_down, own_down_v), mail.move(r2_down, r2_down_v)]
    for load in down_loads:
        load.wait()
    down = outs_job
    finish(
        down,
        lambda side: down.at(own_down_v, side)[...] + down.at(r2_down_v, side)[...].astype(f32),
        fin_down,
        far_down,
        keep_down,
        near_down,
    )

    out_first[0].wait()
    out_load = mail.move(outs_job.span(r1_out, 1 - spot.z_high), r1_out_v.at[0])
    out_load.wait()
    outs_job.second_terms(r1_out_v.at[0], s2_out)
    second_out = mail.send(s2_out, r2_out, spot.far_peer)
    raw_first[1].wait()
    out_first[1].wait()
    own_loads = [
        mail.move(raws.span(r1_raw, spot.z_high), r1_raw_v.at[1]),
        mail.move(outs_job.span(r1_out, spot.z_high), r1_out_v.at[1]),
    ]
    for load in own_loads:
        load.wait()
    def final_of(job, r1_own, r2):
        return lambda side: job.own_term(side, r1_own) + job.at(r2, side)[...].astype(f32)

    for load in (*gate_loads, gate_own, gate_second):
        load.wait()
    finish(gates, final_of(gates, r1_wide.at[1], r2_gate), fin_gate, far_gate, keep_gate, near_gate)

    hidden_load.wait()
    for s in range(2):
        flying["y", s].wait()
        value = y_send[s].astype(f32) + y_recv[s].astype(f32)
        token_keep[mine(s), :] = (hidden_own[mine(s), :] + value).astype(bf16)
        home = pl.ds(pl.multiple_of(spot.core * rows + s * count, count), count)
        flying["keep", s] = mail.move(token_keep.at[mine(s)], out_tokens.at[home])
        flying["tokens", s] = mail.send(
            token_keep.at[mine(s)], out_tokens.at[home], spot.core_peer
        )
    gain_copies = []
    for d in range(1, line):
        gain_copies.append(mail.send(out_wide, wide_z.at[d - 1], spot.ahead[d]))
        gain_copies.append(mail.send(out_narrow, narrow_z.at[d - 1], spot.ahead[d]))

    up_own.wait()
    second_up.wait()
    finish(ups, final_of(ups, r1_wide.at[3], r2_up), fin_up, far_up, keep_up, near_up)
    second_raw.wait()
    finish(raws, final_of(raws, r1_raw_v.at[1], r2_raw), fin_raw, far_raw, keep_raw, near_raw)
    second_out.wait()
    finish(
        outs_job, final_of(outs_job, r1_out_v.at[1], r2_out), fin_out, far_out, keep_out, near_out
    )
    for copy in gain_copies:
        copy.wait()
    for d in range(1, line):
        out_wide[...] = out_wide[...] + wide_z[d - 1]
        out_narrow[...] = out_narrow[...] + narrow_z[d - 1]
    for s in range(2):
        flying["keep", s].wait()
        flying["tokens", s].wait()
    for copy in near_copies + far_copies:
        copy.wait()


def last(small, large):
    f32 = jnp.float32
    bf16 = jnp.bfloat16
    raw, raw_own, raw_x, wide, narrow, attended = small
    hidden, gate = large[0], large[2]
    count, depth = hidden.shape
    units = gate.shape[1]
    half = units // 2
    block = depth // (line * pair)
    columns = attended.shape[1]
    heads_half = columns // 2
    raw_half = raw_own.shape[1]
    rows = count // 2
    any_spec = pl.BlockSpec(memory_space=pl.ANY)
    shape = jax.ShapeDtypeStruct
    vmem = lambda *size: pltpu.VMEM(size, bf16)
    wide_vmem = lambda *size: pltpu.VMEM(size, f32)
    return pl.pallas_call(
        last_kernel,
        in_specs=vmem_specs(6) + [any_spec] * len(large),
        out_specs=[any_spec] * 13 + vmem_specs(2),
        out_shape=[
            shape((half, block), f32),
            shape((block, half), f32),
            shape((block, half), f32),
            shape((block, raw_half), f32),
            shape((heads_half, block), f32),
            shape((half, block), bf16),
            shape((block, half), bf16),
            shape((block, half), bf16),
            shape((block, raw_half), bf16),
            shape((heads_half, block), bf16),
            shape((count, depth), bf16),
            shape((line * block, raw_half), bf16),
            shape((heads_half, line * block), bf16),
            shape(wide.shape, f32),
            shape(narrow.shape, f32),
        ],
        scratch_shapes=[
            vmem(count, depth),
            vmem(count, depth),
            vmem(count, half),
            vmem(count, half),
            vmem(count, half),
            vmem(count, half),
            vmem(count, depth),
            vmem(count, depth),
            vmem(count, depth),
            vmem(count, depth),
            vmem(count, heads_half),
            vmem(count, heads_half),
            vmem(count, heads_half),
            vmem(line * block, raw_half),
            vmem(heads_half, line * block),
            vmem(4, 2 * block, half),
            vmem(2, 2 * block, raw_half),
            vmem(2, heads_half, 2 * block),
            vmem(2 * block, half),
            vmem(2 * block, raw_half),
            vmem(heads_half, 2 * block),
            vmem(2 * block, half),
            vmem(2 * block, half),
            vmem(2 * block, raw_half),
            vmem(heads_half, 2 * block),
            wide_vmem(half, 2 * block),
            vmem(half, 2 * block),
            vmem(half, block),
            vmem(block, half),
            vmem(block, half),
            vmem(block, raw_half),
            vmem(heads_half, block),
            wide_vmem(half, block),
            wide_vmem(block, half),
            wide_vmem(block, half),
            wide_vmem(block, raw_half),
            wide_vmem(heads_half, block),
            vmem(depth, columns),
            wide_vmem(count, depth),
            vmem(2, rows // 2, depth),
            vmem(2, rows // 2, depth),
            vmem(2, rows // 2, depth),
            vmem(2, rows // 2, depth),
            wide_vmem(rows, depth),
            vmem(rows, depth),
            wide_vmem(*wide.shape),
            wide_vmem(*wide.shape),
            wide_vmem(*narrow.shape),
            wide_vmem(line - 1, *wide.shape),
            wide_vmem(line - 1, *narrow.shape),
            pltpu.SemaphoreType.DMA((48,)),
            pltpu.SemaphoreType.DMA((48,)),
            pltpu.SemaphoreType.DMA((40,)),
        ],
        compiler_params=pltpu.CompilerParams(
            vmem_limit_bytes=61800 << 10, collective_id=4, has_side_effects=True
        ),
    )(*small, *large)


def join_kernel(*refs):
    sources, out_output, out_tokens = refs[:12], refs[12], refs[13]
    outs, parts, sems = refs[14:21], refs[21:33], refs[33]
    nears, fars = parts[:5], parts[5:10]
    loads = [
        pltpu.make_async_copy(source, part, sems.at[i])
        for i, (source, part) in enumerate(zip(sources, parts))
    ]
    for load in loads[10:] + loads[:10]:
        load.start()
    copies = []
    for i, target in ((10, out_output), (11, out_tokens)):
        loads[i].wait()
        copies.append(pltpu.make_async_copy(parts[i], target, sems.at[i + 2]))
        copies[-1].start()
    for load in loads[:10]:
        load.wait()
    spot = lax.axis_index("dp")
    x = lax.rem(spot, 2)
    z_low = lax.rem(spot // 2, 2)

    def place(out, near, far, side, axis):
        size = near.shape[axis]
        for value, index in ((near, side), (far.astype(jnp.float32), 1 - side)):
            cut = pl.ds(pl.multiple_of(index * size, size), size)
            if axis == 0:
                out[cut, :] = value
            else:
                out[:, cut] = value

    place(outs[6], nears[0][...], fars[0][...], x, 0)
    place(outs[4], nears[1][...], fars[1][...], z_low, 1)
    place(outs[5], nears[2][...], fars[2][...], z_low, 1)
    width = nears[3].shape[1] // 3
    for which in range(3):
        cut = slice(which * width, (which + 1) * width)
        place(outs[which], nears[3][:, cut], fars[3][:, cut], x, 1)
    place(outs[3], nears[4][...], fars[4][...], x, 0)
    for copy in copies:
        copy.wait()


def join(nears, fars, output, tokens):
    f32 = jnp.float32
    shape = jax.ShapeDtypeStruct
    any_spec = pl.BlockSpec(memory_space=pl.ANY)
    far_spec = pl.BlockSpec(memory_space=pltpu.HBM)
    down, gate, up, raw, out = [part.shape for part in nears]
    third = shape((raw[0], 2 * raw[1] // 3), f32)
    return pl.pallas_call(
        join_kernel,
        in_specs=[far_spec] * 12,
        out_specs=[any_spec] * 2 + vmem_specs(7),
        out_shape=[
            shape(output.shape, output.dtype),
            shape(tokens.shape, tokens.dtype),
            third,
            third,
            third,
            shape((2 * out[0], out[1]), f32),
            shape((gate[0], 2 * gate[1]), f32),
            shape((up[0], 2 * up[1]), f32),
            shape((2 * down[0], down[1]), f32),
        ],
        scratch_shapes=[pltpu.VMEM(part.shape, part.dtype) for part in (*nears, *fars, output, tokens)]
        + [pltpu.SemaphoreType.DMA((14,))],
        compiler_params=pltpu.CompilerParams(vmem_limit_bytes=60 << 20),
    )(*nears, *fars, output, tokens)


def on_device_lines(
    tokens,
    cotangent,
    doc_ids,
    row_ids,
    offsets,
    w_query,
    w_key,
    w_value,
    w_output,
    w_gate,
    w_up,
    w_down,
    gain_query,
    gain_key,
    gain_attn,
    gain_mlp,
):
    f32 = jnp.float32
    bf16 = jnp.bfloat16
    row_count, model_width = tokens.shape
    heads_here, head_width = gain_query.shape
    local_width = heads_here * head_width
    half_rows = row_count // 2
    key_rows = row_count * line * pair
    spot = lax.axis_index("dp")
    z, x = spot // pair, lax.rem(spot, pair)
    z_high, z_low = z // 2, lax.rem(z, 2)
    core = lax.rem(lax.axis_index("mp"), 2)
    place = jnp.stack([core, z, z_low, z_high, x]).astype(jnp.int32)

    quarter = row_count // 4

    def own_rows(value):
        return lax.dynamic_slice_in_dim(value, core * half_rows, half_rows, 0)

    def other_rows(value):
        return lax.dynamic_slice_in_dim(value, (1 - core) * half_rows, half_rows, 0)

    def reorder(value):
        return join_parts(own_rows(value), other_rows(value))

    def restore(own, other):
        whole = jnp.zeros((row_count,) + own.shape[1:], own.dtype)
        whole = lax.dynamic_update_slice_in_dim(whole, own, core * half_rows, 0)
        return lax.dynamic_update_slice_in_dim(whole, other, (1 - core) * half_rows, 0)

    def half_of(value, side):
        width = value.shape[1] // 2
        return lax.dynamic_slice_in_dim(value, side * width, width, 1)

    positions = reorder(offsets[0] + jnp.arange(row_count, dtype=jnp.int32))
    labels = reorder(row_ids[0] * key_rows + doc_ids)
    freqs = rope_base ** (-jnp.arange(0, head_width // 2, dtype=f32) * 2.0 / head_width)
    angles = positions.astype(f32)[:, None] * freqs[None, :]
    cosines, sines = jnp.cos(angles), jnp.sin(angles)
    cosines = jnp.concatenate([cosines, cosines], axis=1)
    sines = jnp.concatenate([-sines, sines], axis=1)
    g_query = gain_query.reshape(1, local_width)
    g_key = gain_key.reshape(1, local_width)
    spots = jnp.stack([labels, positions]).astype(f32)
    queries, pairs, notes, q_raw, k_raw = project(
        tokens, w_query, w_key, w_value, g_query, g_key, cosines, sines, spots
    )
    factors = notes[0, :2]
    codes = notes[:, 2, :].astype(jnp.int32) * key_rows + notes[:, 3, :].astype(jnp.int32)
    lows = notes[:line, 2, :].astype(jnp.int32) * key_rows
    live = (
        (jnp.min(codes, axis=1)[None, :] <= jnp.max(codes[:line], axis=1)[:, None])
        & (jnp.max(codes, axis=1)[None, :] >= jnp.min(lows, axis=1)[:, None])
    ).astype(jnp.int32)

    turned, log_total, queries_n, keys_n, code_columns, code_rows, attended_out = attend(
        key_rows, live, notes, queries, pairs
    )

    def gather_heads(home):
        twice = jnp.concatenate(home + home, axis=1)
        return lax.dynamic_slice_in_dim(
            twice, lax.rem(line - z, line) * head_width, local_width, 1
        )

    def send_home(pieces):
        return [pieces[0]] + [line_shift(pieces[d], line - d) for d in range(1, line)]

    tokens_in = reorder(tokens)
    g_attn = gain_attn.reshape(1, model_width)
    g_mlp = gain_mlp.reshape(1, model_width)
    (
        attended_low,
        tokens_x,
        output,
        hidden_low,
        hidden_z,
        act_low,
        act_x,
        grad_mlp,
        grad_mlp_x,
        grad_gate,
        _,
        grad_gate_z,
        grad_up,
        grad_up_far,
        grad_attn,
        grads,
        grad_hidden,
        wide_gains,
    ) = block(
        attended_out, w_output, g_attn, g_mlp, tokens, cotangent, w_gate, w_up, w_down
    )
    grad_up_z = line_flip(grad_up_far, 1)
    back = attend_back(
        live, code_columns, code_rows, queries_n, keys_n, pairs, turned, log_total, grads
    )
    (
        own_down,
        r2_down,
        r1_gate,
        r1_up,
        r2_gate,
        raw_x,
        _,
        raw,
        raw_own,
        narrow_gains,
    ) = middle(
        (*back, q_raw, k_raw, factors, cosines, sines, g_query, g_key),
        (
            act_low,
            act_x,
            grad_mlp,
            grad_mlp_x,
            hidden_low,
            hidden_z,
            grad_gate,
            grad_gate_z,
            grad_up,
            grad_up_z,
        ),
    )
    results = last(
        (raw, raw_own, raw_x, wide_gains, narrow_gains, attended_low),
        (
            hidden_low,
            hidden_z,
            grad_gate,
            grad_gate_z,
            grad_up,
            grad_up_z,
            grad_attn,
            tokens,
            tokens_x,
            own_down,
            r2_down,
            r1_gate,
            r1_up,
            r2_gate,
            w_query,
            w_key,
            w_value,
            grad_hidden,
        ),
    )
    joined = join(results[:5], results[5:10], output, results[10])
    wide, narrow = results[13:]
    gains = jnp.concatenate([wide.reshape(2 * model_width), narrow.reshape(2 * local_width)])
    piece = head_width // (line * pair)

    def gain_piece(start, rows):
        part = gains[start : start + rows * head_width].reshape(rows, head_width)
        return lax.dynamic_slice_in_dim(part, spot * piece, piece, 1)

    all_heads = model_width // head_width
    return (
        *joined,
        gain_piece(2 * model_width, heads_here),
        gain_piece(2 * model_width + local_width, heads_here),
        gain_piece(0, all_heads),
        gain_piece(model_width, all_heads),
    )


def solution(mesh):
    tuned = mesh.shape["dp"] == line * pair and mesh.shape["mp"] == 4
    body = on_device_lines if tuned else on_device_general
    return jax.shard_map(
        body,
        mesh=mesh,
        in_specs=(
            P("dp", None),
            P("dp", None),
            P("dp"),
            P("dp"),
            P("dp"),
            P(None, "mp"),
            P(None, "mp"),
            P(None, "mp"),
            P("mp", None),
            P(None, "mp"),
            P(None, "mp"),
            P("mp", None),
            P("mp", None),
            P("mp", None),
            P(),
            P(),
        ),
        out_specs=(
            P("dp", None),
            P("dp", None),
            P("dp", "mp"),
            P("dp", "mp"),
            P("dp", "mp"),
            P("mp", "dp"),
            P("dp", "mp"),
            P("dp", "mp"),
            P("mp", "dp"),
            P("mp", "dp"),
            P("mp", "dp"),
            P(None, "dp"),
            P(None, "dp"),
        ),
        check_vma=False,
    )
```

```python
import functools
import math

import jax
import jax.numpy as jnp
from jax import lax
from jax.experimental import pallas as pl
from jax.experimental.pallas import tpu as pltpu
from jax.sharding import PartitionSpec as P

epsilon = 1e-06
rope_base = 500000.0
masked_score = -1e30


def rope_tables(positions, head_width):
    freqs = rope_base ** (-jnp.arange(0, head_width // 2, dtype=jnp.float32) * 2.0 / head_width)
    angles = positions.astype(jnp.float32)[:, None] * freqs[None, :]
    return (jnp.cos(angles)[:, None, :], jnp.sin(angles)[:, None, :])


def rotate(values, cosines, sines):
    half = values.shape[-1] // 2
    first = values[..., :half]
    second = values[..., half:]
    return jnp.concatenate(
        [first * cosines - second * sines, second * cosines + first * sines], axis=-1
    )


def norm_back(grad_normed, normed, factor):
    return factor * (grad_normed - normed * jnp.mean(grad_normed * normed, axis=-1, keepdims=True))


def on_device_general(
    tokens,
    cotangent,
    doc_ids,
    row_ids,
    offsets,
    w_query,
    w_key,
    w_value,
    w_output,
    w_gate,
    w_up,
    w_down,
    gain_query,
    gain_key,
    gain_attn,
    gain_mlp,
):
    f32 = jnp.float32
    bf16 = jnp.bfloat16
    row_count = tokens.shape[0]
    model_width = tokens.shape[1]
    heads_here = gain_query.shape[0]
    head_width = gain_query.shape[1]
    local_width = heads_here * head_width
    groups = lax.axis_size("dp")
    key_rows = row_count * groups
    block_rows = min(key_rows, row_count * max(1, 512 // row_count))
    block_count = key_rows // block_rows
    score_scale = 1.0 / math.sqrt(head_width)
    positions = offsets[0] + jnp.arange(row_count, dtype=jnp.int32)
    labels = row_ids[0] * key_rows + doc_ids
    cosines, sines = rope_tables(positions, head_width)
    q_raw = jnp.dot(tokens, w_query, preferred_element_type=f32)
    k_raw = jnp.dot(tokens, w_key, preferred_element_type=f32)
    v_raw = jnp.dot(tokens, w_value, preferred_element_type=f32)
    squares = lax.psum(
        jnp.stack([jnp.sum(q_raw * q_raw, axis=1), jnp.sum(k_raw * k_raw, axis=1)]), "mp"
    )
    q_factor = lax.rsqrt(squares[0] / model_width + epsilon)[:, None]
    k_factor = lax.rsqrt(squares[1] / model_width + epsilon)[:, None]
    g_query = gain_query.reshape(local_width)
    g_key = gain_key.reshape(local_width)
    q_normed = q_raw * q_factor
    k_normed = k_raw * k_factor
    queries = rotate(
        (q_normed * g_query).reshape(row_count, heads_here, head_width), cosines, sines
    ).astype(bf16)
    keys_low = rotate(
        (k_normed * g_key).reshape(row_count, heads_here, head_width), cosines, sines
    ).astype(bf16)
    values_low = v_raw.astype(bf16)
    all_keys, all_values, all_labels, all_positions = (
        lax.all_gather(keys_low.reshape(row_count, local_width), "dp", axis=0, tiled=True),
        lax.all_gather(values_low, "dp", axis=0, tiled=True),
        lax.all_gather(labels, "dp", axis=0, tiled=True),
        lax.all_gather(positions, "dp", axis=0, tiled=True),
    )
    key_blocks = all_keys.reshape(block_count, block_rows, heads_here, head_width)
    value_blocks = all_values.reshape(block_count, block_rows, heads_here, head_width)
    label_blocks = all_labels.reshape(block_count, block_rows)
    position_blocks = all_positions.reshape(block_count, block_rows)
    scanned = (key_blocks, value_blocks, label_blocks, position_blocks)
    low_label = jnp.min(labels)
    high_label = jnp.max(labels)

    def scores_of(key_block, label_block, position_block):
        scores = (
            jnp.einsum("qhd,khd->hqk", queries, key_block, preferred_element_type=f32) * score_scale
        )
        allowed = (labels[:, None] == label_block[None, :]) & (
            positions[:, None] >= position_block[None, :]
        )
        return (scores, allowed[None])

    def touches(label_block):
        return (jnp.max(label_block) >= low_label) & (jnp.min(label_block) <= high_label)

    def max_step(carry, blocks_in):
        key_block, value_block, label_block, position_block = blocks_in

        def max_live_block(state):
            running, totals = state
            scores, allowed = scores_of(key_block, label_block, position_block)
            highest = jnp.maximum(
                running, jnp.max(jnp.where(allowed, scores, masked_score), axis=2)
            )
            weights = jnp.where(allowed, jnp.exp(scores - highest[:, :, None]), 0.0)
            return (highest, totals * jnp.exp(running - highest) + jnp.sum(weights, axis=2))

        return (lax.cond(touches(label_block), max_live_block, lambda state: state, carry), None)

    start_state = (
        jnp.full((heads_here, row_count), masked_score, f32),
        jnp.zeros((heads_here, row_count), f32),
    )
    (running_max, running_total), _ = lax.scan(max_step, start_state, scanned)
    log_total = running_max + jnp.log(running_total)

    def value_step(accum, blocks_in):
        key_block, value_block, label_block, position_block = blocks_in

        def value_live_block(current):
            scores, allowed = scores_of(key_block, label_block, position_block)
            probs_low = jnp.where(allowed, jnp.exp(scores - log_total[:, :, None]), 0.0).astype(
                bf16
            )
            return current + jnp.einsum(
                "hqk,khd->qhd", probs_low, value_block, preferred_element_type=f32
            )

        return (
            lax.cond(touches(label_block), value_live_block, lambda current: current, accum),
            None,
        )

    attended, _ = lax.scan(value_step, jnp.zeros((row_count, heads_here, head_width), f32), scanned)
    attended_low = attended.reshape(row_count, local_width).astype(bf16)
    attn_sum = lax.psum(
        jnp.dot(attended_low, w_output, preferred_element_type=f32).astype(jnp.bfloat16), "mp"
    ).astype(jnp.float32)
    attn_factor = lax.rsqrt(jnp.mean(attn_sum * attn_sum, axis=1, keepdims=True) + epsilon)
    attn_normed = attn_sum * attn_factor
    g_attn = gain_attn.reshape(model_width)
    hidden = tokens.astype(f32) + attn_normed * g_attn
    hidden_low = hidden.astype(bf16)
    gate_val = jnp.dot(hidden_low, w_gate, preferred_element_type=f32)
    up_val = jnp.dot(hidden_low, w_up, preferred_element_type=f32)
    sigmoid_gate = jax.nn.sigmoid(gate_val)
    silu_gate = gate_val * sigmoid_gate
    act_low = (silu_gate * up_val).astype(bf16)
    mlp_sum = lax.psum(
        jnp.dot(act_low, w_down, preferred_element_type=f32).astype(jnp.bfloat16), "mp"
    ).astype(jnp.float32)
    mlp_factor = lax.rsqrt(jnp.mean(mlp_sum * mlp_sum, axis=1, keepdims=True) + epsilon)
    mlp_normed = mlp_sum * mlp_factor
    g_mlp = gain_mlp.reshape(model_width)
    output = (hidden + mlp_normed * g_mlp).astype(bf16)
    grad_out = cotangent.astype(f32)
    grad_gain_mlp = jnp.sum(grad_out * mlp_normed, axis=0)
    grad_mlp = norm_back(grad_out * g_mlp, mlp_normed, mlp_factor).astype(bf16)
    grad_w_down = jnp.einsum("tf,td->fd", act_low, grad_mlp, preferred_element_type=f32)
    grad_act = jnp.einsum("td,fd->tf", grad_mlp, w_down, preferred_element_type=f32)
    slope = sigmoid_gate * (1.0 + gate_val * (1.0 - sigmoid_gate))
    grad_gate = (grad_act * up_val * slope).astype(bf16)
    grad_up = (grad_act * silu_gate).astype(bf16)
    branch_grad = jnp.einsum(
        "tf,df->td", grad_gate, w_gate, preferred_element_type=f32
    ) + jnp.einsum("tf,df->td", grad_up, w_up, preferred_element_type=f32)
    grad_hidden = grad_out + lax.psum(branch_grad.astype(jnp.bfloat16), "mp").astype(jnp.float32)
    grad_gain_attn = jnp.sum(grad_hidden * attn_normed, axis=0)
    grad_attn = norm_back(grad_hidden * g_attn, attn_normed, attn_factor).astype(bf16)
    grad_w_output = jnp.einsum("tc,td->cd", attended_low, grad_attn, preferred_element_type=f32)
    grad_attended = (
        jnp.einsum("td,cd->tc", grad_attn, w_output, preferred_element_type=f32)
        .astype(bf16)
        .reshape(row_count, heads_here, head_width)
    )
    delta = jnp.sum(grad_attended.astype(f32) * attended, axis=2).T

    def grad_step(grad_q, blocks_in):
        key_block, value_block, label_block, position_block = blocks_in

        def grad_live_block(current):
            scores, allowed = scores_of(key_block, label_block, position_block)
            probs = jnp.where(allowed, jnp.exp(scores - log_total[:, :, None]), 0.0)
            grad_probs = jnp.einsum(
                "qhd,khd->hqk", grad_attended, value_block, preferred_element_type=f32
            )
            grad_scores = (probs * (grad_probs - delta[:, :, None])).astype(bf16)
            value_term = jnp.einsum(
                "hqk,qhd->khd", probs.astype(bf16), grad_attended, preferred_element_type=f32
            )
            key_term = jnp.einsum("hqk,qhd->khd", grad_scores, queries, preferred_element_type=f32)
            updated = current + jnp.einsum(
                "hqk,khd->qhd", grad_scores, key_block, preferred_element_type=f32
            )
            return (updated, (key_term, value_term))

        def skip_block(current):
            nothing = jnp.zeros((block_rows, heads_here, head_width), f32)
            return (current, (nothing, nothing))

        return lax.cond(touches(label_block), grad_live_block, skip_block, grad_q)

    grad_queries, (key_terms, value_terms) = lax.scan(
        grad_step, jnp.zeros((row_count, heads_here, head_width), f32), scanned
    )
    grad_keys, grad_values = (
        lax.psum_scatter(
            (key_terms.reshape(key_rows, local_width) * score_scale).astype(jnp.bfloat16),
            "dp",
            scatter_dimension=0,
            tiled=True,
        ).astype(jnp.float32),
        lax.psum_scatter(
            value_terms.reshape(key_rows, local_width).astype(jnp.bfloat16),
            "dp",
            scatter_dimension=0,
            tiled=True,
        ).astype(jnp.float32),
    )
    grad_values_low = grad_values.astype(bf16)
    back_q = rotate(grad_queries * score_scale, cosines, -sines).reshape(row_count, local_width)
    back_k = rotate(grad_keys.reshape(row_count, heads_here, head_width), cosines, -sines).reshape(
        row_count, local_width
    )
    grad_gain_query = jnp.sum(back_q * q_normed, axis=0).reshape(heads_here, head_width)
    grad_gain_key = jnp.sum(back_k * k_normed, axis=0).reshape(heads_here, head_width)
    scaled_q = back_q * g_query
    scaled_k = back_k * g_key
    inner = lax.psum(
        jnp.stack([jnp.sum(scaled_q * q_normed, axis=1), jnp.sum(scaled_k * k_normed, axis=1)]),
        "mp",
    )
    grad_q_raw = (q_factor * (scaled_q - q_normed * inner[0][:, None] / model_width)).astype(bf16)
    grad_k_raw = (k_factor * (scaled_k - k_normed * inner[1][:, None] / model_width)).astype(bf16)
    input_term = (
        jnp.einsum("tc,dc->td", grad_q_raw, w_query, preferred_element_type=f32)
        + jnp.einsum("tc,dc->td", grad_k_raw, w_key, preferred_element_type=f32)
        + jnp.einsum("tc,dc->td", grad_values_low, w_value, preferred_element_type=f32)
    )
    grad_tokens = (
        grad_hidden + lax.psum(input_term.astype(jnp.bfloat16), "mp").astype(jnp.float32)
    ).astype(bf16)
    local_w_query = jnp.einsum("td,tc->dc", tokens, grad_q_raw, preferred_element_type=f32)
    local_w_key = jnp.einsum("td,tc->dc", tokens, grad_k_raw, preferred_element_type=f32)
    local_w_value = jnp.einsum("td,tc->dc", tokens, grad_values_low, preferred_element_type=f32)
    local_w_gate = jnp.einsum("td,tf->df", hidden_low, grad_gate, preferred_element_type=f32)
    local_w_up = jnp.einsum("td,tf->df", hidden_low, grad_up, preferred_element_type=f32)
    grad_w_query, grad_w_key, grad_w_value, grad_w_gate, grad_w_up = (
        lax.psum_scatter(
            local_w_query.astype(jnp.bfloat16), "dp", scatter_dimension=0, tiled=True
        ).astype(jnp.float32),
        lax.psum_scatter(
            local_w_key.astype(jnp.bfloat16), "dp", scatter_dimension=0, tiled=True
        ).astype(jnp.float32),
        lax.psum_scatter(
            local_w_value.astype(jnp.bfloat16), "dp", scatter_dimension=0, tiled=True
        ).astype(jnp.float32),
        lax.psum_scatter(
            local_w_gate.astype(jnp.bfloat16), "dp", scatter_dimension=0, tiled=True
        ).astype(jnp.float32),
        lax.psum_scatter(
            local_w_up.astype(jnp.bfloat16), "dp", scatter_dimension=0, tiled=True
        ).astype(jnp.float32),
    )
    summed_out, summed_down, summed_gq, summed_gk, summed_ga, summed_gm = (
        lax.psum_scatter(
            grad_w_output.astype(jnp.bfloat16), "dp", scatter_dimension=1, tiled=True
        ).astype(jnp.float32),
        lax.psum_scatter(
            grad_w_down.astype(jnp.bfloat16), "dp", scatter_dimension=1, tiled=True
        ).astype(jnp.float32),
        lax.psum_scatter(
            grad_gain_query.astype(jnp.bfloat16), "dp", scatter_dimension=1, tiled=True
        ).astype(jnp.float32),
        lax.psum_scatter(
            grad_gain_key.astype(jnp.bfloat16), "dp", scatter_dimension=1, tiled=True
        ).astype(jnp.float32),
        lax.psum_scatter(
            grad_gain_attn.reshape(gain_attn.shape).astype(jnp.bfloat16),
            "dp",
            scatter_dimension=1,
            tiled=True,
        ).astype(jnp.float32),
        lax.psum_scatter(
            grad_gain_mlp.reshape(gain_mlp.shape).astype(jnp.bfloat16),
            "dp",
            scatter_dimension=1,
            tiled=True,
        ).astype(jnp.float32),
    )
    return (
        output,
        grad_tokens,
        grad_w_query,
        grad_w_key,
        grad_w_value,
        summed_out,
        grad_w_gate,
        grad_w_up,
        summed_down,
        summed_gq,
        summed_gk,
        summed_ga,
        summed_gm,
    )


line = 4
pair = 2
low_score = -1e30
start_max = -1e20
big_vmem = 56 << 20


def line_shift(value, step):
    moves = [
        (z * pair + x, ((z + step) % line) * pair + x) for z in range(line) for x in range(pair)
    ]
    return lax.ppermute(value, "dp", moves)


def line_flip(value, bit):
    return lax.ppermute(
        value, "dp", [(z * pair + x, (z ^ bit) * pair + x) for z in range(line) for x in range(pair)]
    )


def x_swap(value):
    return lax.ppermute(value, "dp", [(i, i ^ 1) for i in range(line * pair)])


def core_swap(value):
    return lax.ppermute(value, "mp", [(i, i ^ 1) for i in range(4)])


def y_swap(value):
    return lax.ppermute(value, "mp", [(i, i ^ 2) for i in range(4)])


def flip_cores(value, axis):
    quarter = value.shape[axis] // 4
    cuts = [lax.slice_in_dim(value, i * quarter, (i + 1) * quarter, axis=axis) for i in (1, 0, 3, 2)]
    return jnp.concatenate(cuts, axis=axis)


def token_sum(value):
    value = value + flip_cores(core_swap(value), 1)
    return value + y_swap(value)


def own_part(value):
    quarter = value.shape[0] // 4
    return jnp.concatenate([value[:quarter], value[2 * quarter : 3 * quarter]], axis=0)


def other_part(value):
    quarter = value.shape[0] // 4
    return jnp.concatenate([value[quarter : 2 * quarter], value[3 * quarter :]], axis=0)


def join_parts(own, other):
    half = own.shape[0] // 2
    return jnp.concatenate([own[:half], other[:half], own[half:], other[half:]], axis=0)


def reduce_own_rows(partial_low):
    f32 = jnp.float32
    arrived = core_swap(other_part(partial_low))
    chip_sum = (own_part(partial_low).astype(f32) + arrived.astype(f32)).astype(jnp.bfloat16)
    return chip_sum.astype(f32) + y_swap(chip_sum).astype(f32)


def dot_t(first, second):
    return lax.dot_general(
        first, second, (((0,), (0,)), ((), ())), preferred_element_type=jnp.float32
    )


def dot_nt(first, second):
    return lax.dot_general(
        first, second, (((1,), (1,)), ((), ())), preferred_element_type=jnp.float32
    )


def vmem_specs(count):
    return [pl.BlockSpec(memory_space=pltpu.VMEM)] * count


def project_kernel(
    tokens,
    wq,
    wk,
    wv,
    gq,
    gk,
    cosines,
    sines,
    spots,
    out_queries,
    out_pairs,
    out_notes,
    out_q_raw,
    out_k_raw,
    rows_keep,
    query_keep,
    pair_keep,
    squares,
    squares_core,
    squares_y,
    send_sems,
    recv_sems,
    local_sems,
):
    f32 = jnp.float32
    bf16 = jnp.bfloat16
    width = cosines.shape[1]
    depth = wq.shape[0]
    rows = rows_keep.shape[0] // 2
    count = rows // 2
    mp = lax.axis_index("mp")
    spot = lax.axis_index("dp")
    core = lax.rem(mp, 2)
    x = lax.rem(spot, 2)
    z = spot // 2
    core_peer = {"mp": mp + 1 - 2 * core}
    y_peer = {"mp": lax.rem(mp + 2, 4)}
    x_peer = {"dp": spot + 1 - 2 * x}
    ahead = [{"dp": lax.rem(spot + 2 * d, 2 * line)} for d in range(line)]
    head = [lax.rem(z + d, line) for d in range(line)]
    both = lambda s: pl.ds(s * rows, rows)
    remote = []

    def send(source, target, peer):
        index = len(remote)
        copy = pltpu.make_async_remote_copy(
            src_ref=source,
            dst_ref=target,
            send_sem=send_sems.at[index],
            recv_sem=recv_sems.at[index],
            device_id=peer,
            device_id_type=pl.DeviceIdType.MESH,
        )
        remote.append(copy)
        copy.start()
        return copy

    loads = []
    for s in range(2):
        for part, place in ((0, core), (1, 1 - core)):
            start = pl.multiple_of(place * rows + s * count, count)
            copy = pltpu.make_async_copy(
                tokens.at[pl.ds(start, count)],
                rows_keep.at[pl.ds(s * rows + part * count, count)],
                local_sems.at[2 * s + part],
            )
            copy.start()
            loads.append(copy)

    barrier = pltpu.get_barrier_semaphore()
    peers = (core_peer, y_peer, x_peer, ahead[1], ahead[2], ahead[3])
    for peer in peers:
        pl.semaphore_signal(barrier, inc=1, device_id=peer, device_id_type=pl.DeviceIdType.MESH)
    pl.semaphore_wait(barrier, len(peers))

    def turned(raw, gain, s, h):
        part = raw[:, h * width : (h + 1) * width] * gain[:, h * width : (h + 1) * width]
        return (
            part * cosines[both(s), :] + pltpu.roll(part, width // 2, 1) * sines[both(s), :]
        ).astype(bf16)

    flying = {}
    for s in range(2):
        loads[2 * s].wait()
        loads[2 * s + 1].wait()
        k_raw = jnp.dot(rows_keep[both(s), :], wk[...], preferred_element_type=f32)
        out_k_raw[both(s), :] = k_raw
        squares[1:2, both(s)] = jnp.sum((k_raw * k_raw).T, axis=0, keepdims=True)
        v_raw = jnp.dot(rows_keep[both(s), :], wv[...], preferred_element_type=f32)
        for h in range(line):
            pair_keep[h, 0, both(s), :] = turned(k_raw, gk[...], s, h)
            pair_keep[h, 1, both(s), :] = v_raw[:, h * width : (h + 1) * width].astype(bf16)
        for d in (2, 1, 3):
            flying["pair", s, d] = send(
                pair_keep.at[head[d], :, both(s)], out_pairs.at[d, :, both(s)], ahead[d]
            )
        flying["far", s, 0] = send(
            pair_keep.at[z, :, both(s)], out_pairs.at[line, :, both(s)], x_peer
        )
        q_raw = jnp.dot(rows_keep[both(s), :], wq[...], preferred_element_type=f32)
        out_q_raw[both(s), :] = q_raw
        squares[0:1, both(s)] = jnp.sum((q_raw * q_raw).T, axis=0, keepdims=True)
        for h in range(line):
            query_keep[h, both(s), :] = turned(q_raw, gq[...], s, h)

    core_copy = send(squares, squares_core, core_peer)
    core_copy.wait()
    arrived = squares_core[...]
    cuts = [arrived[:, i * count : (i + 1) * count] for i in (1, 0, 3, 2)]
    chip = squares[...] + jnp.concatenate(cuts, axis=1)
    squares[...] = chip
    y_copy = send(squares, squares_y, y_peer)
    y_copy.wait()
    out_notes[0, 0:2, :] = lax.rsqrt((chip + squares_y[...]) / depth + epsilon)
    out_notes[0, 2:4, :] = spots[...]
    for d in range(1, line):
        flying["note", d] = send(out_notes.at[0], out_notes.at[d], ahead[d])
    flying["far_note", 0] = send(out_notes.at[0], out_notes.at[line], x_peer)
    for d in range(1, line):
        flying["query", d] = send(query_keep.at[head[d]], out_queries.at[d], ahead[d])
    out_queries[0] = query_keep[z]
    out_pairs[0] = pair_keep[z]
    for s in range(2):
        for d in (2, 1, 3):
            flying["pair", s, d].wait()
            flying["far", s, d] = send(
                out_pairs.at[d, :, both(s)], out_pairs.at[line + d, :, both(s)], x_peer
            )
    for d in range(1, line):
        flying["note", d].wait()
        flying["far_note", d] = send(out_notes.at[d], out_notes.at[line + d], x_peer)
    for d in range(1, line):
        flying["query", d].wait()
    for d in range(line):
        flying["far_note", d].wait()
        for s in range(2):
            flying["far", s, d].wait()


def project(tokens, wq, wk, wv, gq, gk, cosines, sines, spots):
    rows, depth = tokens.shape
    columns = wq.shape[1]
    width = columns // line
    f32 = jnp.float32
    bf16 = jnp.bfloat16
    return pl.pallas_call(
        project_kernel,
        in_specs=[pl.BlockSpec(memory_space=pl.ANY)] + vmem_specs(8),
        out_specs=vmem_specs(5),
        out_shape=[
            jax.ShapeDtypeStruct((line, rows, width), bf16),
            jax.ShapeDtypeStruct((2 * line, 2, rows, width), bf16),
            jax.ShapeDtypeStruct((2 * line, 4, rows), f32),
            jax.ShapeDtypeStruct((rows, columns), f32),
            jax.ShapeDtypeStruct((rows, columns), f32),
        ],
        scratch_shapes=[
            pltpu.VMEM((rows, depth), bf16),
            pltpu.VMEM((line, rows, width), bf16),
            pltpu.VMEM((line, 2, rows, width), bf16),
            pltpu.VMEM((2, rows), f32),
            pltpu.VMEM((2, rows), f32),
            pltpu.VMEM((2, rows), f32),
            pltpu.SemaphoreType.DMA((28,)),
            pltpu.SemaphoreType.DMA((28,)),
            pltpu.SemaphoreType.DMA((4,)),
        ],
        compiler_params=pltpu.CompilerParams(
            vmem_limit_bytes=48 << 20, collective_id=2, has_side_effects=True
        ),
        cost_estimate=pl.CostEstimate(flops=0, bytes_accessed=0, transcendentals=0),
    )(tokens, wq, wk, wv, gq, gk, cosines, sines, spots)


def visible_scores(key, query, key_code, query_code, query_low, factor):
    scores = dot_nt(key, query) * factor
    codes = jnp.concatenate([key_code] * (query.shape[0] // key_code.shape[1]), axis=1)
    return jnp.where((codes <= query_code) & (codes >= query_low), scores, low_score)


def fill_keys(key_rows, notes, pairs, keys, codes):
    count, width = keys.shape[1:]

    def column(row):
        return jnp.broadcast_to(row, (width, count)).T

    for k in range(2 * line):
        factor = column(notes[k, 1:2, :])
        keys[k] = (pairs[k, 0].astype(jnp.float32) * factor).astype(jnp.bfloat16)
        labels = column(notes[k, 2:3, :]).astype(jnp.int32)
        codes[k] = labels * key_rows + column(notes[k, 3:4, :]).astype(jnp.int32)


def attend_kernel(factor, key_rows, live, notes, *refs):
    queries, pairs = refs[:2]
    out_turned, out_log, out_query, out_rows, out = refs[2:7]
    top, total, accum, out_key, out_codes = refs[7:]
    f32 = jnp.float32
    bf16 = jnp.bfloat16
    count, width = queries.shape[1:]

    def column(row):
        return jnp.broadcast_to(row, (width, count)).T

    fill_keys(key_rows, notes, pairs, out_key, out_codes)
    for q in range(line):
        out_query[q] = (queries[q].astype(f32) * column(notes[q, 0:1, :])).astype(bf16)
        base = notes[q, 2:3, :].astype(jnp.int32) * key_rows
        out_rows[q : q + 1, :] = base + notes[q, 3:4, :].astype(jnp.int32)
        out_rows[line + q : line + q + 1, :] = base

    for q in range(line):
        top[...] = jnp.full_like(top, start_max)
        total[...] = jnp.zeros_like(total)
        accum[...] = jnp.zeros_like(accum)
        @pl.loop(0, 2 * line)
        def _(k, q=q):
            @pl.when(live[q, k] > 0)
            def _():
                scores = visible_scores(
                    out_key[k],
                    out_query[q],
                    out_codes[k],
                    out_rows[q : q + 1, :],
                    out_rows[line + q : line + q + 1, :],
                    factor,
                )
                highest = jnp.maximum(top[...], jnp.max(scores, axis=0, keepdims=True))
                weights = jnp.exp2(scores - highest)
                fade = jnp.exp2(top[...] - highest)
                total[...] = total[...] * fade + jnp.sum(weights, axis=0, keepdims=True)
                accum[...] = accum[...] * fade + dot_t(pairs[k, 1], weights.astype(bf16))
                top[...] = highest

        turned = accum[...] / total[...]
        out_turned[q] = turned
        out_log[q : q + 1, :] = top[...] + jnp.log2(total[...])
        out[q] = turned.T.astype(bf16)


def attend_back_kernel(factor, scale, key_rows, live, notes, rows, queries, *refs):
    pairs, turned, log_total, grads = refs[:4]
    out_query, out_near, out_far, key_sum, value_sum, query_sum, keys, codes = refs[4:]
    fill_keys(key_rows, notes, pairs, keys, codes)
    f32 = jnp.float32
    bf16 = jnp.bfloat16
    key_sum[...] = jnp.zeros_like(key_sum)
    value_sum[...] = jnp.zeros_like(value_sum)
    for q in range(line):
        query_sum[...] = jnp.zeros_like(query_sum)
        delta = jnp.sum(grads[q].astype(f32).T * turned[q], axis=0, keepdims=True)
        @pl.loop(0, 2 * line)
        def _(k, q=q, delta=delta):
            @pl.when(live[q, k] > 0)
            def _():
                query, key, grad = queries[q], keys[k], grads[q]
                scores = visible_scores(
                    key,
                    query,
                    codes[k],
                    rows[q : q + 1, :],
                    rows[line + q : line + q + 1, :],
                    factor,
                )
                probs = jnp.exp2(scores - log_total[q : q + 1, :])
                grad_probs = dot_nt(pairs[k, 1], grad)
                grad_scores = (probs * (grad_probs - delta)).astype(bf16)
                value_sum[k] += jnp.dot(
                    probs.astype(bf16), grad, preferred_element_type=f32
                )
                key_sum[k] += jnp.dot(grad_scores, query, preferred_element_type=f32)
                query_sum[...] += dot_t(key, grad_scores)

        out_query[q] = (query_sum[...] * scale).T.astype(bf16)
    for k in range(line):
        for out, base in ((out_near, 0), (out_far, line)):
            out[k, 0] = (key_sum[base + k] * scale).astype(bf16)
            out[k, 1] = value_sum[base + k].astype(bf16)


def attend(key_rows, live, notes, queries, pairs):
    _, count, width = queries.shape
    factor = math.log2(math.e) / math.sqrt(width)
    f32 = jnp.float32
    bf16 = jnp.bfloat16
    return pl.pallas_call(
        functools.partial(attend_kernel, factor, key_rows),
        out_shape=[
            jax.ShapeDtypeStruct((line, width, count), f32),
            jax.ShapeDtypeStruct((2 * line, count), f32),
            jax.ShapeDtypeStruct((line, count, width), bf16),
            jax.ShapeDtypeStruct((2 * line, count), jnp.int32),
        ]
        + [jax.ShapeDtypeStruct((line, count, width), bf16)],
        in_specs=[pl.BlockSpec(memory_space=pltpu.SMEM)] + vmem_specs(3),
        out_specs=vmem_specs(5),
        scratch_shapes=[
            pltpu.VMEM((1, count), f32),
            pltpu.VMEM((1, count), f32),
            pltpu.VMEM((width, count), f32),
            pltpu.VMEM((2 * line, count, width), bf16),
            pltpu.VMEM((2 * line, count, width), jnp.int32),
        ],
        compiler_params=pltpu.CompilerParams(vmem_limit_bytes=40 << 20),
        cost_estimate=pl.CostEstimate(flops=0, bytes_accessed=0, transcendentals=0),
    )(live, notes, queries, pairs)


def attend_back(key_rows, live, notes, rows, queries, pairs, turned, log_total, grads):
    _, count, width = queries.shape
    scale = 1.0 / math.sqrt(width)
    factor = math.log2(math.e) * scale
    f32 = jnp.float32
    return pl.pallas_call(
        functools.partial(attend_back_kernel, factor, scale, key_rows),
        out_shape=[jax.ShapeDtypeStruct((line, count, width), jnp.bfloat16)]
        + [jax.ShapeDtypeStruct((line, 2, count, width), jnp.bfloat16)] * 2,
        in_specs=[pl.BlockSpec(memory_space=pltpu.SMEM)] + vmem_specs(7),
        out_specs=vmem_specs(3),
        scratch_shapes=[
            pltpu.VMEM((2 * line, count, width), f32),
            pltpu.VMEM((2 * line, count, width), f32),
            pltpu.VMEM((width, count), f32),
            pltpu.VMEM((2 * line, count, width), jnp.bfloat16),
            pltpu.VMEM((2 * line, count, width), jnp.int32),
        ],
        compiler_params=pltpu.CompilerParams(vmem_limit_bytes=40 << 20),
        cost_estimate=pl.CostEstimate(
            flops=20 * line * line * count * count * width,
            bytes_accessed=12 << 20,
            transcendentals=2 * line * line * count * count,
        ),
    )(live, notes, rows, queries, pairs, turned, log_total, grads)


def block_kernel(
    pieces,
    w_out,
    g_attn,
    g_mlp,
    tokens,
    cotangent,
    w_gate_in,
    w_up_in,
    w_down_in,
    out_heads,
    out_tokens_x,
    out_output,
    out_hidden,
    out_hidden_z,
    out_act,
    out_act_x,
    out_mlp,
    out_mlp_x,
    out_gate,
    out_gate_far,
    out_gate_z,
    out_up,
    out_up_far,
    out_attn,
    out_grads,
    out_grad_hidden,
    out_gain,
    w_gate,
    w_up,
    w_down,
    gate_keep,
    up_keep,
    act_keep,
    hidden_keep,
    mlp_keep,
    attn_keep,
    grad_gate,
    grad_up,
    own_factor,
    own_normed,
    own_tokens,
    own_cotangent,
    attended,
    heads_keep,
    total,
    part_send,
    part_recv,
    y_send,
    y_recv,
    send_sems,
    recv_sems,
    local_sems,
):
    f32 = jnp.float32
    bf16 = jnp.bfloat16
    depth = w_out.shape[1]
    units = w_gate.shape[1]
    tile = 512
    count = own_tokens.shape[0] // 2
    rows = 2 * count
    mp = lax.axis_index("mp")
    spot = lax.axis_index("dp")
    core = lax.rem(mp, 2)
    core_peer = {"mp": mp + 1 - 2 * core}
    y_peer = {"mp": lax.rem(mp + 2, 4)}
    z = spot // 2
    z_low = lax.rem(z, 2)
    z_peer = {"dp": spot + 2 - 4 * z_low}
    x = lax.rem(spot, 2)
    x_peer = {"dp": spot + 1 - 2 * x}
    width = pieces.shape[2]
    ahead = [{"dp": lax.rem(spot + 2 * d, 2 * line)} for d in range(line)]
    head = lambda d: pl.ds(pl.multiple_of(lax.rem(z + d, line) * width, width), width)

    remote, started, local = [], [], []

    def send(source, target, peer):
        index = len(remote)
        copy = pltpu.make_async_remote_copy(
            src_ref=source,
            dst_ref=target,
            send_sem=send_sems.at[index],
            recv_sem=recv_sems.at[index],
            device_id=peer,
            device_id_type=pl.DeviceIdType.MESH,
        )
        remote.append(copy)
        copy.start()
        return copy

    def keep_out(source, target, waited=False):
        copy = pltpu.make_async_copy(source, target, local_sems.at[len(started)])
        started.append(copy)
        if not waited:
            local.append(copy)
        copy.start()
        return copy

    own = lambda s: pl.ds(s * rows, count)
    other = lambda s: pl.ds(s * rows + count, count)
    both = lambda s: pl.ds(s * rows, rows)
    mine = lambda s: pl.ds(s * count, count)
    at_home = lambda s: pl.ds(pl.multiple_of(core * rows + s * count, count), count)
    cut = lambda t: pl.ds(pl.multiple_of(t * tile, tile), tile)
    flying = {}

    home_rows = pl.ds(pl.multiple_of(core * rows, rows), rows)
    loads = [
        keep_out(tokens.at[home_rows], own_tokens, True),
        keep_out(cotangent.at[home_rows], own_cotangent, True),
        keep_out(w_gate_in, w_gate, True),
        keep_out(w_up_in, w_up, True),
        keep_out(w_down_in, w_down, True),
    ]
    barrier = pltpu.get_barrier_semaphore()
    peers = (core_peer, y_peer, x_peer, ahead[1], ahead[2], ahead[3])
    for peer in peers:
        pl.semaphore_signal(barrier, inc=1, device_id=peer, device_id_type=pl.DeviceIdType.MESH)
    pl.semaphore_wait(barrier, len(peers))
    for s in range(2):
        for d in range(1, line):
            flying["heads", s, d] = send(
                pieces.at[d, both(s)], attended.at[both(s), head(0)], ahead[line - d]
            )
    attended[:, head(0)] = pieces[0]

    loads[0].wait()
    for s in range(2):
        flying["tokens", s] = send(own_tokens.at[mine(s)], out_tokens_x.at[own(s)], x_peer)

    def forward_core(name, s, array):
        flying[name, s].wait()
        flying[name + "_core", s] = send(array.at[own(s)], array.at[other(s)], core_peer)

    def reduce_start(stage, s):
        part_send[s] = total[count:, :].astype(bf16)
        copy = send(part_send.at[s], part_recv.at[s], core_peer)
        copy.wait()
        y_send[s] = (total[:count, :] + part_recv[s].astype(f32)).astype(bf16)
        flying[stage, s] = send(y_send.at[s], y_recv.at[stage, s], y_peer)

    def reduced(stage, s):
        flying[stage, s].wait()
        return y_send[s].astype(f32) + y_recv[stage, s].astype(f32)

    def factor_of(value):
        return lax.rsqrt(jnp.mean(value * value, axis=1, keepdims=True) + epsilon)

    def share(keep, s):
        flying["share", s] = send(keep.at[own(s)], keep.at[other(s)], core_peer)

    def project_out(s):
        for d in range(1, line):
            flying["heads", s, d].wait()
        keep_out(attended.at[both(s)], out_heads.at[both(s)])
        total[...] = jnp.dot(attended[both(s), :], w_out[...], preferred_element_type=f32)
        reduce_start(0, s)

    def after_attention(s):
        value = reduced(0, s)
        factor = factor_of(value)
        normed = value * factor
        own_factor[mine(s), :] = jnp.broadcast_to(factor, (count, own_factor.shape[1]))
        own_normed[mine(s), :] = normed
        hidden = own_tokens[mine(s), :].astype(f32) + normed * g_attn[...]
        out_grad_hidden[mine(s), :] = hidden
        hidden_keep[own(s), :] = hidden.astype(bf16)
        share(hidden_keep, s)

    def forward(s):
        flying["hidden", s] = send(hidden_keep.at[own(s)], out_hidden_z.at[own(s)], z_peer)
        flying["share", s].wait()
        keep_out(hidden_keep.at[both(s)], out_hidden.at[both(s)])

        def step(t):
            hidden = hidden_keep[both(s), :]
            gate = jnp.dot(hidden, w_gate[:, cut(t)], preferred_element_type=f32)
            up = jnp.dot(hidden, w_up[:, cut(t)], preferred_element_type=f32)
            gate_keep[both(s), cut(t)] = gate.astype(bf16)
            up_keep[both(s), cut(t)] = up.astype(bf16)
            act = (gate * jax.nn.sigmoid(gate) * up).astype(bf16)
            act_keep[both(s), cut(t)] = act
            return jnp.dot(act, w_down[cut(t), :], preferred_element_type=f32)

        total[...] = step(0)

        @pl.loop(1, units // tile)
        def _(t):
            total[...] += step(t)

        reduce_start(1, s)
        keep_out(act_keep.at[both(s)], out_act.at[both(s)])
        half = units // 2
        far = pl.ds(pl.multiple_of((1 - x) * half, half), half)
        flying["act", s] = send(act_keep.at[both(s), far], out_act_x.at[both(s)], x_peer)

    def turn_point(s):
        value = reduced(1, s)
        factor = factor_of(value)
        normed = value * factor
        forward_core("tokens", s, out_tokens_x)
        own_tokens[mine(s), :] = (out_grad_hidden[mine(s), :] + normed * g_mlp[...]).astype(bf16)
        keep_out(own_tokens.at[mine(s)], out_output.at[at_home(s)])
        flying["output", s] = send(own_tokens.at[mine(s)], out_output.at[at_home(s)], core_peer)
        grad = own_cotangent[mine(s), :].astype(f32)
        gain = jnp.sum(grad * normed, axis=0, keepdims=True)
        out_gain[1:2, :] = gain if s == 0 else out_gain[1:2, :] + gain
        mlp_keep[own(s), :] = norm_back(grad * g_mlp[...], normed, factor).astype(bf16)
        share(mlp_keep, s)

    def backward(s):
        flying["mlp", s] = send(mlp_keep.at[own(s)], out_mlp_x.at[own(s)], x_peer)
        flying["share", s].wait()
        keep_out(mlp_keep.at[both(s)], out_mlp.at[both(s)])

        def step(t):
            grad_act = dot_nt(mlp_keep[both(s), :], w_down[cut(t), :])
            gate = gate_keep[both(s), cut(t)].astype(f32)
            up = up_keep[both(s), cut(t)].astype(f32)
            sigmoid = jax.nn.sigmoid(gate)
            to_gate = (grad_act * up * (sigmoid * (1.0 + gate * (1.0 - sigmoid)))).astype(bf16)
            to_up = (grad_act * (gate * sigmoid)).astype(bf16)
            grad_gate[:, cut(t)] = to_gate
            grad_up[:, cut(t)] = to_up
            return dot_nt(to_gate, w_gate[:, cut(t)]) + dot_nt(to_up, w_up[:, cut(t)])

        if s > 0:
            gate_to_z(0)
        total[...] = step(0)

        @pl.loop(1, units // tile)
        def _(t):
            total[...] += step(t)

        reduce_start(2, s)
        half = units // 2
        far = pl.ds(pl.multiple_of((1 - z_low) * half, half), half)
        flying["grads"] = [
            keep_out(source, target.at[both(s)], waited=True)
            for source, target in (
                (grad_gate, out_gate),
                (grad_gate.at[:, far], out_gate_far),
                (grad_up, out_up),
                (grad_up.at[:, far], out_up_far),
            )
        ]

    def gate_to_z(s):
        for copy in flying["grads"]:
            copy.wait()
        flying["gate_z", s] = send(out_gate_far.at[both(s)], out_gate_z.at[both(s)], z_peer)

    def to_attention(s):
        value = reduced(2, s)
        grad = own_cotangent[mine(s), :].astype(f32) + value
        out_grad_hidden[mine(s), :] = grad
        normed = own_normed[mine(s), :]
        gain = jnp.sum(grad * normed, axis=0, keepdims=True)
        out_gain[0:1, :] = gain if s == 0 else out_gain[0:1, :] + gain
        factor = own_factor[mine(s), 0:1]
        attn_keep[own(s), :] = norm_back(grad * g_attn[...], normed, factor).astype(bf16)
        share(attn_keep, s)

    def attended_grad(s):
        flying["share", s].wait()
        keep_out(attn_keep.at[both(s)], out_attn.at[both(s)])
        heads_keep[both(s), :] = dot_nt(attn_keep[both(s), :], w_out[...]).astype(bf16)
        for d in range(1, line):
            flying["grads", s, d] = send(
                heads_keep.at[both(s), head(d)], out_grads.at[d, both(s)], ahead[d]
            )
        keep_out(heads_keep.at[both(s), head(0)], out_grads.at[0, both(s)])

    project_out(0)
    project_out(1)
    for load in loads[1:]:
        load.wait()
    after_attention(0)
    forward(0)
    after_attention(1)
    forward(1)
    turn_point(0)
    backward(0)
    turn_point(1)
    backward(1)
    gate_to_z(1)
    for s in range(2):
        forward_core("hidden", s, out_hidden_z)
    to_attention(0)
    attended_grad(0)
    to_attention(1)
    attended_grad(1)
    for s in range(2):
        flying["act", s].wait()
        flying["output", s].wait()
        forward_core("mlp", s, out_mlp_x)
    for s in range(2):
        flying["tokens_core", s].wait()
        flying["gate_z", s].wait()
        flying["hidden_core", s].wait()
        flying["mlp_core", s].wait()
        for d in range(1, line):
            flying["grads", s, d].wait()
    for copy in local:
        copy.wait()


def block(pieces, w_out, g_attn, g_mlp, tokens, cotangent, w_gate, w_up, w_down):
    _, rows, width = pieces.shape
    columns = line * width
    depth, units = w_gate.shape
    half = rows // 2
    quarter = rows // 4
    f32 = jnp.float32
    bf16 = jnp.bfloat16
    wide = jax.ShapeDtypeStruct((rows, depth), bf16)
    tall = jax.ShapeDtypeStruct((rows, units), bf16)
    any_spec = pl.BlockSpec(memory_space=pl.ANY)
    return pl.pallas_call(
        block_kernel,
        out_shape=[
            jax.ShapeDtypeStruct((rows, columns), bf16),
            wide,
            wide,
            wide,
            wide,
            tall,
            jax.ShapeDtypeStruct((rows, units // 2), bf16),
            wide,
            wide,
            tall,
            jax.ShapeDtypeStruct((rows, units // 2), bf16),
            jax.ShapeDtypeStruct((rows, units // 2), bf16),
            tall,
            jax.ShapeDtypeStruct((rows, units // 2), bf16),
            wide,
            jax.ShapeDtypeStruct((line, rows, width), bf16),
            jax.ShapeDtypeStruct((half, depth), f32),
            jax.ShapeDtypeStruct((2, depth), f32),
        ],
        in_specs=vmem_specs(4) + [any_spec] * 5,
        out_specs=[any_spec] * 16 + vmem_specs(2),
        scratch_shapes=[
            pltpu.VMEM((depth, units), bf16),
            pltpu.VMEM((depth, units), bf16),
            pltpu.VMEM((units, depth), bf16),
            pltpu.VMEM((rows, units), bf16),
            pltpu.VMEM((rows, units), bf16),
            pltpu.VMEM((rows, units), bf16),
            pltpu.VMEM((rows, depth), bf16),
            pltpu.VMEM((rows, depth), bf16),
            pltpu.VMEM((rows, depth), bf16),
            pltpu.VMEM((half, units), bf16),
            pltpu.VMEM((half, units), bf16),
            pltpu.VMEM((half, 128), f32),
            pltpu.VMEM((half, depth), f32),
            pltpu.VMEM((half, depth), bf16),
            pltpu.VMEM((half, depth), bf16),
            pltpu.VMEM((rows, columns), bf16),
            pltpu.VMEM((rows, columns), bf16),
            pltpu.VMEM((half, depth), f32),
            pltpu.VMEM((2, quarter, depth), bf16),
            pltpu.VMEM((2, quarter, depth), bf16),
            pltpu.VMEM((2, quarter, depth), bf16),
            pltpu.VMEM((3, 2, quarter, depth), bf16),
            pltpu.SemaphoreType.DMA((56,)),
            pltpu.SemaphoreType.DMA((56,)),
            pltpu.SemaphoreType.DMA((32,)),
        ],
        compiler_params=pltpu.CompilerParams(
            vmem_limit_bytes=61800 << 10, collective_id=1, has_side_effects=True
        ),
        cost_estimate=pl.CostEstimate(flops=0, bytes_accessed=0, transcendentals=0),
    )(pieces, w_out, g_attn, g_mlp, tokens, cotangent, w_gate, w_up, w_down)


class Courier:
    def __init__(self, send_sems, recv_sems, local_sems):
        self.send_sems, self.recv_sems, self.local_sems = send_sems, recv_sems, local_sems
        self.remote, self.local = 0, 0

    def send(self, source, target, peer):
        copy = pltpu.make_async_remote_copy(
            src_ref=source,
            dst_ref=target,
            send_sem=self.send_sems.at[self.remote],
            recv_sem=self.recv_sems.at[self.remote],
            device_id=peer,
            device_id_type=pl.DeviceIdType.MESH,
        )
        self.remote += 1
        copy.start()
        return copy

    def move(self, source, target):
        copy = pltpu.make_async_copy(source, target, self.local_sems.at[self.local])
        self.local += 1
        copy.start()
        return copy


def greet(peers):
    barrier = pltpu.get_barrier_semaphore()
    for peer in peers:
        pl.semaphore_signal(barrier, inc=1, device_id=peer, device_id_type=pl.DeviceIdType.MESH)
    pl.semaphore_wait(barrier, len(peers))


class Spot:
    def __init__(self):
        mp = lax.axis_index("mp")
        spot = lax.axis_index("dp")
        self.core = lax.rem(mp, 2)
        self.x = lax.rem(spot, 2)
        self.z = spot // 2
        self.z_low = lax.rem(self.z, 2)
        self.z_high = self.z // 2
        self.core_peer = {"mp": mp + 1 - 2 * self.core}
        self.y_peer = {"mp": lax.rem(mp + 2, 4)}
        self.x_peer = {"dp": spot + 1 - 2 * self.x}
        self.z_peer = {"dp": spot + 2 - 4 * self.z_low}
        self.far_peer = {"dp": lax.rem(spot + 4, 8)}
        self.ahead = [{"dp": lax.rem(spot + 2 * d, 2 * line)} for d in range(line)]
        self.all = (self.core_peer, self.y_peer, self.x_peer) + tuple(self.ahead[1:])


class Job:
    def __init__(self, spot, over_x, first, first_far, second, second_far, cut_first):
        self.operands, self.cut_first = (first, first_far, second, second_far), cut_first
        self.tile = (first if cut_first else second).shape[1] // (line * pair)
        self.spot, self.over_x = spot, over_x
        self.side = spot.x if over_x else spot.z_low
        self.partner = spot.x_peer if over_x else spot.z_peer
        self.first_peer = spot.z_peer if over_x else spot.x_peer

    def at(self, ref, index):
        block = pl.ds(pl.multiple_of(index * self.tile, self.tile), self.tile)
        return ref.at[block, :] if self.cut_first else ref.at[:, block]

    def span(self, ref, index):
        block = pl.ds(pl.multiple_of(index * 2 * self.tile, 2 * self.tile), 2 * self.tile)
        return ref.at[block, :] if self.cut_first else ref.at[:, block]

    def term(self, index):
        first, first_far, second, second_far = self.operands
        block = pl.ds(pl.multiple_of(index * self.tile, self.tile), self.tile)
        if self.cut_first:
            return dot_t(first[:, block], second[...]) + dot_t(first_far[:, block], second_far[...])
        return dot_t(first[...], second[:, block]) + dot_t(first_far[...], second_far[:, block])

    def block_of(self, high, index):
        if self.over_x:
            return (2 * high + self.spot.z_low) * pair + index
        return (2 * high + index) * pair + self.spot.x

    def make_half(self, target, high):
        @pl.loop(0, 2)
        def _(i):
            if self.over_x:
                index = (2 * high + 1 - self.spot.z_low) * pair + i
            else:
                index = (2 * high + i) * pair + 1 - self.spot.x
            self.at(target, 2 * high + i)[...] = self.term(index).astype(jnp.bfloat16)

    def send_half(self, mail, target, remote, high):
        return mail.send(self.span(target, high), self.span(remote, high), self.first_peer)

    def start_first(self, mail, target, remote):
        copies = []
        for high in (1 - self.spot.z_high, self.spot.z_high):
            self.make_half(target, high)
            copies.append(self.send_half(mail, target, remote, high))
        return copies

    def second_term(self, arrived, target, i):
        total = self.term(self.block_of(1 - self.spot.z_high, i))
        total = total + self.at(arrived, i)[...].astype(jnp.float32)
        self.at(target, i)[...] = total.astype(jnp.bfloat16)

    def second_terms(self, arrived, target):
        @pl.loop(0, 2)
        def _(i):
            self.second_term(arrived, target, i)

    def own_term(self, side, arrived):
        total = self.term(self.block_of(self.spot.z_high, side))
        return total + self.at(arrived, side)[...].astype(jnp.float32)


def middle_kernel(
    grad_queries_in,
    near_in,
    far,
    q_raw,
    k_raw,
    factors,
    cosines,
    sines,
    gq,
    gk,
    act,
    act_x,
    mlp,
    mlp_x,
    hidden,
    hidden_z,
    gate,
    gate_z,
    up,
    up_z,
    out_own_down,
    out_r2_down,
    out_r1_gate,
    out_r1_up,
    out_r2_gate,
    out_raw_x,
    r1_down,
    out_raw,
    out_raw_own,
    out_gain,
    act_v,
    act_zv,
    mlp_v,
    mlp_zv,
    hidden_v,
    hidden_zv,
    gate_v,
    gate_zv,
    up_v,
    up_zv,
    send_down,
    send_gate,
    send_up,
    r1_v,
    r1_own,
    s2_v,
    own_v,
    r1_gate_v,
    s2_gate,
    grad_queries,
    near,
    far_in,
    sums,
    query_home,
    pair_home,
    scaled,
    raw_far,
    inner,
    inner_core,
    inner_y,
    send_sems,
    recv_sems,
    local_sems,
):
    f32 = jnp.float32
    bf16 = jnp.bfloat16
    spot = Spot()
    mail = Courier(send_sems, recv_sems, local_sems)
    count, width = cosines.shape
    columns = line * width
    depth = mlp_v.shape[1]
    half = act_v.shape[1]
    own_half = pl.ds(pl.multiple_of(spot.z_low * half, half), half)
    x_half = pl.ds(pl.multiple_of(spot.x * half, half), half)
    loads = [
        mail.move(act.at[:, x_half], act_v),
        mail.move(act_x, act_zv),
        mail.move(mlp, mlp_v),
        mail.move(mlp_x, mlp_zv),
        mail.move(hidden, hidden_v),
        mail.move(hidden_z, hidden_zv),
        mail.move(gate.at[:, own_half], gate_v),
        mail.move(gate_z, gate_zv),
        mail.move(up.at[:, own_half], up_v),
        mail.move(up_z, up_zv),
    ]
    small_loads = [mail.move(grad_queries_in, grad_queries), mail.move(near_in, near)]
    greet(spot.all)
    far_copy = mail.send(far, far_in, spot.x_peer)
    my_head = pl.ds(pl.multiple_of(spot.z * width, width), width)
    for load in small_loads:
        load.wait()
    query_copies = [
        mail.send(grad_queries.at[d], query_home.at[:, my_head], spot.ahead[line - d])
        for d in range(1, line)
    ]
    query_home[:, my_head] = grad_queries[0]
    for load in loads[:4]:
        load.wait()
    down = Job(spot, True, act_v, act_zv, mlp_v, mlp_zv, False)
    down_first = down.start_first(mail, send_down, r1_down)
    for load in loads[4:]:
        load.wait()
    gates = Job(spot, False, hidden_v, hidden_zv, gate_v, gate_zv, True)
    both = (1 - spot.z_high, spot.z_high)
    for high in both:
        gates.make_half(send_gate, high)
    far_copy.wait()
    gate_first = [gates.send_half(mail, send_gate, out_r1_gate, high) for high in both]
    sums[...] = (near[...].astype(f32) + far_in[...].astype(f32)).astype(bf16)
    pair_copies = [
        mail.send(sums.at[d], pair_home.at[:, :, my_head], spot.ahead[line - d])
        for d in range(1, line)
    ]
    pair_home[:, :, my_head] = sums[0]
    ups = Job(spot, False, hidden_v, hidden_zv, up_v, up_zv, True)
    up_first = ups.start_first(mail, send_up, out_r1_up)

    down_first[0].wait()
    down_load = mail.move(down.span(r1_down, 1 - spot.z_high), r1_v)
    down_load.wait()
    down.second_terms(r1_v, s2_v)
    second_copy = mail.send(s2_v, out_r2_down, spot.far_peer)
    gate_first[0].wait()
    gate_load = mail.move(gates.span(out_r1_gate, 1 - spot.z_high), r1_gate_v)
    gate_load.wait()
    gates.second_terms(r1_gate_v, s2_gate)
    gate_second = mail.send(s2_gate, out_r2_gate, spot.far_peer)
    for copy in query_copies + pair_copies:
        copy.wait()

    def column(row):
        return jnp.broadcast_to(row, (width, count)).T

    sources = ((query_home, None, q_raw, gq), (pair_home, 0, k_raw, gk))
    factor_columns = [column(factors[which : which + 1, :]) for which in range(2)]
    for which, (home, slot, raw, gain) in enumerate(sources):
        inner_sum = jnp.zeros((count, width), f32)
        for h in range(line):
            cut = slice(h * width, (h + 1) * width)
            part = (home[:, cut] if slot is None else home[slot, :, cut]).astype(f32)
            back = part * cosines[...] - pltpu.roll(part, width // 2, 1) * sines[...]
            normed = raw[:, cut] * factor_columns[which]
            out_gain[which : which + 1, cut] = jnp.sum(back * normed, axis=0, keepdims=True)
            value = back * gain[:, cut]
            scaled[which, :, cut] = value
            inner_sum = inner_sum + value * normed
        inner[which : which + 1, :] = jnp.sum(inner_sum.T, axis=0, keepdims=True)
    core_copy = mail.send(inner, inner_core, spot.core_peer)
    core_copy.wait()
    arrived = inner_core[...]
    quarter = count // 4
    cuts = [arrived[:, i * quarter : (i + 1) * quarter] for i in (1, 0, 3, 2)]
    chip = inner[...] + jnp.concatenate(cuts, axis=1)
    inner[...] = chip
    y_copy = mail.send(inner, inner_y, spot.y_peer)
    y_copy.wait()
    inner_all = (chip + inner_y[...]) / depth
    for which, (home, slot, raw, gain) in enumerate(sources):
        inner_column = column(inner_all[which : which + 1, :])
        for h in range(line):
            cut = slice(h * width, (h + 1) * width)
            normed = raw[:, cut] * factor_columns[which]
            value = factor_columns[which] * (scaled[which, :, cut] - normed * inner_column)
            base = which * columns + h * width
            out_raw[:, base : base + width] = value.astype(bf16)
    out_raw[:, 2 * columns :] = pair_home[1]
    part_width = columns // 2
    for which in range(3):
        cut = slice(which * part_width, (which + 1) * part_width)
        base = which * columns

        def side(index):
            start = pl.multiple_of(base + index * part_width, part_width)
            return out_raw[:, pl.ds(start, part_width)]

        out_raw_own[:, cut] = side(spot.x)
        raw_far[:, cut] = side(1 - spot.x)
    raw_copy = mail.send(raw_far, out_raw_x, spot.x_peer)

    down_first[1].wait()
    own_load = mail.move(down.span(r1_down, spot.z_high), r1_own)
    own_load.wait()

    @pl.loop(0, 2)
    def _(i):
        down.at(own_v, i)[...] = down.own_term(i, r1_own)

    keep_own = mail.move(own_v, out_own_down)
    for copy in (gate_second, gate_first[1], *up_first, raw_copy, second_copy, keep_own):
        copy.wait()


def middle(small, large):
    f32 = jnp.float32
    bf16 = jnp.bfloat16
    grad_queries, near, far, q_raw = small[:4]
    act, act_x, grad_mlp = large[:3]
    _, count, width = grad_queries.shape
    columns = line * width
    depth = grad_mlp.shape[1]
    units = act.shape[1]
    half = units // 2
    cut = depth // 2
    any_spec = pl.BlockSpec(memory_space=pl.ANY)
    shape = jax.ShapeDtypeStruct
    return pl.pallas_call(
        middle_kernel,
        in_specs=[pl.BlockSpec(memory_space=pltpu.HBM)] * 3 + vmem_specs(7) + [any_spec] * 10,
        out_specs=[any_spec] * 7 + vmem_specs(3),
        out_shape=[
            shape((half, cut // 2), f32),
            shape((half, cut // 2), bf16),
            shape((cut, half), bf16),
            shape((cut, half), bf16),
            shape((cut // 2, half), bf16),
            shape((count, 3 * columns // 2), bf16),
            shape((half, cut), bf16),
            shape((count, 3 * columns), bf16),
            shape((count, 3 * columns // 2), bf16),
            shape((2, columns), f32),
        ],
        scratch_shapes=[
            pltpu.VMEM((count, half), bf16),
            pltpu.VMEM((count, half), bf16),
            pltpu.VMEM((count, depth), bf16),
            pltpu.VMEM((count, depth), bf16),
            pltpu.VMEM((count, depth), bf16),
            pltpu.VMEM((count, depth), bf16),
            pltpu.VMEM((count, half), bf16),
            pltpu.VMEM((count, half), bf16),
            pltpu.VMEM((count, half), bf16),
            pltpu.VMEM((count, half), bf16),
            pltpu.VMEM((half, cut), bf16),
            pltpu.VMEM((cut, half), bf16),
            pltpu.VMEM((cut, half), bf16),
            pltpu.VMEM((half, cut // 2), bf16),
            pltpu.VMEM((half, cut // 2), bf16),
            pltpu.VMEM((half, cut // 2), bf16),
            pltpu.VMEM((half, cut // 2), f32),
            pltpu.VMEM((cut // 2, half), bf16),
            pltpu.VMEM((cut // 2, half), bf16),
            pltpu.VMEM(grad_queries.shape, bf16),
            pltpu.VMEM(near.shape, bf16),
            pltpu.VMEM(near.shape, bf16),
            pltpu.VMEM(near.shape, bf16),
            pltpu.VMEM((count, columns), bf16),
            pltpu.VMEM((2, count, columns), bf16),
            pltpu.VMEM((2, count, columns), f32),
            pltpu.VMEM((count, 3 * columns // 2), bf16),
            pltpu.VMEM((2, count), f32),
            pltpu.VMEM((2, count), f32),
            pltpu.VMEM((2, count), f32),
            pltpu.SemaphoreType.DMA((28,)),
            pltpu.SemaphoreType.DMA((28,)),
            pltpu.SemaphoreType.DMA((28,)),
        ],
        compiler_params=pltpu.CompilerParams(
            vmem_limit_bytes=60 << 20, collective_id=3, has_side_effects=True
        ),
    )(*small, *large)


def last_kernel(
    raw,
    raw_own,
    raw_x,
    wide,
    narrow,
    attended,
    hidden,
    hidden_z,
    gate,
    gate_z,
    up,
    up_z,
    attn,
    tokens,
    tokens_x,
    own_down,
    r2_down,
    r1_gate,
    r1_up,
    r2_gate_in,
    w_query,
    w_key,
    w_value,
    grad_hidden,
    *refs,
):
    outs, refs = refs[:13], refs[13:]
    near_down, near_gate, near_up, near_raw, near_out = outs[:5]
    far_down, far_gate, far_up, far_raw, far_out = outs[5:10]
    out_tokens, r1_raw, r1_out = outs[10:]
    out_wide, out_narrow = refs[:2]
    (
        hidden_v,
        hidden_zv,
        gate_v,
        gate_zv,
        up_v,
        up_zv,
        tokens_v,
        tokens_xv,
        attn_v,
        attn_xv,
        heads_v,
        heads_far,
        heads_xv,
        send_raw,
        send_out,
        r1_wide,
        r1_raw_v,
        r1_out_v,
        s2_up,
        s2_raw,
        s2_out,
        r2_gate,
        r2_up,
        r2_raw,
        r2_out,
        own_down_v,
        r2_down_v,
        fin_down,
        fin_gate,
        fin_up,
        fin_raw,
        fin_out,
        keep_down,
        keep_gate,
        keep_up,
        keep_raw,
        keep_out,
        weight_v,
        total,
        part_send,
        part_recv,
        y_send,
        y_recv,
        hidden_own,
        token_keep,
        wide_core,
        wide_x,
        narrow_x,
        wide_z,
        narrow_z,
        send_sems,
        recv_sems,
        local_sems,
    ) = refs[2:]
    f32 = jnp.float32
    bf16 = jnp.bfloat16
    spot = Spot()
    mail = Courier(send_sems, recv_sems, local_sems)
    rows_all = tokens_v.shape[0]
    rows = rows_all // 2
    count = rows // 2
    half = gate_v.shape[1]
    own_half = pl.ds(pl.multiple_of(spot.z_low * half, half), half)
    heads_half = heads_v.shape[1]
    side_heads = lambda side: pl.ds(pl.multiple_of(side * heads_half, heads_half), heads_half)
    own = lambda s: pl.ds(s * rows, count)
    other = lambda s: pl.ds(s * rows + count, count)
    both = lambda s: pl.ds(s * rows, rows)
    mine = lambda s: pl.ds(s * count, count)

    token_loads = [mail.move(tokens_x, tokens_xv)]
    for s in range(2):
        for part, place in ((0, spot.core), (1, 1 - spot.core)):
            start = pl.multiple_of(place * rows + s * count, count)
            target = tokens_v.at[pl.ds(s * rows + part * count, count)]
            token_loads.append(mail.move(tokens.at[pl.ds(start, count)], target))
    attn_load = mail.move(attn, attn_v)
    r1_loads = []
    first_loads = [mail.move(hidden, hidden_v), mail.move(hidden_z, hidden_zv)]
    gate_loads = [mail.move(gate.at[:, own_half], gate_v), mail.move(gate_z, gate_zv)]
    up_loads = [mail.move(up.at[:, own_half], up_v), mail.move(up_z, up_zv)]
    ups = Job(spot, False, hidden_v, hidden_zv, up_v, up_zv, True)
    gates = Job(spot, False, hidden_v, hidden_zv, gate_v, gate_zv, True)
    raws = Job(spot, True, tokens_v, tokens_xv, raw_own, raw_x, True)
    outs_job = Job(spot, True, heads_v, heads_xv, attn_v, attn_xv, False)
    gate_second = mail.move(r2_gate_in, r2_gate)
    gate_own = mail.move(gates.span(r1_gate, spot.z_high), r1_wide.at[1])
    up_second = mail.move(ups.span(r1_up, 1 - spot.z_high), r1_wide.at[2])
    up_own = mail.move(ups.span(r1_up, spot.z_high), r1_wide.at[3])
    greet(spot.all)
    wide_copy = mail.send(wide, wide_core, spot.core_peer)
    attn_load.wait()
    attn_copies = [
        mail.send(attn_v.at[own(s)], attn_xv.at[own(s)], spot.x_peer) for s in range(2)
    ]
    heads_far[...] = attended[:, side_heads(1 - spot.x)]
    heads_v[...] = attended[:, side_heads(spot.x)]
    heads_copy = mail.send(heads_far, heads_xv, spot.x_peer)
    for load in token_loads:
        load.wait()
    raw_first = raws.start_first(mail, send_raw, r1_raw)
    wide_copy.wait()
    out_wide[...] = wide[...] + wide_core[...]
    out_narrow[...] = narrow[...]
    wide_x_copy = mail.send(out_wide, wide_x, spot.x_peer)
    narrow_x_copy = mail.send(out_narrow, narrow_x, spot.x_peer)

    for load in (*first_loads, *up_loads, up_second):
        load.wait()
    ups.second_terms(r1_wide.at[2], s2_up)
    second_up = mail.send(s2_up, r2_up, spot.far_peer)

    for s in range(2):
        attn_copies[s].wait()
    attn_core = [
        mail.send(attn_xv.at[own(s)], attn_xv.at[other(s)], spot.core_peer) for s in range(2)
    ]
    for copy in attn_core:
        copy.wait()
    heads_copy.wait()
    out_first = outs_job.start_first(mail, send_out, r1_out)

    raw_first[0].wait()
    raw_load = mail.move(raws.span(r1_raw, 1 - spot.z_high), r1_raw_v.at[0])
    raw_load.wait()
    raws.second_terms(r1_raw_v.at[0], s2_raw)
    second_raw = mail.send(s2_raw, r2_raw, spot.far_peer)
    input_weights = (w_query, w_key, w_value)
    columns = w_query.shape[1]
    flying = {}
    for which, source in enumerate(input_weights):
        load = mail.move(source, weight_v)
        load.wait()
        for s in range(2):
            term = dot_nt(raw[both(s), which * columns : (which + 1) * columns], weight_v[...])
            total[both(s), :] = term if which == 0 else total[both(s), :] + term
    for s in range(2):
        part_send[s] = total[other(s), :].astype(bf16)
        flying["core", s] = mail.send(part_send.at[s], part_recv.at[s], spot.core_peer)
    hidden_load = mail.move(grad_hidden, hidden_own)
    for s in range(2):
        flying["core", s].wait()
        y_send[s] = (total[own(s), :] + part_recv[s].astype(f32)).astype(bf16)
        flying["y", s] = mail.send(y_send.at[s], y_recv.at[s], spot.y_peer)

    wide_x_copy.wait()
    narrow_x_copy.wait()
    out_wide[...] = out_wide[...] + wide_x[...]
    out_narrow[...] = out_narrow[...] + narrow_x[...]
    near_copies, far_copies = [], []

    def finish(job, value_of, fin, far, keep, target):
        fin[...] = value_of(1 - job.side).astype(bf16)
        far_copies.append(mail.send(fin, far, job.partner))
        keep[...] = value_of(job.side)
        near_copies.append(mail.move(keep, target))

    down_loads = [mail.move(own_down, own_down_v), mail.move(r2_down, r2_down_v)]
    for load in down_loads:
        load.wait()
    down = outs_job
    finish(
        down,
        lambda side: down.at(own_down_v, side)[...] + down.at(r2_down_v, side)[...].astype(f32),
        fin_down,
        far_down,
        keep_down,
        near_down,
    )

    out_first[0].wait()
    out_load = mail.move(outs_job.span(r1_out, 1 - spot.z_high), r1_out_v.at[0])
    out_load.wait()
    outs_job.second_terms(r1_out_v.at[0], s2_out)
    second_out = mail.send(s2_out, r2_out, spot.far_peer)
    raw_first[1].wait()
    out_first[1].wait()
    own_loads = [
        mail.move(raws.span(r1_raw, spot.z_high), r1_raw_v.at[1]),
        mail.move(outs_job.span(r1_out, spot.z_high), r1_out_v.at[1]),
    ]
    for load in own_loads:
        load.wait()
    def final_of(job, r1_own, r2):
        return lambda side: job.own_term(side, r1_own) + job.at(r2, side)[...].astype(f32)

    for load in (*gate_loads, gate_own, gate_second):
        load.wait()
    finish(gates, final_of(gates, r1_wide.at[1], r2_gate), fin_gate, far_gate, keep_gate, near_gate)

    hidden_load.wait()
    for s in range(2):
        flying["y", s].wait()
        value = y_send[s].astype(f32) + y_recv[s].astype(f32)
        token_keep[mine(s), :] = (hidden_own[mine(s), :] + value).astype(bf16)
        home = pl.ds(pl.multiple_of(spot.core * rows + s * count, count), count)
        flying["keep", s] = mail.move(token_keep.at[mine(s)], out_tokens.at[home])
        flying["tokens", s] = mail.send(
            token_keep.at[mine(s)], out_tokens.at[home], spot.core_peer
        )
    gain_copies = []
    for d in range(1, line):
        gain_copies.append(mail.send(out_wide, wide_z.at[d - 1], spot.ahead[d]))
        gain_copies.append(mail.send(out_narrow, narrow_z.at[d - 1], spot.ahead[d]))

    up_own.wait()
    second_up.wait()
    finish(ups, final_of(ups, r1_wide.at[3], r2_up), fin_up, far_up, keep_up, near_up)
    second_raw.wait()
    finish(raws, final_of(raws, r1_raw_v.at[1], r2_raw), fin_raw, far_raw, keep_raw, near_raw)
    second_out.wait()
    finish(
        outs_job, final_of(outs_job, r1_out_v.at[1], r2_out), fin_out, far_out, keep_out, near_out
    )
    for copy in gain_copies:
        copy.wait()
    for d in range(1, line):
        out_wide[...] = out_wide[...] + wide_z[d - 1]
        out_narrow[...] = out_narrow[...] + narrow_z[d - 1]
    for s in range(2):
        flying["keep", s].wait()
        flying["tokens", s].wait()
    for copy in near_copies + far_copies:
        copy.wait()


def last(small, large):
    f32 = jnp.float32
    bf16 = jnp.bfloat16
    raw, raw_own, raw_x, wide, narrow, attended = small
    hidden, gate = large[0], large[2]
    count, depth = hidden.shape
    units = gate.shape[1]
    half = units // 2
    block = depth // (line * pair)
    columns = attended.shape[1]
    heads_half = columns // 2
    raw_half = raw_own.shape[1]
    rows = count // 2
    any_spec = pl.BlockSpec(memory_space=pl.ANY)
    shape = jax.ShapeDtypeStruct
    vmem = lambda *size: pltpu.VMEM(size, bf16)
    wide_vmem = lambda *size: pltpu.VMEM(size, f32)
    return pl.pallas_call(
        last_kernel,
        in_specs=vmem_specs(6) + [any_spec] * len(large),
        out_specs=[any_spec] * 13 + vmem_specs(2),
        out_shape=[
            shape((half, block), f32),
            shape((block, half), f32),
            shape((block, half), f32),
            shape((block, raw_half), f32),
            shape((heads_half, block), f32),
            shape((half, block), bf16),
            shape((block, half), bf16),
            shape((block, half), bf16),
            shape((block, raw_half), bf16),
            shape((heads_half, block), bf16),
            shape((count, depth), bf16),
            shape((line * block, raw_half), bf16),
            shape((heads_half, line * block), bf16),
            shape(wide.shape, f32),
            shape(narrow.shape, f32),
        ],
        scratch_shapes=[
            vmem(count, depth),
            vmem(count, depth),
            vmem(count, half),
            vmem(count, half),
            vmem(count, half),
            vmem(count, half),
            vmem(count, depth),
            vmem(count, depth),
            vmem(count, depth),
            vmem(count, depth),
            vmem(count, heads_half),
            vmem(count, heads_half),
            vmem(count, heads_half),
            vmem(line * block, raw_half),
            vmem(heads_half, line * block),
            vmem(4, 2 * block, half),
            vmem(2, 2 * block, raw_half),
            vmem(2, heads_half, 2 * block),
            vmem(2 * block, half),
            vmem(2 * block, raw_half),
            vmem(heads_half, 2 * block),
            vmem(2 * block, half),
            vmem(2 * block, half),
            vmem(2 * block, raw_half),
            vmem(heads_half, 2 * block),
            wide_vmem(half, 2 * block),
            vmem(half, 2 * block),
            vmem(half, block),
            vmem(block, half),
            vmem(block, half),
            vmem(block, raw_half),
            vmem(heads_half, block),
            wide_vmem(half, block),
            wide_vmem(block, half),
            wide_vmem(block, half),
            wide_vmem(block, raw_half),
            wide_vmem(heads_half, block),
            vmem(depth, columns),
            wide_vmem(count, depth),
            vmem(2, rows // 2, depth),
            vmem(2, rows // 2, depth),
            vmem(2, rows // 2, depth),
            vmem(2, rows // 2, depth),
            wide_vmem(rows, depth),
            vmem(rows, depth),
            wide_vmem(*wide.shape),
            wide_vmem(*wide.shape),
            wide_vmem(*narrow.shape),
            wide_vmem(line - 1, *wide.shape),
            wide_vmem(line - 1, *narrow.shape),
            pltpu.SemaphoreType.DMA((48,)),
            pltpu.SemaphoreType.DMA((48,)),
            pltpu.SemaphoreType.DMA((40,)),
        ],
        compiler_params=pltpu.CompilerParams(
            vmem_limit_bytes=61800 << 10, collective_id=4, has_side_effects=True
        ),
    )(*small, *large)


def join_kernel(*refs):
    nears, fars, whole = refs[:5], refs[5:10], refs[10:12]
    outs, refs = refs[12:21], refs[21:]
    stages, far_parts, whole_parts, sems = refs[:7], refs[7:12], refs[12:14], refs[14]
    spot = lax.axis_index("dp")
    x = lax.rem(spot, 2)
    z_low = lax.rem(spot // 2, 2)
    started = []

    def move(source, target):
        copy = pltpu.make_async_copy(source, target, sems.at[len(started)])
        started.append(copy)
        copy.start()
        return copy

    width = nears[3].shape[1] // 3
    plan = [(4, 1, None, z_low, 1), (5, 2, None, z_low, 1), (6, 0, None, x, 0)]
    plan += [(i, 3, slice(i * width, (i + 1) * width), x, 1) for i in range(3)]
    plan += [(3, 4, None, x, 0)]

    def half(ref, side, axis):
        size = ref.shape[axis] // 2
        cut = pl.ds(pl.multiple_of(side * size, size), size)
        return ref.at[cut, :] if axis == 0 else ref.at[:, cut]

    whole_loads = [move(source, part) for source, part in zip(whole, whole_parts)]
    far_loads, near_loads = {}, {}
    for result, source, columns, side, axis in plan:
        if source not in far_loads:
            far_loads[source] = move(fars[source], far_parts[source])
        near = nears[source] if columns is None else nears[source].at[:, columns]
        near_loads[result] = move(near, half(stages[result], side, axis))
    leaving = []
    for load, part, out in zip(whole_loads, whole_parts, outs[:2]):
        load.wait()
        leaving.append(move(part, out))
    waited = set()
    for result, source, columns, side, axis in plan:
        if source not in waited:
            far_loads[source].wait()
            waited.add(source)
        far = far_parts[source][...] if columns is None else far_parts[source][:, columns]
        half(stages[result], 1 - side, axis)[...] = far.astype(jnp.float32)
        near_loads[result].wait()
        leaving.append(move(stages[result], outs[2 + result]))
    for copy in leaving:
        copy.wait()


def join(nears, fars, output, tokens):
    f32 = jnp.float32
    shape = jax.ShapeDtypeStruct
    any_spec = pl.BlockSpec(memory_space=pl.ANY)
    down, gate, up, raw, out = [part.shape for part in nears]
    third = (raw[0], 2 * raw[1] // 3)
    results = [third] * 3 + [
        (2 * out[0], out[1]),
        (gate[0], 2 * gate[1]),
        (up[0], 2 * up[1]),
        (2 * down[0], down[1]),
    ]
    return pl.pallas_call(
        join_kernel,
        in_specs=[any_spec] * 12,
        out_specs=[any_spec] * 9,
        out_shape=[shape(output.shape, output.dtype), shape(tokens.shape, tokens.dtype)]
        + [shape(size, f32) for size in results],
        scratch_shapes=[pltpu.VMEM(size, f32) for size in results]
        + [pltpu.VMEM(part.shape, part.dtype) for part in (*fars, output, tokens)]
        + [pltpu.SemaphoreType.DMA((24,))],
        compiler_params=pltpu.CompilerParams(vmem_limit_bytes=60 << 20),
    )(*nears, *fars, output, tokens)


def on_device_lines(
    tokens,
    cotangent,
    doc_ids,
    row_ids,
    offsets,
    w_query,
    w_key,
    w_value,
    w_output,
    w_gate,
    w_up,
    w_down,
    gain_query,
    gain_key,
    gain_attn,
    gain_mlp,
):
    f32 = jnp.float32
    bf16 = jnp.bfloat16
    row_count, model_width = tokens.shape
    heads_here, head_width = gain_query.shape
    local_width = heads_here * head_width
    half_rows = row_count // 2
    key_rows = row_count * line * pair
    spot = lax.axis_index("dp")
    z, x = spot // pair, lax.rem(spot, pair)
    z_high, z_low = z // 2, lax.rem(z, 2)
    core = lax.rem(lax.axis_index("mp"), 2)
    place = jnp.stack([core, z, z_low, z_high, x]).astype(jnp.int32)

    quarter = row_count // 4

    def own_rows(value):
        return lax.dynamic_slice_in_dim(value, core * half_rows, half_rows, 0)

    def other_rows(value):
        return lax.dynamic_slice_in_dim(value, (1 - core) * half_rows, half_rows, 0)

    def reorder(value):
        return join_parts(own_rows(value), other_rows(value))

    def restore(own, other):
        whole = jnp.zeros((row_count,) + own.shape[1:], own.dtype)
        whole = lax.dynamic_update_slice_in_dim(whole, own, core * half_rows, 0)
        return lax.dynamic_update_slice_in_dim(whole, other, (1 - core) * half_rows, 0)

    def half_of(value, side):
        width = value.shape[1] // 2
        return lax.dynamic_slice_in_dim(value, side * width, width, 1)

    positions = reorder(offsets[0] + jnp.arange(row_count, dtype=jnp.int32))
    labels = reorder(row_ids[0] * key_rows + doc_ids)
    freqs = rope_base ** (-jnp.arange(0, head_width // 2, dtype=f32) * 2.0 / head_width)
    angles = positions.astype(f32)[:, None] * freqs[None, :]
    cosines, sines = jnp.cos(angles), jnp.sin(angles)
    cosines = jnp.concatenate([cosines, cosines], axis=1)
    sines = jnp.concatenate([-sines, sines], axis=1)
    g_query = gain_query.reshape(1, local_width)
    g_key = gain_key.reshape(1, local_width)
    spots = jnp.stack([labels, positions]).astype(f32)
    queries, pairs, notes, q_raw, k_raw = project(
        tokens, w_query, w_key, w_value, g_query, g_key, cosines, sines, spots
    )
    factors = notes[0, :2]
    codes = notes[:, 2, :].astype(jnp.int32) * key_rows + notes[:, 3, :].astype(jnp.int32)
    lows = notes[:line, 2, :].astype(jnp.int32) * key_rows
    live = (
        (jnp.min(codes, axis=1)[None, :] <= jnp.max(codes[:line], axis=1)[:, None])
        & (jnp.max(codes, axis=1)[None, :] >= jnp.min(lows, axis=1)[:, None])
    ).astype(jnp.int32)

    turned, log_total, queries_n, code_rows, attended_out = attend(
        key_rows, live, notes, queries, pairs
    )

    def gather_heads(home):
        twice = jnp.concatenate(home + home, axis=1)
        return lax.dynamic_slice_in_dim(
            twice, lax.rem(line - z, line) * head_width, local_width, 1
        )

    def send_home(pieces):
        return [pieces[0]] + [line_shift(pieces[d], line - d) for d in range(1, line)]

    tokens_in = reorder(tokens)
    g_attn = gain_attn.reshape(1, model_width)
    g_mlp = gain_mlp.reshape(1, model_width)
    (
        attended_low,
        tokens_x,
        output,
        hidden_low,
        hidden_z,
        act_low,
        act_x,
        grad_mlp,
        grad_mlp_x,
        grad_gate,
        _,
        grad_gate_z,
        grad_up,
        grad_up_far,
        grad_attn,
        grads,
        grad_hidden,
        wide_gains,
    ) = block(
        attended_out, w_output, g_attn, g_mlp, tokens, cotangent, w_gate, w_up, w_down
    )
    grad_up_z = line_flip(grad_up_far, 1)
    back = attend_back(
        key_rows, live, notes, code_rows, queries_n, pairs, turned, log_total, grads
    )
    (
        own_down,
        r2_down,
        r1_gate,
        r1_up,
        r2_gate,
        raw_x,
        _,
        raw,
        raw_own,
        narrow_gains,
    ) = middle(
        (*back, q_raw, k_raw, factors, cosines, sines, g_query, g_key),
        (
            act_low,
            act_x,
            grad_mlp,
            grad_mlp_x,
            hidden_low,
            hidden_z,
            grad_gate,
            grad_gate_z,
            grad_up,
            grad_up_z,
        ),
    )
    results = last(
        (raw, raw_own, raw_x, wide_gains, narrow_gains, attended_low),
        (
            hidden_low,
            hidden_z,
            grad_gate,
            grad_gate_z,
            grad_up,
            grad_up_z,
            grad_attn,
            tokens,
            tokens_x,
            own_down,
            r2_down,
            r1_gate,
            r1_up,
            r2_gate,
            w_query,
            w_key,
            w_value,
            grad_hidden,
        ),
    )
    joined = join(results[:5], results[5:10], output, results[10])
    wide, narrow = results[13:]
    gains = jnp.concatenate([wide.reshape(2 * model_width), narrow.reshape(2 * local_width)])
    piece = head_width // (line * pair)

    def gain_piece(start, rows):
        part = gains[start : start + rows * head_width].reshape(rows, head_width)
        return lax.dynamic_slice_in_dim(part, spot * piece, piece, 1)

    all_heads = model_width // head_width
    return (
        *joined,
        gain_piece(2 * model_width, heads_here),
        gain_piece(2 * model_width + local_width, heads_here),
        gain_piece(0, all_heads),
        gain_piece(model_width, all_heads),
    )


def solution(mesh):
    tuned = mesh.shape["dp"] == line * pair and mesh.shape["mp"] == 4
    body = on_device_lines if tuned else on_device_general
    return jax.shard_map(
        body,
        mesh=mesh,
        in_specs=(
            P("dp", None),
            P("dp", None),
            P("dp"),
            P("dp"),
            P("dp"),
            P(None, "mp"),
            P(None, "mp"),
            P(None, "mp"),
            P("mp", None),
            P(None, "mp"),
            P(None, "mp"),
            P("mp", None),
            P("mp", None),
            P("mp", None),
            P(),
            P(),
        ),
        out_specs=(
            P("dp", None),
            P("dp", None),
            P("dp", "mp"),
            P("dp", "mp"),
            P("dp", "mp"),
            P("mp", "dp"),
            P("dp", "mp"),
            P("dp", "mp"),
            P("mp", "dp"),
            P("mp", "dp"),
            P("mp", "dp"),
            P(None, "dp"),
            P(None, "dp"),
        ),
        check_vma=False,
    )
```

```python
import functools
import math

import jax
import jax.numpy as jnp
from jax import lax
from jax.experimental import pallas as pl
from jax.experimental.pallas import tpu as pltpu
from jax.sharding import PartitionSpec as P

epsilon = 1e-06
rope_base = 500000.0
masked_score = -1e30


def rope_tables(positions, head_width):
    freqs = rope_base ** (-jnp.arange(0, head_width // 2, dtype=jnp.float32) * 2.0 / head_width)
    angles = positions.astype(jnp.float32)[:, None] * freqs[None, :]
    return (jnp.cos(angles)[:, None, :], jnp.sin(angles)[:, None, :])


def rotate(values, cosines, sines):
    half = values.shape[-1] // 2
    first = values[..., :half]
    second = values[..., half:]
    return jnp.concatenate(
        [first * cosines - second * sines, second * cosines + first * sines], axis=-1
    )


def norm_back(grad_normed, normed, factor):
    return factor * (grad_normed - normed * jnp.mean(grad_normed * normed, axis=-1, keepdims=True))


def on_device_general(
    tokens,
    cotangent,
    doc_ids,
    row_ids,
    offsets,
    w_query,
    w_key,
    w_value,
    w_output,
    w_gate,
    w_up,
    w_down,
    gain_query,
    gain_key,
    gain_attn,
    gain_mlp,
):
    f32 = jnp.float32
    bf16 = jnp.bfloat16
    row_count = tokens.shape[0]
    model_width = tokens.shape[1]
    heads_here = gain_query.shape[0]
    head_width = gain_query.shape[1]
    local_width = heads_here * head_width
    groups = lax.axis_size("dp")
    key_rows = row_count * groups
    block_rows = min(key_rows, row_count * max(1, 512 // row_count))
    block_count = key_rows // block_rows
    score_scale = 1.0 / math.sqrt(head_width)
    positions = offsets[0] + jnp.arange(row_count, dtype=jnp.int32)
    labels = row_ids[0] * key_rows + doc_ids
    cosines, sines = rope_tables(positions, head_width)
    q_raw = jnp.dot(tokens, w_query, preferred_element_type=f32)
    k_raw = jnp.dot(tokens, w_key, preferred_element_type=f32)
    v_raw = jnp.dot(tokens, w_value, preferred_element_type=f32)
    squares = lax.psum(
        jnp.stack([jnp.sum(q_raw * q_raw, axis=1), jnp.sum(k_raw * k_raw, axis=1)]), "mp"
    )
    q_factor = lax.rsqrt(squares[0] / model_width + epsilon)[:, None]
    k_factor = lax.rsqrt(squares[1] / model_width + epsilon)[:, None]
    g_query = gain_query.reshape(local_width)
    g_key = gain_key.reshape(local_width)
    q_normed = q_raw * q_factor
    k_normed = k_raw * k_factor
    queries = rotate(
        (q_normed * g_query).reshape(row_count, heads_here, head_width), cosines, sines
    ).astype(bf16)
    keys_low = rotate(
        (k_normed * g_key).reshape(row_count, heads_here, head_width), cosines, sines
    ).astype(bf16)
    values_low = v_raw.astype(bf16)
    all_keys, all_values, all_labels, all_positions = (
        lax.all_gather(keys_low.reshape(row_count, local_width), "dp", axis=0, tiled=True),
        lax.all_gather(values_low, "dp", axis=0, tiled=True),
        lax.all_gather(labels, "dp", axis=0, tiled=True),
        lax.all_gather(positions, "dp", axis=0, tiled=True),
    )
    key_blocks = all_keys.reshape(block_count, block_rows, heads_here, head_width)
    value_blocks = all_values.reshape(block_count, block_rows, heads_here, head_width)
    label_blocks = all_labels.reshape(block_count, block_rows)
    position_blocks = all_positions.reshape(block_count, block_rows)
    scanned = (key_blocks, value_blocks, label_blocks, position_blocks)
    low_label = jnp.min(labels)
    high_label = jnp.max(labels)

    def scores_of(key_block, label_block, position_block):
        scores = (
            jnp.einsum("qhd,khd->hqk", queries, key_block, preferred_element_type=f32) * score_scale
        )
        allowed = (labels[:, None] == label_block[None, :]) & (
            positions[:, None] >= position_block[None, :]
        )
        return (scores, allowed[None])

    def touches(label_block):
        return (jnp.max(label_block) >= low_label) & (jnp.min(label_block) <= high_label)

    def max_step(carry, blocks_in):
        key_block, value_block, label_block, position_block = blocks_in

        def max_live_block(state):
            running, totals = state
            scores, allowed = scores_of(key_block, label_block, position_block)
            highest = jnp.maximum(
                running, jnp.max(jnp.where(allowed, scores, masked_score), axis=2)
            )
            weights = jnp.where(allowed, jnp.exp(scores - highest[:, :, None]), 0.0)
            return (highest, totals * jnp.exp(running - highest) + jnp.sum(weights, axis=2))

        return (lax.cond(touches(label_block), max_live_block, lambda state: state, carry), None)

    start_state = (
        jnp.full((heads_here, row_count), masked_score, f32),
        jnp.zeros((heads_here, row_count), f32),
    )
    (running_max, running_total), _ = lax.scan(max_step, start_state, scanned)
    log_total = running_max + jnp.log(running_total)

    def value_step(accum, blocks_in):
        key_block, value_block, label_block, position_block = blocks_in

        def value_live_block(current):
            scores, allowed = scores_of(key_block, label_block, position_block)
            probs_low = jnp.where(allowed, jnp.exp(scores - log_total[:, :, None]), 0.0).astype(
                bf16
            )
            return current + jnp.einsum(
                "hqk,khd->qhd", probs_low, value_block, preferred_element_type=f32
            )

        return (
            lax.cond(touches(label_block), value_live_block, lambda current: current, accum),
            None,
        )

    attended, _ = lax.scan(value_step, jnp.zeros((row_count, heads_here, head_width), f32), scanned)
    attended_low = attended.reshape(row_count, local_width).astype(bf16)
    attn_sum = lax.psum(
        jnp.dot(attended_low, w_output, preferred_element_type=f32).astype(jnp.bfloat16), "mp"
    ).astype(jnp.float32)
    attn_factor = lax.rsqrt(jnp.mean(attn_sum * attn_sum, axis=1, keepdims=True) + epsilon)
    attn_normed = attn_sum * attn_factor
    g_attn = gain_attn.reshape(model_width)
    hidden = tokens.astype(f32) + attn_normed * g_attn
    hidden_low = hidden.astype(bf16)
    gate_val = jnp.dot(hidden_low, w_gate, preferred_element_type=f32)
    up_val = jnp.dot(hidden_low, w_up, preferred_element_type=f32)
    sigmoid_gate = jax.nn.sigmoid(gate_val)
    silu_gate = gate_val * sigmoid_gate
    act_low = (silu_gate * up_val).astype(bf16)
    mlp_sum = lax.psum(
        jnp.dot(act_low, w_down, preferred_element_type=f32).astype(jnp.bfloat16), "mp"
    ).astype(jnp.float32)
    mlp_factor = lax.rsqrt(jnp.mean(mlp_sum * mlp_sum, axis=1, keepdims=True) + epsilon)
    mlp_normed = mlp_sum * mlp_factor
    g_mlp = gain_mlp.reshape(model_width)
    output = (hidden + mlp_normed * g_mlp).astype(bf16)
    grad_out = cotangent.astype(f32)
    grad_gain_mlp = jnp.sum(grad_out * mlp_normed, axis=0)
    grad_mlp = norm_back(grad_out * g_mlp, mlp_normed, mlp_factor).astype(bf16)
    grad_w_down = jnp.einsum("tf,td->fd", act_low, grad_mlp, preferred_element_type=f32)
    grad_act = jnp.einsum("td,fd->tf", grad_mlp, w_down, preferred_element_type=f32)
    slope = sigmoid_gate * (1.0 + gate_val * (1.0 - sigmoid_gate))
    grad_gate = (grad_act * up_val * slope).astype(bf16)
    grad_up = (grad_act * silu_gate).astype(bf16)
    branch_grad = jnp.einsum(
        "tf,df->td", grad_gate, w_gate, preferred_element_type=f32
    ) + jnp.einsum("tf,df->td", grad_up, w_up, preferred_element_type=f32)
    grad_hidden = grad_out + lax.psum(branch_grad.astype(jnp.bfloat16), "mp").astype(jnp.float32)
    grad_gain_attn = jnp.sum(grad_hidden * attn_normed, axis=0)
    grad_attn = norm_back(grad_hidden * g_attn, attn_normed, attn_factor).astype(bf16)
    grad_w_output = jnp.einsum("tc,td->cd", attended_low, grad_attn, preferred_element_type=f32)
    grad_attended = (
        jnp.einsum("td,cd->tc", grad_attn, w_output, preferred_element_type=f32)
        .astype(bf16)
        .reshape(row_count, heads_here, head_width)
    )
    delta = jnp.sum(grad_attended.astype(f32) * attended, axis=2).T

    def grad_step(grad_q, blocks_in):
        key_block, value_block, label_block, position_block = blocks_in

        def grad_live_block(current):
            scores, allowed = scores_of(key_block, label_block, position_block)
            probs = jnp.where(allowed, jnp.exp(scores - log_total[:, :, None]), 0.0)
            grad_probs = jnp.einsum(
                "qhd,khd->hqk", grad_attended, value_block, preferred_element_type=f32
            )
            grad_scores = (probs * (grad_probs - delta[:, :, None])).astype(bf16)
            value_term = jnp.einsum(
                "hqk,qhd->khd", probs.astype(bf16), grad_attended, preferred_element_type=f32
            )
            key_term = jnp.einsum("hqk,qhd->khd", grad_scores, queries, preferred_element_type=f32)
            updated = current + jnp.einsum(
                "hqk,khd->qhd", grad_scores, key_block, preferred_element_type=f32
            )
            return (updated, (key_term, value_term))

        def skip_block(current):
            nothing = jnp.zeros((block_rows, heads_here, head_width), f32)
            return (current, (nothing, nothing))

        return lax.cond(touches(label_block), grad_live_block, skip_block, grad_q)

    grad_queries, (key_terms, value_terms) = lax.scan(
        grad_step, jnp.zeros((row_count, heads_here, head_width), f32), scanned
    )
    grad_keys, grad_values = (
        lax.psum_scatter(
            (key_terms.reshape(key_rows, local_width) * score_scale).astype(jnp.bfloat16),
            "dp",
            scatter_dimension=0,
            tiled=True,
        ).astype(jnp.float32),
        lax.psum_scatter(
            value_terms.reshape(key_rows, local_width).astype(jnp.bfloat16),
            "dp",
            scatter_dimension=0,
            tiled=True,
        ).astype(jnp.float32),
    )
    grad_values_low = grad_values.astype(bf16)
    back_q = rotate(grad_queries * score_scale, cosines, -sines).reshape(row_count, local_width)
    back_k = rotate(grad_keys.reshape(row_count, heads_here, head_width), cosines, -sines).reshape(
        row_count, local_width
    )
    grad_gain_query = jnp.sum(back_q * q_normed, axis=0).reshape(heads_here, head_width)
    grad_gain_key = jnp.sum(back_k * k_normed, axis=0).reshape(heads_here, head_width)
    scaled_q = back_q * g_query
    scaled_k = back_k * g_key
    inner = lax.psum(
        jnp.stack([jnp.sum(scaled_q * q_normed, axis=1), jnp.sum(scaled_k * k_normed, axis=1)]),
        "mp",
    )
    grad_q_raw = (q_factor * (scaled_q - q_normed * inner[0][:, None] / model_width)).astype(bf16)
    grad_k_raw = (k_factor * (scaled_k - k_normed * inner[1][:, None] / model_width)).astype(bf16)
    input_term = (
        jnp.einsum("tc,dc->td", grad_q_raw, w_query, preferred_element_type=f32)
        + jnp.einsum("tc,dc->td", grad_k_raw, w_key, preferred_element_type=f32)
        + jnp.einsum("tc,dc->td", grad_values_low, w_value, preferred_element_type=f32)
    )
    grad_tokens = (
        grad_hidden + lax.psum(input_term.astype(jnp.bfloat16), "mp").astype(jnp.float32)
    ).astype(bf16)
    local_w_query = jnp.einsum("td,tc->dc", tokens, grad_q_raw, preferred_element_type=f32)
    local_w_key = jnp.einsum("td,tc->dc", tokens, grad_k_raw, preferred_element_type=f32)
    local_w_value = jnp.einsum("td,tc->dc", tokens, grad_values_low, preferred_element_type=f32)
    local_w_gate = jnp.einsum("td,tf->df", hidden_low, grad_gate, preferred_element_type=f32)
    local_w_up = jnp.einsum("td,tf->df", hidden_low, grad_up, preferred_element_type=f32)
    grad_w_query, grad_w_key, grad_w_value, grad_w_gate, grad_w_up = (
        lax.psum_scatter(
            local_w_query.astype(jnp.bfloat16), "dp", scatter_dimension=0, tiled=True
        ).astype(jnp.float32),
        lax.psum_scatter(
            local_w_key.astype(jnp.bfloat16), "dp", scatter_dimension=0, tiled=True
        ).astype(jnp.float32),
        lax.psum_scatter(
            local_w_value.astype(jnp.bfloat16), "dp", scatter_dimension=0, tiled=True
        ).astype(jnp.float32),
        lax.psum_scatter(
            local_w_gate.astype(jnp.bfloat16), "dp", scatter_dimension=0, tiled=True
        ).astype(jnp.float32),
        lax.psum_scatter(
            local_w_up.astype(jnp.bfloat16), "dp", scatter_dimension=0, tiled=True
        ).astype(jnp.float32),
    )
    summed_out, summed_down, summed_gq, summed_gk, summed_ga, summed_gm = (
        lax.psum_scatter(
            grad_w_output.astype(jnp.bfloat16), "dp", scatter_dimension=1, tiled=True
        ).astype(jnp.float32),
        lax.psum_scatter(
            grad_w_down.astype(jnp.bfloat16), "dp", scatter_dimension=1, tiled=True
        ).astype(jnp.float32),
        lax.psum_scatter(
            grad_gain_query.astype(jnp.bfloat16), "dp", scatter_dimension=1, tiled=True
        ).astype(jnp.float32),
        lax.psum_scatter(
            grad_gain_key.astype(jnp.bfloat16), "dp", scatter_dimension=1, tiled=True
        ).astype(jnp.float32),
        lax.psum_scatter(
            grad_gain_attn.reshape(gain_attn.shape).astype(jnp.bfloat16),
            "dp",
            scatter_dimension=1,
            tiled=True,
        ).astype(jnp.float32),
        lax.psum_scatter(
            grad_gain_mlp.reshape(gain_mlp.shape).astype(jnp.bfloat16),
            "dp",
            scatter_dimension=1,
            tiled=True,
        ).astype(jnp.float32),
    )
    return (
        output,
        grad_tokens,
        grad_w_query,
        grad_w_key,
        grad_w_value,
        summed_out,
        grad_w_gate,
        grad_w_up,
        summed_down,
        summed_gq,
        summed_gk,
        summed_ga,
        summed_gm,
    )


line = 4
pair = 2
low_score = -1e30
start_max = -1e20
big_vmem = 56 << 20


def line_shift(value, step):
    moves = [
        (z * pair + x, ((z + step) % line) * pair + x) for z in range(line) for x in range(pair)
    ]
    return lax.ppermute(value, "dp", moves)


def line_flip(value, bit):
    return lax.ppermute(
        value, "dp", [(z * pair + x, (z ^ bit) * pair + x) for z in range(line) for x in range(pair)]
    )


def x_swap(value):
    return lax.ppermute(value, "dp", [(i, i ^ 1) for i in range(line * pair)])


def core_swap(value):
    return lax.ppermute(value, "mp", [(i, i ^ 1) for i in range(4)])


def y_swap(value):
    return lax.ppermute(value, "mp", [(i, i ^ 2) for i in range(4)])


def flip_cores(value, axis):
    quarter = value.shape[axis] // 4
    cuts = [lax.slice_in_dim(value, i * quarter, (i + 1) * quarter, axis=axis) for i in (1, 0, 3, 2)]
    return jnp.concatenate(cuts, axis=axis)


def token_sum(value):
    value = value + flip_cores(core_swap(value), 1)
    return value + y_swap(value)


def own_part(value):
    quarter = value.shape[0] // 4
    return jnp.concatenate([value[:quarter], value[2 * quarter : 3 * quarter]], axis=0)


def other_part(value):
    quarter = value.shape[0] // 4
    return jnp.concatenate([value[quarter : 2 * quarter], value[3 * quarter :]], axis=0)


def join_parts(own, other):
    half = own.shape[0] // 2
    return jnp.concatenate([own[:half], other[:half], own[half:], other[half:]], axis=0)


def reduce_own_rows(partial_low):
    f32 = jnp.float32
    arrived = core_swap(other_part(partial_low))
    chip_sum = (own_part(partial_low).astype(f32) + arrived.astype(f32)).astype(jnp.bfloat16)
    return chip_sum.astype(f32) + y_swap(chip_sum).astype(f32)


def dot_t(first, second):
    return lax.dot_general(
        first, second, (((0,), (0,)), ((), ())), preferred_element_type=jnp.float32
    )


def dot_nt(first, second):
    return lax.dot_general(
        first, second, (((1,), (1,)), ((), ())), preferred_element_type=jnp.float32
    )


def vmem_specs(count):
    return [pl.BlockSpec(memory_space=pltpu.VMEM)] * count


def project_kernel(
    tokens,
    wq,
    wk,
    wv,
    gq,
    gk,
    cosines,
    sines,
    spots,
    out_queries,
    out_pairs,
    out_notes,
    out_q_raw,
    out_k_raw,
    rows_keep,
    query_keep,
    pair_keep,
    squares,
    squares_core,
    squares_y,
    send_sems,
    recv_sems,
    local_sems,
):
    f32 = jnp.float32
    bf16 = jnp.bfloat16
    width = cosines.shape[1]
    depth = wq.shape[0]
    rows = rows_keep.shape[0] // 2
    count = rows // 2
    mp = lax.axis_index("mp")
    spot = lax.axis_index("dp")
    core = lax.rem(mp, 2)
    x = lax.rem(spot, 2)
    z = spot // 2
    core_peer = {"mp": mp + 1 - 2 * core}
    y_peer = {"mp": lax.rem(mp + 2, 4)}
    x_peer = {"dp": spot + 1 - 2 * x}
    ahead = [{"dp": lax.rem(spot + 2 * d, 2 * line)} for d in range(line)]
    head = [lax.rem(z + d, line) for d in range(line)]
    both = lambda s: pl.ds(s * rows, rows)
    remote = []

    def send(source, target, peer):
        index = len(remote)
        copy = pltpu.make_async_remote_copy(
            src_ref=source,
            dst_ref=target,
            send_sem=send_sems.at[index],
            recv_sem=recv_sems.at[index],
            device_id=peer,
            device_id_type=pl.DeviceIdType.MESH,
        )
        remote.append(copy)
        copy.start()
        return copy

    loads = []
    for s in range(2):
        for part, place in ((0, core), (1, 1 - core)):
            start = pl.multiple_of(place * rows + s * count, count)
            copy = pltpu.make_async_copy(
                tokens.at[pl.ds(start, count)],
                rows_keep.at[pl.ds(s * rows + part * count, count)],
                local_sems.at[2 * s + part],
            )
            copy.start()
            loads.append(copy)

    barrier = pltpu.get_barrier_semaphore()
    peers = (core_peer, y_peer, x_peer, ahead[1], ahead[2], ahead[3])
    for peer in peers:
        pl.semaphore_signal(barrier, inc=1, device_id=peer, device_id_type=pl.DeviceIdType.MESH)
    pl.semaphore_wait(barrier, len(peers))

    def turned(raw, gain, s, h):
        part = raw[:, h * width : (h + 1) * width] * gain[:, h * width : (h + 1) * width]
        return (
            part * cosines[both(s), :] + pltpu.roll(part, width // 2, 1) * sines[both(s), :]
        ).astype(bf16)

    flying = {}
    for s in range(2):
        loads[2 * s].wait()
        loads[2 * s + 1].wait()
        k_raw = jnp.dot(rows_keep[both(s), :], wk[...], preferred_element_type=f32)
        out_k_raw[both(s), :] = k_raw
        squares[1:2, both(s)] = jnp.sum((k_raw * k_raw).T, axis=0, keepdims=True)
        v_raw = jnp.dot(rows_keep[both(s), :], wv[...], preferred_element_type=f32)
        for h in range(line):
            pair_keep[h, 0, both(s), :] = turned(k_raw, gk[...], s, h)
            pair_keep[h, 1, both(s), :] = v_raw[:, h * width : (h + 1) * width].astype(bf16)
        for d in (2, 1, 3):
            flying["pair", s, d] = send(
                pair_keep.at[head[d], :, both(s)], out_pairs.at[d, :, both(s)], ahead[d]
            )
        flying["far", s, 0] = send(
            pair_keep.at[z, :, both(s)], out_pairs.at[line, :, both(s)], x_peer
        )
        q_raw = jnp.dot(rows_keep[both(s), :], wq[...], preferred_element_type=f32)
        out_q_raw[both(s), :] = q_raw
        squares[0:1, both(s)] = jnp.sum((q_raw * q_raw).T, axis=0, keepdims=True)
        for h in range(line):
            query_keep[h, both(s), :] = turned(q_raw, gq[...], s, h)

    core_copy = send(squares, squares_core, core_peer)
    core_copy.wait()
    arrived = squares_core[...]
    cuts = [arrived[:, i * count : (i + 1) * count] for i in (1, 0, 3, 2)]
    chip = squares[...] + jnp.concatenate(cuts, axis=1)
    squares[...] = chip
    y_copy = send(squares, squares_y, y_peer)
    y_copy.wait()
    out_notes[0, 0:2, :] = lax.rsqrt((chip + squares_y[...]) / depth + epsilon)
    out_notes[0, 2:4, :] = spots[...]
    for d in range(1, line):
        flying["note", d] = send(out_notes.at[0], out_notes.at[d], ahead[d])
    flying["far_note", 0] = send(out_notes.at[0], out_notes.at[line], x_peer)
    for d in range(1, line):
        flying["query", d] = send(query_keep.at[head[d]], out_queries.at[d], ahead[d])
    out_queries[0] = query_keep[z]
    out_pairs[0] = pair_keep[z]
    for s in range(2):
        for d in (2, 1, 3):
            flying["pair", s, d].wait()
            flying["far", s, d] = send(
                out_pairs.at[d, :, both(s)], out_pairs.at[line + d, :, both(s)], x_peer
            )
    for d in range(1, line):
        flying["note", d].wait()
        flying["far_note", d] = send(out_notes.at[d], out_notes.at[line + d], x_peer)
    for d in range(1, line):
        flying["query", d].wait()
    for d in range(line):
        flying["far_note", d].wait()
        for s in range(2):
            flying["far", s, d].wait()


def project(tokens, wq, wk, wv, gq, gk, cosines, sines, spots):
    rows, depth = tokens.shape
    columns = wq.shape[1]
    width = columns // line
    f32 = jnp.float32
    bf16 = jnp.bfloat16
    return pl.pallas_call(
        project_kernel,
        in_specs=[pl.BlockSpec(memory_space=pl.ANY)] + vmem_specs(8),
        out_specs=vmem_specs(5),
        out_shape=[
            jax.ShapeDtypeStruct((line, rows, width), bf16),
            jax.ShapeDtypeStruct((2 * line, 2, rows, width), bf16),
            jax.ShapeDtypeStruct((2 * line, 4, rows), f32),
            jax.ShapeDtypeStruct((rows, columns), f32),
            jax.ShapeDtypeStruct((rows, columns), f32),
        ],
        scratch_shapes=[
            pltpu.VMEM((rows, depth), bf16),
            pltpu.VMEM((line, rows, width), bf16),
            pltpu.VMEM((line, 2, rows, width), bf16),
            pltpu.VMEM((2, rows), f32),
            pltpu.VMEM((2, rows), f32),
            pltpu.VMEM((2, rows), f32),
            pltpu.SemaphoreType.DMA((28,)),
            pltpu.SemaphoreType.DMA((28,)),
            pltpu.SemaphoreType.DMA((4,)),
        ],
        compiler_params=pltpu.CompilerParams(
            vmem_limit_bytes=48 << 20, collective_id=2, has_side_effects=True
        ),
        cost_estimate=pl.CostEstimate(flops=0, bytes_accessed=0, transcendentals=0),
    )(tokens, wq, wk, wv, gq, gk, cosines, sines, spots)


def visible_scores(key, query, key_code, query_code, query_low, factor):
    scores = dot_nt(key, query) * factor
    codes = jnp.concatenate([key_code] * (query.shape[0] // key_code.shape[1]), axis=1)
    return jnp.where((codes <= query_code) & (codes >= query_low), scores, low_score)


def fill_keys(key_rows, notes, pairs, keys, codes):
    count, width = keys.shape[1:]

    def column(row):
        return jnp.broadcast_to(row, (width, count)).T

    for k in range(2 * line):
        factor = column(notes[k, 1:2, :])
        keys[k] = (pairs[k, 0].astype(jnp.float32) * factor).astype(jnp.bfloat16)
        labels = column(notes[k, 2:3, :]).astype(jnp.int32)
        codes[k] = labels * key_rows + column(notes[k, 3:4, :]).astype(jnp.int32)


def attend_kernel(factor, key_rows, live, notes, *refs):
    queries, pairs = refs[:2]
    out_turned, out_log, out_query, out_rows, out = refs[2:7]
    top, total, accum, out_key, out_codes = refs[7:]
    f32 = jnp.float32
    bf16 = jnp.bfloat16
    count, width = queries.shape[1:]

    def column(row):
        return jnp.broadcast_to(row, (width, count)).T

    fill_keys(key_rows, notes, pairs, out_key, out_codes)
    for q in range(line):
        out_query[q] = (queries[q].astype(f32) * column(notes[q, 0:1, :])).astype(bf16)
        base = notes[q, 2:3, :].astype(jnp.int32) * key_rows
        out_rows[q : q + 1, :] = base + notes[q, 3:4, :].astype(jnp.int32)
        out_rows[line + q : line + q + 1, :] = base

    for q in range(line):
        top[...] = jnp.full_like(top, start_max)
        total[...] = jnp.zeros_like(total)
        accum[...] = jnp.zeros_like(accum)
        @pl.loop(0, 2 * line)
        def _(k, q=q):
            @pl.when(live[q, k] > 0)
            def _():
                scores = visible_scores(
                    out_key[k],
                    out_query[q],
                    out_codes[k],
                    out_rows[q : q + 1, :],
                    out_rows[line + q : line + q + 1, :],
                    factor,
                )
                highest = jnp.maximum(top[...], jnp.max(scores, axis=0, keepdims=True))
                weights = jnp.exp2(scores - highest)
                fade = jnp.exp2(top[...] - highest)
                total[...] = total[...] * fade + jnp.sum(weights, axis=0, keepdims=True)
                accum[...] = accum[...] * fade + dot_t(pairs[k, 1], weights.astype(bf16))
                top[...] = highest

        turned = accum[...] / total[...]
        out_turned[q] = turned
        out_log[q : q + 1, :] = top[...] + jnp.log2(total[...])
        out[q] = turned.T.astype(bf16)


def attend_back_kernel(factor, scale, key_rows, live, notes, rows, queries, *refs):
    pairs, turned, log_total, grads = refs[:4]
    out_query, out_near, out_far, key_sum, value_sum, query_sum, keys, codes = refs[4:]
    fill_keys(key_rows, notes, pairs, keys, codes)
    f32 = jnp.float32
    bf16 = jnp.bfloat16
    key_sum[...] = jnp.zeros_like(key_sum)
    value_sum[...] = jnp.zeros_like(value_sum)
    for q in range(line):
        query_sum[...] = jnp.zeros_like(query_sum)
        delta = jnp.sum(grads[q].astype(f32).T * turned[q], axis=0, keepdims=True)
        @pl.loop(0, 2 * line)
        def _(k, q=q, delta=delta):
            @pl.when(live[q, k] > 0)
            def _():
                query, key, grad = queries[q], keys[k], grads[q]
                scores = visible_scores(
                    key,
                    query,
                    codes[k],
                    rows[q : q + 1, :],
                    rows[line + q : line + q + 1, :],
                    factor,
                )
                probs = jnp.exp2(scores - log_total[q : q + 1, :])
                grad_probs = dot_nt(pairs[k, 1], grad)
                grad_scores = (probs * (grad_probs - delta)).astype(bf16)
                value_sum[k] += jnp.dot(
                    probs.astype(bf16), grad, preferred_element_type=f32
                )
                key_sum[k] += jnp.dot(grad_scores, query, preferred_element_type=f32)
                query_sum[...] += dot_t(key, grad_scores)

        out_query[q] = (query_sum[...] * scale).T.astype(bf16)
    for k in range(line):
        for out, base in ((out_near, 0), (out_far, line)):
            out[k, 0] = (key_sum[base + k] * scale).astype(bf16)
            out[k, 1] = value_sum[base + k].astype(bf16)


def attend(key_rows, live, notes, queries, pairs):
    _, count, width = queries.shape
    factor = math.log2(math.e) / math.sqrt(width)
    f32 = jnp.float32
    bf16 = jnp.bfloat16
    return pl.pallas_call(
        functools.partial(attend_kernel, factor, key_rows),
        out_shape=[
            jax.ShapeDtypeStruct((line, width, count), f32),
            jax.ShapeDtypeStruct((2 * line, count), f32),
            jax.ShapeDtypeStruct((line, count, width), bf16),
            jax.ShapeDtypeStruct((2 * line, count), jnp.int32),
        ]
        + [jax.ShapeDtypeStruct((line, count, width), bf16)],
        in_specs=[pl.BlockSpec(memory_space=pltpu.SMEM)] + vmem_specs(3),
        out_specs=vmem_specs(5),
        scratch_shapes=[
            pltpu.VMEM((1, count), f32),
            pltpu.VMEM((1, count), f32),
            pltpu.VMEM((width, count), f32),
            pltpu.VMEM((2 * line, count, width), bf16),
            pltpu.VMEM((2 * line, count, width), jnp.int32),
        ],
        compiler_params=pltpu.CompilerParams(vmem_limit_bytes=40 << 20),
        cost_estimate=pl.CostEstimate(flops=0, bytes_accessed=0, transcendentals=0),
    )(live, notes, queries, pairs)


def attend_back(key_rows, live, notes, rows, queries, pairs, turned, log_total, grads):
    _, count, width = queries.shape
    scale = 1.0 / math.sqrt(width)
    factor = math.log2(math.e) * scale
    f32 = jnp.float32
    return pl.pallas_call(
        functools.partial(attend_back_kernel, factor, scale, key_rows),
        out_shape=[jax.ShapeDtypeStruct((line, count, width), jnp.bfloat16)]
        + [jax.ShapeDtypeStruct((line, 2, count, width), jnp.bfloat16)] * 2,
        in_specs=[pl.BlockSpec(memory_space=pltpu.SMEM)] + vmem_specs(7),
        out_specs=vmem_specs(3),
        scratch_shapes=[
            pltpu.VMEM((2 * line, count, width), f32),
            pltpu.VMEM((2 * line, count, width), f32),
            pltpu.VMEM((width, count), f32),
            pltpu.VMEM((2 * line, count, width), jnp.bfloat16),
            pltpu.VMEM((2 * line, count, width), jnp.int32),
        ],
        compiler_params=pltpu.CompilerParams(vmem_limit_bytes=40 << 20),
        cost_estimate=pl.CostEstimate(
            flops=20 * line * line * count * count * width,
            bytes_accessed=12 << 20,
            transcendentals=2 * line * line * count * count,
        ),
    )(live, notes, rows, queries, pairs, turned, log_total, grads)


def block_kernel(
    pieces,
    w_out,
    g_attn,
    g_mlp,
    tokens,
    cotangent,
    w_gate_in,
    w_up_in,
    w_down_in,
    out_heads,
    out_tokens_x,
    out_output,
    out_hidden,
    out_hidden_z,
    out_act,
    out_act_x,
    out_mlp,
    out_mlp_x,
    out_gate,
    out_gate_far,
    out_gate_z,
    out_up,
    out_up_fa,
    out_up_fb,
    out_attn,
    out_grads,
    out_grad_hidden,
    out_gain,
    w_gate,
    w_up,
    w_down,
    gate_keep,
    up_keep,
    act_keep,
    hidden_keep,
    mlp_keep,
    attn_keep,
    grad_gate,
    grad_up,
    own_factor,
    own_normed,
    own_tokens,
    own_cotangent,
    attended,
    heads_keep,
    total,
    part_send,
    part_recv,
    y_send,
    y_recv,
    send_sems,
    recv_sems,
    local_sems,
):
    f32 = jnp.float32
    bf16 = jnp.bfloat16
    depth = w_out.shape[1]
    units = w_gate.shape[1]
    tile = 512
    count = own_tokens.shape[0] // 2
    rows = 2 * count
    mp = lax.axis_index("mp")
    spot = lax.axis_index("dp")
    core = lax.rem(mp, 2)
    core_peer = {"mp": mp + 1 - 2 * core}
    y_peer = {"mp": lax.rem(mp + 2, 4)}
    z = spot // 2
    z_low = lax.rem(z, 2)
    z_peer = {"dp": spot + 2 - 4 * z_low}
    x = lax.rem(spot, 2)
    x_peer = {"dp": spot + 1 - 2 * x}
    width = pieces.shape[2]
    ahead = [{"dp": lax.rem(spot + 2 * d, 2 * line)} for d in range(line)]
    head = lambda d: pl.ds(pl.multiple_of(lax.rem(z + d, line) * width, width), width)

    remote, started, local = [], [], []

    def send(source, target, peer):
        index = len(remote)
        copy = pltpu.make_async_remote_copy(
            src_ref=source,
            dst_ref=target,
            send_sem=send_sems.at[index],
            recv_sem=recv_sems.at[index],
            device_id=peer,
            device_id_type=pl.DeviceIdType.MESH,
        )
        remote.append(copy)
        copy.start()
        return copy

    def keep_out(source, target, waited=False):
        copy = pltpu.make_async_copy(source, target, local_sems.at[len(started)])
        started.append(copy)
        if not waited:
            local.append(copy)
        copy.start()
        return copy

    own = lambda s: pl.ds(s * rows, count)
    other = lambda s: pl.ds(s * rows + count, count)
    both = lambda s: pl.ds(s * rows, rows)
    mine = lambda s: pl.ds(s * count, count)
    at_home = lambda s: pl.ds(pl.multiple_of(core * rows + s * count, count), count)
    cut = lambda t: pl.ds(pl.multiple_of(t * tile, tile), tile)
    flying = {}

    home_rows = pl.ds(pl.multiple_of(core * rows, rows), rows)
    loads = [
        keep_out(tokens.at[home_rows], own_tokens, True),
        keep_out(cotangent.at[home_rows], own_cotangent, True),
        keep_out(w_gate_in, w_gate, True),
        keep_out(w_up_in, w_up, True),
        keep_out(w_down_in, w_down, True),
    ]
    barrier = pltpu.get_barrier_semaphore()
    peers = (core_peer, y_peer, x_peer, ahead[1], ahead[2], ahead[3])
    for peer in peers:
        pl.semaphore_signal(barrier, inc=1, device_id=peer, device_id_type=pl.DeviceIdType.MESH)
    pl.semaphore_wait(barrier, len(peers))
    for s in range(2):
        for d in range(1, line):
            flying["heads", s, d] = send(
                pieces.at[d, both(s)], attended.at[both(s), head(0)], ahead[line - d]
            )
    attended[:, head(0)] = pieces[0]

    loads[0].wait()
    for s in range(2):
        flying["tokens", s] = send(own_tokens.at[mine(s)], out_tokens_x.at[own(s)], x_peer)

    def forward_core(name, s, array):
        flying[name, s].wait()
        flying[name + "_core", s] = send(array.at[own(s)], array.at[other(s)], core_peer)

    def reduce_start(stage, s):
        part_send[s] = total[count:, :].astype(bf16)
        copy = send(part_send.at[s], part_recv.at[s], core_peer)
        copy.wait()
        y_send[s] = (total[:count, :] + part_recv[s].astype(f32)).astype(bf16)
        flying[stage, s] = send(y_send.at[s], y_recv.at[stage, s], y_peer)

    def reduced(stage, s):
        flying[stage, s].wait()
        return y_send[s].astype(f32) + y_recv[stage, s].astype(f32)

    def factor_of(value):
        return lax.rsqrt(jnp.mean(value * value, axis=1, keepdims=True) + epsilon)

    def share(keep, s):
        flying["share", s] = send(keep.at[own(s)], keep.at[other(s)], core_peer)

    def project_out(s):
        for d in range(1, line):
            flying["heads", s, d].wait()
        keep_out(attended.at[both(s)], out_heads.at[both(s)])
        total[...] = jnp.dot(attended[both(s), :], w_out[...], preferred_element_type=f32)
        reduce_start(0, s)

    def after_attention(s):
        value = reduced(0, s)
        factor = factor_of(value)
        normed = value * factor
        own_factor[mine(s), :] = jnp.broadcast_to(factor, (count, own_factor.shape[1]))
        own_normed[mine(s), :] = normed
        hidden = own_tokens[mine(s), :].astype(f32) + normed * g_attn[...]
        out_grad_hidden[mine(s), :] = hidden
        hidden_keep[own(s), :] = hidden.astype(bf16)
        share(hidden_keep, s)

    def forward(s):
        flying["hidden", s] = send(hidden_keep.at[own(s)], out_hidden_z.at[own(s)], z_peer)
        flying["share", s].wait()
        keep_out(hidden_keep.at[both(s)], out_hidden.at[both(s)])

        def step(t):
            hidden = hidden_keep[both(s), :]
            gate = jnp.dot(hidden, w_gate[:, cut(t)], preferred_element_type=f32)
            up = jnp.dot(hidden, w_up[:, cut(t)], preferred_element_type=f32)
            gate_keep[both(s), cut(t)] = gate.astype(bf16)
            up_keep[both(s), cut(t)] = up.astype(bf16)
            act = (gate * jax.nn.sigmoid(gate) * up).astype(bf16)
            act_keep[both(s), cut(t)] = act
            return jnp.dot(act, w_down[cut(t), :], preferred_element_type=f32)

        total[...] = step(0)

        @pl.loop(1, units // tile)
        def _(t):
            total[...] += step(t)

        reduce_start(1, s)
        keep_out(act_keep.at[both(s)], out_act.at[both(s)])
        half = units // 2
        far = pl.ds(pl.multiple_of((1 - x) * half, half), half)
        flying["act", s] = send(act_keep.at[both(s), far], out_act_x.at[both(s)], x_peer)

    def turn_point(s):
        value = reduced(1, s)
        factor = factor_of(value)
        normed = value * factor
        forward_core("tokens", s, out_tokens_x)
        own_tokens[mine(s), :] = (out_grad_hidden[mine(s), :] + normed * g_mlp[...]).astype(bf16)
        keep_out(own_tokens.at[mine(s)], out_output.at[at_home(s)])
        flying["output", s] = send(own_tokens.at[mine(s)], out_output.at[at_home(s)], core_peer)
        grad = own_cotangent[mine(s), :].astype(f32)
        gain = jnp.sum(grad * normed, axis=0, keepdims=True)
        out_gain[1:2, :] = gain if s == 0 else out_gain[1:2, :] + gain
        mlp_keep[own(s), :] = norm_back(grad * g_mlp[...], normed, factor).astype(bf16)
        share(mlp_keep, s)

    def backward(s):
        flying["mlp", s] = send(mlp_keep.at[own(s)], out_mlp_x.at[own(s)], x_peer)
        flying["share", s].wait()
        keep_out(mlp_keep.at[both(s)], out_mlp.at[both(s)])

        def step(t):
            grad_act = dot_nt(mlp_keep[both(s), :], w_down[cut(t), :])
            gate = gate_keep[both(s), cut(t)].astype(f32)
            up = up_keep[both(s), cut(t)].astype(f32)
            sigmoid = jax.nn.sigmoid(gate)
            to_gate = (grad_act * up * (sigmoid * (1.0 + gate * (1.0 - sigmoid)))).astype(bf16)
            to_up = (grad_act * (gate * sigmoid)).astype(bf16)
            grad_gate[:, cut(t)] = to_gate
            grad_up[:, cut(t)] = to_up
            return dot_nt(to_gate, w_gate[:, cut(t)]) + dot_nt(to_up, w_up[:, cut(t)])

        if s > 0:
            gate_to_z(0)
        total[...] = step(0)

        @pl.loop(1, units // tile)
        def _(t):
            total[...] += step(t)

        reduce_start(2, s)
        half = units // 2
        far = pl.ds(pl.multiple_of((1 - z_low) * half, half), half)
        flying["grads"] = [
            keep_out(source, target, waited=True)
            for source, target in (
                (grad_gate, out_gate.at[both(s)]),
                (grad_gate.at[:, far], out_gate_far.at[both(s)]),
                (grad_up, out_up.at[both(s)]),
                (grad_up.at[:, far], (out_up_fa, out_up_fb)[s]),
            )
        ]

    def gate_to_z(s):
        for copy in flying["grads"]:
            copy.wait()
        flying["gate_z", s] = send(out_gate_far.at[both(s)], out_gate_z.at[both(s)], z_peer)

    def to_attention(s):
        value = reduced(2, s)
        grad = own_cotangent[mine(s), :].astype(f32) + value
        out_grad_hidden[mine(s), :] = grad
        normed = own_normed[mine(s), :]
        gain = jnp.sum(grad * normed, axis=0, keepdims=True)
        out_gain[0:1, :] = gain if s == 0 else out_gain[0:1, :] + gain
        factor = own_factor[mine(s), 0:1]
        attn_keep[own(s), :] = norm_back(grad * g_attn[...], normed, factor).astype(bf16)
        share(attn_keep, s)

    def attended_grad(s):
        flying["share", s].wait()
        keep_out(attn_keep.at[both(s)], out_attn.at[both(s)])
        heads_keep[both(s), :] = dot_nt(attn_keep[both(s), :], w_out[...]).astype(bf16)
        for d in range(1, line):
            flying["grads", s, d] = send(
                heads_keep.at[both(s), head(d)], out_grads.at[d, both(s)], ahead[d]
            )
        keep_out(heads_keep.at[both(s), head(0)], out_grads.at[0, both(s)])

    project_out(0)
    project_out(1)
    for load in loads[1:]:
        load.wait()
    after_attention(0)
    forward(0)
    after_attention(1)
    forward(1)
    turn_point(0)
    backward(0)
    turn_point(1)
    backward(1)
    gate_to_z(1)
    for s in range(2):
        forward_core("hidden", s, out_hidden_z)
    to_attention(0)
    attended_grad(0)
    to_attention(1)
    attended_grad(1)
    for s in range(2):
        flying["act", s].wait()
        flying["output", s].wait()
        forward_core("mlp", s, out_mlp_x)
    for s in range(2):
        flying["tokens_core", s].wait()
        flying["gate_z", s].wait()
        flying["hidden_core", s].wait()
        flying["mlp_core", s].wait()
        for d in range(1, line):
            flying["grads", s, d].wait()
    for copy in local:
        copy.wait()


def block(pieces, w_out, g_attn, g_mlp, tokens, cotangent, w_gate, w_up, w_down):
    _, rows, width = pieces.shape
    columns = line * width
    depth, units = w_gate.shape
    half = rows // 2
    quarter = rows // 4
    f32 = jnp.float32
    bf16 = jnp.bfloat16
    wide = jax.ShapeDtypeStruct((rows, depth), bf16)
    tall = jax.ShapeDtypeStruct((rows, units), bf16)
    any_spec = pl.BlockSpec(memory_space=pl.ANY)
    return pl.pallas_call(
        block_kernel,
        out_shape=[
            jax.ShapeDtypeStruct((rows, columns), bf16),
            wide,
            wide,
            wide,
            wide,
            tall,
            jax.ShapeDtypeStruct((rows, units // 2), bf16),
            wide,
            wide,
            tall,
            jax.ShapeDtypeStruct((rows, units // 2), bf16),
            jax.ShapeDtypeStruct((rows, units // 2), bf16),
            tall,
            jax.ShapeDtypeStruct((half, units // 2), bf16),
            jax.ShapeDtypeStruct((half, units // 2), bf16),
            wide,
            jax.ShapeDtypeStruct((line, rows, width), bf16),
            jax.ShapeDtypeStruct((half, depth), f32),
            jax.ShapeDtypeStruct((2, depth), f32),
        ],
        in_specs=vmem_specs(4) + [any_spec] * 5,
        out_specs=[any_spec] * 17 + vmem_specs(2),
        scratch_shapes=[
            pltpu.VMEM((depth, units), bf16),
            pltpu.VMEM((depth, units), bf16),
            pltpu.VMEM((units, depth), bf16),
            pltpu.VMEM((rows, units), bf16),
            pltpu.VMEM((rows, units), bf16),
            pltpu.VMEM((rows, units), bf16),
            pltpu.VMEM((rows, depth), bf16),
            pltpu.VMEM((rows, depth), bf16),
            pltpu.VMEM((rows, depth), bf16),
            pltpu.VMEM((half, units), bf16),
            pltpu.VMEM((half, units), bf16),
            pltpu.VMEM((half, 128), f32),
            pltpu.VMEM((half, depth), f32),
            pltpu.VMEM((half, depth), bf16),
            pltpu.VMEM((half, depth), bf16),
            pltpu.VMEM((rows, columns), bf16),
            pltpu.VMEM((rows, columns), bf16),
            pltpu.VMEM((half, depth), f32),
            pltpu.VMEM((2, quarter, depth), bf16),
            pltpu.VMEM((2, quarter, depth), bf16),
            pltpu.VMEM((2, quarter, depth), bf16),
            pltpu.VMEM((3, 2, quarter, depth), bf16),
            pltpu.SemaphoreType.DMA((56,)),
            pltpu.SemaphoreType.DMA((56,)),
            pltpu.SemaphoreType.DMA((32,)),
        ],
        compiler_params=pltpu.CompilerParams(
            vmem_limit_bytes=61800 << 10, collective_id=1, has_side_effects=True
        ),
        cost_estimate=pl.CostEstimate(flops=0, bytes_accessed=0, transcendentals=0),
    )(pieces, w_out, g_attn, g_mlp, tokens, cotangent, w_gate, w_up, w_down)


class Courier:
    def __init__(self, send_sems, recv_sems, local_sems):
        self.send_sems, self.recv_sems, self.local_sems = send_sems, recv_sems, local_sems
        self.remote, self.local = 0, 0

    def send(self, source, target, peer):
        copy = pltpu.make_async_remote_copy(
            src_ref=source,
            dst_ref=target,
            send_sem=self.send_sems.at[self.remote],
            recv_sem=self.recv_sems.at[self.remote],
            device_id=peer,
            device_id_type=pl.DeviceIdType.MESH,
        )
        self.remote += 1
        copy.start()
        return copy

    def move(self, source, target):
        copy = pltpu.make_async_copy(source, target, self.local_sems.at[self.local])
        self.local += 1
        copy.start()
        return copy


def greet(peers):
    barrier = pltpu.get_barrier_semaphore()
    for peer in peers:
        pl.semaphore_signal(barrier, inc=1, device_id=peer, device_id_type=pl.DeviceIdType.MESH)
    pl.semaphore_wait(barrier, len(peers))


class Spot:
    def __init__(self):
        mp = lax.axis_index("mp")
        spot = lax.axis_index("dp")
        self.core = lax.rem(mp, 2)
        self.x = lax.rem(spot, 2)
        self.z = spot // 2
        self.z_low = lax.rem(self.z, 2)
        self.z_high = self.z // 2
        self.core_peer = {"mp": mp + 1 - 2 * self.core}
        self.y_peer = {"mp": lax.rem(mp + 2, 4)}
        self.x_peer = {"dp": spot + 1 - 2 * self.x}
        self.z_peer = {"dp": spot + 2 - 4 * self.z_low}
        self.far_peer = {"dp": lax.rem(spot + 4, 8)}
        self.ahead = [{"dp": lax.rem(spot + 2 * d, 2 * line)} for d in range(line)]
        self.all = (self.core_peer, self.y_peer, self.x_peer) + tuple(self.ahead[1:])


class Job:
    def __init__(self, spot, over_x, first, first_far, second, second_far, cut_first):
        self.operands, self.cut_first = (first, first_far, second, second_far), cut_first
        self.tile = (first if cut_first else second).shape[1] // (line * pair)
        self.spot, self.over_x = spot, over_x
        self.side = spot.x if over_x else spot.z_low
        self.partner = spot.x_peer if over_x else spot.z_peer
        self.first_peer = spot.z_peer if over_x else spot.x_peer

    def at(self, ref, index):
        block = pl.ds(pl.multiple_of(index * self.tile, self.tile), self.tile)
        return ref.at[block, :] if self.cut_first else ref.at[:, block]

    def span(self, ref, index):
        block = pl.ds(pl.multiple_of(index * 2 * self.tile, 2 * self.tile), 2 * self.tile)
        return ref.at[block, :] if self.cut_first else ref.at[:, block]

    def term(self, index):
        first, first_far, second, second_far = self.operands
        block = pl.ds(pl.multiple_of(index * self.tile, self.tile), self.tile)
        if self.cut_first:
            return dot_t(first[:, block], second[...]) + dot_t(first_far[:, block], second_far[...])
        return dot_t(first[...], second[:, block]) + dot_t(first_far[...], second_far[:, block])

    def block_of(self, high, index):
        if self.over_x:
            return (2 * high + self.spot.z_low) * pair + index
        return (2 * high + index) * pair + self.spot.x

    def make_half(self, target, high):
        @pl.loop(0, 2)
        def _(i):
            if self.over_x:
                index = (2 * high + 1 - self.spot.z_low) * pair + i
            else:
                index = (2 * high + i) * pair + 1 - self.spot.x
            self.at(target, 2 * high + i)[...] = self.term(index).astype(jnp.bfloat16)

    def send_half(self, mail, target, remote, high):
        return mail.send(self.span(target, high), self.span(remote, high), self.first_peer)

    def start_first(self, mail, target, remote):
        copies = []
        for high in (1 - self.spot.z_high, self.spot.z_high):
            self.make_half(target, high)
            copies.append(self.send_half(mail, target, remote, high))
        return copies

    def second_term(self, arrived, target, i):
        total = self.term(self.block_of(1 - self.spot.z_high, i))
        total = total + self.at(arrived, i)[...].astype(jnp.float32)
        self.at(target, i)[...] = total.astype(jnp.bfloat16)

    def second_terms(self, arrived, target):
        @pl.loop(0, 2)
        def _(i):
            self.second_term(arrived, target, i)

    def own_term(self, side, arrived):
        total = self.term(self.block_of(self.spot.z_high, side))
        return total + self.at(arrived, side)[...].astype(jnp.float32)


def middle_kernel(
    grad_queries_in,
    near_in,
    far,
    q_raw,
    k_raw,
    factors,
    cosines,
    sines,
    gq,
    gk,
    act,
    act_x,
    mlp,
    mlp_x,
    hidden,
    hidden_z,
    gate,
    gate_z,
    up,
    up_za,
    up_fb,
    out_own_down,
    out_r2_down,
    out_r1_gate,
    out_r1_up,
    out_r2_gate,
    out_up_zb,
    out_raw_x,
    r1_down,
    out_raw,
    out_raw_own,
    out_gain,
    act_v,
    act_zv,
    mlp_v,
    mlp_zv,
    hidden_v,
    hidden_zv,
    gate_v,
    gate_zv,
    up_v,
    up_zv,
    send_down,
    send_gate,
    send_up,
    r1_v,
    r1_own,
    s2_v,
    own_v,
    r1_gate_v,
    s2_gate,
    grad_queries,
    near,
    far_in,
    sums,
    query_home,
    pair_home,
    scaled,
    raw_far,
    inner,
    inner_core,
    inner_y,
    send_sems,
    recv_sems,
    local_sems,
):
    f32 = jnp.float32
    bf16 = jnp.bfloat16
    spot = Spot()
    mail = Courier(send_sems, recv_sems, local_sems)
    count, width = cosines.shape
    columns = line * width
    depth = mlp_v.shape[1]
    half = act_v.shape[1]
    own_half = pl.ds(pl.multiple_of(spot.z_low * half, half), half)
    x_half = pl.ds(pl.multiple_of(spot.x * half, half), half)
    loads = [
        mail.move(act.at[:, x_half], act_v),
        mail.move(act_x, act_zv),
        mail.move(mlp, mlp_v),
        mail.move(mlp_x, mlp_zv),
        mail.move(hidden, hidden_v),
        mail.move(hidden_z, hidden_zv),
        mail.move(gate.at[:, own_half], gate_v),
        mail.move(gate_z, gate_zv),
        mail.move(up.at[:, own_half], up_v),
        mail.move(up_za, up_zv.at[: count // 2]),
    ]
    small_loads = [mail.move(grad_queries_in, grad_queries), mail.move(near_in, near)]
    greet(spot.all)
    far_copy = mail.send(far, far_in, spot.x_peer)
    my_head = pl.ds(pl.multiple_of(spot.z * width, width), width)
    for load in small_loads:
        load.wait()
    query_copies = [
        mail.send(grad_queries.at[d], query_home.at[:, my_head], spot.ahead[line - d])
        for d in range(1, line)
    ]
    up_copy = mail.send(up_fb, up_zv.at[count // 2 :], spot.z_peer)
    query_home[:, my_head] = grad_queries[0]
    for load in loads[:4]:
        load.wait()
    down = Job(spot, True, act_v, act_zv, mlp_v, mlp_zv, False)
    down_first = down.start_first(mail, send_down, r1_down)
    for load in loads[4:]:
        load.wait()
    gates = Job(spot, False, hidden_v, hidden_zv, gate_v, gate_zv, True)
    both = (1 - spot.z_high, spot.z_high)
    for high in both:
        gates.make_half(send_gate, high)
    far_copy.wait()
    gate_first = [gates.send_half(mail, send_gate, out_r1_gate, high) for high in both]
    sums[...] = (near[...].astype(f32) + far_in[...].astype(f32)).astype(bf16)
    pair_copies = [
        mail.send(sums.at[d], pair_home.at[:, :, my_head], spot.ahead[line - d])
        for d in range(1, line)
    ]
    pair_home[:, :, my_head] = sums[0]
    up_copy.wait()
    keep_up = mail.move(up_zv.at[count // 2 :], out_up_zb)
    ups = Job(spot, False, hidden_v, hidden_zv, up_v, up_zv, True)
    up_first = ups.start_first(mail, send_up, out_r1_up)

    down_first[0].wait()
    down_load = mail.move(down.span(r1_down, 1 - spot.z_high), r1_v)
    down_load.wait()
    down.second_terms(r1_v, s2_v)
    second_copy = mail.send(s2_v, out_r2_down, spot.far_peer)
    gate_first[0].wait()
    gate_load = mail.move(gates.span(out_r1_gate, 1 - spot.z_high), r1_gate_v)
    gate_load.wait()
    gates.second_terms(r1_gate_v, s2_gate)
    gate_second = mail.send(s2_gate, out_r2_gate, spot.far_peer)
    for copy in query_copies + pair_copies:
        copy.wait()

    def column(row):
        return jnp.broadcast_to(row, (width, count)).T

    sources = ((query_home, None, q_raw, gq), (pair_home, 0, k_raw, gk))
    factor_columns = [column(factors[which : which + 1, :]) for which in range(2)]
    for which, (home, slot, raw, gain) in enumerate(sources):
        inner_sum = jnp.zeros((count, width), f32)
        for h in range(line):
            cut = slice(h * width, (h + 1) * width)
            part = (home[:, cut] if slot is None else home[slot, :, cut]).astype(f32)
            back = part * cosines[...] - pltpu.roll(part, width // 2, 1) * sines[...]
            normed = raw[:, cut] * factor_columns[which]
            out_gain[which : which + 1, cut] = jnp.sum(back * normed, axis=0, keepdims=True)
            value = back * gain[:, cut]
            scaled[which, :, cut] = value
            inner_sum = inner_sum + value * normed
        inner[which : which + 1, :] = jnp.sum(inner_sum.T, axis=0, keepdims=True)
    core_copy = mail.send(inner, inner_core, spot.core_peer)
    core_copy.wait()
    arrived = inner_core[...]
    quarter = count // 4
    cuts = [arrived[:, i * quarter : (i + 1) * quarter] for i in (1, 0, 3, 2)]
    chip = inner[...] + jnp.concatenate(cuts, axis=1)
    inner[...] = chip
    y_copy = mail.send(inner, inner_y, spot.y_peer)
    y_copy.wait()
    inner_all = (chip + inner_y[...]) / depth
    for which, (home, slot, raw, gain) in enumerate(sources):
        inner_column = column(inner_all[which : which + 1, :])
        for h in range(line):
            cut = slice(h * width, (h + 1) * width)
            normed = raw[:, cut] * factor_columns[which]
            value = factor_columns[which] * (scaled[which, :, cut] - normed * inner_column)
            base = which * columns + h * width
            out_raw[:, base : base + width] = value.astype(bf16)
    out_raw[:, 2 * columns :] = pair_home[1]
    part_width = columns // 2
    for which in range(3):
        cut = slice(which * part_width, (which + 1) * part_width)
        base = which * columns

        def side(index):
            start = pl.multiple_of(base + index * part_width, part_width)
            return out_raw[:, pl.ds(start, part_width)]

        out_raw_own[:, cut] = side(spot.x)
        raw_far[:, cut] = side(1 - spot.x)
    raw_copy = mail.send(raw_far, out_raw_x, spot.x_peer)

    down_first[1].wait()
    own_load = mail.move(down.span(r1_down, spot.z_high), r1_own)
    own_load.wait()

    @pl.loop(0, 2)
    def _(i):
        down.at(own_v, i)[...] = down.own_term(i, r1_own)

    keep_own = mail.move(own_v, out_own_down)
    for copy in (keep_up, gate_second, gate_first[1], *up_first, raw_copy, second_copy, keep_own):
        copy.wait()


def middle(small, large):
    f32 = jnp.float32
    bf16 = jnp.bfloat16
    grad_queries, near, far, q_raw = small[:4]
    act, act_x, grad_mlp = large[:3]
    _, count, width = grad_queries.shape
    columns = line * width
    depth = grad_mlp.shape[1]
    units = act.shape[1]
    half = units // 2
    cut = depth // 2
    any_spec = pl.BlockSpec(memory_space=pl.ANY)
    shape = jax.ShapeDtypeStruct
    return pl.pallas_call(
        middle_kernel,
        in_specs=[pl.BlockSpec(memory_space=pltpu.HBM)] * 3 + vmem_specs(7) + [any_spec] * 11,
        out_specs=[any_spec] * 8 + vmem_specs(3),
        out_shape=[
            shape((half, cut // 2), f32),
            shape((half, cut // 2), bf16),
            shape((cut, half), bf16),
            shape((cut, half), bf16),
            shape((cut // 2, half), bf16),
            shape((count // 2, half), bf16),
            shape((count, 3 * columns // 2), bf16),
            shape((half, cut), bf16),
            shape((count, 3 * columns), bf16),
            shape((count, 3 * columns // 2), bf16),
            shape((2, columns), f32),
        ],
        scratch_shapes=[
            pltpu.VMEM((count, half), bf16),
            pltpu.VMEM((count, half), bf16),
            pltpu.VMEM((count, depth), bf16),
            pltpu.VMEM((count, depth), bf16),
            pltpu.VMEM((count, depth), bf16),
            pltpu.VMEM((count, depth), bf16),
            pltpu.VMEM((count, half), bf16),
            pltpu.VMEM((count, half), bf16),
            pltpu.VMEM((count, half), bf16),
            pltpu.VMEM((count, half), bf16),
            pltpu.VMEM((half, cut), bf16),
            pltpu.VMEM((cut, half), bf16),
            pltpu.VMEM((cut, half), bf16),
            pltpu.VMEM((half, cut // 2), bf16),
            pltpu.VMEM((half, cut // 2), bf16),
            pltpu.VMEM((half, cut // 2), bf16),
            pltpu.VMEM((half, cut // 2), f32),
            pltpu.VMEM((cut // 2, half), bf16),
            pltpu.VMEM((cut // 2, half), bf16),
            pltpu.VMEM(grad_queries.shape, bf16),
            pltpu.VMEM(near.shape, bf16),
            pltpu.VMEM(near.shape, bf16),
            pltpu.VMEM(near.shape, bf16),
            pltpu.VMEM((count, columns), bf16),
            pltpu.VMEM((2, count, columns), bf16),
            pltpu.VMEM((2, count, columns), f32),
            pltpu.VMEM((count, 3 * columns // 2), bf16),
            pltpu.VMEM((2, count), f32),
            pltpu.VMEM((2, count), f32),
            pltpu.VMEM((2, count), f32),
            pltpu.SemaphoreType.DMA((28,)),
            pltpu.SemaphoreType.DMA((28,)),
            pltpu.SemaphoreType.DMA((28,)),
        ],
        compiler_params=pltpu.CompilerParams(
            vmem_limit_bytes=60 << 20, collective_id=3, has_side_effects=True
        ),
    )(*small, *large)


def last_kernel(
    raw,
    raw_own,
    raw_x,
    wide,
    narrow,
    attended,
    hidden,
    hidden_z,
    gate,
    gate_z,
    up,
    up_za,
    up_zb,
    attn,
    tokens,
    tokens_x,
    own_down,
    r2_down,
    r1_gate,
    r1_up,
    r2_gate_in,
    w_query,
    w_key,
    w_value,
    grad_hidden,
    *refs,
):
    outs, refs = refs[:13], refs[13:]
    near_down, near_gate, near_up, near_raw, near_out = outs[:5]
    far_down, far_gate, far_up, far_raw, far_out = outs[5:10]
    out_tokens, r1_raw, r1_out = outs[10:]
    out_wide, out_narrow = refs[:2]
    (
        hidden_v,
        hidden_zv,
        gate_v,
        gate_zv,
        up_v,
        up_zv,
        tokens_v,
        tokens_xv,
        attn_v,
        attn_xv,
        heads_v,
        heads_far,
        heads_xv,
        send_raw,
        send_out,
        r1_wide,
        r1_raw_v,
        r1_out_v,
        s2_up,
        s2_raw,
        s2_out,
        r2_gate,
        r2_up,
        r2_raw,
        r2_out,
        own_down_v,
        r2_down_v,
        fin_down,
        fin_gate,
        fin_up,
        fin_raw,
        fin_out,
        keep_down,
        keep_gate,
        keep_up,
        keep_raw,
        keep_out,
        weight_v,
        total,
        part_send,
        part_recv,
        y_send,
        y_recv,
        hidden_own,
        token_keep,
        wide_core,
        wide_x,
        narrow_x,
        wide_z,
        narrow_z,
        send_sems,
        recv_sems,
        local_sems,
    ) = refs[2:]
    f32 = jnp.float32
    bf16 = jnp.bfloat16
    spot = Spot()
    mail = Courier(send_sems, recv_sems, local_sems)
    rows_all = tokens_v.shape[0]
    rows = rows_all // 2
    count = rows // 2
    half = gate_v.shape[1]
    own_half = pl.ds(pl.multiple_of(spot.z_low * half, half), half)
    heads_half = heads_v.shape[1]
    side_heads = lambda side: pl.ds(pl.multiple_of(side * heads_half, heads_half), heads_half)
    own = lambda s: pl.ds(s * rows, count)
    other = lambda s: pl.ds(s * rows + count, count)
    both = lambda s: pl.ds(s * rows, rows)
    mine = lambda s: pl.ds(s * count, count)

    token_loads = [mail.move(tokens_x, tokens_xv)]
    for s in range(2):
        for part, place in ((0, spot.core), (1, 1 - spot.core)):
            start = pl.multiple_of(place * rows + s * count, count)
            target = tokens_v.at[pl.ds(s * rows + part * count, count)]
            token_loads.append(mail.move(tokens.at[pl.ds(start, count)], target))
    attn_load = mail.move(attn, attn_v)
    r1_loads = []
    first_loads = [mail.move(hidden, hidden_v), mail.move(hidden_z, hidden_zv)]
    gate_loads = [mail.move(gate.at[:, own_half], gate_v), mail.move(gate_z, gate_zv)]
    up_loads = [mail.move(up.at[:, own_half], up_v), mail.move(up_za, up_zv.at[:rows]), mail.move(up_zb, up_zv.at[rows:])]
    ups = Job(spot, False, hidden_v, hidden_zv, up_v, up_zv, True)
    gates = Job(spot, False, hidden_v, hidden_zv, gate_v, gate_zv, True)
    raws = Job(spot, True, tokens_v, tokens_xv, raw_own, raw_x, True)
    outs_job = Job(spot, True, heads_v, heads_xv, attn_v, attn_xv, False)
    gate_second = mail.move(r2_gate_in, r2_gate)
    gate_own = mail.move(gates.span(r1_gate, spot.z_high), r1_wide.at[1])
    up_second = mail.move(ups.span(r1_up, 1 - spot.z_high), r1_wide.at[2])
    up_own = mail.move(ups.span(r1_up, spot.z_high), r1_wide.at[3])
    greet(spot.all)
    wide_copy = mail.send(wide, wide_core, spot.core_peer)
    attn_load.wait()
    attn_copies = [
        mail.send(attn_v.at[own(s)], attn_xv.at[own(s)], spot.x_peer) for s in range(2)
    ]
    heads_far[...] = attended[:, side_heads(1 - spot.x)]
    heads_v[...] = attended[:, side_heads(spot.x)]
    heads_copy = mail.send(heads_far, heads_xv, spot.x_peer)
    for load in token_loads:
        load.wait()
    raw_first = raws.start_first(mail, send_raw, r1_raw)
    wide_copy.wait()
    out_wide[...] = wide[...] + wide_core[...]
    out_narrow[...] = narrow[...]
    wide_x_copy = mail.send(out_wide, wide_x, spot.x_peer)
    narrow_x_copy = mail.send(out_narrow, narrow_x, spot.x_peer)

    for load in (*first_loads, *up_loads, up_second):
        load.wait()
    ups.second_terms(r1_wide.at[2], s2_up)
    second_up = mail.send(s2_up, r2_up, spot.far_peer)

    for s in range(2):
        attn_copies[s].wait()
    attn_core = [
        mail.send(attn_xv.at[own(s)], attn_xv.at[other(s)], spot.core_peer) for s in range(2)
    ]
    for copy in attn_core:
        copy.wait()
    heads_copy.wait()
    out_first = outs_job.start_first(mail, send_out, r1_out)

    raw_first[0].wait()
    raw_load = mail.move(raws.span(r1_raw, 1 - spot.z_high), r1_raw_v.at[0])
    raw_load.wait()
    raws.second_terms(r1_raw_v.at[0], s2_raw)
    second_raw = mail.send(s2_raw, r2_raw, spot.far_peer)
    input_weights = (w_query, w_key, w_value)
    columns = w_query.shape[1]
    flying = {}
    for which, source in enumerate(input_weights):
        load = mail.move(source, weight_v)
        load.wait()
        for s in range(2):
            term = dot_nt(raw[both(s), which * columns : (which + 1) * columns], weight_v[...])
            total[both(s), :] = term if which == 0 else total[both(s), :] + term
    for s in range(2):
        part_send[s] = total[other(s), :].astype(bf16)
        flying["core", s] = mail.send(part_send.at[s], part_recv.at[s], spot.core_peer)
    hidden_load = mail.move(grad_hidden, hidden_own)
    for s in range(2):
        flying["core", s].wait()
        y_send[s] = (total[own(s), :] + part_recv[s].astype(f32)).astype(bf16)
        flying["y", s] = mail.send(y_send.at[s], y_recv.at[s], spot.y_peer)

    wide_x_copy.wait()
    narrow_x_copy.wait()
    out_wide[...] = out_wide[...] + wide_x[...]
    out_narrow[...] = out_narrow[...] + narrow_x[...]
    near_copies, far_copies = [], []

    def finish(job, value_of, fin, far, keep, target):
        fin[...] = value_of(1 - job.side).astype(bf16)
        far_copies.append(mail.send(fin, far, job.partner))
        keep[...] = value_of(job.side)
        near_copies.append(mail.move(keep, target))

    down_loads = [mail.move(own_down, own_down_v), mail.move(r2_down, r2_down_v)]
    for load in down_loads:
        load.wait()
    down = outs_job
    finish(
        down,
        lambda side: down.at(own_down_v, side)[...] + down.at(r2_down_v, side)[...].astype(f32),
        fin_down,
        far_down,
        keep_down,
        near_down,
    )

    out_first[0].wait()
    out_load = mail.move(outs_job.span(r1_out, 1 - spot.z_high), r1_out_v.at[0])
    out_load.wait()
    outs_job.second_terms(r1_out_v.at[0], s2_out)
    second_out = mail.send(s2_out, r2_out, spot.far_peer)
    raw_first[1].wait()
    out_first[1].wait()
    own_loads = [
        mail.move(raws.span(r1_raw, spot.z_high), r1_raw_v.at[1]),
        mail.move(outs_job.span(r1_out, spot.z_high), r1_out_v.at[1]),
    ]
    for load in own_loads:
        load.wait()
    def final_of(job, r1_own, r2):
        return lambda side: job.own_term(side, r1_own) + job.at(r2, side)[...].astype(f32)

    for load in (*gate_loads, gate_own, gate_second):
        load.wait()
    finish(gates, final_of(gates, r1_wide.at[1], r2_gate), fin_gate, far_gate, keep_gate, near_gate)

    hidden_load.wait()
    for s in range(2):
        flying["y", s].wait()
        value = y_send[s].astype(f32) + y_recv[s].astype(f32)
        token_keep[mine(s), :] = (hidden_own[mine(s), :] + value).astype(bf16)
        home = pl.ds(pl.multiple_of(spot.core * rows + s * count, count), count)
        flying["keep", s] = mail.move(token_keep.at[mine(s)], out_tokens.at[home])
        flying["tokens", s] = mail.send(
            token_keep.at[mine(s)], out_tokens.at[home], spot.core_peer
        )
    gain_copies = []
    for d in range(1, line):
        gain_copies.append(mail.send(out_wide, wide_z.at[d - 1], spot.ahead[d]))
        gain_copies.append(mail.send(out_narrow, narrow_z.at[d - 1], spot.ahead[d]))

    up_own.wait()
    second_up.wait()
    finish(ups, final_of(ups, r1_wide.at[3], r2_up), fin_up, far_up, keep_up, near_up)
    second_raw.wait()
    finish(raws, final_of(raws, r1_raw_v.at[1], r2_raw), fin_raw, far_raw, keep_raw, near_raw)
    second_out.wait()
    finish(
        outs_job, final_of(outs_job, r1_out_v.at[1], r2_out), fin_out, far_out, keep_out, near_out
    )
    for copy in gain_copies:
        copy.wait()
    for d in range(1, line):
        out_wide[...] = out_wide[...] + wide_z[d - 1]
        out_narrow[...] = out_narrow[...] + narrow_z[d - 1]
    for s in range(2):
        flying["keep", s].wait()
        flying["tokens", s].wait()
    for copy in near_copies + far_copies:
        copy.wait()


def last(small, large):
    f32 = jnp.float32
    bf16 = jnp.bfloat16
    raw, raw_own, raw_x, wide, narrow, attended = small
    hidden, gate = large[0], large[2]
    count, depth = hidden.shape
    units = gate.shape[1]
    half = units // 2
    block = depth // (line * pair)
    columns = attended.shape[1]
    heads_half = columns // 2
    raw_half = raw_own.shape[1]
    rows = count // 2
    any_spec = pl.BlockSpec(memory_space=pl.ANY)
    shape = jax.ShapeDtypeStruct
    vmem = lambda *size: pltpu.VMEM(size, bf16)
    wide_vmem = lambda *size: pltpu.VMEM(size, f32)
    return pl.pallas_call(
        last_kernel,
        in_specs=vmem_specs(6) + [any_spec] * len(large),
        out_specs=[any_spec] * 13 + vmem_specs(2),
        out_shape=[
            shape((half, block), f32),
            shape((block, half), f32),
            shape((block, half), f32),
            shape((block, raw_half), f32),
            shape((heads_half, block), f32),
            shape((half, block), bf16),
            shape((block, half), bf16),
            shape((block, half), bf16),
            shape((block, raw_half), bf16),
            shape((heads_half, block), bf16),
            shape((count, depth), bf16),
            shape((line * block, raw_half), bf16),
            shape((heads_half, line * block), bf16),
            shape(wide.shape, f32),
            shape(narrow.shape, f32),
        ],
        scratch_shapes=[
            vmem(count, depth),
            vmem(count, depth),
            vmem(count, half),
            vmem(count, half),
            vmem(count, half),
            vmem(count, half),
            vmem(count, depth),
            vmem(count, depth),
            vmem(count, depth),
            vmem(count, depth),
            vmem(count, heads_half),
            vmem(count, heads_half),
            vmem(count, heads_half),
            vmem(line * block, raw_half),
            vmem(heads_half, line * block),
            vmem(4, 2 * block, half),
            vmem(2, 2 * block, raw_half),
            vmem(2, heads_half, 2 * block),
            vmem(2 * block, half),
            vmem(2 * block, raw_half),
            vmem(heads_half, 2 * block),
            vmem(2 * block, half),
            vmem(2 * block, half),
            vmem(2 * block, raw_half),
            vmem(heads_half, 2 * block),
            wide_vmem(half, 2 * block),
            vmem(half, 2 * block),
            vmem(half, block),
            vmem(block, half),
            vmem(block, half),
            vmem(block, raw_half),
            vmem(heads_half, block),
            wide_vmem(half, block),
            wide_vmem(block, half),
            wide_vmem(block, half),
            wide_vmem(block, raw_half),
            wide_vmem(heads_half, block),
            vmem(depth, columns),
            wide_vmem(count, depth),
            vmem(2, rows // 2, depth),
            vmem(2, rows // 2, depth),
            vmem(2, rows // 2, depth),
            vmem(2, rows // 2, depth),
            wide_vmem(rows, depth),
            vmem(rows, depth),
            wide_vmem(*wide.shape),
            wide_vmem(*wide.shape),
            wide_vmem(*narrow.shape),
            wide_vmem(line - 1, *wide.shape),
            wide_vmem(line - 1, *narrow.shape),
            pltpu.SemaphoreType.DMA((48,)),
            pltpu.SemaphoreType.DMA((48,)),
            pltpu.SemaphoreType.DMA((40,)),
        ],
        compiler_params=pltpu.CompilerParams(
            vmem_limit_bytes=61800 << 10, collective_id=4, has_side_effects=True
        ),
    )(*small, *large)


def join_kernel(*refs):
    nears, fars, whole = refs[:5], refs[5:10], refs[10:12]
    outs, refs = refs[12:21], refs[21:]
    stages, far_parts, whole_parts, sems = refs[:7], refs[7:12], refs[12:14], refs[14]
    spot = lax.axis_index("dp")
    x = lax.rem(spot, 2)
    z_low = lax.rem(spot // 2, 2)
    started = []

    def move(source, target):
        copy = pltpu.make_async_copy(source, target, sems.at[len(started)])
        started.append(copy)
        copy.start()
        return copy

    width = nears[3].shape[1] // 3
    plan = [(4, 1, None, z_low, 1), (5, 2, None, z_low, 1), (6, 0, None, x, 0)]
    plan += [(i, 3, slice(i * width, (i + 1) * width), x, 1) for i in range(3)]
    plan += [(3, 4, None, x, 0)]

    def half(ref, side, axis):
        size = ref.shape[axis] // 2
        cut = pl.ds(pl.multiple_of(side * size, size), size)
        return ref.at[cut, :] if axis == 0 else ref.at[:, cut]

    whole_loads = [move(source, part) for source, part in zip(whole, whole_parts)]
    far_loads, near_loads = {}, {}
    for result, source, columns, side, axis in plan:
        if source not in far_loads:
            far_loads[source] = move(fars[source], far_parts[source])
        near = nears[source] if columns is None else nears[source].at[:, columns]
        near_loads[result] = move(near, half(stages[result], side, axis))
    leaving = []
    for load, part, out in zip(whole_loads, whole_parts, outs[:2]):
        load.wait()
        leaving.append(move(part, out))
    waited = set()
    for result, source, columns, side, axis in plan:
        if source not in waited:
            far_loads[source].wait()
            waited.add(source)
        far = far_parts[source][...] if columns is None else far_parts[source][:, columns]
        half(stages[result], 1 - side, axis)[...] = far.astype(jnp.float32)
        near_loads[result].wait()
        leaving.append(move(stages[result], outs[2 + result]))
    for copy in leaving:
        copy.wait()


def join(nears, fars, output, tokens):
    f32 = jnp.float32
    shape = jax.ShapeDtypeStruct
    any_spec = pl.BlockSpec(memory_space=pl.ANY)
    down, gate, up, raw, out = [part.shape for part in nears]
    third = (raw[0], 2 * raw[1] // 3)
    results = [third] * 3 + [
        (2 * out[0], out[1]),
        (gate[0], 2 * gate[1]),
        (up[0], 2 * up[1]),
        (2 * down[0], down[1]),
    ]
    return pl.pallas_call(
        join_kernel,
        in_specs=[any_spec] * 12,
        out_specs=[any_spec] * 9,
        out_shape=[shape(output.shape, output.dtype), shape(tokens.shape, tokens.dtype)]
        + [shape(size, f32) for size in results],
        scratch_shapes=[pltpu.VMEM(size, f32) for size in results]
        + [pltpu.VMEM(part.shape, part.dtype) for part in (*fars, output, tokens)]
        + [pltpu.SemaphoreType.DMA((24,))],
        compiler_params=pltpu.CompilerParams(vmem_limit_bytes=60 << 20),
    )(*nears, *fars, output, tokens)


def on_device_lines(
    tokens,
    cotangent,
    doc_ids,
    row_ids,
    offsets,
    w_query,
    w_key,
    w_value,
    w_output,
    w_gate,
    w_up,
    w_down,
    gain_query,
    gain_key,
    gain_attn,
    gain_mlp,
):
    f32 = jnp.float32
    bf16 = jnp.bfloat16
    row_count, model_width = tokens.shape
    heads_here, head_width = gain_query.shape
    local_width = heads_here * head_width
    half_rows = row_count // 2
    key_rows = row_count * line * pair
    spot = lax.axis_index("dp")
    z, x = spot // pair, lax.rem(spot, pair)
    z_high, z_low = z // 2, lax.rem(z, 2)
    core = lax.rem(lax.axis_index("mp"), 2)
    place = jnp.stack([core, z, z_low, z_high, x]).astype(jnp.int32)

    quarter = row_count // 4

    def own_rows(value):
        return lax.dynamic_slice_in_dim(value, core * half_rows, half_rows, 0)

    def other_rows(value):
        return lax.dynamic_slice_in_dim(value, (1 - core) * half_rows, half_rows, 0)

    def reorder(value):
        return join_parts(own_rows(value), other_rows(value))

    def restore(own, other):
        whole = jnp.zeros((row_count,) + own.shape[1:], own.dtype)
        whole = lax.dynamic_update_slice_in_dim(whole, own, core * half_rows, 0)
        return lax.dynamic_update_slice_in_dim(whole, other, (1 - core) * half_rows, 0)

    def half_of(value, side):
        width = value.shape[1] // 2
        return lax.dynamic_slice_in_dim(value, side * width, width, 1)

    positions = reorder(offsets[0] + jnp.arange(row_count, dtype=jnp.int32))
    labels = reorder(row_ids[0] * key_rows + doc_ids)
    freqs = rope_base ** (-jnp.arange(0, head_width // 2, dtype=f32) * 2.0 / head_width)
    angles = positions.astype(f32)[:, None] * freqs[None, :]
    cosines, sines = jnp.cos(angles), jnp.sin(angles)
    cosines = jnp.concatenate([cosines, cosines], axis=1)
    sines = jnp.concatenate([-sines, sines], axis=1)
    g_query = gain_query.reshape(1, local_width)
    g_key = gain_key.reshape(1, local_width)
    spots = jnp.stack([labels, positions]).astype(f32)
    queries, pairs, notes, q_raw, k_raw = project(
        tokens, w_query, w_key, w_value, g_query, g_key, cosines, sines, spots
    )
    factors = notes[0, :2]
    codes = notes[:, 2, :].astype(jnp.int32) * key_rows + notes[:, 3, :].astype(jnp.int32)
    lows = notes[:line, 2, :].astype(jnp.int32) * key_rows
    live = (
        (jnp.min(codes, axis=1)[None, :] <= jnp.max(codes[:line], axis=1)[:, None])
        & (jnp.max(codes, axis=1)[None, :] >= jnp.min(lows, axis=1)[:, None])
    ).astype(jnp.int32)

    turned, log_total, queries_n, code_rows, attended_out = attend(
        key_rows, live, notes, queries, pairs
    )

    def gather_heads(home):
        twice = jnp.concatenate(home + home, axis=1)
        return lax.dynamic_slice_in_dim(
            twice, lax.rem(line - z, line) * head_width, local_width, 1
        )

    def send_home(pieces):
        return [pieces[0]] + [line_shift(pieces[d], line - d) for d in range(1, line)]

    tokens_in = reorder(tokens)
    g_attn = gain_attn.reshape(1, model_width)
    g_mlp = gain_mlp.reshape(1, model_width)
    (
        attended_low,
        tokens_x,
        output,
        hidden_low,
        hidden_z,
        act_low,
        act_x,
        grad_mlp,
        grad_mlp_x,
        grad_gate,
        _,
        grad_gate_z,
        grad_up,
        grad_up_fa,
        grad_up_fb,
        grad_attn,
        grads,
        grad_hidden,
        wide_gains,
    ) = block(
        attended_out, w_output, g_attn, g_mlp, tokens, cotangent, w_gate, w_up, w_down
    )
    grad_up_za = line_flip(grad_up_fa, 1)
    back = attend_back(
        key_rows, live, notes, code_rows, queries_n, pairs, turned, log_total, grads
    )
    (
        own_down,
        r2_down,
        r1_gate,
        r1_up,
        r2_gate,
        grad_up_zb,
        raw_x,
        _,
        raw,
        raw_own,
        narrow_gains,
    ) = middle(
        (*back, q_raw, k_raw, factors, cosines, sines, g_query, g_key),
        (
            act_low,
            act_x,
            grad_mlp,
            grad_mlp_x,
            hidden_low,
            hidden_z,
            grad_gate,
            grad_gate_z,
            grad_up,
            grad_up_za,
            grad_up_fb,
        ),
    )
    results = last(
        (raw, raw_own, raw_x, wide_gains, narrow_gains, attended_low),
        (
            hidden_low,
            hidden_z,
            grad_gate,
            grad_gate_z,
            grad_up,
            grad_up_za,
            grad_up_zb,
            grad_attn,
            tokens,
            tokens_x,
            own_down,
            r2_down,
            r1_gate,
            r1_up,
            r2_gate,
            w_query,
            w_key,
            w_value,
            grad_hidden,
        ),
    )
    joined = join(results[:5], results[5:10], output, results[10])
    wide, narrow = results[13:]
    gains = jnp.concatenate([wide.reshape(2 * model_width), narrow.reshape(2 * local_width)])
    piece = head_width // (line * pair)

    def gain_piece(start, rows):
        part = gains[start : start + rows * head_width].reshape(rows, head_width)
        return lax.dynamic_slice_in_dim(part, spot * piece, piece, 1)

    all_heads = model_width // head_width
    return (
        *joined,
        gain_piece(2 * model_width, heads_here),
        gain_piece(2 * model_width + local_width, heads_here),
        gain_piece(0, all_heads),
        gain_piece(model_width, all_heads),
    )


def solution(mesh):
    tuned = mesh.shape["dp"] == line * pair and mesh.shape["mp"] == 4
    body = on_device_lines if tuned else on_device_general
    return jax.shard_map(
        body,
        mesh=mesh,
        in_specs=(
            P("dp", None),
            P("dp", None),
            P("dp"),
            P("dp"),
            P("dp"),
            P(None, "mp"),
            P(None, "mp"),
            P(None, "mp"),
            P("mp", None),
            P(None, "mp"),
            P(None, "mp"),
            P("mp", None),
            P("mp", None),
            P("mp", None),
            P(),
            P(),
        ),
        out_specs=(
            P("dp", None),
            P("dp", None),
            P("dp", "mp"),
            P("dp", "mp"),
            P("dp", "mp"),
            P("mp", "dp"),
            P("dp", "mp"),
            P("dp", "mp"),
            P("mp", "dp"),
            P("mp", "dp"),
            P("mp", "dp"),
            P(None, "dp"),
            P(None, "dp"),
        ),
        check_vma=False,
    )
```
